32 devices in a mesh: batch: 8 (over z, x), head: 4 (over y, core).
Axes of the slice: x: 2, y: 2, z: 4, core: 2. Of those that a mesh axis runs over, the one named last changes fastest.
Arguments:
- tokens: bfloat16 [16, 1024, 768], P('batch', 'head'), may hold values from -6 to 6
- memory: bfloat16 [16, 1024, 768], P('batch', 'head'), may hold values from -6 to 6
- cotangent: bfloat16 [16, 1024, 768], P('batch', 'head'), may hold values from -6 to 6
- target_segments: int32 [16, 1024], P('batch'), may hold values from 0 to 7, as said below
- memory_segments: int32 [16, 1024], P('batch'), may hold values from -1 to 7, as said below
- self_gain: float32 [768], replicated, may hold values from 0.5 to 1.5
- self_query: bfloat16 [768, 768], P(None, 'head'), may hold values from -0.109375 to 0.109375
- self_key: bfloat16 [768, 768], P(None, 'head'), may hold values from -0.109375 to 0.109375
- self_value: bfloat16 [768, 768], P(None, 'head'), may hold values from -0.21875 to 0.21875
- self_out: bfloat16 [768, 768], replicated, may hold values from -0.875 to 0.875
- position_bias: float32 [32, 12], P(None, 'head'), may hold values from -4 to 4
- cross_gain: float32 [768], replicated, may hold values from 0.5 to 1.5
- cross_query: bfloat16 [768, 768], P(None, 'head'), may hold values from -0.109375 to 0.109375
- cross_key: bfloat16 [768, 768], P(None, 'head'), may hold values from -0.109375 to 0.109375
- cross_value: bfloat16 [768, 768], P(None, 'head'), may hold values from -0.21875 to 0.21875
- cross_out: bfloat16 [768, 768], replicated, may hold values from -0.875 to 0.875
- ff_gain: float32 [768], replicated, may hold values from 0.5 to 1.5
- ff_gate: bfloat16 [768, 2048], replicated, may hold values from -0.21875 to 0.21875
- ff_up: bfloat16 [768, 2048], replicated, may hold values from -0.21875 to 0.21875
- ff_down: bfloat16 [2048, 768], replicated, may hold values from -0.125 to 0.125
Outputs:
- layer_out: bfloat16 [16, 1024, 768], P('batch', 'head')
- tokens_grad: bfloat16 [16, 1024, 768], P('batch', 'head')
- memory_grad: bfloat16 [16, 1024, 768], P('batch', 'head')
- self_gain_grad: float32 [768], P(('batch', 'head'))
- self_query_grad: float32 [768, 768], P('batch', 'head')
- self_key_grad: float32 [768, 768], P('batch', 'head')
- self_value_grad: float32 [768, 768], P('batch', 'head')
- self_out_grad: float32 [768, 768], P(None, ('batch', 'head'))
- position_bias_grad: float32 [32, 12], P(None, 'head')
- cross_gain_grad: float32 [768], P(('batch', 'head'))
- cross_query_grad: float32 [768, 768], P('batch', 'head')
- cross_key_grad: float32 [768, 768], P('batch', 'head')
- cross_value_grad: float32 [768, 768], P('batch', 'head')
- cross_out_grad: float32 [768, 768], P(None, ('batch', 'head'))
- ff_gain_grad: float32 [768], P(('batch', 'head'))
- ff_gate_grad: float32 [768, 2048], P(None, ('batch', 'head'))
- ff_up_grad: float32 [768, 2048], P(None, ('batch', 'head'))
- ff_down_grad: float32 [2048, 768], P(None, ('batch', 'head'))
The draws below stay inside these ranges and needn't reach their ends.
Inputs may be any that keep to these rules, and one draw needn't show every extreme that they name: `target_segments`: each row is cut into aligned blocks of 512 tokens; each block is split into whole segments of 128, 256 or 512 tokens, numbered along the row from 0 without falling. The first row has segments of 128 tokens only. `memory_segments`: each row repeats its target_segments row, except that in every segment between 1 and 64 of the last tokens are padding, marked -1.
All inputs are finite; a program needn't handle non-finite values.
Results may differ from the reference program's by a relative error of at most 0.023.
The reference program's roundings to bfloat16 on the way count: a program that leaves them out, or rounds other values in their place, can miss the bound.
Values may be sent and summed in bfloat16 or wider, within the bound.
A program may use at most 384 MiB of HBM per device.

```python
import jax
import jax.numpy as jnp
import numpy as np
from jax import lax

D = 768
H = 12
DK = 64
FF = 2048
NB = 32
LEN = 1024
SEGLEN = 128
INNER = 768
ROWS = 16


START_FLAGS = np.array([[1, 0, 0, 0], [1, 0, 1, 0], [1, 0, 1, 1], [1, 1, 1, 0], [1, 1, 1, 1]], dtype=np.int32)


def unit_starts(key):
    unit_count = LEN // SEGLEN
    pattern = jax.random.randint(jax.random.fold_in(key, 7), (ROWS, unit_count // 4), 0, 5)
    pattern = pattern.at[0].set(4)
    return jnp.asarray(START_FLAGS)[pattern].reshape(ROWS, unit_count)


def draw_target_segments(key, part):
    starts = unit_starts(key)
    unit_ids = jnp.cumsum(starts, axis=1) - 1
    return jnp.repeat(unit_ids, SEGLEN, axis=1).astype(jnp.int32)


def draw_memory_segments(key, part):
    starts = unit_starts(key)
    unit_count = starts.shape[1]
    unit_ids = jnp.cumsum(starts, axis=1) - 1
    last_unit = jnp.concatenate((starts[:, 1:], jnp.ones((ROWS, 1), jnp.int32)), axis=1) == 1
    padding = jax.random.randint(jax.random.fold_in(key, 9), (ROWS, unit_count), 1, SEGLEN // 2 + 1)
    offset = jnp.arange(SEGLEN, dtype=jnp.int32)
    padded = last_unit[:, :, None] & (offset[None, None, :] >= SEGLEN - padding[:, :, None])
    token_ids = jnp.broadcast_to(unit_ids[:, :, None], padded.shape)
    return jnp.where(padded, -1, token_ids).reshape(ROWS, LEN).astype(jnp.int32)


def levels(rng, extent, shards, low, top_value):
    loudness = 1.0
    for position, blocks in shards:
        steps = jax.random.uniform(jax.random.fold_in(jax.random.fold_in(rng, 6), position), (blocks,), jnp.float32, low / len(shards), top_value / len(shards))
        loudness = loudness * jnp.repeat(jnp.exp(steps), extent[position] // blocks).reshape((-1,) + (1,) * (len(extent) - 1 - position))
    return loudness


def scatter_about(stream_key, dims, scale, limit, split=(), kind=jnp.bfloat16):
    drawn = jax.random.normal(stream_key, dims, jnp.float32) * scale
    if len(split) > 0:
        drawn = levels(stream_key, dims, split, -0.22, 0.18) * drawn
    return jnp.clip(drawn, min=-limit, max=limit).astype(kind)


def setup_inputs(seed: int = 0) -> dict:
    key_list = jax.random.split(jax.random.key(seed), 21)
    return {
        "tokens": scatter_about(key_list[0], (ROWS, LEN, D), 1.0, 6.0, ((0, 8), (1, 4))),
        "memory": scatter_about(key_list[1], (ROWS, LEN, D), 1.0, 6.0, ((0, 8), (1, 4))),
        "cotangent": scatter_about(key_list[2], (ROWS, LEN, D), 1.0, 6.0, ((0, 8), (1, 4))),
        "target_segments": draw_target_segments(jax.random.fold_in(key_list[20], 71), 0),
        "memory_segments": draw_memory_segments(jax.random.fold_in(key_list[20], 71), 0),
        "self_gain": jnp.clip(1.0 + 0.1 * jax.random.normal(key_list[5], (D,), jnp.float32), 0.5, 1.5),
        "self_query": scatter_about(key_list[6], (D, INNER), (4 * D) ** -0.5, 0.109375, ((1, 4),)),
        "self_key": scatter_about(key_list[7], (D, INNER), (4 * D) ** -0.5, 0.109375, ((1, 4),)),
        "self_value": scatter_about(key_list[8], (D, INNER), D ** -0.5, 0.21875, ((1, 4),)),
        "self_out": scatter_about(key_list[9], (INNER, D), (INNER // 16) ** -0.5, 0.875),
        "position_bias": scatter_about(key_list[10], (NB, H), 1.0, 4.0, ((1, 4),), jnp.float32),
        "cross_gain": jnp.clip(1.0 + 0.1 * jax.random.normal(key_list[11], (D,), jnp.float32), 0.5, 1.5),
        "cross_query": scatter_about(key_list[12], (D, INNER), (4 * D) ** -0.5, 0.109375, ((1, 4),)),
        "cross_key": scatter_about(key_list[13], (D, INNER), (4 * D) ** -0.5, 0.109375, ((1, 4),)),
        "cross_value": scatter_about(key_list[14], (D, INNER), D ** -0.5, 0.21875, ((1, 4),)),
        "cross_out": scatter_about(key_list[15], (INNER, D), (INNER // 16) ** -0.5, 0.875),
        "ff_gain": jnp.clip(1.0 + 0.1 * jax.random.normal(key_list[16], (D,), jnp.float32), 0.5, 1.5),
        "ff_gate": scatter_about(key_list[17], (D, FF), D ** -0.5, 0.21875),
        "ff_up": scatter_about(key_list[18], (D, FF), D ** -0.5, 0.21875),
        "ff_down": scatter_about(key_list[19], (FF, D), FF ** -0.5, 0.125),
    }


@jax.custom_vjp
def low(v):
    return lax.optimization_barrier(v.astype(jnp.bfloat16)).astype(jnp.float32)

@jax.custom_vjp
def low_back(v):
    return v

def low_keep(v):
    return (low(v), None)

def low_pass(kept, grad):
    return (grad,)

def back_keep(v):
    return (v, None)

def back_low(kept, grad):
    return (low(grad),)
low.defvjp(low_keep, low_pass)
low_back.defvjp(back_keep, back_low)
NORM_EPS = 1e-06
MASKED_SCORE = -1e+30
PRECISE = lax.Precision.HIGHEST

def bucket_edges():
    distance = np.arange(1.0, 8192.0)
    far_bucket = 16.0 + np.floor(np.log(np.maximum(distance, 16.0) / 16.0) / np.log(8.0) * 16.0)
    bucket_value = np.where(distance < 16, distance, np.minimum(far_bucket, 31.0))
    return [int(distance[np.argmax(bucket_value >= bucket_level)]) for bucket_level in range(1, 32)]

def product(left_side, right_side):
    return jnp.dot(left_side, right_side, precision=PRECISE)

def rms_norm(hidden, gain_vector):
    inv_scale = lax.rsqrt(lax.optimization_barrier(jnp.mean(hidden * hidden, axis=-1, keepdims=True)) + NORM_EPS)
    return hidden * inv_scale * gain_vector

def attend(query_heads, key_heads, value_heads, allowed, bias_heads):
    scores = jnp.einsum('qhd,khd->hqk', query_heads, key_heads, precision=PRECISE)
    scores = low_back(scores + bias_heads)
    masked = jnp.where(allowed[None], scores, MASKED_SCORE)
    weights = low(jax.nn.softmax(masked, axis=-1))
    return jnp.einsum('hqk,khd->qhd', weights, value_heads, precision=PRECISE)

def heads_of(matrix):
    return matrix.reshape(matrix.shape[0], H, DK)

def layer_row(tok_row, mem_row, target_row, memory_row, params):
    self_gain, self_query, self_key, self_value, self_out, position_bias, cross_gain, cross_query, cross_key, cross_value, cross_out, ff_gain, ff_gate, ff_up, ff_down = params
    length = tok_row.shape[0]
    positions = jnp.arange(length, dtype=jnp.int32)
    distance = positions[:, None] - positions[None, :]
    bucket_ids = jnp.zeros(distance.shape, jnp.int32)
    for edge_value in bucket_edges():
        bucket_ids = bucket_ids + (distance >= edge_value).astype(jnp.int32)
    bias_heads = jnp.transpose(position_bias[bucket_ids], (2, 0, 1))
    self_allowed = (target_row[:, None] == target_row[None, :]) & (distance >= 0)
    cross_allowed = target_row[:, None] == memory_row[None, :]
    normed_one = low(rms_norm(tok_row, self_gain))
    query_one = low(low_back(product(normed_one, self_query)))
    key_one = low(low_back(product(normed_one, self_key)))
    value_one = low(low_back(product(normed_one, self_value)))
    context_one = attend(heads_of(query_one), heads_of(key_one), heads_of(value_one), self_allowed, bias_heads)
    context_one = low(low_back(context_one.reshape(length, H * DK)))
    first_sum = tok_row + low_back(product(context_one, self_out))
    normed_two = low(rms_norm(first_sum, cross_gain))
    query_two = low(low_back(product(normed_two, cross_query)))
    key_two = low(low_back(product(mem_row, cross_key)))
    value_two = low(low_back(product(mem_row, cross_value)))
    context_two = attend(heads_of(query_two), heads_of(key_two), heads_of(value_two), cross_allowed, 0.0)
    context_two = low(low_back(context_two.reshape(length, H * DK)))
    second_sum = first_sum + low_back(product(context_two, cross_out))
    normed_three = low(rms_norm(second_sum, ff_gain))
    gate_value = low_back(product(normed_three, ff_gate))
    up_value = low_back(product(normed_three, ff_up))
    activation = low(jax.nn.gelu(gate_value, approximate=True) * up_value)
    return second_sum + product(activation, ff_down)

def reference(tokens, memory, cotangent, target_segments, memory_segments, self_gain, self_query, self_key, self_value, self_out, position_bias, cross_gain, cross_query, cross_key, cross_value, cross_out, ff_gain, ff_gate, ff_up, ff_down):
    params = tuple((weight_item.astype(jnp.float32) for weight_item in (self_gain, self_query, self_key, self_value, self_out, position_bias, cross_gain, cross_query, cross_key, cross_value, cross_out, ff_gain, ff_gate, ff_up, ff_down)))

    def one_row(grad_sums, row_items):
        tok_row, mem_row, cot_row, target_row, memory_row = row_items

        def forward(tok_in, mem_in, weight_set):
            return layer_row(tok_in, mem_in, target_row, memory_row, weight_set)
        out_row, pullback = jax.vjp(forward, tok_row.astype(jnp.float32), mem_row.astype(jnp.float32), params)
        tok_grad, mem_grad, weight_grads = pullback(cot_row.astype(jnp.float32))
        grad_sums = jax.tree.map(jnp.add, grad_sums, weight_grads)
        return (grad_sums, (out_row.astype(jnp.bfloat16), tok_grad.astype(jnp.bfloat16), mem_grad.astype(jnp.bfloat16)))
    zero_grads = tuple((jnp.zeros(weight_item.shape, jnp.float32) for weight_item in params))
    grad_sums, stacked = lax.scan(one_row, zero_grads, (tokens, memory, cotangent, target_segments, memory_segments))
    return (stacked[0], stacked[1], stacked[2], grad_sums[0], grad_sums[1], grad_sums[2], grad_sums[3], grad_sums[4], grad_sums[5], grad_sums[6], grad_sums[7], grad_sums[8], grad_sums[9], grad_sums[10], grad_sums[11], grad_sums[12], grad_sums[13], grad_sums[14])
```

```python
import jax
import jax.numpy as jnp
import numpy as np
from jax import lax
from jax.experimental import pallas as pl
from jax.experimental.pallas import tpu as pltpu
from jax.sharding import PartitionSpec as P

NORM_EPS = 1e-06
MASKED = -1e30
BLOCK = 512
TILE = 128
F32 = jnp.float32
BF16 = jnp.bfloat16


def bucket_edges():
    distance = np.arange(1.0, 8192.0)
    far_bucket = 16.0 + np.floor(np.log(np.maximum(distance, 16.0) / 16.0) / np.log(8.0) * 16.0)
    bucket_value = np.where(distance < 16, distance, np.minimum(far_bucket, 31.0))
    return [int(distance[np.argmax(bucket_value >= bucket_level)]) for bucket_level in range(1, 32)]


def bucket_one_hot(buckets):
    ids = np.zeros(2 * TILE, np.int32)
    for edge in bucket_edges():
        ids += np.arange(2 * TILE) >= edge
    assert bucket_edges()[-1] <= TILE + 1
    return (np.arange(buckets)[:, None] == ids[None, :]).astype(np.float32)


def dot(left, right):
    return lax.dot_general(left, right, (((1,), (0,)), ((), ())), preferred_element_type=F32)


def pair_view(token_major, index, heads, size):
    first = index - index % 2
    count = min(2, heads - first)
    return token_major[:, first * size : (first + count) * size], index - first, count


def spread(head_rows, place, count):
    if count == 1:
        return head_rows
    blank = jnp.zeros_like(head_rows)
    return jnp.concatenate((head_rows, blank) if place == 0 else (blank, head_rows), axis=0)


def only_lanes(pair, place, count, size):
    if count == 1:
        return pair
    lane = lax.broadcasted_iota(jnp.int32, pair.shape, 1)
    keep = lane < size if place == 0 else lane >= size
    return jnp.where(keep, pair, jnp.zeros_like(pair))


def bias_tiles(table, index, one_hot):
    column = table[:, index : index + 1]
    by_distance = jnp.sum(column * one_hot, axis=0, keepdims=True)
    wide = jnp.broadcast_to(by_distance, (TILE, 2 * TILE))
    turned = pltpu.roll(wide, 0, 1, stride=1, stride_axis=0)
    key = lax.broadcasted_iota(jnp.int32, (TILE, TILE), 0)
    query = lax.broadcasted_iota(jnp.int32, (TILE, TILE), 1)
    near = jnp.where(key <= query, turned[:, :TILE], MASKED)
    return near, turned[:, TILE:], table[table.shape[0] - 1, index]


def self_tile(scores, key_tile, query_tile, tiles, seg_ref, base):
    near, next_one, far = tiles
    if key_tile == query_tile:
        return scores + near
    same = seg_ref[base + key_tile] == seg_ref[base + query_tile]
    shift = jnp.where(same, 0.0, MASKED)
    if key_tile == query_tile - 1:
        return scores + next_one + shift
    return scores + (far + shift)


def self_forward_kernel(heads, size, seg_ref, where_ref, q_ref, k_ref, v_ref, tab_ref, hot_ref, o_ref, lse_ref):
    base = pl.program_id(1) * (BLOCK // TILE)
    keys = jnp.transpose(k_ref[0])
    table = tab_ref[0]
    for index in range(heads):
        rows = slice(index * size, (index + 1) * size)
        pair, place, count = pair_view(keys, index, heads, size)
        query = spread(q_ref[0, rows, :], place, count)
        tiles = bias_tiles(table, index, hot_ref[...])
        for half in range(2):
            end = (half + 1) * 2 * TILE
            scores = dot(pair[:end], query[:, half * 256 : (half + 1) * 256])
            columns = []
            totals = []
            for part in range(2):
                query_tile = 2 * half + part
                parts = [
                    self_tile(
                        scores[kt * TILE : (kt + 1) * TILE, part * TILE : (part + 1) * TILE],
                        kt, query_tile, tiles, seg_ref, base,
                    )
                    for kt in range(query_tile + 1)
                ]
                top = jnp.max(parts[0], axis=0, keepdims=True)
                for piece in parts[1:]:
                    top = jnp.maximum(top, jnp.max(piece, axis=0, keepdims=True))
                probs = [jnp.exp(piece - top) for piece in parts]
                total = jnp.sum(probs[0], axis=0, keepdims=True)
                for piece in probs[1:]:
                    total = total + jnp.sum(piece, axis=0, keepdims=True)
                probs = [piece.astype(BF16) for piece in probs]
                if part == 0:
                    probs.append(jnp.zeros((TILE, TILE), BF16))
                columns.append(jnp.concatenate(probs, axis=0))
                totals.append(total)
                lse_ref[0, index : index + 1, query_tile * TILE : (query_tile + 1) * TILE] = top + jnp.log(total)
            weights = jnp.concatenate(columns, axis=1)
            context = dot(v_ref[0, rows, :end], weights)
            context = context / jnp.concatenate(totals, axis=1)
            o_ref[rows, half * 256 : (half + 1) * 256] = context.astype(BF16)


def key_mask(seg_ref, base, memseg_ref, mask_ref):
    rows = jnp.transpose(jnp.broadcast_to(memseg_ref[0].astype(F32), (TILE, BLOCK)))
    for tile in range(BLOCK // TILE):
        wanted = seg_ref[base + tile].astype(F32)
        mask_ref[:, tile * TILE : (tile + 1) * TILE] = jnp.where(rows == wanted, 0.0, MASKED)


def cross_forward_kernel(heads, size, seg_ref, where_ref, q_ref, k_ref, v_ref, memseg_ref, o_ref, lse_ref, mask_ref):
    base = pl.program_id(1) * (BLOCK // TILE)
    key_mask(seg_ref, base, memseg_ref, mask_ref)
    keys = jnp.transpose(k_ref[0])
    for index in range(heads):
        rows = slice(index * size, (index + 1) * size)
        pair, place, count = pair_view(keys, index, heads, size)
        query = spread(q_ref[0, rows, :], place, count)
        for half in range(2):
            lanes = slice(half * 256, (half + 1) * 256)
            scores = dot(pair, query[:, lanes]) + mask_ref[:, lanes]
            top = jnp.max(scores, axis=0, keepdims=True)
            probs = jnp.exp(scores - top)
            total = jnp.sum(probs, axis=0, keepdims=True)
            context = dot(v_ref[0, rows, :], probs.astype(BF16)) / total
            o_ref[rows, lanes] = context.astype(BF16)
            lse_ref[0, index : index + 1, lanes] = top + jnp.log(total)


def back_common(heads, size, q_ref, k_ref, v_ref, do_ref):
    return (
        jnp.transpose(q_ref[0]),
        jnp.transpose(k_ref[0]),
        jnp.transpose(v_ref[0]),
        jnp.transpose(do_ref[...]),
    )


def store_sums(heads, size, sums, ref, start):
    wide = jnp.concatenate([s.astype(BF16) for s in sums], axis=1)
    ref[0, start : start + heads * size, :] = jnp.transpose(wide)


def grow(old, new):
    if old is None:
        return new
    shared = old.shape[0]
    if shared == new.shape[0]:
        return old + new
    return jnp.concatenate((old + new[:shared], new[shared:]), axis=0)


def self_backward_kernel(heads, size, seg_ref, where_ref, q_ref, k_ref, v_ref, o_ref, do_ref, lse_ref, tab_ref, hot_ref, d_ref, tabgrad_ref):
    block = pl.program_id(1)
    base = block * (BLOCK // TILE)
    width = heads * size
    query_tok, keys, values, grad_tok = back_common(heads, size, q_ref, k_ref, v_ref, do_ref)
    table = tab_ref[0]
    one_hot = hot_ref[...]
    key_sums, value_sums = [], []
    buckets = one_hot.shape[0]
    lane = lax.broadcasted_iota(jnp.int32, (buckets, TILE), 1)
    bucket = lax.broadcasted_iota(jnp.int32, (buckets, TILE), 0)
    table_grad = jnp.zeros((buckets, TILE), F32)
    key = lax.broadcasted_iota(jnp.int32, (TILE, TILE), 0)
    query = lax.broadcasted_iota(jnp.int32, (TILE, TILE), 1)
    for index in range(heads):
        rows = slice(index * size, (index + 1) * size)
        key_pair, place, count = pair_view(keys, index, heads, size)
        value_pair = pair_view(values, index, heads, size)[0]
        query_pair = only_lanes(pair_view(query_tok, index, heads, size)[0], place, count, size)
        grad_pair = only_lanes(pair_view(grad_tok, index, heads, size)[0], place, count, size)
        query_rows = spread(q_ref[0, rows, :], place, count)
        grad = spread(do_ref[rows, :], place, count)
        inner = jnp.sum(do_ref[rows, :].astype(F32) * o_ref[rows, :].astype(F32), axis=0, keepdims=True)
        tiles = bias_tiles(table, index, one_hot)
        key_sum = value_sum = None
        near_sum = next_sum = far_sum = None
        for half in range(2):
            end = (half + 1) * 2 * TILE
            lanes = slice(half * 256, (half + 1) * 256)
            scores = dot(key_pair[:end], query_rows[:, lanes])
            grad_probs = dot(value_pair[:end], grad[:, lanes])
            prob_columns, grad_columns = [], []
            for part in range(2):
                query_tile = 2 * half + part
                cut = slice(query_tile * TILE, (query_tile + 1) * TILE)
                here = slice(part * TILE, (part + 1) * TILE)
                total = lse_ref[0, index : index + 1, cut]
                probs, grads = [], []
                for kt in range(query_tile + 1):
                    there = slice(kt * TILE, (kt + 1) * TILE)
                    prob = jnp.exp(self_tile(scores[there, here], kt, query_tile, tiles, seg_ref, base) - total)
                    ds = prob * (grad_probs[there, here] - inner[:, cut])
                    if kt == query_tile:
                        near_sum = ds if near_sum is None else near_sum + ds
                    elif kt == query_tile - 1:
                        next_sum = ds if next_sum is None else next_sum + ds
                    else:
                        far_sum = ds if far_sum is None else far_sum + ds
                    probs.append(prob.astype(BF16))
                    grads.append(ds.astype(BF16))
                if part == 0:
                    probs.append(jnp.zeros((TILE, TILE), BF16))
                    grads.append(jnp.zeros((TILE, TILE), BF16))
                prob_columns.append(jnp.concatenate(probs, axis=0))
                grad_columns.append(jnp.concatenate(grads, axis=0))
            probs = jnp.concatenate(prob_columns, axis=1)
            grads = jnp.concatenate(grad_columns, axis=1)
            value_sum = grow(value_sum, dot(probs, grad_pair[lanes]))
            key_sum = grow(key_sum, dot(grads, query_pair[lanes]))
            d_ref[0, rows, lanes] = dot(k_ref[0, rows, :end], grads).astype(BF16)
        if place == 0:
            key_sums.append(key_sum)
            value_sums.append(value_sum)
        else:
            key_sums[-1] = key_sums[-1] + key_sum
            value_sums[-1] = value_sums[-1] + value_sum
        both = jnp.concatenate((near_sum, next_sum), axis=1)
        flip = (key + query == TILE - 1).astype(F32)
        both = jnp.dot(flip, both, precision=lax.Precision.HIGHEST, preferred_element_type=F32)
        turned = pltpu.roll(both, 2 * TILE - (TILE - 1), 1, stride=1, stride_axis=0)
        by_distance = jnp.sum(turned, axis=0, keepdims=True)
        column = jnp.sum(by_distance * one_hot, axis=1, keepdims=True)
        far_total = jnp.sum(jnp.sum(far_sum, axis=0, keepdims=True), axis=1, keepdims=True)
        column = jnp.where(bucket == buckets - 1, column + far_total, column)
        table_grad = table_grad + jnp.where(lane == index, column, 0.0)
    store_sums(heads, size, key_sums, d_ref, width)
    store_sums(heads, size, value_sums, d_ref, 2 * width)

    @pl.when(block == 0)
    def _():
        tabgrad_ref[0] = table_grad

    @pl.when(block > 0)
    def _():
        tabgrad_ref[0] = tabgrad_ref[0] + table_grad


def cross_backward_kernel(heads, size, seg_ref, where_ref, q_ref, k_ref, v_ref, o_ref, do_ref, lse_ref, memseg_ref, dq_ref, dkv_ref, mask_ref):
    base = pl.program_id(1) * (BLOCK // TILE)
    width = heads * size
    key_mask(seg_ref, base, memseg_ref, mask_ref)
    query_tok, keys, values, grad_tok = back_common(heads, size, q_ref, k_ref, v_ref, do_ref)
    key_sums, value_sums = [], []
    for index in range(heads):
        rows = slice(index * size, (index + 1) * size)
        key_pair, place, count = pair_view(keys, index, heads, size)
        value_pair = pair_view(values, index, heads, size)[0]
        query_pair = only_lanes(pair_view(query_tok, index, heads, size)[0], place, count, size)
        grad_pair = only_lanes(pair_view(grad_tok, index, heads, size)[0], place, count, size)
        query = spread(q_ref[0, rows, :], place, count)
        grad = spread(do_ref[rows, :], place, count)
        inner = jnp.sum(do_ref[rows, :].astype(F32) * o_ref[rows, :].astype(F32), axis=0, keepdims=True)
        key_sum = value_sum = None
        for half in range(2):
            lanes = slice(half * 256, (half + 1) * 256)
            scores = dot(key_pair, query[:, lanes]) + mask_ref[:, lanes]
            probs = jnp.exp(scores - lse_ref[0, index : index + 1, lanes])
            grads = probs * (dot(value_pair, grad[:, lanes]) - inner[:, lanes])
            probs, grads = probs.astype(BF16), grads.astype(BF16)
            value_sum = grow(value_sum, dot(probs, grad_pair[lanes]))
            key_sum = grow(key_sum, dot(grads, query_pair[lanes]))
            dq_ref[0, rows, lanes] = dot(k_ref[0, rows, :], grads).astype(BF16)
        if place == 0:
            key_sums.append(key_sum)
            value_sums.append(value_sum)
        else:
            key_sums[-1] = key_sums[-1] + key_sum
            value_sums[-1] = value_sums[-1] + value_sum
    store_sums(heads, size, key_sums, dkv_ref, 0)
    store_sums(heads, size, value_sums, dkv_ref, width)


class Attention:
    def __init__(self, slots, blocks, heads, size):
        self.slots, self.blocks, self.heads, self.size = slots, blocks, heads, size
        self.width = heads * size
        self.tokens = blocks * BLOCK

    def spec(self, rows, part):
        return pl.BlockSpec((1, rows, BLOCK), lambda s, n, seg, here: (s, part, n))

    def by_group(self):
        return pl.BlockSpec((self.width, BLOCK), lambda s, n, seg, here: (jnp.bitwise_xor(here[0], s), n))

    def call(self, kernel, in_specs, out_specs, out_shape, scratch, flops, args):
        size = sum(np.prod(a.shape) * a.dtype.itemsize for a in args)
        return pl.pallas_call(
            kernel,
            grid_spec=pltpu.PrefetchScalarGridSpec(
                num_scalar_prefetch=2,
                grid=(self.slots, self.blocks),
                in_specs=in_specs,
                out_specs=out_specs,
                scratch_shapes=scratch,
            ),
            out_shape=out_shape,
            cost_estimate=pl.CostEstimate(
                flops=int(flops * self.slots * self.blocks * self.heads * BLOCK * BLOCK * self.size),
                bytes_accessed=int(size),
                transcendentals=int(self.slots * self.blocks * self.heads * BLOCK * BLOCK),
            ),
        )(*args)

    def kernel(self, body):
        def run(*refs):
            return body(self.heads, self.size, *refs)

        return run

    def lse_spec(self):
        return pl.BlockSpec((1, 8, BLOCK), lambda s, n, seg, here: (s, 0, n))

    def table_spec(self, table):
        return pl.BlockSpec((1,) + table.shape[1:], lambda s, n, seg, here: (s, 0, 0))

    def whole(self, array):
        return pl.BlockSpec(array.shape, lambda s, n, seg, here: (0,) * array.ndim)

    def memseg_spec(self):
        return pl.BlockSpec((1, 1, BLOCK), lambda s, n, seg, here: (n, 0, 0))

    def forward_shapes(self):
        return (
            jax.ShapeDtypeStruct((self.slots * self.width, self.tokens), BF16),
            jax.ShapeDtypeStruct((self.slots, 8, self.tokens), F32),
        )

    def self_forward(self, segs, here, qkv, table, one_hot):
        w = self.width
        return self.call(
            self.kernel(self_forward_kernel),
            [self.spec(w, 0), self.spec(w, 1), self.spec(w, 2), self.table_spec(table), self.whole(one_hot)],
            [self.by_group(), self.lse_spec()],
            self.forward_shapes(), [], 4, (segs, here, qkv, qkv, qkv, table, one_hot),
        )

    def cross_forward(self, segs, here, q, kv, memseg):
        w = self.width
        return self.call(
            self.kernel(cross_forward_kernel),
            [self.spec(w, 0), self.spec(w, 0), self.spec(w, 1), self.memseg_spec()],
            [self.by_group(), self.lse_spec()],
            self.forward_shapes(), [pltpu.VMEM((BLOCK, BLOCK), F32)], 4, (segs, here, q, kv, kv, memseg),
        )

    def self_backward(self, segs, here, qkv, context, grad, lse, table, one_hot):
        w = self.width
        return self.call(
            self.kernel(self_backward_kernel),
            [self.spec(w, 0), self.spec(w, 1), self.spec(w, 2), self.by_group(), self.by_group(),
             self.lse_spec(), self.table_spec(table), self.whole(one_hot)],
            [self.spec(3 * w, 0), pl.BlockSpec((1, table.shape[1], TILE), lambda s, n, seg, here: (s, 0, 0))],
            (jax.ShapeDtypeStruct((self.slots, 3 * w, self.tokens), BF16),
             jax.ShapeDtypeStruct((self.slots, table.shape[1], TILE), F32)),
            [], 10, (segs, here, qkv, qkv, qkv, context, grad, lse, table, one_hot),
        )

    def cross_backward(self, segs, here, q, kv, context, grad, lse, memseg):
        w = self.width
        return self.call(
            self.kernel(cross_backward_kernel),
            [self.spec(w, 0), self.spec(w, 0), self.spec(w, 1), self.by_group(), self.by_group(),
             self.lse_spec(), self.memseg_spec()],
            [self.spec(w, 0), self.spec(2 * w, 0)],
            (jax.ShapeDtypeStruct((self.slots, w, self.tokens), BF16),
             jax.ShapeDtypeStruct((self.slots, 2 * w, self.tokens), BF16)),
            [pltpu.VMEM((BLOCK, BLOCK), F32)], 10, (segs, here, q, kv, kv, context, grad, lse, memseg),
        )


def swap(array, axis, mask):
    size = lax.axis_size(axis)
    return lax.ppermute(array, axis, [(i, i ^ mask) for i in range(size)])


def pick(array, dim, index):
    return lax.dynamic_index_in_dim(array, index, dim, keepdims=False)


def plus(*arrays):
    total = arrays[0].astype(F32)
    for a in arrays[1:]:
        total = total + a.astype(F32)
    return total.astype(BF16)


def halve(array, axis, mask, dim, bit):
    got = swap(pick(array, dim, 1 - bit), axis, mask)
    return plus(pick(array, dim, bit), got)


def over_batch(array, low_first):
    size = lax.axis_size("batch")
    me = lax.axis_index("batch")
    done = 0
    while (1 << done) < size:
        left = size >> done
        if done == 0 and low_first and left > 1:
            array = halve(array.reshape(left // 2, 2, *array.shape[1:]), "batch", 1, 1, me & 1)
            done = 1
        elif left >= 4:
            array = array.reshape(left // 4, 4, *array.shape[1:])
            mine = (me >> done) & 3
            terms = [pick(array, 1, mine)]
            for k in (1, 2, 3):
                terms.append(swap(pick(array, 1, mine ^ k), "batch", k << done))
            array = plus(*terms) if left > 4 else sum(t.astype(F32) for t in terms)
            done += 2
        else:
            array = halve(array.reshape(left // 2, 2, *array.shape[1:]), "batch", 1 << done, 1, (me >> done) & 1)
            done += 1
    return array[0].astype(F32)


def summed_slots(parts):
    first = plus(parts[0], swap(parts[1], "head", 1))
    if len(parts) == 2:
        return first
    return plus(first, swap(plus(parts[2], swap(parts[3], "head", 1)), "head", 2))


def summed_shared(keep, send, rows_last):
    head, batch = lax.axis_size("head"), lax.axis_size("batch")
    me = lax.axis_index("head")
    core = me & 1
    total = plus(keep, swap(send, "head", 1))
    rows = total.shape[0] // (batch * head)
    total = total.reshape(batch, head // 2, 2 * rows, total.shape[1])
    if rows_last:
        total = total.reshape(batch // 2, 2, head // 2, 2 * rows, total.shape[-1])
        total = halve(total, "batch", 1, 1, lax.axis_index("batch") & 1)
        total = halve(total, "head", 2, 1, me >> 1)
        total = rest_of_batch(total)
    else:
        total = halve(total, "head", 2, 1, me >> 1)
        total = over_batch(total, True)
    total = total.reshape(2, rows, total.shape[-1])
    got = swap(pick(total, 0, 1 - core), "head", 1)
    mine = pick(total, 0, core)
    return jnp.where(core == 0, jnp.concatenate((mine, got), axis=1), jnp.concatenate((got, mine), axis=1))


def rest_of_batch(array):
    size = lax.axis_size("batch")
    me = lax.axis_index("batch")
    done = 1
    while (1 << done) < size:
        left = size >> done
        if left >= 4:
            array = array.reshape(left // 4, 4, *array.shape[1:])
            mine = (me >> done) & 3
            terms = [pick(array, 1, mine)]
            for k in (1, 2, 3):
                terms.append(swap(pick(array, 1, mine ^ k), "batch", k << done))
            array = plus(*terms) if left > 4 else sum(t.astype(F32) for t in terms)
            done += 2
        else:
            array = halve(array.reshape(left // 2, 2, *array.shape[1:]), "batch", 1 << done, 1, (me >> done) & 1)
            done += 1
    return array[0].astype(F32)


def everywhere(array, axes):
    for axis in axes:
        mask = 1
        while mask < lax.axis_size(axis):
            array = array + swap(array, axis, mask)
            mask *= 2
    return array


def norm(hidden, gain):
    scale = lax.rsqrt(jnp.mean(hidden * hidden, axis=-1, keepdims=True) + NORM_EPS)
    return (hidden * scale * gain).astype(BF16)


def norm_back(hidden, gain, grad):
    scale = lax.rsqrt(jnp.mean(hidden * hidden, axis=-1, keepdims=True) + NORM_EPS)
    weighted = grad * gain
    inner = jnp.mean(weighted * hidden, axis=-1, keepdims=True)
    return weighted * scale - hidden * (scale * scale * scale * inner), jnp.sum(grad * hidden * scale, axis=0)


def over_tokens(left, right):
    return lax.dot_general(left, right, (((0,), (0,)), ((), ())), preferred_element_type=F32)


def by_transpose(left, right):
    return lax.dot_general(left, right, (((1,), (1,)), ((), ())), preferred_element_type=F32)


def rows_first(weights, hidden):
    return lax.dot_general(weights, hidden, (((0,), (1,)), ((), ())), preferred_element_type=F32).astype(BF16)


def gelu_parts(value):
    inner = np.float32(np.sqrt(2.0 / np.pi)) * (value + 0.044715 * (value * value * value))
    bend = jnp.tanh(inner)
    slope = np.float32(np.sqrt(2.0 / np.pi)) * (1.0 + 3.0 * 0.044715 * (value * value))
    gelu = 0.5 * value * (1.0 + bend)
    return gelu, 0.5 * (1.0 + bend) + 0.5 * value * (1.0 - bend * bend) * slope


def on_device(
    tokens, memory, cotangent, target_segments, memory_segments, self_gain, self_query, self_key,
    self_value, self_out, position_bias, cross_gain, cross_query, cross_key, cross_value, cross_out,
    ff_gain, ff_gate, ff_up, ff_down,
):
    heads_axis, batch_axis = lax.axis_size("head"), lax.axis_size("batch")
    me, row = lax.axis_index("head"), lax.axis_index("batch")
    core = me & 1
    rows, part, model = tokens.shape
    assert part * 2 == BLOCK and rows % 2 == 0 and heads_axis in (2, 4)
    width = self_query.shape[1]
    heads = position_bias.shape[1]
    size = width // heads
    blocks = rows // 2
    count = blocks * BLOCK
    attention = Attention(heads_axis, blocks, heads, size)
    here = jnp.reshape(me, (1,)).astype(jnp.int32)
    one_hot = jnp.asarray(bucket_one_hot(position_bias.shape[0]))

    def to_blocks(array):
        mine = lax.dynamic_slice_in_dim(array, core * blocks, blocks, 0)
        other = swap(lax.dynamic_slice_in_dim(array, (1 - core) * blocks, blocks, 0), "head", 1)
        both = jnp.where(core == 0, jnp.concatenate((mine, other), 1), jnp.concatenate((other, mine), 1))
        return both.reshape(count, model)

    def from_blocks(array):
        halves = array.reshape(blocks, 2, part, model)
        mine = pick(halves, 1, core)
        other = swap(pick(halves, 1, 1 - core), "head", 1)
        return jnp.where(core == 0, jnp.concatenate((mine, other), 0), jnp.concatenate((other, mine), 0))

    def block_segments(segments):
        mine = lax.dynamic_slice_in_dim(segments, core * blocks, blocks, 0)
        return lax.dynamic_slice_in_dim(mine, (me >> 1) * BLOCK, BLOCK, 1)

    tile_segments = block_segments(target_segments)[:, ::TILE].reshape(-1)
    key_segments = block_segments(memory_segments).reshape(blocks, 1, BLOCK)

    def gathered(array):
        slots = [array, swap(array, "head", 1)]
        if heads_axis == 4:
            slots.append(swap(array, "head", 2))
            slots.append(swap(slots[2], "head", 1))
        return slots

    tok = to_blocks(tokens)
    self_weights = jnp.concatenate(gathered(jnp.concatenate((self_query, self_key, self_value), axis=1)), axis=1)
    table = jnp.stack(gathered(position_bias))
    mem = to_blocks(memory)
    pair_weights = jnp.concatenate(gathered(jnp.concatenate((cross_key, cross_value), axis=1)), axis=1)
    query_weights = jnp.concatenate(gathered(cross_query), axis=1)
    cot = to_blocks(cotangent)

    tok = tok.astype(F32)
    normed_one = norm(tok, self_gain)
    qkv = rows_first(self_weights, normed_one).reshape(heads_axis, 3 * width, count)
    context_one, lse_one = attention.self_forward(tile_segments, here, qkv, table, one_hot)
    kv_two = rows_first(pair_weights, mem).reshape(heads_axis, 2 * width, count)
    first_sum = tok + over_tokens(context_one, self_out)
    normed_two = norm(first_sum, cross_gain)
    q_two = rows_first(query_weights, normed_two).reshape(heads_axis, width, count)
    context_two, lse_two = attention.cross_forward(tile_segments, here, q_two, kv_two, key_segments)
    second_sum = first_sum + over_tokens(context_two, cross_out)
    normed_three = norm(second_sum, ff_gain)
    gate_value = dot(normed_three, ff_gate)
    up_value = dot(normed_three, ff_up)
    gelu, slope = gelu_parts(gate_value)
    activation = (gelu * up_value).astype(BF16)
    layer_out = from_blocks((second_sum + dot(activation, ff_down)).astype(BF16))

    def halves(array):
        lanes = array.shape[1] // 2
        return (
            lax.dynamic_slice_in_dim(array, core * lanes, lanes, 1),
            lax.dynamic_slice_in_dim(array, (1 - core) * lanes, lanes, 1),
        )

    def shared_sum(left, right, second):
        keep, send = halves(left)
        send = over_tokens(right, send).astype(BF16)
        keep = over_tokens(right, keep).astype(BF16)
        return jnp.transpose(summed_shared(keep, send, second))

    grad_act = by_transpose(cot, ff_down)
    grad_gate = (grad_act * up_value * slope).astype(BF16)
    grad_up = (grad_act * gelu).astype(BF16)
    ff_gate_grad = shared_sum(normed_three, grad_gate, False)
    ff_up_grad = shared_sum(normed_three, grad_up, True)
    ff_down_grad = shared_sum(activation, cot, False)
    grad_three = by_transpose(grad_gate, ff_gate) + by_transpose(grad_up, ff_up)
    back, ff_gain_grad = norm_back(second_sum, ff_gain, grad_three)
    grad_second = cot.astype(F32) + back
    branch_two = grad_second.astype(BF16)

    context_two_tok = jnp.transpose(context_two)
    context_one_tok = jnp.transpose(context_one)
    cross_out_grad = shared_sum(context_two_tok, branch_two, True)
    grad_context = by_transpose(cross_out, branch_two).astype(BF16)
    dq_two, dkv_two = attention.cross_backward(
        tile_segments, here, q_two, kv_two, context_two, grad_context, lse_two, key_segments
    )

    def slot_grads(hidden, grads):
        return [
            lax.dot_general(hidden, grads[s], (((0,), (1,)), ((), ())), preferred_element_type=F32).astype(BF16)
            for s in range(heads_axis)
        ]

    def head_sum(parts):
        total = summed_slots(parts)
        return over_batch(total.reshape(batch_axis, total.shape[0] // batch_axis, total.shape[1]), True)

    cross_query_grad = head_sum(slot_grads(normed_two, dq_two))
    pair_grad = head_sum(slot_grads(mem, dkv_two))
    grad_two = lax.dot_general(
        dq_two.reshape(-1, count), query_weights, (((0,), (1,)), ((), ())), preferred_element_type=F32
    )
    back, cross_gain_grad = norm_back(first_sum, cross_gain, grad_two)
    grad_first = grad_second + back
    branch_one = grad_first.astype(BF16)

    self_out_grad = shared_sum(context_one_tok, branch_one, True)
    grad_context = by_transpose(self_out, branch_one).astype(BF16)
    dqkv, table_grad = attention.self_backward(
        tile_segments, here, qkv, context_one, grad_context, lse_one, table, one_hot
    )
    self_grad = head_sum(slot_grads(normed_one, dqkv))
    memory_grad = from_blocks(
        lax.dot_general(
            dkv_two.reshape(-1, count), pair_weights, (((0,), (1,)), ((), ())), preferred_element_type=F32
        ).astype(BF16)
    )
    grad_one = lax.dot_general(
        dqkv.reshape(-1, count), self_weights, (((0,), (1,)), ((), ())), preferred_element_type=F32
    )
    back, self_gain_grad = norm_back(tok, self_gain, grad_one)
    tokens_grad = from_blocks((grad_first + back).astype(BF16))

    table_parts = [table_grad[s, :, :heads] for s in range(heads_axis)]
    bias = table_parts[0] + swap(table_parts[1], "head", 1)
    if heads_axis == 4:
        bias = bias + swap(table_parts[2] + swap(table_parts[3], "head", 1), "head", 2)
    bias_total = everywhere(bias, ("batch",))
    gains = everywhere(jnp.stack((self_gain_grad, cross_gain_grad, ff_gain_grad)), ("head", "batch"))
    share = model // (heads_axis * batch_axis)
    gains = lax.dynamic_slice_in_dim(gains, (row * heads_axis + me) * share, share, 1)

    return (
        layer_out,
        tokens_grad,
        memory_grad,
        gains[0],
        self_grad[:, :width],
        self_grad[:, width : 2 * width],
        self_grad[:, 2 * width :],
        self_out_grad,
        bias_total,
        gains[1],
        cross_query_grad,
        pair_grad[:, :width],
        pair_grad[:, width:],
        cross_out_grad,
        gains[2],
        ff_gate_grad,
        ff_up_grad,
        ff_down_grad,
    )


def solution(mesh):
    tokens = P("batch", "head", None)
    rows = P("batch", None)
    columns = P(None, "head")
    split = P("batch", "head")
    every = P(None, ("batch", "head"))
    gain = P(("batch", "head"))
    return jax.shard_map(
        on_device,
        mesh=mesh,
        in_specs=(
            tokens, tokens, tokens, rows, rows, P(), columns, columns, columns, P(), columns, P(),
            columns, columns, columns, P(), P(), P(), P(), P(),
        ),
        out_specs=(
            tokens, tokens, tokens, gain, split, split, split, every, columns, gain,
            split, split, split, every, gain, every, every, every,
        ),
        check_vma=False,
    )
```

```python
import jax
import jax.numpy as jnp
import numpy as np
from jax import lax
from jax.experimental import pallas as pl
from jax.experimental.pallas import tpu as pltpu
from jax.sharding import PartitionSpec as P

NORM_EPS = 1e-06
MASKED = -1e30
BLOCK = 512
TILE = 128
HALF = 256
SIZE = 64
HEADS = 3
GROUP = HEADS * SIZE
F32 = jnp.float32
BF16 = jnp.bfloat16
MESH = pl.DeviceIdType.MESH


def bucket_edges():
    distance = np.arange(1.0, 8192.0)
    far_bucket = 16.0 + np.floor(np.log(np.maximum(distance, 16.0) / 16.0) / np.log(8.0) * 16.0)
    bucket_value = np.where(distance < 16, distance, np.minimum(far_bucket, 31.0))
    return [int(distance[np.argmax(bucket_value >= bucket_level)]) for bucket_level in range(1, 32)]


def bucket_one_hot(buckets):
    ids = np.zeros(2 * TILE, np.int32)
    for edge in bucket_edges():
        ids += np.arange(2 * TILE) >= edge
    assert bucket_edges()[-1] <= TILE + 1
    return (np.arange(buckets)[:, None] == ids[None, :]).astype(np.float32)


def dot(left, right):
    return lax.dot_general(left, right, (((1,), (0,)), ((), ())), preferred_element_type=F32)


KEY_AT = ((0, 0), (0, 1), (2, 0))
VALUE_AT = ((1, 0), (1, 1), (2, 1))
QUERY_START = 2 * GROUP


def rows_of(at):
    tile, place = at
    return slice(tile * 128 + place * SIZE, tile * 128 + (place + 1) * SIZE)


def lanes_of(at):
    return slice(at[0] * 128, (at[0] + 1) * 128)


def spread(head_rows, place):
    blank = jnp.zeros_like(head_rows)
    return jnp.concatenate((head_rows, blank) if place == 0 else (blank, head_rows), axis=0)


def bias_tiles(table, index, one_hot):
    column = table[:, index : index + 1]
    by_distance = jnp.sum(column * one_hot, axis=0, keepdims=True)
    wide = jnp.broadcast_to(by_distance, (TILE, 2 * TILE))
    turned = pltpu.roll(wide, 0, 1, stride=1, stride_axis=0)
    key = lax.broadcasted_iota(jnp.int32, (TILE, TILE), 0)
    query = lax.broadcasted_iota(jnp.int32, (TILE, TILE), 1)
    near = jnp.where(key <= query, turned[:, :TILE], MASKED)
    return near, turned[:, TILE:], table[table.shape[0] - 1, index]


def self_tile(scores, key_tile, query_tile, tiles, seg_ref, base):
    near, next_one, far = tiles
    if key_tile == query_tile:
        return scores + near
    same = seg_ref[base + key_tile] == seg_ref[base + query_tile]
    shift = jnp.where(same, 0.0, MASKED)
    if key_tile == query_tile - 1:
        return scores + next_one + shift
    return scores + (far + shift)


def self_forward_kernel(seg_ref, where_ref, kv_ref, q_ref, tab_ref, hot_ref, o_ref, lse_ref):
    key_values = jnp.transpose(kv_ref[0])
    table = tab_ref[0]
    for index in range(HEADS):
        rows = slice(index * SIZE, (index + 1) * SIZE)
        keys = key_values[:, lanes_of(KEY_AT[index])]
        value_rows = kv_ref[0, rows_of(VALUE_AT[index]), :]
        query = spread(q_ref[0, rows, :], KEY_AT[index][1])
        tiles = bias_tiles(table, index, hot_ref[...])
        for half in range(2):
            end = (half + 1) * HALF
            scores = dot(keys[:end], query[:, half * HALF : (half + 1) * HALF])
            columns, totals = [], []
            for part in range(2):
                query_tile = 2 * half + part
                parts = [
                    self_tile(
                        scores[kt * TILE : (kt + 1) * TILE, part * TILE : (part + 1) * TILE],
                        kt, query_tile, tiles, seg_ref, 0,
                    )
                    for kt in range(query_tile + 1)
                ]
                top = jnp.max(parts[0], axis=0, keepdims=True)
                for piece in parts[1:]:
                    top = jnp.maximum(top, jnp.max(piece, axis=0, keepdims=True))
                probs = [jnp.exp(piece - top) for piece in parts]
                total = jnp.sum(probs[0], axis=0, keepdims=True)
                for piece in probs[1:]:
                    total = total + jnp.sum(piece, axis=0, keepdims=True)
                probs = [piece.astype(BF16) for piece in probs]
                if part == 0:
                    probs.append(jnp.zeros((TILE, TILE), BF16))
                columns.append(jnp.concatenate(probs, axis=0))
                totals.append(total)
                lse_ref[0, index : index + 1, query_tile * TILE : (query_tile + 1) * TILE] = top + jnp.log(total)
            weights = jnp.concatenate(columns, axis=1)
            context = dot(value_rows[:, :end], weights)
            context = context / jnp.concatenate(totals, axis=1)
            o_ref[rows, half * HALF : (half + 1) * HALF] = context.astype(BF16)


def key_mask(seg_ref, memseg, mask_ref):
    rows = jnp.transpose(jnp.broadcast_to(memseg.astype(F32), (TILE, BLOCK)))
    for tile in range(BLOCK // TILE):
        wanted = seg_ref[tile].astype(F32)
        mask_ref[:, tile * TILE : (tile + 1) * TILE] = jnp.where(rows == wanted, 0.0, MASKED).astype(mask_ref.dtype)


def cross_forward_kernel(seg_ref, where_ref, kv_ref, q_ref, memseg_ref, o_ref, lse_ref, mask_ref):
    @pl.when(pl.program_id(0) == 0)
    def _():
        key_mask(seg_ref, memseg_ref[...], mask_ref)

    key_values = jnp.transpose(kv_ref[0])
    for index in range(HEADS):
        rows = slice(index * SIZE, (index + 1) * SIZE)
        keys = key_values[:, lanes_of(KEY_AT[index])]
        value_rows = kv_ref[0, rows_of(VALUE_AT[index]), :]
        query = spread(q_ref[0, rows, :], KEY_AT[index][1])
        for half in range(2):
            lanes = slice(half * HALF, (half + 1) * HALF)
            scores = dot(keys, query[:, lanes]) + mask_ref[:, lanes]
            top = jnp.max(scores, axis=0, keepdims=True)
            probs = jnp.exp(scores - top)
            total = jnp.sum(probs, axis=0, keepdims=True)
            context = dot(value_rows, probs.astype(BF16)) / total
            o_ref[rows, lanes] = context.astype(BF16)
            lse_ref[0, index : index + 1, lanes] = top + jnp.log(total)


def attention_forward(kernel, segs, here, kv, kv_part, q, q_part, extra, extra_specs, scratch):
    slots = kv.shape[0]
    return pl.pallas_call(
        kernel,
        grid_spec=pltpu.PrefetchScalarGridSpec(
            num_scalar_prefetch=2,
            grid=(slots,),
            in_specs=[
                pl.BlockSpec((1, 2 * GROUP, BLOCK), lambda s, seg, at: (s, kv_part, 0)),
                pl.BlockSpec((1, GROUP, BLOCK), lambda s, seg, at: (s, q_part, 0)),
            ]
            + extra_specs,
            out_specs=[
                pl.BlockSpec((GROUP, BLOCK), lambda s, seg, at: (jnp.bitwise_xor(at[0], s), 0)),
                pl.BlockSpec((1, 8, BLOCK), lambda s, seg, at: (s, 0, 0)),
            ],
            scratch_shapes=scratch,
        ),
        out_shape=(
            jax.ShapeDtypeStruct((slots * GROUP, BLOCK), BF16),
            jax.ShapeDtypeStruct((slots, 8, BLOCK), F32),
        ),
        cost_estimate=pl.CostEstimate(
            flops=4 * slots * GROUP * BLOCK * BLOCK,
            bytes_accessed=8 * slots * GROUP * BLOCK,
            transcendentals=slots * HEADS * BLOCK * BLOCK,
        ),
    )(segs, here, kv, q, *extra)


def grow(old, new):
    if old is None:
        return new
    shared = old.shape[0]
    if shared == new.shape[0]:
        return old + new
    return jnp.concatenate((old + new[:shared], new[shared:]), axis=0)


def only_lanes(wide, at):
    pair = wide[:, lanes_of(at)]
    lane = lax.broadcasted_iota(jnp.int32, pair.shape, 1)
    keep = lane < SIZE if at[1] == 0 else lane >= SIZE
    return jnp.where(keep, pair, jnp.zeros_like(pair))


def moved(wide, index, place):
    if index < 2:
        assert place == index
        return only_lanes(wide, (0, index))
    part = wide[:, 128:192]
    blank = jnp.zeros_like(part)
    return jnp.concatenate((part, blank) if place == 0 else (blank, part), axis=1)


def attention_back(read, tile_of, skip, note, dq_ref, sums_ref, tick):
    key_values = jnp.transpose(read.kv())
    query_tok = jnp.transpose(read.q(slice(0, GROUP)))
    grad_tok = jnp.transpose(read.do(slice(0, GROUP)))
    sums = [None, None, None]
    for index in range(HEADS):
        rows = slice(index * SIZE, (index + 1) * SIZE)
        k_at, v_at = KEY_AT[index], VALUE_AT[index]
        key_pair, value_pair = key_values[:, lanes_of(k_at)], key_values[:, lanes_of(v_at)]
        query_pair = moved(query_tok, index, k_at[1])
        grad_pair = moved(grad_tok, index, v_at[1])
        query_rows = spread(read.q(rows), k_at[1])
        grad_rows = spread(read.do(rows), v_at[1])
        inner = jnp.sum(read.do(rows).astype(F32) * read.o(rows).astype(F32), axis=0, keepdims=True)
        key_sum = value_sum = None
        for half in range(2):
            end = (half + 1) * HALF if skip else BLOCK
            lanes = slice(half * HALF, (half + 1) * HALF)
            scores = dot(key_pair[:end], query_rows[:, lanes])
            grad_probs = dot(value_pair[:end], grad_rows[:, lanes])
            prob_columns, grad_columns = [], []
            for part in range(2):
                query_tile = 2 * half + part
                cut = slice(query_tile * TILE, (query_tile + 1) * TILE)
                here = slice(part * TILE, (part + 1) * TILE)
                total = read.lse(index, cut)
                probs, grads = [], []
                for kt in range(query_tile + 1 if skip else BLOCK // TILE):
                    there = slice(kt * TILE, (kt + 1) * TILE)
                    prob = jnp.exp(tile_of(scores[there, here], index, kt, query_tile) - total)
                    ds = prob * (grad_probs[there, here] - inner[:, cut])
                    note(index, kt, query_tile, ds)
                    probs.append(prob.astype(BF16))
                    grads.append(ds.astype(BF16))
                if skip and part == 0:
                    probs.append(jnp.zeros((TILE, TILE), BF16))
                    grads.append(jnp.zeros((TILE, TILE), BF16))
                prob_columns.append(jnp.concatenate(probs, axis=0))
                grad_columns.append(jnp.concatenate(grads, axis=0))
            probs = jnp.concatenate(prob_columns, axis=1)
            grads = jnp.concatenate(grad_columns, axis=1)
            value_sum = grow(value_sum, dot(probs, grad_pair[lanes]))
            key_sum = grow(key_sum, dot(grads, query_pair[lanes]))
            dq_ref[rows, lanes] = dot(read.k(index, end), grads).astype(BF16)
        for at, total in ((k_at, key_sum), (v_at, value_sum)):
            sums[at[0]] = total if sums[at[0]] is None else sums[at[0]] + total
        tick(index)
    for tile in range(3):
        sums_ref[:, tile * 128 : (tile + 1) * 128] = sums[tile].astype(BF16)
    sums_ref[:, QUERY_START : QUERY_START + GROUP] = jnp.transpose(dq_ref[...])


class Read:
    def __init__(self, kv, k, q, do, o, lse):
        self.kv, self.k, self.q, self.do, self.o, self.lse = kv, k, q, do, o, lse


class Named:
    def __init__(self, tree):
        for key, value in tree.items():
            setattr(self, key, Named(value) if isinstance(value, dict) else value)


class Copies:
    def __init__(self, send, recv):
        self.send, self.recv, self.count, self.sent = send, recv, 0, []

    def new(self, source, target, device):
        at = self.count
        self.count += 1
        return Copy(self, at, source, target, device)


class Copy:
    def __init__(self, owner, at, source, target, device):
        self.owner, self.at, self.source, self.target, self.device = owner, at, source, target, device

    def make(self):
        return pltpu.make_async_remote_copy(
            src_ref=self.source(), dst_ref=self.target(), send_sem=self.owner.send.at[self.at],
            recv_sem=self.owner.recv.at[self.at], device_id=self.device, device_id_type=MESH,
        )

    def start(self):
        self.make().start()

    def got(self):
        self.make().wait_recv()

    def sent(self):
        self.make().wait_send()

    def done(self):
        self.make().wait()


class Place:
    def __init__(self, depth):
        b, h = lax.axis_index("batch"), lax.axis_index("head")
        self.depth = depth
        self.core, self.y, self.x, self.z = h % 2, h // 2, b % 2, b // 2
        self.to_core = (b, h + 1 - 2 * self.core)
        self.to_y = (b, h + 2 - 4 * self.y)
        self.to_x = (b + 1 - 2 * self.x, h)
        self.to_z = [(lax.rem(self.z + k, depth) * 2 + self.x, h) for k in range(1, depth)]

    def group(self, slot):
        low, high = slot % 2, slot // 2
        return (self.core + low - 2 * self.core * low) + 2 * (self.y + high - 2 * self.y * high)

    def everyone(self):
        return [self.to_core, self.to_y, self.to_x] + self.to_z


Z, X, Y = range(3)


class Sum:
    def __init__(self, place, copies, total, got, order):
        self.place, self.total, self.got, self.order = place, total, got, order
        self.dims = len(total.shape) - 2
        self.stages = []
        for at, axis in enumerate(order):
            room = got[at]
            if axis == Z:
                stage = [
                    copies.new(self.source(at, k), (lambda room, k: lambda: room.at[k - 1])(room, k), place.to_z[k - 1])
                    for k in range(1, place.depth)
                ]
            else:
                device = place.to_x if axis == X else place.to_y
                stage = [copies.new(self.source(at, 1), (lambda room: lambda: room)(room), device)]
            self.stages.append(stage)

    @staticmethod
    def rooms(depth, dims, order, rows, lanes):
        sizes = {Z: depth, X: 2, Y: 2}
        free = list(range(dims))
        shapes = []
        for axis in order:
            free.remove(axis)
            lead = (depth - 1,) if axis == Z else ()
            shapes.append(lead + tuple(sizes[d] for d in free) + (rows, lanes))
        return shapes

    def mine(self, axis):
        return (self.place.z, self.place.x, self.place.y)[axis]

    def source(self, at, k):
        def view():
            index = [slice(None)] * self.dims
            for axis in self.order[:at]:
                index[axis] = self.mine(axis)
            axis = self.order[at]
            index[axis] = lax.rem(self.place.z + k, self.place.depth) if axis == Z else 1 - self.mine(axis)
            return self.total.at[tuple(index)]

        return view

    def start(self, at):
        for copy in self.stages[at]:
            copy.start()

    def value(self, at, free):
        axis = self.order[at]
        later = sorted(self.order[at + 1 :])
        index = [None] * self.dims
        for done in self.order[: at + 1]:
            index[done] = self.mine(done)
        for d, i in zip(later, free):
            index[d] = i
        got = [self.got[at].at[k] for k in range(self.place.depth - 1)] if axis == Z else [self.got[at]]
        return tuple(index), [g[tuple(free)] if free else g[...] for g in got]

    def add(self, at):
        for copy in self.stages[at]:
            copy.got()
        later = sorted(self.order[at + 1 :])

        def one(free):
            index, got = self.value(at, free)
            if len(got) == 1:
                self.total[index] = self.total[index] + got[0]
            else:
                total = self.total[index].astype(F32)
                for g in got:
                    total = total + g.astype(F32)
                self.total[index] = total.astype(BF16)

        def over(dims, free):
            if not dims:
                one(free)
            elif dims[0] == Z:

                @pl.loop(0, self.place.depth)
                def _(z):
                    over(dims[1:], free + [z])

            else:
                for i in range(2):
                    over(dims[1:], free + [i])

        over(later, [])
        self.start(at + 1)

    def finish(self):
        at = len(self.order) - 1
        for copy in self.stages[at]:
            copy.got()
        index, got = self.value(at, [])
        total = self.total[index].astype(F32)
        for g in got:
            total = total + g.astype(F32)
        return total

    def sent(self):
        for stage in self.stages:
            for copy in stage:
                copy.sent()


def add_loop(depth, target, other, inner):
    @pl.loop(0, depth)
    def _(z):
        for index in np.ndindex(*inner):
            target[(z, *index)] = target[(z, *index)] + other[(z, *index)]


class Shared:
    def __init__(self, place, copies, room, order, send, pair):
        self.place, self.room, self.from_pair = place, room, pair
        self.sum = Sum(place, copies, room.total, room.got, order)
        self.pair = copies.new(lambda: send, lambda: pair, place.to_core)
        self.swap = copies.new(lambda: room.last.at[1 - place.core], lambda: room.other, place.to_core)

    def enter(self, keep=None):
        self.pair.got()
        if keep is not None:
            keep.wait()
        add_loop(self.place.depth, self.room.total, self.from_pair, (2, 2))
        self.sum.start(0)

    def last(self):
        total = self.sum.finish()
        rows = total.shape[0] // 2
        self.room.last[0] = total[:rows]
        self.room.last[1] = total[rows:]
        self.swap.start()

    def store(self, out, offset, half):
        self.swap.got()
        lanes = self.room.other.shape[1]
        core = self.place.core
        for which, value in ((core, self.room.last[core]), (1 - core, self.room.other[...])):
            at = pl.ds(pl.multiple_of(which * half + offset, 8), lanes)
            out[at, :] = jnp.transpose(value)

    def sent(self):
        self.swap.sent()
        self.sum.sent()


class Slots:
    def __init__(self, place, copies, room, sends, y_first, order):
        self.place, self.room, self.y_first = place, room, y_first
        self.pair = [copies.new((lambda j: lambda: sends.at[j])(j), (lambda j: lambda: room.pair.at[j])(j), place.to_core) for j in range(2)]
        self.own = Sum(place, copies, room.total.at[0], room.got, order)
        if y_first:
            self.across = copies.new(lambda: room.total.at[1], lambda: room.across, place.to_y)
        else:
            self.far = Sum(place, copies, room.total.at[1], room.far, order)
            self.across = copies.new(lambda: room.chunk, lambda: room.across, place.to_y)

    def enter(self, j):
        self.pair[j].got()
        add_loop(self.place.depth, self.room.total.at[j], self.room.pair.at[j], (2,))
        if j == 1:
            if self.y_first:
                self.across.start()
            else:
                self.far.start(0)
        elif not self.y_first:
            self.own.start(0)

    def take(self):
        self.across.got()
        add_loop(self.place.depth, self.room.total.at[0], self.room.across, (2,))
        self.own.start(0)

    def give(self):
        self.room.chunk[...] = self.far.finish().astype(BF16)
        self.across.start()

    def finish(self):
        total = self.own.finish()
        if not self.y_first:
            self.across.got()
            total = total + self.room.across[...].astype(F32)
        return total

    def sent(self):
        self.own.sent()
        self.across.sent()
        if not self.y_first:
            self.far.sent()


SHARED_ORDER = dict(
    gate=(Z, X, Y), up=(Y, X, Z), down_a=(X, Y, Z), down_b=(X, Y, Z), out_two=(X, Y, Z), out_one=(X, Y, Z)
)
SLOT_ORDER = dict(kv_two=(True, (X, Z)), q_two=(False, (X, Z)), kv_one=(True, (X, Z)), q_one=(True, (X, Z)))
KV = slice(0, 2 * GROUP)
QS = slice(2 * GROUP, 3 * GROUP)


def put_heads(ref, kv):
    key_out, value_out = ref
    key_out[:, :128] = kv[:, :128]
    key_out[:, 128:] = kv[:, 256:320]
    value_out[:, :128] = kv[:, 128:256]
    value_out[:, 128:] = kv[:, 320:384]


def backward_kernel(depth, ins, outs, r):
    place = Place(depth)
    step = pl.program_id(0)
    core = place.core
    copies = Copies(r.send, r.recv)

    shared = Named({
        name: Shared(
            place, copies, getattr(r, name), order, getattr(ins.sends, name, r.out_send), getattr(r.pairs, name, r.out_pair)
        )
        for name, order in SHARED_ORDER.items()
    })
    slots = Named({
        name: Slots(place, copies, getattr(r, name), r.kv_send if order_at < 1 else r.q_send, y_first, order)
        for name, (y_first, order), order_at in (
            (n, o, int(getattr(r, n).total.shape[-1] == GROUP)) for n, o in SLOT_ORDER.items()
        )
    })
    layer_swap = copies.new(lambda: r.block.at[1 - core], lambda: outs.layer.at[core], place.to_core)
    memory_swap = copies.new(lambda: r.block.at[1 - core], lambda: outs.memory.at[core], place.to_core)
    tokens_swap = copies.new(lambda: r.block.at[1 - core], lambda: outs.tokens.at[core], place.to_core)
    gain_copies = [
        copies.new(lambda: r.gains, (lambda k: lambda: r.gains_got.at[k])(k), d)
        for k, d in enumerate([place.to_core, place.to_y, place.to_x] + place.to_z)
    ]
    bias_copies = [
        copies.new((lambda s: lambda: r.bias.at[s])(s), (lambda k: lambda: r.bias_got.at[k])(k), d)
        for k, (s, d) in enumerate(
            zip([1, 3, 2, 0] + [0] * (depth - 1), [place.to_core, place.to_core, place.to_y, place.to_x] + place.to_z)
        )
    ]
    assert copies.count == r.send.shape[0], copies.count

    loads = []

    def load(source, target):
        loads.append(pltpu.make_async_copy(source, target, r.load.at[len(loads)]))
        return loads[-1]

    i = ins.loaded
    after, wo_two, ctx_two = load(i.after, r.after), load(i.wo_two, r.wo), load(i.ctx_two, r.ctx)
    n_two, mem, first, tok = load(i.n_two, r.n), load(i.mem, r.mem), load(i.first, r.hidden), load(i.tok, r.hidden)
    wo_one, ctx_one, n_one = load(i.wo_one, r.wo), load(i.ctx_one, r.ctx), load(i.n_one, r.n)
    keeps = Named({
        name: load(getattr(ins.keeps, name), getattr(r, name).total) for name in SHARED_ORDER if hasattr(ins.keeps, name)
    })
    layer_in = load(ins.layer, r.block)
    layer_put = load(r.block.at[core], outs.layer.at[core])
    memory_put = load(r.block.at[core], outs.memory.at[core])
    tokens_put = load(r.block.at[core], outs.tokens.at[core])

    def out_products(unit, context, branch):
        lanes = context.shape[0] // 2
        for which, target in ((1 - core, r.out_send), (core, unit.room.total)):
            side = jnp.transpose(context[pl.ds(pl.multiple_of(which * lanes, 16), lanes), :])
            per = branch.shape[0] // 2
            for part in range(2):
                product = dot(branch[part * per : (part + 1) * per, :], side).astype(BF16)
                rows = target.shape[3]
                for piece in range(per // rows):
                    at = part * (per // rows) + piece
                    target[at // 4, (at // 2) % 2, at % 2] = product[piece * rows : (piece + 1) * rows]
            if which is not core:
                unit.pair.start()

    def weight_products(target, left, lanes):
        rows = target.shape[2]
        per = left.shape[0] // 2
        for part in range(2):
            product = dot(left[part * per : (part + 1) * per, :], r.dqkv[:, lanes]).astype(BF16)
            for piece in range(per // rows):
                at = part * (per // rows) + piece
                target[at // 2, at % 2] = product[piece * rows : (piece + 1) * rows]

    def add_rows(target, lanes, weights, fresh):
        for part in range(2):
            rows = slice(part * HALF, (part + 1) * HALF)
            product = dot(r.dqkv[rows, lanes], weights)

            @pl.when(fresh)
            def _():
                target[rows, :] = product

            @pl.when(jnp.logical_not(fresh))
            def _():
                target[rows, :] = target[rows, :] + product

    def norm_back(hidden, gain, incoming, onto, gain_row, branch):
        total = jnp.zeros((1, hidden.shape[1]), F32)
        for part in range(4):
            rows = slice(part * TILE, (part + 1) * TILE)
            h = hidden[rows, :].astype(F32)
            e = incoming[rows, :]
            scale = lax.rsqrt(jnp.mean(h * h, axis=-1, keepdims=True) + NORM_EPS)
            weighted = e * gain[...]
            inner = jnp.mean(weighted * h, axis=-1, keepdims=True)
            result = onto[rows, :] + weighted * scale - h * (scale * scale * scale * inner)
            total = total + jnp.sum(e * h * scale, axis=0, keepdims=True)
            if branch is None:
                r.block[part // 2, (part % 2) * TILE : (part % 2 + 1) * TILE, :] = result.astype(BF16)
            else:
                onto[rows, :] = result
                branch[:, rows] = jnp.transpose(result.astype(BF16))
        r.gains[gain_row : gain_row + 1, :] = total

    plan = {}

    def at(point, *tasks):
        plan.setdefault(point, []).extend(tasks)

    sh, sl = shared, slots
    at((0, 0), lambda: sh.up.enter(keeps.up), sh.out_two.enter)
    at((0, 1), lambda: sh.down_a.enter(keeps.down_a))
    at((0, 2), lambda: sh.down_b.enter(keeps.down_b))
    at((0, 3), sl.kv_two.pair[1].start, sl.q_two.pair[1].start)
    at((1, 0), lambda: sh.out_two.sum.add(0))
    at((1, 3), lambda: sl.kv_two.enter(1), lambda: sl.q_two.enter(1))
    at((2, 3), sl.kv_two.pair[0].start, sl.q_two.pair[0].start)
    at((3, 0), lambda: sh.up.sum.add(0), lambda: sh.down_a.sum.add(0))
    at((3, 3), lambda: sl.kv_two.enter(0), lambda: sl.q_two.enter(0))
    at((4, 0), lambda: sh.down_b.sum.add(0), sh.out_one.enter, lambda: sl.q_two.far.add(0))
    at((4, 2), sl.kv_two.take)
    at((4, 3), sl.kv_one.pair[1].start, sl.q_one.pair[1].start, lambda: sh.gate.sum.add(0), lambda: sl.q_two.own.add(0))
    at((5, 0), lambda: sh.out_two.sum.add(1))
    at((5, 2), lambda: sh.down_a.sum.add(1))
    at((5, 3), lambda: sl.kv_one.enter(1), lambda: sl.q_one.enter(1), sl.q_two.give)
    at((6, 0), lambda: sh.up.sum.add(1), lambda: sh.down_b.sum.add(1))
    at((6, 2), lambda: sh.out_one.sum.add(0))
    at((6, 3), sl.kv_one.pair[0].start, sl.q_one.pair[0].start)
    at((7, 2), lambda: sl.kv_two.own.add(0))

    def tick(steps, index):
        for k in steps:
            if (k, index) in plan:

                def run(tasks=plan[k, index]):
                    for task in tasks:
                        task()

                pl.when(step == k)(run)

    @pl.when(step == 0)
    def _():
        barrier = pltpu.get_barrier_semaphore()
        for device in place.everyone():
            pl.semaphore_signal(barrier, inc=1, device_id=device, device_id_type=MESH)
        for copy in (after, wo_two, ctx_two, layer_in):
            copy.start()
        pl.semaphore_wait(barrier, len(place.everyone()))
        for name in SHARED_ORDER:
            if hasattr(keeps, name):
                getattr(shared, name).pair.start()
                getattr(keeps, name).start()
        for copy in (n_two, mem, first):
            copy.start()
        after.wait()
        for part in range(4):
            rows = slice(part * TILE, (part + 1) * TILE)
            r.branch[:, rows] = jnp.transpose(r.after[rows, :].astype(BF16))
        key_mask(ins.segs, ins.memsegs[...], r.mask)
        wo_two.wait()
        ctx_two.wait()
        layer_in.wait()
        layer_swap.start()
        layer_put.start()
        sh.gate.enter(keeps.gate)
        out_products(sh.out_two, r.ctx, r.branch)
        n_two.wait()
        mem.wait()
        r.gains[...] = jnp.zeros_like(r.gains)
        r.gains[2:3, :] = ins.ff_gain_grad[...]

    slot = 3 - step % 4
    odd = slot % 2 == 1
    rows_at = pl.ds(pl.multiple_of(place.group(slot) * GROUP, 16), GROUP)

    def slot_products(kv, q, kv_left, q_left):
        @pl.when(odd)
        def _():
            weight_products(r.kv_send.at[slot // 2], kv_left, KV)
            weight_products(r.q_send.at[slot // 2], q_left, QS)

        @pl.when(jnp.logical_not(odd))
        def _():
            weight_products(kv.room.total.at[slot // 2], kv_left, KV)
            weight_products(q.room.total.at[slot // 2], q_left, QS)

    @pl.when(step < 4)
    def _():
        r.do[...] = dot(r.wo[rows_at, :], r.branch[...]).astype(BF16)
        kv, q, lse = ins.kv_two, ins.q_two, ins.lse_two
        context = r.ctx.at[rows_at, :]
        read = Read(
            lambda: kv[0], lambda h, end: kv[0, rows_of(KEY_AT[h]), :end], lambda rows: q[0, rows, :],
            lambda rows: r.do[rows, :], lambda rows: context[rows, :], lambda h, cut: lse[0, h : h + 1, cut],
        )

        def tile_of(scores, index, kt, qt):
            return scores + r.mask[kt * TILE : (kt + 1) * TILE, qt * TILE : (qt + 1) * TILE].astype(F32)

        attention_back(read, tile_of, False, lambda *a: None, r.dq, r.dqkv, lambda h: tick(range(4), h))
        slot_products(sl.kv_two, sl.q_two, r.mem, r.n)
        tick(range(4), 3)
        add_rows(r.acc_b, KV, ins.wt_two[0, KV, :], step == 0)
        add_rows(r.acc_a, QS, ins.wt_two[0, QS, :], step == 0)

    @pl.when(step == 3)
    def _():
        for copy in (wo_one, ctx_one, n_one):
            copy.start()
        first.wait()
        layer_swap.sent()
        layer_put.wait()
        norm_back(r.hidden, ins.cross_gain, r.acc_a, r.after, 1, r.branch)
        tok.start()
        for part in range(4):
            rows = slice(part * TILE, (part + 1) * TILE)
            r.block[part // 2, (part % 2) * TILE : (part % 2 + 1) * TILE, :] = r.acc_b[rows, :].astype(BF16)
        memory_swap.start()
        memory_put.start()
        for copy in (wo_one, ctx_one, n_one):
            copy.wait()
        sh.out_two.pair.sent()
        out_products(sh.out_one, r.ctx, r.branch)

    @pl.when(step >= 4)
    def _():
        r.do[...] = dot(r.wo[rows_at, :], r.branch[...]).astype(BF16)
        qkv, lse = ins.qkv_one, ins.lse_one
        context = r.ctx.at[rows_at, :]
        read = Read(
            lambda: qkv[0, KV, :], lambda h, end: qkv[0, rows_of(KEY_AT[h]), :end],
            lambda rows: qkv[0, QUERY_START + rows.start : QUERY_START + rows.stop, :],
            lambda rows: r.do[rows, :], lambda rows: context[rows, :], lambda h, cut: lse[0, h : h + 1, cut],
        )
        table, one_hot = ins.table[0], ins.hot[...]
        tiles = [bias_tiles(table, index, one_hot) for index in range(HEADS)]
        kept = {}

        def note(index, kt, qt, ds):
            key = (index, min(qt - kt, 2))
            kept[key] = kept[key] + ds if key in kept else ds

        attention_back(
            read, lambda scores, index, kt, qt: self_tile(scores, kt, qt, tiles[index], ins.segs, 0), True, note,
            r.dq, r.dqkv, lambda h: tick(range(4, 8), h),
        )
        buckets = one_hot.shape[0]
        lane = lax.broadcasted_iota(jnp.int32, (buckets, TILE), 1)
        bucket = lax.broadcasted_iota(jnp.int32, (buckets, TILE), 0)
        key = lax.broadcasted_iota(jnp.int32, (TILE, TILE), 0)
        query = lax.broadcasted_iota(jnp.int32, (TILE, TILE), 1)
        flip = (key + query == TILE - 1).astype(F32)
        table_grad = jnp.zeros((buckets, TILE), F32)
        for index in range(HEADS):
            both = jnp.concatenate((kept[index, 0], kept[index, 1]), axis=1)
            both = jnp.dot(flip, both, precision=lax.Precision.HIGHEST, preferred_element_type=F32)
            turned = pltpu.roll(both, TILE + 1, 1, stride=1, stride_axis=0)
            by_distance = jnp.sum(turned, axis=0, keepdims=True)
            column = jnp.sum(by_distance * one_hot, axis=1, keepdims=True)
            far_total = jnp.sum(jnp.sum(kept[index, 2], axis=0, keepdims=True), axis=1, keepdims=True)
            column = jnp.where(bucket == buckets - 1, column + far_total, column)
            table_grad = table_grad + jnp.where(lane == index, column, 0.0)
        r.bias[slot] = table_grad

        for k, j in ((4, 1), (6, 0)):

            @pl.when(step == k)
            def _(j=j):
                sl.kv_two.pair[j].sent()
                sl.q_two.pair[j].sent()

        slot_products(sl.kv_one, sl.q_one, r.n, r.n)
        tick(range(4, 8), 3)
        add_rows(r.acc_a, slice(0, 3 * GROUP), ins.wt_one[0], step == 4)

    @pl.when(step == 7)
    def _():
        sl.kv_one.enter(0)
        sl.q_one.enter(0)
        gains, bias = r.gains, r.bias
        memory_swap.sent()
        memory_put.wait()
        tok.wait()
        norm_back(r.hidden, ins.self_gain, r.acc_a, r.after, 0, None)
        tokens_swap.start()
        tokens_put.start()
        gain_copies[0].start()
        bias_copies[0].start()
        bias_copies[1].start()
        sl.kv_one.take()
        sh.gate.sum.add(1)
        sh.up.last()
        sh.down_a.last()
        gain_copies[0].done()
        gains[...] = gains[...] + r.gains_got[0]
        bias_copies[0].done()
        bias_copies[1].done()
        bias[0] = bias[0] + r.bias_got[0]
        bias[2] = bias[2] + r.bias_got[1]
        gain_copies[1].start()
        bias_copies[2].start()
        sh.down_b.last()
        sl.q_one.take()
        sl.kv_one.own.add(0)
        gain_copies[1].done()
        gains[...] = gains[...] + r.gains_got[1]
        bias_copies[2].done()
        bias[0] = bias[0] + r.bias_got[2]
        gain_copies[2].start()
        bias_copies[3].start()
        sh.out_one.sum.add(1)
        sl.q_one.own.add(0)
        sh.gate.last()
        sh.out_two.last()
        gain_copies[2].done()
        gains[...] = gains[...] + r.gains_got[2]
        bias_copies[3].done()
        bias[0] = bias[0] + r.bias_got[3]
        for k in range(depth - 1):
            gain_copies[3 + k].start()
            bias_copies[4 + k].start()
        outs.wq_two[...] = sl.q_two.finish()
        put_heads((outs.wk_two, outs.wv_two), sl.kv_two.finish())
        put_heads((outs.wk_one, outs.wv_one), sl.kv_one.finish())
        gain_total, bias_total = gains[...], bias[0]
        for k in range(depth - 1):
            gain_copies[3 + k].done()
            bias_copies[4 + k].done()
            gain_total = gain_total + r.gains_got[3 + k]
            bias_total = bias_total + r.bias_got[4 + k]
        outs.gains[...] = gain_total
        outs.bias[...] = bias_total
        sh.up.store(outs.up, 0, outs.up.shape[0] // 2)
        sh.down_a.store(outs.down, 0, outs.down.shape[0] // 2)
        sh.down_b.store(outs.down, outs.down.shape[0] // 4, outs.down.shape[0] // 2)
        sh.gate.store(outs.gate, 0, outs.gate.shape[0] // 2)
        sh.out_two.store(outs.out_two, 0, outs.out_two.shape[0] // 2)
        sh.out_one.last()
        outs.wq_one[...] = sl.q_one.finish()
        sh.out_one.store(outs.out_one, 0, outs.out_one.shape[0] // 2)
        for name in SHARED_ORDER:
            unit = getattr(shared, name)
            unit.sent()
            if unit is not sh.out_two:
                unit.pair.sent()
        for name in SLOT_ORDER:
            getattr(slots, name).sent()
        for j in range(2):
            sl.kv_one.pair[j].sent()
            sl.q_one.pair[j].sent()
        layer_swap.got()
        memory_swap.got()
        tokens_swap.done()
        tokens_put.wait()


def backward_call(batch_size, operands):
    depth = batch_size // 2
    tok = operands["loaded"]["tok"]
    model = tok.shape[1]
    share = model // batch_size
    anywhere = pl.BlockSpec(memory_space=pl.ANY)

    def fixed(shape):
        return pl.BlockSpec(shape, lambda t: (0,) * len(shape))

    def early(array):
        return pl.BlockSpec((1,) + array.shape[1:], lambda t: (3 - t + (t // 4) * (t - 3), 0, 0))

    def late(array):
        return pl.BlockSpec((1,) + array.shape[1:], lambda t: (3 - (t // 4) * (t - 4), 0, 0))

    kinds = dict(
        segs=lambda a: pl.BlockSpec(memory_space=pltpu.SMEM), kv_two=early, q_two=early, lse_two=early, wt_two=early,
        qkv_one=late, lse_one=late, wt_one=late, table=late, loaded=lambda a: anywhere, sends=lambda a: anywhere,
        keeps=lambda a: anywhere, layer=lambda a: anywhere,
    )
    in_specs = {
        name: jax.tree.map(kinds.get(name, lambda a: fixed(a.shape)), value) for name, value in operands.items()
    }
    keeps = operands["keeps"]
    shapes = {name: keeps[name].shape[3:] for name in keeps}
    shapes.update(out_two=(model // (4 * depth), model // 2), out_one=(model // (4 * depth), model // 2))
    block = jax.ShapeDtypeStruct((2, HALF, model), BF16)

    def wide(rows, columns):
        return jax.ShapeDtypeStruct((rows, columns), F32)

    head = wide(share, GROUP)
    buckets = operands["hot"].shape[0]
    outs = dict(
        layer=block, memory=block, tokens=block,
        gate=wide(2 * shapes["gate"][1], shapes["gate"][0] // 2), up=wide(2 * shapes["up"][1], shapes["up"][0] // 2),
        down=wide(4 * shapes["down_a"][1], shapes["down_a"][0] // 2),
        out_two=wide(model, shapes["out_two"][0] // 2), out_one=wide(model, shapes["out_one"][0] // 2),
        wq_two=head, wk_two=head, wv_two=head, wq_one=head, wk_one=head, wv_one=head,
        gains=wide(8, model), bias=wide(buckets, TILE),
    )
    out_specs = {name: anywhere if s is block else fixed(s.shape) for name, s in outs.items()}

    def room(*shape, kind=BF16):
        return pltpu.VMEM(shape, kind)

    scratch = {}
    for name, order in SHARED_ORDER.items():
        rows, lanes = shapes[name]
        scratch[name] = dict(
            total=room(depth, 2, 2, rows, lanes),
            got=[room(*s) for s in Sum.rooms(depth, 3, order, rows, lanes)],
            last=room(2, rows // 2, lanes, kind=F32), other=room(rows // 2, lanes, kind=F32),
        )
    for name, (y_first, order) in SLOT_ORDER.items():
        lanes = 2 * GROUP if name.startswith("kv") else GROUP
        got = [room(*s) for s in Sum.rooms(depth, 2, order, share, lanes)]
        both = room(2, depth, 2, share, lanes)
        scratch[name] = dict(total=both, pair=both, got=got)
        if y_first:
            scratch[name].update(across=room(depth, 2, share, lanes))
        else:
            scratch[name].update(across=room(share, lanes), chunk=room(share, lanes), far=list(got))
    scratch.update(
        pairs={name: room(depth, 2, 2, *shapes[name]) for name in keeps},
        out_send=room(depth, 2, 2, *shapes["out_one"]), out_pair=room(depth, 2, 2, *shapes["out_one"]), kv_send=room(2, depth, 2, share, 2 * GROUP),
        q_send=room(2, depth, 2, share, GROUP), block=room(2, HALF, model), branch=room(model, BLOCK),
        acc_a=room(BLOCK, model, kind=F32), acc_b=room(BLOCK, model, kind=F32), dqkv=room(BLOCK, 3 * GROUP),
        dq=room(GROUP, BLOCK), do=room(GROUP, BLOCK), mask=room(BLOCK, BLOCK), gains=room(8, model, kind=F32),
        gains_got=room(depth + 2, 8, model, kind=F32), bias=room(4, buckets, TILE, kind=F32),
        bias_got=room(depth + 3, buckets, TILE, kind=F32),
        after=room(BLOCK, model, kind=F32), hidden=room(BLOCK, model, kind=F32),
        wo=room(model, model), ctx=room(model, BLOCK), n=room(model, BLOCK), mem=room(model, BLOCK),
    )
    z = depth - 1
    copies = sum(2 + 2 + z for _ in SHARED_ORDER) + 3 + (3 + z) + (4 + z)
    copies += sum(2 + (1 + z) + 1 + (0 if y_first else 1 + z) for y_first, _ in SLOT_ORDER.values())
    scratch.update(send=pltpu.SemaphoreType.DMA((copies,)), recv=pltpu.SemaphoreType.DMA((copies,)))
    scratch.update(load=pltpu.SemaphoreType.DMA((18,)))

    arrays, in_tree = jax.tree.flatten(operands)
    out_shapes, out_tree = jax.tree.flatten(outs)
    rooms, room_tree = jax.tree.flatten(scratch)

    def kernel(*refs):
        a, b = len(arrays), len(arrays) + len(out_shapes)
        backward_kernel(
            depth, Named(jax.tree.unflatten(in_tree, refs[:a])), Named(jax.tree.unflatten(out_tree, refs[a:b])),
            Named(jax.tree.unflatten(room_tree, refs[b:])),
        )

    results = pl.pallas_call(
        kernel,
        grid=(8,),
        in_specs=jax.tree.leaves(in_specs),
        out_specs=jax.tree.leaves(out_specs),
        out_shape=out_shapes,
        scratch_shapes=rooms,
        compiler_params=pltpu.CompilerParams(
            collective_id=0, has_side_effects=True, vmem_limit_bytes=66_000_000, dimension_semantics=("arbitrary",)
        ),
        cost_estimate=pl.CostEstimate(flops=20_000_000_000, bytes_accessed=40_000_000, transcendentals=6_000_000),
    )(*arrays)
    return Named(jax.tree.unflatten(out_tree, results))


def swap(array, axis, mask):
    size = lax.axis_size(axis)
    return lax.ppermute(array, axis, [(i, i ^ mask) for i in range(size)])


def norm(hidden, gain):
    scale = lax.rsqrt(jnp.mean(hidden * hidden, axis=-1, keepdims=True) + NORM_EPS)
    return (hidden * scale * gain).astype(BF16)


def norm_back(hidden, gain, grad):
    scale = lax.rsqrt(jnp.mean(hidden * hidden, axis=-1, keepdims=True) + NORM_EPS)
    weighted = grad * gain
    inner = jnp.mean(weighted * hidden, axis=-1, keepdims=True)
    return weighted * scale - hidden * (scale * scale * scale * inner), jnp.sum(grad * hidden * scale, axis=0)


def over_tokens(left, right):
    return lax.dot_general(left, right, (((0,), (0,)), ((), ())), preferred_element_type=F32)


def by_transpose(left, right):
    return lax.dot_general(left, right, (((1,), (1,)), ((), ())), preferred_element_type=F32)


def gelu_parts(value):
    inner = np.float32(np.sqrt(2.0 / np.pi)) * (value + 0.044715 * (value * value * value))
    bend = jnp.tanh(inner)
    slope = np.float32(np.sqrt(2.0 / np.pi)) * (1.0 + 3.0 * 0.044715 * (value * value))
    gelu = 0.5 * value * (1.0 + bend)
    return gelu, 0.5 * (1.0 + bend) + 0.5 * value * (1.0 - bend * bend) * slope


def group_rows(query, key, value):
    q, k, v = query.T, key.T, value.T
    return jnp.concatenate((k[:128], v[:128], k[128:], v[128:], q), axis=0)


def on_device(
    tokens, memory, cotangent, target_segments, memory_segments, self_gain, self_query, self_key,
    self_value, self_out, position_bias, cross_gain, cross_query, cross_key, cross_value, cross_out,
    ff_gain, ff_gate, ff_up, ff_down,
):
    heads_axis, batch_axis = lax.axis_size("head"), lax.axis_size("batch")
    me, row = lax.axis_index("head"), lax.axis_index("batch")
    core = me & 1
    rows, part, model = tokens.shape
    assert part * 2 == BLOCK and rows == 2 and heads_axis == 4
    assert position_bias.shape[1] == HEADS and self_query.shape[1] == GROUP
    here = jnp.reshape(me, (1,)).astype(jnp.int32)
    one_hot = jnp.asarray(bucket_one_hot(position_bias.shape[0]))

    def to_block(array):
        mine = lax.dynamic_index_in_dim(array, core, 0, keepdims=False)
        other = swap(lax.dynamic_index_in_dim(array, 1 - core, 0, keepdims=False), "head", 1)
        return jnp.where(core == 0, jnp.concatenate((mine, other), 0), jnp.concatenate((other, mine), 0))

    def block_segments(segments):
        mine = lax.dynamic_index_in_dim(segments, core, 0, keepdims=False)
        return lax.dynamic_slice_in_dim(mine, (me >> 1) * BLOCK, BLOCK, 0)

    tile_segments = block_segments(target_segments)[::TILE]
    key_segments = block_segments(memory_segments).reshape(1, BLOCK)

    def gathered(array):
        slots = [array, swap(array, "head", 1), swap(array, "head", 2)]
        slots.append(swap(slots[2], "head", 1))
        return jnp.stack(slots)

    tok = to_block(tokens)
    wt_one = gathered(group_rows(self_query, self_key, self_value))
    table = gathered(position_bias)
    mem = to_block(memory)
    wt_two = gathered(group_rows(cross_query, cross_key, cross_value))
    cot = to_block(cotangent)

    wide = tok.astype(F32)
    normed_one = jnp.transpose(norm(wide, self_gain))
    qkv = dot(wt_one.reshape(-1, model), normed_one).astype(BF16).reshape(4, 3 * GROUP, BLOCK)
    hot_spec = pl.BlockSpec(one_hot.shape, lambda s, seg, at: (0, 0))
    context_one, lse_one = attention_forward(
        self_forward_kernel, tile_segments, here, qkv, 0, qkv, 2, (table, one_hot),
        [pl.BlockSpec((1,) + table.shape[1:], lambda s, seg, at: (s, 0, 0)), hot_spec], [],
    )
    mem_rows = jnp.transpose(mem)
    kv_two = jnp.einsum("sad,dt->sat", wt_two[:, :QUERY_START], mem_rows, preferred_element_type=F32).astype(BF16)
    first_sum = wide + over_tokens(context_one, self_out)
    normed_two = jnp.transpose(norm(first_sum, cross_gain))
    q_two = jnp.einsum("sad,dt->sat", wt_two[:, QUERY_START:], normed_two, preferred_element_type=F32).astype(BF16)
    context_two, lse_two = attention_forward(
        cross_forward_kernel, tile_segments, here, kv_two, 0, q_two, 0, (key_segments,),
        [pl.BlockSpec((1, BLOCK), lambda s, seg, at: (0, 0))], [pltpu.VMEM((BLOCK, BLOCK), F32)],
    )
    second_sum = first_sum + over_tokens(context_two, cross_out)
    normed_three = norm(second_sum, ff_gain)
    gate_value = dot(normed_three, ff_gate)
    up_value = dot(normed_three, ff_up)
    gelu, slope = gelu_parts(gate_value)
    activation = (gelu * up_value).astype(BF16)
    layer = (second_sum + dot(activation, ff_down)).astype(BF16)

    grad_act = by_transpose(cot, ff_down)
    grad_gate = (grad_act * up_value * slope).astype(BF16)
    grad_up = (grad_act * gelu).astype(BF16)
    grad_three = by_transpose(grad_gate, ff_gate) + by_transpose(grad_up, ff_up)
    back, ff_gain_grad = norm_back(second_sum, ff_gain, grad_three)
    grad_second = cot.astype(F32) + back

    def halves(left, right, pieces):
        lanes = left.shape[1] // (2 * pieces)
        chunks = batch_axis // 2, 2, 2, right.shape[1] // (2 * batch_axis), lanes
        found = []
        for piece in range(pieces):
            found.append([
                over_tokens(
                    right, lax.dynamic_slice_in_dim(left, (which * pieces + piece) * lanes, lanes, 1)
                ).astype(BF16).reshape(chunks)
                for which in (1 - core, core)
            ])
        return found

    (gate,) = halves(normed_three, grad_gate, 1)
    (up,) = halves(normed_three, grad_up, 1)
    down_a, down_b = halves(activation, cot, 2)
    done = backward_call(
        batch_axis,
        dict(
            segs=tile_segments, memsegs=key_segments, hot=one_hot, self_gain=self_gain.reshape(1, -1),
            cross_gain=cross_gain.reshape(1, -1), ff_gain_grad=ff_gain_grad.reshape(1, -1),
            kv_two=kv_two, q_two=q_two, lse_two=lse_two, wt_two=wt_two,
            qkv_one=qkv, lse_one=lse_one, wt_one=wt_one, table=table,
            loaded=dict(
                after=grad_second, wo_two=cross_out, ctx_two=context_two, n_two=normed_two, mem=mem_rows,
                first=first_sum, wo_one=self_out, ctx_one=context_one, n_one=normed_one, tok=wide,
            ),
            sends=dict(gate=gate[0], up=up[0], down_a=down_a[0], down_b=down_b[0]),
            keeps=dict(gate=gate[1], up=up[1], down_a=down_a[1], down_b=down_b[1]),
            layer=layer.reshape(2, part, model),
        ),
    )
    share = model // (heads_axis * batch_axis)
    gain_sums = lax.dynamic_slice_in_dim(done.gains, (row * heads_axis + me) * share, share, 1)
    return (
        done.layer, done.tokens, done.memory, gain_sums[0], done.wq_one, done.wk_one, done.wv_one, done.out_one,
        done.bias[:, :HEADS], gain_sums[1], done.wq_two, done.wk_two, done.wv_two, done.out_two, gain_sums[2],
        done.gate, done.up, done.down,
    )


def solution(mesh):
    tokens = P("batch", "head", None)
    rows = P("batch", None)
    columns = P(None, "head")
    split = P("batch", "head")
    every = P(None, ("batch", "head"))
    gain = P(("batch", "head"))
    return jax.shard_map(
        on_device,
        mesh=mesh,
        in_specs=(
            tokens, tokens, tokens, rows, rows, P(), columns, columns, columns, P(), columns, P(),
            columns, columns, columns, P(), P(), P(), P(), P(),
        ),
        out_specs=(
            tokens, tokens, tokens, gain, split, split, split, every, columns, gain,
            split, split, split, every, gain, every, every, every,
        ),
        check_vma=False,
    )
```

```python
import jax
import jax.numpy as jnp
import numpy as np
from jax import lax
from jax.experimental import pallas as pl
from jax.experimental.pallas import tpu as pltpu
from jax.sharding import PartitionSpec as P

NORM_EPS = 1e-06
MASKED = -1e30
BLOCK = 512
TILE = 128
HALF = 256
SIZE = 64
HEADS = 3
GROUP = HEADS * SIZE
F32 = jnp.float32
BF16 = jnp.bfloat16
MESH = pl.DeviceIdType.MESH


def bucket_edges():
    distance = np.arange(1.0, 8192.0)
    far_bucket = 16.0 + np.floor(np.log(np.maximum(distance, 16.0) / 16.0) / np.log(8.0) * 16.0)
    bucket_value = np.where(distance < 16, distance, np.minimum(far_bucket, 31.0))
    return [int(distance[np.argmax(bucket_value >= bucket_level)]) for bucket_level in range(1, 32)]


def bucket_one_hot(buckets):
    ids = np.zeros(2 * TILE, np.int32)
    for edge in bucket_edges():
        ids += np.arange(2 * TILE) >= edge
    assert bucket_edges()[-1] <= TILE + 1
    assert buckets <= TILE and ids[-1] == buckets - 1
    return (np.arange(TILE)[:, None] == ids[None, :]).astype(np.float32)


def dot(left, right):
    return lax.dot_general(left, right, (((1,), (0,)), ((), ())), preferred_element_type=F32)


KEY_AT = ((0, 0), (0, 1), (2, 0))
VALUE_AT = ((1, 0), (1, 1), (2, 1))
QUERY_START = 2 * GROUP


def rows_of(at):
    tile, place = at
    return slice(tile * 128 + place * SIZE, tile * 128 + (place + 1) * SIZE)


def lanes_of(at):
    return slice(at[0] * 128, (at[0] + 1) * 128)


def spread(head_rows, place):
    blank = jnp.zeros_like(head_rows)
    return jnp.concatenate((head_rows, blank) if place == 0 else (blank, head_rows), axis=0)


def bias_tiles(table, index, one_hot):
    by_distance = jnp.dot(
        table, one_hot, precision=lax.Precision.HIGHEST, preferred_element_type=F32
    )[index : index + 1]
    wide = jnp.broadcast_to(by_distance, (TILE, 2 * TILE))
    turned = pltpu.roll(wide, 0, 1, stride=1, stride_axis=0)
    key = lax.broadcasted_iota(jnp.int32, (TILE, TILE), 0)
    query = lax.broadcasted_iota(jnp.int32, (TILE, TILE), 1)
    near = jnp.where(key <= query, turned[:, :TILE], MASKED)
    return near, turned[:, TILE:], by_distance[0, 2 * TILE - 1]


def self_tile(scores, key_tile, query_tile, tiles, seg_ref, base):
    near, next_one, far = tiles
    if key_tile == query_tile:
        return scores + near
    same = seg_ref[base + key_tile] == seg_ref[base + query_tile]
    shift = jnp.where(same, 0.0, MASKED)
    if key_tile == query_tile - 1:
        return scores + next_one + shift
    return scores + (far + shift)


def self_forward(kv, q, table, one_hot, seg_ref, out, lse, tick):
    key_values = jnp.transpose(kv[...])
    for index in range(HEADS):
        rows = slice(index * SIZE, (index + 1) * SIZE)
        keys = key_values[:, lanes_of(KEY_AT[index])]
        query = spread(q[rows, :], KEY_AT[index][1])
        tiles = bias_tiles(table, index, one_hot)
        for half in range(2):
            end = (half + 1) * HALF
            scores = dot(keys[:end], query[:, half * HALF : (half + 1) * HALF])
            columns, totals = [], []
            for part in range(2):
                query_tile = 2 * half + part
                parts = [
                    self_tile(
                        scores[kt * TILE : (kt + 1) * TILE, part * TILE : (part + 1) * TILE],
                        kt, query_tile, tiles, seg_ref, 0,
                    )
                    for kt in range(query_tile + 1)
                ]
                top = jnp.max(parts[0], axis=0, keepdims=True)
                for piece in parts[1:]:
                    top = jnp.maximum(top, jnp.max(piece, axis=0, keepdims=True))
                probs = [jnp.exp(piece - top) for piece in parts]
                total = jnp.sum(probs[0], axis=0, keepdims=True)
                for piece in probs[1:]:
                    total = total + jnp.sum(piece, axis=0, keepdims=True)
                probs = [piece.astype(BF16) for piece in probs]
                if part == 0:
                    probs.append(jnp.zeros((TILE, TILE), BF16))
                columns.append(jnp.concatenate(probs, axis=0))
                totals.append(total)
                lse[index : index + 1, query_tile * TILE : (query_tile + 1) * TILE] = top + jnp.log(total)
            weights = jnp.concatenate(columns, axis=1)
            context = dot(kv[rows_of(VALUE_AT[index]), :end], weights)
            context = context / jnp.concatenate(totals, axis=1)
            out[rows, half * HALF : (half + 1) * HALF] = context.astype(BF16)
        tick(index)


def key_mask(seg_ref, memseg, mask_ref):
    rows = jnp.transpose(jnp.broadcast_to(memseg.astype(F32), (TILE, BLOCK)))
    for tile in range(BLOCK // TILE):
        wanted = seg_ref[tile].astype(F32)
        shift = jnp.where(rows == wanted, 0.0, MASKED)
        mask_ref[:, tile * TILE : (tile + 1) * TILE] = shift.astype(mask_ref.dtype)


def cross_forward(kv, q, mask, out, lse, tick):
    key_values = jnp.transpose(kv[...])
    for index in range(HEADS):
        rows = slice(index * SIZE, (index + 1) * SIZE)
        keys = key_values[:, lanes_of(KEY_AT[index])]
        query = spread(q[rows, :], KEY_AT[index][1])
        for half in range(2):
            lanes = slice(half * HALF, (half + 1) * HALF)
            scores = dot(keys, query[:, lanes]) + mask[:, lanes]
            top = jnp.max(scores, axis=0, keepdims=True)
            probs = jnp.exp(scores - top)
            total = jnp.sum(probs, axis=0, keepdims=True)
            context = dot(kv[rows_of(VALUE_AT[index]), :], probs.astype(BF16)) / total
            out[rows, lanes] = context.astype(BF16)
            lse[index : index + 1, lanes] = top + jnp.log(total)
        tick(index)


def grow(old, new):
    if old is None:
        return new
    shared = old.shape[0]
    if shared == new.shape[0]:
        return old + new
    return jnp.concatenate((old + new[:shared], new[shared:]), axis=0)


def only_lanes(wide, at):
    pair = wide[:, lanes_of(at)]
    lane = lax.broadcasted_iota(jnp.int32, pair.shape, 1)
    keep = lane < SIZE if at[1] == 0 else lane >= SIZE
    return jnp.where(keep, pair, jnp.zeros_like(pair))


def moved(wide, index, place):
    if index < 2:
        assert place == index
        return only_lanes(wide, (0, index))
    part = wide[:, 128:192]
    blank = jnp.zeros_like(part)
    return jnp.concatenate((part, blank) if place == 0 else (blank, part), axis=1)


def attention_back(read, tile_of, skip, note, dq_ref, sums_ref, tick):
    key_values = jnp.transpose(read.kv())
    query_tok = jnp.transpose(read.q(slice(0, GROUP)))
    grad_tok = jnp.transpose(read.do(slice(0, GROUP)))
    sums = [None, None, None]
    for index in range(HEADS):
        rows = slice(index * SIZE, (index + 1) * SIZE)
        k_at, v_at = KEY_AT[index], VALUE_AT[index]
        key_pair, value_pair = key_values[:, lanes_of(k_at)], key_values[:, lanes_of(v_at)]
        query_pair = moved(query_tok, index, k_at[1])
        grad_pair = moved(grad_tok, index, v_at[1])
        query_rows = spread(read.q(rows), k_at[1])
        grad_rows = spread(read.do(rows), v_at[1])
        inner = jnp.sum(read.do(rows).astype(F32) * read.o(rows).astype(F32), axis=0, keepdims=True)
        key_sum = value_sum = None
        for half in range(2):
            end = (half + 1) * HALF if skip else BLOCK
            lanes = slice(half * HALF, (half + 1) * HALF)
            scores = dot(key_pair[:end], query_rows[:, lanes])
            grad_probs = dot(value_pair[:end], grad_rows[:, lanes])
            prob_columns, grad_columns = [], []
            for part in range(2):
                query_tile = 2 * half + part
                cut = slice(query_tile * TILE, (query_tile + 1) * TILE)
                here = slice(part * TILE, (part + 1) * TILE)
                total = read.lse(index, cut)
                probs, grads = [], []
                for kt in range(query_tile + 1 if skip else BLOCK // TILE):
                    there = slice(kt * TILE, (kt + 1) * TILE)
                    prob = jnp.exp(tile_of(scores[there, here], index, kt, query_tile) - total)
                    ds = prob * (grad_probs[there, here] - inner[:, cut])
                    note(index, kt, query_tile, ds)
                    probs.append(prob.astype(BF16))
                    grads.append(ds.astype(BF16))
                if skip and part == 0:
                    probs.append(jnp.zeros((TILE, TILE), BF16))
                    grads.append(jnp.zeros((TILE, TILE), BF16))
                prob_columns.append(jnp.concatenate(probs, axis=0))
                grad_columns.append(jnp.concatenate(grads, axis=0))
            probs = jnp.concatenate(prob_columns, axis=1)
            grads = jnp.concatenate(grad_columns, axis=1)
            value_sum = grow(value_sum, dot(probs, grad_pair[lanes]))
            key_sum = grow(key_sum, dot(grads, query_pair[lanes]))
            dq_ref[rows, lanes] = dot(read.k(index, end), grads).astype(BF16)
        for at, total in ((k_at, key_sum), (v_at, value_sum)):
            sums[at[0]] = total if sums[at[0]] is None else sums[at[0]] + total
        tick(index)
    for tile in range(3):
        sums_ref[:, tile * 128 : (tile + 1) * 128] = sums[tile].astype(BF16)
    sums_ref[:, QUERY_START : QUERY_START + GROUP] = jnp.transpose(dq_ref[...])


def row_of(ref):
    return jnp.reshape(ref[...], (1, ref.shape[0]))


class Tiles:
    def __init__(self, place, ref):
        self.place, self.ref = place, ref

    def __getitem__(self, tile):
        return self.ref[self.place.core, self.place.y * BLOCK + tile * TILE]


def key_segments(place, ref):
    lanes = pl.ds(pl.multiple_of(place.y * BLOCK, BLOCK), BLOCK)
    return jnp.where(place.core == 0, ref[0:1, lanes], ref[1:2, lanes])


class Read:
    def __init__(self, kv, k, q, do, o, lse):
        self.kv, self.k, self.q, self.do, self.o, self.lse = kv, k, q, do, o, lse


class Named:
    def __init__(self, tree):
        for key, value in tree.items():
            setattr(self, key, Named(value) if isinstance(value, dict) else value)


class Copies:
    def __init__(self, send, recv):
        self.send, self.recv, self.count, self.sent = send, recv, 0, []

    def new(self, source, target, device):
        at = self.count
        self.count += 1
        return Copy(self, at, source, target, device)


class Copy:
    def __init__(self, owner, at, source, target, device):
        self.owner, self.at, self.source, self.target, self.device = owner, at, source, target, device

    def make(self):
        return pltpu.make_async_remote_copy(
            src_ref=self.source(), dst_ref=self.target(), send_sem=self.owner.send.at[self.at],
            recv_sem=self.owner.recv.at[self.at], device_id=self.device, device_id_type=MESH,
        )

    def start(self):
        self.make().start()

    def got(self):
        self.make().wait_recv()

    def sent(self):
        self.make().wait_send()

    def done(self):
        self.make().wait()


class Place:
    def __init__(self, depth):
        b, h = lax.axis_index("batch"), lax.axis_index("head")
        self.depth = depth
        self.core, self.y, self.x, self.z = h % 2, h // 2, b % 2, b // 2
        self.to_core = (b, h + 1 - 2 * self.core)
        self.to_y = (b, h + 2 - 4 * self.y)
        self.to_x = (b + 1 - 2 * self.x, h)
        self.to_z = [(lax.rem(self.z + k, depth) * 2 + self.x, h) for k in range(1, depth)]

    def group(self, slot):
        low, high = slot % 2, slot // 2
        return (self.core + low - 2 * self.core * low) + 2 * (self.y + high - 2 * self.y * high)

    def everyone(self):
        return [self.to_core, self.to_y, self.to_x] + self.to_z


Z, X, Y = range(3)


class Sum:
    def __init__(self, place, copies, total, got, order):
        self.place, self.total, self.got, self.order = place, total, got, order
        self.dims = len(total.shape) - 2
        self.stages = []
        for at, axis in enumerate(order):
            room = got[at]
            if axis == Z:
                stage = [
                    copies.new(self.source(at, k), (lambda room, k: lambda: room.at[k - 1])(room, k), place.to_z[k - 1])
                    for k in range(1, place.depth)
                ]
            else:
                device = place.to_x if axis == X else place.to_y
                stage = [copies.new(self.source(at, 1), (lambda room: lambda: room)(room), device)]
            self.stages.append(stage)

    @staticmethod
    def rooms(depth, dims, order, rows, lanes):
        sizes = {Z: depth, X: 2, Y: 2}
        free = list(range(dims))
        shapes = []
        for axis in order:
            free.remove(axis)
            lead = (depth - 1,) if axis == Z else ()
            shapes.append(lead + tuple(sizes[d] for d in free) + (rows, lanes))
        return shapes

    def mine(self, axis):
        return (self.place.z, self.place.x, self.place.y)[axis]

    def source(self, at, k):
        def view():
            index = [slice(None)] * self.dims
            for axis in self.order[:at]:
                index[axis] = self.mine(axis)
            axis = self.order[at]
            index[axis] = lax.rem(self.place.z + k, self.place.depth) if axis == Z else 1 - self.mine(axis)
            return self.total.at[tuple(index)]

        return view

    def start(self, at):
        for copy in self.stages[at]:
            copy.start()

    def value(self, at, free):
        axis = self.order[at]
        later = sorted(self.order[at + 1 :])
        index = [None] * self.dims
        for done in self.order[: at + 1]:
            index[done] = self.mine(done)
        for d, i in zip(later, free):
            index[d] = i
        got = [self.got[at].at[k] for k in range(self.place.depth - 1)] if axis == Z else [self.got[at]]
        return tuple(index), [g[tuple(free)] if free else g[...] for g in got]

    def add(self, at):
        for copy in self.stages[at]:
            copy.got()
        later = sorted(self.order[at + 1 :])

        def one(free):
            index, got = self.value(at, free)
            if len(got) == 1:
                self.total[index] = self.total[index] + got[0]
            else:
                total = self.total[index].astype(F32)
                for g in got:
                    total = total + g.astype(F32)
                self.total[index] = total.astype(BF16)

        def over(dims, free):
            if not dims:
                one(free)
            elif dims[0] == Z:

                @pl.loop(0, self.place.depth)
                def _(z):
                    over(dims[1:], free + [z])

            else:
                for i in range(2):
                    over(dims[1:], free + [i])

        over(later, [])
        self.start(at + 1)

    def finish(self):
        at = len(self.order) - 1
        for copy in self.stages[at]:
            copy.got()
        index, got = self.value(at, [])
        total = self.total[index].astype(F32)
        for g in got:
            total = total + g.astype(F32)
        return total

    def sent(self):
        for stage in self.stages:
            for copy in stage:
                copy.sent()


def add_loop(depth, target, other, inner):
    @pl.loop(0, depth)
    def _(z):
        for index in np.ndindex(*inner):
            target[(z, *index)] = target[(z, *index)] + other[(z, *index)]


class Shared:
    def __init__(self, place, copies, room, order, send, pair):
        self.place, self.room, self.from_pair = place, room, pair
        self.sum = Sum(place, copies, room.total, room.got, order)
        self.pair = copies.new(lambda: send, lambda: pair, place.to_core)
        self.swap = copies.new(lambda: room.last.at[1 - place.core], lambda: room.other, place.to_core)

    def enter(self, keep=None):
        self.pair.got()
        if keep is not None:
            keep.wait()
        add_loop(self.place.depth, self.room.total, self.from_pair, (2, 2))
        self.sum.start(0)

    def last(self):
        total = self.sum.finish()
        rows = total.shape[0] // 2
        self.room.last[0] = total[:rows]
        self.room.last[1] = total[rows:]
        self.swap.start()

    def store(self, out, offset, half):
        self.swap.got()
        lanes = self.room.other.shape[1]
        mine, other = self.room.last[self.place.core], self.room.other[...]
        for which in range(2):
            at = slice(which * half + offset, which * half + offset + lanes)
            out[:, at] = jnp.where(self.place.core == which, mine, other)

    def sent(self):
        self.swap.sent()
        self.sum.sent()


class Slots:
    def __init__(self, place, copies, room, sends, y_first, order):
        self.place, self.room, self.y_first = place, room, y_first
        self.pair = [copies.new((lambda j: lambda: sends.at[j])(j), (lambda j: lambda: room.pair.at[j])(j), place.to_core) for j in range(2)]
        self.own = Sum(place, copies, room.total.at[0], room.got, order)
        if y_first:
            self.across = copies.new(lambda: room.total.at[1], lambda: room.across, place.to_y)
        else:
            self.far = Sum(place, copies, room.total.at[1], room.far, order)
            self.across = copies.new(lambda: room.chunk, lambda: room.across, place.to_y)

    def enter(self, j):
        self.pair[j].got()
        add_loop(self.place.depth, self.room.total.at[j], self.room.pair.at[j], (2,))
        if j == 1:
            if self.y_first:
                self.across.start()
            else:
                self.far.start(0)
        elif not self.y_first:
            self.own.start(0)

    def take(self):
        self.across.got()
        add_loop(self.place.depth, self.room.total.at[0], self.room.across, (2,))
        self.own.start(0)

    def give(self):
        self.room.chunk[...] = self.far.finish().astype(BF16)
        self.across.start()

    def finish(self):
        total = self.own.finish()
        if not self.y_first:
            self.across.got()
            total = total + self.room.across[...].astype(F32)
        return total

    def sent(self):
        self.own.sent()
        self.across.sent()
        if not self.y_first:
            self.far.sent()


SHARED_ORDER = dict(
    gate=(Z, X, Y), up=(Y, X, Z), down_a=(X, Y, Z), down_b=(X, Y, Z), out_two=(X, Y, Z), out_one=(X, Y, Z)
)
SLOT_ORDER = dict(kv_two=(True, (X, Z)), q_two=(False, (X, Z)), kv_one=(True, (X, Z)), q_one=(True, (X, Z)))
KV = slice(0, 2 * GROUP)
QS = slice(2 * GROUP, 3 * GROUP)


def put_heads(ref, kv):
    key_out, value_out = ref
    key_out[:, :128] = kv[:, :128]
    key_out[:, 128:] = kv[:, 256:320]
    value_out[:, :128] = kv[:, 128:256]
    value_out[:, 128:] = kv[:, 320:384]


def backward_kernel(depth, ins, outs, r):
    place = Place(depth)
    step = pl.program_id(0)
    core = place.core
    copies = Copies(r.send, r.recv)
    segs = Tiles(place, ins.segs)

    shared = Named({
        name: Shared(
            place, copies, getattr(r, name), order, getattr(ins.sends, name, r.out_send), getattr(r.pairs, name, r.out_pair)
        )
        for name, order in SHARED_ORDER.items()
    })
    slots = Named({
        name: Slots(place, copies, getattr(r, name), r.kv_send if order_at < 1 else r.q_send, y_first, order)
        for name, (y_first, order), order_at in (
            (n, o, int(getattr(r, n).total.shape[-1] == GROUP)) for n, o in SLOT_ORDER.items()
        )
    })
    layer_swap = copies.new(lambda: r.block.at[1 - core], lambda: outs.layer.at[core], place.to_core)
    memory_swap = copies.new(lambda: r.block.at[1 - core], lambda: outs.memory.at[core], place.to_core)
    tokens_swap = copies.new(lambda: r.block.at[1 - core], lambda: outs.tokens.at[core], place.to_core)
    gain_copies = [
        copies.new(lambda: r.gains, (lambda k: lambda: r.gains_got.at[k])(k), d)
        for k, d in enumerate([place.to_core, place.to_y, place.to_x] + place.to_z)
    ]
    bias_copies = [
        copies.new((lambda s: lambda: r.bias.at[s])(s), (lambda k: lambda: r.bias_got.at[k])(k), d)
        for k, (s, d) in enumerate(
            zip([1, 3, 2, 0] + [0] * (depth - 1), [place.to_core, place.to_core, place.to_y, place.to_x] + place.to_z)
        )
    ]
    assert copies.count == r.send.shape[0], copies.count

    loads = []

    def load(source, target):
        loads.append(pltpu.make_async_copy(source, target, r.load.at[len(loads)]))
        return loads[-1]

    i = ins.loaded
    after, wo_two, ctx_two = load(i.after, r.after), load(i.wo_two, r.wo), load(i.ctx_two, r.ctx)
    n_two, mem, first, tok = load(i.n_two, r.n), load(i.mem, r.mem), load(i.first, r.hidden), load(i.tok, r.hidden)
    wo_one, ctx_one, n_one = load(i.wo_one, r.wo), load(i.ctx_one, r.ctx), load(i.n_one, r.n)
    keeps = Named({
        name: load(getattr(ins.keeps, name), getattr(r, name).total) for name in SHARED_ORDER if hasattr(ins.keeps, name)
    })
    layer_in = load(ins.layer, r.block)
    layer_put = load(r.block.at[core], outs.layer.at[core])
    memory_put = load(r.block.at[core], outs.memory.at[core])
    tokens_put = load(r.block.at[core], outs.tokens.at[core])

    def out_products(unit, context, branch):
        lanes = context.shape[0] // 2
        for which, target in ((1 - core, r.out_send), (core, unit.room.total)):
            side = jnp.transpose(context[pl.ds(pl.multiple_of(which * lanes, 16), lanes), :])
            per = branch.shape[0] // 2
            for part in range(2):
                product = dot(branch[part * per : (part + 1) * per, :], side).astype(BF16)
                rows = target.shape[3]
                for piece in range(per // rows):
                    at = part * (per // rows) + piece
                    target[at // 4, (at // 2) % 2, at % 2] = product[piece * rows : (piece + 1) * rows]
            if which is not core:
                unit.pair.start()

    def weight_products(target, left, lanes):
        rows = target.shape[2]
        per = left.shape[0] // 2
        for part in range(2):
            product = dot(left[part * per : (part + 1) * per, :], r.dqkv[:, lanes]).astype(BF16)
            for piece in range(per // rows):
                at = part * (per // rows) + piece
                target[at // 2, at % 2] = product[piece * rows : (piece + 1) * rows]

    def add_rows(target, lanes, weights, fresh):
        for part in range(2):
            rows = slice(part * HALF, (part + 1) * HALF)
            product = dot(r.dqkv[rows, lanes], weights)

            @pl.when(fresh)
            def _():
                target[rows, :] = product

            @pl.when(jnp.logical_not(fresh))
            def _():
                target[rows, :] = target[rows, :] + product

    def norm_back(hidden, gain, incoming, onto, gain_row, branch):
        total = jnp.zeros((1, hidden.shape[1]), F32)
        for part in range(4):
            rows = slice(part * TILE, (part + 1) * TILE)
            h = hidden[rows, :].astype(F32)
            e = incoming[rows, :]
            scale = lax.rsqrt(jnp.mean(h * h, axis=-1, keepdims=True) + NORM_EPS)
            weighted = e * row_of(gain)
            inner = jnp.mean(weighted * h, axis=-1, keepdims=True)
            result = onto[rows, :] + weighted * scale - h * (scale * scale * scale * inner)
            total = total + jnp.sum(e * h * scale, axis=0, keepdims=True)
            if branch is None:
                r.block[part // 2, (part % 2) * TILE : (part % 2 + 1) * TILE, :] = result.astype(BF16)
            else:
                onto[rows, :] = result
                branch[:, rows] = jnp.transpose(result.astype(BF16))
        r.gains[gain_row : gain_row + 1, :] = total

    plan = {}

    def at(point, *tasks):
        plan.setdefault(point, []).extend(tasks)

    sh, sl = shared, slots
    at((0, 0), lambda: sh.up.enter(keeps.up), sh.out_two.enter)
    at((0, 1), lambda: sh.down_a.enter(keeps.down_a))
    at((0, 2), lambda: sh.down_b.enter(keeps.down_b))
    at((0, 3), sl.kv_two.pair[1].start, sl.q_two.pair[1].start)
    at((1, 0), lambda: sh.out_two.sum.add(0))
    at((1, 3), lambda: sl.kv_two.enter(1), lambda: sl.q_two.enter(1))
    at((2, 3), sl.kv_two.pair[0].start, sl.q_two.pair[0].start)
    at((3, 0), lambda: sh.up.sum.add(0), lambda: sh.down_a.sum.add(0))
    at((3, 3), lambda: sl.kv_two.enter(0), lambda: sl.q_two.enter(0))
    at((4, 0), lambda: sh.down_b.sum.add(0), sh.out_one.enter, lambda: sl.q_two.far.add(0))
    at((4, 2), sl.kv_two.take)
    at((4, 3), sl.kv_one.pair[1].start, sl.q_one.pair[1].start, lambda: sh.gate.sum.add(0), lambda: sl.q_two.own.add(0))
    at((5, 0), lambda: sh.out_two.sum.add(1))
    at((5, 2), lambda: sh.down_a.sum.add(1))
    at((5, 3), lambda: sl.kv_one.enter(1), lambda: sl.q_one.enter(1), sl.q_two.give)
    at((6, 0), lambda: sh.up.sum.add(1), lambda: sh.down_b.sum.add(1))
    at((6, 2), lambda: sh.out_one.sum.add(0))
    at((6, 3), sl.kv_one.pair[0].start, sl.q_one.pair[0].start)
    at((7, 2), lambda: sl.kv_two.own.add(0))

    def tick(steps, index):
        for k in steps:
            if (k, index) in plan:

                def run(tasks=plan[k, index]):
                    for task in tasks:
                        task()

                pl.when(step == k)(run)

    @pl.when(step == 0)
    def _():
        barrier = pltpu.get_barrier_semaphore()
        for device in place.everyone():
            pl.semaphore_signal(barrier, inc=1, device_id=device, device_id_type=MESH)
        for copy in (after, wo_two, ctx_two, layer_in):
            copy.start()
        pl.semaphore_wait(barrier, len(place.everyone()))
        for name in SHARED_ORDER:
            if hasattr(keeps, name):
                getattr(shared, name).pair.start()
                getattr(keeps, name).start()
        for copy in (n_two, mem, first):
            copy.start()
        after.wait()
        for part in range(4):
            rows = slice(part * TILE, (part + 1) * TILE)
            r.branch[:, rows] = jnp.transpose(r.after[rows, :].astype(BF16))
        key_mask(segs, key_segments(place, ins.memsegs), r.mask)
        wo_two.wait()
        ctx_two.wait()
        layer_in.wait()
        layer_swap.start()
        layer_put.start()
        sh.gate.enter(keeps.gate)
        out_products(sh.out_two, r.ctx, r.branch)
        n_two.wait()
        mem.wait()
        r.gains[...] = jnp.zeros_like(r.gains)
        r.gains[2:3, :] = row_of(ins.ff_gain_grad)

    slot = 3 - step % 4
    odd = slot % 2 == 1
    rows_at = pl.ds(pl.multiple_of(place.group(slot) * GROUP, 16), GROUP)

    def slot_products(kv, q, kv_left, q_left):
        @pl.when(odd)
        def _():
            weight_products(r.kv_send.at[slot // 2], kv_left, KV)
            weight_products(r.q_send.at[slot // 2], q_left, QS)

        @pl.when(jnp.logical_not(odd))
        def _():
            weight_products(kv.room.total.at[slot // 2], kv_left, KV)
            weight_products(q.room.total.at[slot // 2], q_left, QS)

    @pl.when(step < 4)
    def _():
        r.do[...] = dot(r.wo[rows_at, :], r.branch[...]).astype(BF16)
        kv, q, lse = ins.kv_two, ins.q_two, ins.lse_two
        context = r.ctx.at[rows_at, :]
        read = Read(
            lambda: kv[0], lambda h, end: kv[0, rows_of(KEY_AT[h]), :end], lambda rows: q[0, rows, :],
            lambda rows: r.do[rows, :], lambda rows: context[rows, :], lambda h, cut: lse[0, h : h + 1, cut],
        )

        def tile_of(scores, index, kt, qt):
            return scores + r.mask[kt * TILE : (kt + 1) * TILE, qt * TILE : (qt + 1) * TILE].astype(F32)

        attention_back(read, tile_of, False, lambda *a: None, r.dq, r.dqkv, lambda h: tick(range(4), h))
        slot_products(sl.kv_two, sl.q_two, r.mem, r.n)
        tick(range(4), 3)
        add_rows(r.acc_b, KV, ins.wt_two[0, KV, :], step == 0)
        add_rows(r.acc_a, QS, ins.wt_two[0, QS, :], step == 0)

    @pl.when(step == 3)
    def _():
        for copy in (wo_one, ctx_one, n_one):
            copy.start()
        first.wait()
        layer_swap.sent()
        layer_put.wait()
        norm_back(r.hidden, ins.cross_gain, r.acc_a, r.after, 1, r.branch)
        tok.start()
        for part in range(4):
            rows = slice(part * TILE, (part + 1) * TILE)
            r.block[part // 2, (part % 2) * TILE : (part % 2 + 1) * TILE, :] = r.acc_b[rows, :].astype(BF16)
        memory_swap.start()
        memory_put.start()
        for copy in (wo_one, ctx_one, n_one):
            copy.wait()
        sh.out_two.pair.sent()
        out_products(sh.out_one, r.ctx, r.branch)

    @pl.when(step >= 4)
    def _():
        r.do[...] = dot(r.wo[rows_at, :], r.branch[...]).astype(BF16)
        qkv, lse = ins.qkv_one, ins.lse_one
        context = r.ctx.at[rows_at, :]
        read = Read(
            lambda: qkv[0, KV, :], lambda h, end: qkv[0, rows_of(KEY_AT[h]), :end],
            lambda rows: qkv[0, QUERY_START + rows.start : QUERY_START + rows.stop, :],
            lambda rows: r.do[rows, :], lambda rows: context[rows, :], lambda h, cut: lse[0, h : h + 1, cut],
        )
        table, one_hot = ins.table[0], ins.hot[...]
        tiles = [bias_tiles(table, index, one_hot) for index in range(HEADS)]
        kept = {}

        def note(index, kt, qt, ds):
            key = (index, min(qt - kt, 2))
            kept[key] = kept[key] + ds if key in kept else ds

        attention_back(
            read, lambda scores, index, kt, qt: self_tile(scores, kt, qt, tiles[index], segs, 0), True, note,
            r.dq, r.dqkv, lambda h: tick(range(4, 8), h),
        )
        key = lax.broadcasted_iota(jnp.int32, (TILE, TILE), 0)
        query = lax.broadcasted_iota(jnp.int32, (TILE, TILE), 1)
        flip = (key + query == TILE - 1).astype(F32)
        row = lax.broadcasted_iota(jnp.int32, (8, 2 * TILE), 0)
        lane = lax.broadcasted_iota(jnp.int32, (8, 2 * TILE), 1)
        by_distance = jnp.zeros((8, 2 * TILE), F32)
        for index in range(HEADS):
            both = jnp.concatenate((kept[index, 0], kept[index, 1]), axis=1)
            both = jnp.dot(flip, both, precision=lax.Precision.HIGHEST, preferred_element_type=F32)
            turned = jnp.sum(pltpu.roll(both, TILE + 1, 1, stride=1, stride_axis=0), axis=0, keepdims=True)
            far_total = jnp.sum(jnp.sum(kept[index, 2], axis=0, keepdims=True), axis=1, keepdims=True)
            turned = turned + jnp.where(lane[:1] == 2 * TILE - 1, far_total, 0.0)
            by_distance = by_distance + jnp.where(row == index, turned, 0.0)
        r.bias[slot] = lax.dot_general(
            by_distance, one_hot, (((1,), (1,)), ((), ())), precision=lax.Precision.HIGHEST, preferred_element_type=F32
        )
        for k, j in ((4, 1), (6, 0)):

            @pl.when(step == k)
            def _(j=j):
                sl.kv_two.pair[j].sent()
                sl.q_two.pair[j].sent()

        slot_products(sl.kv_one, sl.q_one, r.n, r.n)
        tick(range(4, 8), 3)
        add_rows(r.acc_a, slice(0, 3 * GROUP), ins.wt_one[0], step == 4)

    @pl.when(step == 7)
    def _():
        sl.kv_one.enter(0)
        sl.q_one.enter(0)
        gains, bias = r.gains, r.bias
        memory_swap.sent()
        memory_put.wait()
        tok.wait()
        norm_back(r.hidden, ins.self_gain, r.acc_a, r.after, 0, None)
        tokens_swap.start()
        tokens_put.start()
        gain_copies[0].start()
        bias_copies[0].start()
        bias_copies[1].start()
        sl.kv_one.take()
        sh.gate.sum.add(1)
        sh.up.last()
        sh.down_a.last()
        gain_copies[0].done()
        gains[...] = gains[...] + r.gains_got[0]
        bias_copies[0].done()
        bias_copies[1].done()
        bias[0] = bias[0] + r.bias_got[0]
        bias[2] = bias[2] + r.bias_got[1]
        gain_copies[1].start()
        bias_copies[2].start()
        sh.down_b.last()
        sl.q_one.take()
        sl.kv_one.own.add(0)
        gain_copies[1].done()
        gains[...] = gains[...] + r.gains_got[1]
        bias_copies[2].done()
        bias[0] = bias[0] + r.bias_got[2]
        gain_copies[2].start()
        bias_copies[3].start()
        sh.out_one.sum.add(1)
        sl.q_one.own.add(0)
        sh.gate.last()
        sh.out_two.last()
        gain_copies[2].done()
        gains[...] = gains[...] + r.gains_got[2]
        bias_copies[3].done()
        bias[0] = bias[0] + r.bias_got[3]
        for k in range(depth - 1):
            gain_copies[3 + k].start()
            bias_copies[4 + k].start()
        outs.wq_two[...] = sl.q_two.finish()
        put_heads((outs.wk_two, outs.wv_two), sl.kv_two.finish())
        put_heads((outs.wk_one, outs.wv_one), sl.kv_one.finish())
        gain_total, bias_total = gains[...], bias[0]
        for k in range(depth - 1):
            gain_copies[3 + k].done()
            bias_copies[4 + k].done()
            gain_total = gain_total + r.gains_got[3 + k]
            bias_total = bias_total + r.bias_got[4 + k]
        outs.gains[...] = gain_total
        outs.bias[...] = bias_total
        sh.up.store(outs.up, 0, outs.up.shape[1] // 2)
        sh.down_a.store(outs.down, 0, outs.down.shape[1] // 2)
        sh.down_b.store(outs.down, outs.down.shape[1] // 4, outs.down.shape[1] // 2)
        sh.gate.store(outs.gate, 0, outs.gate.shape[1] // 2)
        sh.out_two.store(outs.out_two, 0, outs.out_two.shape[1] // 2)
        sh.out_one.last()
        outs.wq_one[...] = sl.q_one.finish()
        sh.out_one.store(outs.out_one, 0, outs.out_one.shape[1] // 2)
        for name in SHARED_ORDER:
            unit = getattr(shared, name)
            unit.sent()
            if unit is not sh.out_two:
                unit.pair.sent()
        for name in SLOT_ORDER:
            getattr(slots, name).sent()
        for j in range(2):
            sl.kv_one.pair[j].sent()
            sl.q_one.pair[j].sent()
        layer_swap.got()
        memory_swap.got()
        tokens_swap.done()
        tokens_put.wait()


def backward_call(batch_size, operands):
    depth = batch_size // 2
    tok = operands["loaded"]["tok"]
    model = tok.shape[1]
    share = model // batch_size
    anywhere = pl.BlockSpec(memory_space=pl.ANY)

    def fixed(shape):
        return pl.BlockSpec(shape, lambda t: (0,) * len(shape))

    def early(array):
        return pl.BlockSpec((1,) + array.shape[1:], lambda t: (3 - t + (t // 4) * (t - 3), 0, 0))

    def late(array):
        return pl.BlockSpec((1,) + array.shape[1:], lambda t: (3 - (t // 4) * (t - 4), 0, 0))

    kinds = dict(
        segs=lambda a: pl.BlockSpec(memory_space=pltpu.SMEM), kv_two=early, q_two=early, lse_two=early, wt_two=early,
        qkv_one=late, lse_one=late, wt_one=late, table=late, loaded=lambda a: anywhere, sends=lambda a: anywhere,
        keeps=lambda a: anywhere, layer=lambda a: anywhere,
    )
    in_specs = {
        name: jax.tree.map(kinds.get(name, lambda a: fixed(a.shape)), value) for name, value in operands.items()
    }
    keeps = operands["keeps"]
    shapes = {name: keeps[name].shape[3:] for name in keeps}
    shapes.update(out_two=(model // (4 * depth), model // 2), out_one=(model // (4 * depth), model // 2))
    block = jax.ShapeDtypeStruct((2, HALF, model), BF16)

    def wide(rows, columns):
        return jax.ShapeDtypeStruct((rows, columns), F32)

    head = wide(share, GROUP)
    outs = dict(
        layer=block, memory=block, tokens=block,
        gate=wide(shapes["gate"][0] // 2, 2 * shapes["gate"][1]), up=wide(shapes["up"][0] // 2, 2 * shapes["up"][1]),
        down=wide(shapes["down_a"][0] // 2, 4 * shapes["down_a"][1]),
        out_two=wide(shapes["out_two"][0] // 2, model), out_one=wide(shapes["out_one"][0] // 2, model),
        wq_two=head, wk_two=head, wv_two=head, wq_one=head, wk_one=head, wv_one=head,
        gains=wide(8, model), bias=wide(8, TILE),
    )
    out_specs = {name: anywhere if s is block else fixed(s.shape) for name, s in outs.items()}

    def room(*shape, kind=BF16):
        return pltpu.VMEM(shape, kind)

    scratch = {}
    for name, order in SHARED_ORDER.items():
        rows, lanes = shapes[name]
        scratch[name] = dict(
            total=room(depth, 2, 2, rows, lanes),
            got=[room(*s) for s in Sum.rooms(depth, 3, order, rows, lanes)],
            last=room(2, rows // 2, lanes, kind=F32), other=room(rows // 2, lanes, kind=F32),
        )
    for name, (y_first, order) in SLOT_ORDER.items():
        lanes = 2 * GROUP if name.startswith("kv") else GROUP
        got = [room(*s) for s in Sum.rooms(depth, 2, order, share, lanes)]
        both = room(2, depth, 2, share, lanes)
        scratch[name] = dict(total=both, pair=both, got=got)
        if y_first:
            scratch[name].update(across=room(depth, 2, share, lanes))
        else:
            scratch[name].update(across=room(share, lanes), chunk=room(share, lanes), far=list(got))
    scratch.update(
        pairs={name: room(depth, 2, 2, *shapes[name]) for name in keeps},
        out_send=room(depth, 2, 2, *shapes["out_one"]), out_pair=room(depth, 2, 2, *shapes["out_one"]), kv_send=room(2, depth, 2, share, 2 * GROUP),
        q_send=room(2, depth, 2, share, GROUP), block=room(2, HALF, model), branch=room(model, BLOCK),
        acc_a=room(BLOCK, model, kind=F32), acc_b=room(BLOCK, model, kind=F32), dqkv=room(BLOCK, 3 * GROUP),
        dq=room(GROUP, BLOCK), do=room(GROUP, BLOCK), mask=room(BLOCK, BLOCK), gains=room(8, model, kind=F32),
        gains_got=room(depth + 2, 8, model, kind=F32), bias=room(4, 8, TILE, kind=F32),
        bias_got=room(depth + 3, 8, TILE, kind=F32),
        after=room(BLOCK, model, kind=F32), hidden=room(BLOCK, model, kind=F32),
        wo=room(model, model), ctx=room(model, BLOCK), n=room(model, BLOCK), mem=room(model, BLOCK),
    )
    z = depth - 1
    copies = sum(2 + 2 + z for _ in SHARED_ORDER) + 3 + (3 + z) + (4 + z)
    copies += sum(2 + (1 + z) + 1 + (0 if y_first else 1 + z) for y_first, _ in SLOT_ORDER.values())
    scratch.update(send=pltpu.SemaphoreType.DMA((copies,)), recv=pltpu.SemaphoreType.DMA((copies,)))
    scratch.update(load=pltpu.SemaphoreType.DMA((18,)))

    arrays, in_tree = jax.tree.flatten(operands)
    out_shapes, out_tree = jax.tree.flatten(outs)
    rooms, room_tree = jax.tree.flatten(scratch)

    def kernel(*refs):
        a, b = len(arrays), len(arrays) + len(out_shapes)
        backward_kernel(
            depth, Named(jax.tree.unflatten(in_tree, refs[:a])), Named(jax.tree.unflatten(out_tree, refs[a:b])),
            Named(jax.tree.unflatten(room_tree, refs[b:])),
        )

    results = pl.pallas_call(
        kernel,
        grid=(8,),
        in_specs=jax.tree.leaves(in_specs),
        out_specs=jax.tree.leaves(out_specs),
        out_shape=out_shapes,
        scratch_shapes=rooms,
        compiler_params=pltpu.CompilerParams(
            collective_id=0, has_side_effects=True, vmem_limit_bytes=66_000_000, dimension_semantics=("arbitrary",)
        ),
        cost_estimate=pl.CostEstimate(flops=20_000_000_000, bytes_accessed=40_000_000, transcendentals=6_000_000),
    )(*arrays)
    return Named(jax.tree.unflatten(out_tree, results))


PIECES = 3


class Gather:
    def __init__(self, place, copies, slots):
        self.slots = slots
        half = slots.shape[1] // 2
        size = half // PIECES
        self.core = copies.new(lambda: slots.at[0], lambda: slots.at[1], place.to_core)

        def rows(side, j):
            return pl.ds(pl.multiple_of(side * half + j * size, 32), size)

        def make(source, target, side, device):
            return [
                copies.new(
                    (lambda j: lambda: slots.at[source, rows(side, j)])(j),
                    (lambda j: lambda: slots.at[target, rows(side, j)])(j), device,
                )
                for j in range(PIECES)
            ]

        self.over_y = make(0, 2, place.x, place.to_y)
        self.over_x = make(2, 2, place.x, place.to_x)
        self.near = make(2, 3, place.x, place.to_core)
        self.far = make(2, 3, 1 - place.x, place.to_core)

    def start(self):
        for copy in self.over_y:
            copy.start()
        self.core.start()

    def pass_y(self, j):
        self.over_y[j].got()
        self.over_x[j].start()
        self.near[j].start()

    def pass_x(self, j):
        self.over_x[j].got()
        self.far[j].start()

    def ready(self):
        for copy in self.near + self.far:
            copy.got()

    def sent(self):
        for copy in [self.core] + self.over_y + self.over_x + self.near + self.far:
            copy.sent()


def forward_kernel(ins, outs, r):
    place = Place(1)
    step = pl.program_id(0)
    core = place.core
    copies = Copies(r.send, r.recv)
    segs = Tiles(place, ins.segs)
    gather_one = Gather(place, copies, r.wt_one)
    gather_two = Gather(place, copies, r.wt_two)
    tables = [
        copies.new((lambda a: lambda: r.table.at[a])(a), (lambda b: lambda: r.table.at[b])(b), d)
        for a, b, d in ((0, 1, place.to_core), (0, 2, place.to_y), (2, 3, place.to_core))
    ]
    swaps = {}
    tok_swap = copies.new(lambda: ins.tokens.at[1 - core], lambda: r.tok_in.at[core], place.to_core)
    mem_swap = copies.new(lambda: ins.memory.at[1 - core], lambda: r.mem_in.at[core], place.to_core)
    cot_swap = copies.new(lambda: ins.cotangent.at[1 - core], lambda: r.cot_in.at[core], place.to_core)
    assert copies.count == r.send.shape[0], copies.count
    count = [0]

    def load(source, target):
        count[0] += 1
        return pltpu.make_async_copy(source, target, r.load.at[count[0] - 1])

    tok_own = load(ins.tokens.at[core], r.tok_in.at[core])
    mem_own = load(ins.memory.at[core], r.mem_in.at[core])
    cot_own = load(ins.cotangent.at[core], r.cot_in.at[core])

    def load_group(key, value, query, slots):
        return [
            load(source.at[pl.ds(at, size)], slots.at[0, pl.ds(to, size)])
            for source, at, to, size in (
                (key, 0, 0, 128), (value, 0, 128, 128), (key, 128, 256, 64), (value, 128, 320, 64), (query, 0, 384, GROUP)
            )
        ]

    raw_one = load_group(ins.self_key, ins.self_value, ins.self_query, r.wt_one)
    raw_two = load_group(ins.cross_key, ins.cross_value, ins.cross_query, r.wt_two)
    out_one, out_two = load(ins.self_out, r.wo_one), load(ins.cross_out, r.wo_two)
    puts = Named({name: load(getattr(r, name), getattr(outs, name)) for name in vars(outs)})


    def normed(hidden, gain, target):
        for part in range(4):
            rows = slice(part * TILE, (part + 1) * TILE)
            h = hidden[rows, :]
            scale = lax.rsqrt(jnp.mean(h * h, axis=-1, keepdims=True) + NORM_EPS)
            target[:, rows] = jnp.transpose((h * scale * row_of(gain)).astype(BF16))

    def project_out(context, weights, base, target):
        for part in range(2):
            rows = slice(part * HALF, (part + 1) * HALF)
            target[rows, :] = base[rows, :] + dot(jnp.transpose(context[:, rows]), weights[...])

    def cross_keys(slot):
        r.kv_two[slot] = dot(r.wt_two[slot, KV, :], r.mem[...]).astype(BF16)

    plan = {}

    def at(point, *tasks):
        plan.setdefault(point, []).extend(tasks)

    one, two = gather_one, gather_two
    at((0, 1), lambda: one.pass_y(0))
    at((1, 0), lambda: one.pass_y(1))
    at((1, 1), lambda: one.pass_x(0), tables[1].got, tables[2].start)
    at((2, 1), lambda: two.pass_y(0))
    at((2, 2), lambda: two.pass_y(1), lambda: two.pass_x(0))
    at((3, 1), lambda: two.pass_y(2), lambda: two.pass_x(1))
    at((4, 0), lambda: two.pass_x(2))

    def tick(steps, index):
        for k in steps:
            if (k, index) in plan:

                def run(tasks=plan[k, index]):
                    for task in tasks:
                        task()

                pl.when(step == k)(run)

    @pl.when(step == 0)
    def _():
        barrier = pltpu.get_barrier_semaphore()
        for device in (place.to_core, place.to_y, place.to_x):
            pl.semaphore_signal(barrier, inc=1, device_id=device, device_id_type=MESH)
        for copy in raw_one + [tok_own] + raw_two + [mem_own, out_one, out_two, cot_own]:
            copy.start()
        r.table[0] = jnp.zeros_like(r.table[0])
        r.table[0, :HEADS, : ins.table.shape[1]] = ins.table[...]
        for copy in raw_one:
            copy.wait()
        pl.semaphore_wait(barrier, 3)
        tok_swap.start()
        gather_one.start()
        tables[0].start()
        tables[1].start()
        mem_swap.start()
        cot_swap.start()
        tok_own.wait()
        tok_swap.got()
        for half in range(2):
            r.tok[half * HALF : (half + 1) * HALF, :] = r.tok_in[half].astype(F32)
        puts.tok.start()
        normed(r.tok, ins.self_gain, r.n_one)
        puts.n_one.start()
        for copy in raw_two:
            copy.wait()
        gather_two.start()

    @pl.when(step == 1)
    def _():
        gather_one.core.got()
        tables[0].got()

    @pl.when(step == 2)
    def _():
        mem_own.wait()
        mem_swap.got()
        for half in range(2):
            r.mem[:, half * HALF : (half + 1) * HALF] = jnp.transpose(r.mem_in[half])
        puts.mem.start()
        cot_own.wait()
        cot_swap.got()
        for half in range(2):
            r.cot[half * HALF : (half + 1) * HALF, :] = r.cot_in[half]
        puts.cot.start()
        one.pass_y(2)
        one.pass_x(1)
        gather_two.core.got()
        cross_keys(0)
        cross_keys(1)
        one.pass_x(2)
        one.ready()
        puts.wt_one.start()
        tables[2].got()
        puts.table.start()

    slot = step % 4
    rows_at = pl.ds(pl.multiple_of(place.group(slot) * GROUP, 16), GROUP)

    @pl.when(step < 4)
    def _():
        r.qkv_one[slot] = dot(r.wt_one[slot], r.n_one[...]).astype(BF16)
        self_forward(
            r.qkv_one.at[slot, KV], r.qkv_one.at[slot, QS], r.table[slot], ins.hot[...], segs,
            r.ctx_one.at[rows_at], r.lse_one.at[slot], lambda h: tick(range(4), h),
        )

    @pl.when(step == 4)
    def _():
        puts.qkv_one.start()
        puts.ctx_one.start()
        puts.lse_one.start()
        out_one.wait()
        project_out(r.ctx_one, r.wo_one, r.tok, r.first)
        puts.first.start()
        normed(r.first, ins.cross_gain, r.n_two)
        puts.n_two.start()
        key_mask(segs, key_segments(place, ins.memsegs), r.mask)

    @pl.when(step == 6)
    def _():
        two.ready()
        puts.wt_two.start()

    @pl.when(step >= 4)
    def _():
        @pl.when(step >= 6)
        def _():
            cross_keys(slot)

        r.q_two[slot] = dot(r.wt_two[slot, QS, :], r.n_two[...]).astype(BF16)
        cross_forward(
            r.kv_two.at[slot], r.q_two.at[slot], r.mask, r.ctx_two.at[rows_at], r.lse_two.at[slot],
            lambda h: tick(range(4, 8), h),
        )

    @pl.when(step == 7)
    def _():
        out_two.wait()
        project_out(r.ctx_two, r.wo_two, r.first, r.second)
        for put in (puts.second, puts.ctx_two, puts.q_two, puts.kv_two, puts.lse_two):
            put.start()
        gather_one.sent()
        gather_two.sent()
        for copy in tables + [tok_swap, mem_swap, cot_swap]:
            copy.sent()
        for name in vars(outs):
            getattr(puts, name).wait()


def forward_call(operands):
    tokens = operands["tokens"]
    model = tokens.shape[2]
    anywhere = pl.BlockSpec(memory_space=pl.ANY)

    def fixed(array):
        return pl.BlockSpec(array.shape, lambda t: (0,) * array.ndim)

    small = dict(self_gain=fixed, cross_gain=fixed, table=fixed, hot=fixed, memsegs=fixed)
    small.update(segs=lambda a: pl.BlockSpec(memory_space=pltpu.SMEM))
    in_specs = {name: small.get(name, lambda a: anywhere)(a) for name, a in operands.items()}

    def room(*shape, kind=BF16):
        return pltpu.VMEM(shape, kind)

    kept = dict(
        tok=room(BLOCK, model, kind=F32), mem=room(model, BLOCK), cot=room(BLOCK, model), n_one=room(model, BLOCK),
        n_two=room(model, BLOCK), qkv_one=room(4, 3 * GROUP, BLOCK), kv_two=room(4, 2 * GROUP, BLOCK),
        q_two=room(4, GROUP, BLOCK), ctx_one=room(model, BLOCK), ctx_two=room(model, BLOCK),
        lse_one=room(4, 8, BLOCK, kind=F32), lse_two=room(4, 8, BLOCK, kind=F32),
        first=room(BLOCK, model, kind=F32), second=room(BLOCK, model, kind=F32),
        wt_one=room(4, 3 * GROUP, model), wt_two=room(4, 3 * GROUP, model), table=room(4, 8, TILE, kind=F32),
    )
    block = tokens.shape[1:]
    copies = 2 * (1 + 4 * PIECES) + 3 + 3
    scratch = dict(
        kept, tok_in=room(2, *block), mem_in=room(2, *block), cot_in=room(2, *block),
        wo_one=room(model, model), wo_two=room(model, model), mask=room(BLOCK, BLOCK, kind=F32),
        send=pltpu.SemaphoreType.DMA((copies,)), recv=pltpu.SemaphoreType.DMA((copies,)),
        load=pltpu.SemaphoreType.DMA((15 + len(kept),)),
    )
    outs = {name: jax.ShapeDtypeStruct(m.shape, m.dtype) for name, m in kept.items()}
    arrays, in_tree = jax.tree.flatten(operands)
    out_shapes, out_tree = jax.tree.flatten(outs)
    rooms, room_tree = jax.tree.flatten(scratch)

    def kernel(*refs):
        a, b = len(arrays), len(arrays) + len(out_shapes)
        forward_kernel(
            Named(jax.tree.unflatten(in_tree, refs[:a])), Named(jax.tree.unflatten(out_tree, refs[a:b])),
            Named(jax.tree.unflatten(room_tree, refs[b:])),
        )

    results = pl.pallas_call(
        kernel,
        grid=(8,),
        in_specs=jax.tree.leaves(in_specs),
        out_specs=[anywhere] * len(out_shapes),
        out_shape=out_shapes,
        scratch_shapes=rooms,
        compiler_params=pltpu.CompilerParams(
            collective_id=1, has_side_effects=True, vmem_limit_bytes=60_000_000, dimension_semantics=("arbitrary",)
        ),
        cost_estimate=pl.CostEstimate(flops=10_000_000_000, bytes_accessed=40_000_000, transcendentals=6_000_000),
    )(*arrays)
    return Named(jax.tree.unflatten(out_tree, results))


def finish_call(results, devices, buckets):
    plain = {name: a for name, a in results.items() if name not in ("gains", "bias")}
    share = results["gains"].shape[1] // devices
    outs = {name: jax.ShapeDtypeStruct(a.shape, a.dtype) for name, a in plain.items()}
    anywhere = pl.BlockSpec(memory_space=pl.ANY)
    count = len(plain)

    def kernel(gains, bias, *refs):
        sources, (bias_out, *gain_outs), targets = refs[:count], refs[count : count + 4], refs[count + 4 : 2 * count + 4]
        rooms, semaphores = refs[2 * count + 4 : 3 * count + 4], refs[3 * count + 4]
        takes = [pltpu.make_async_copy(s, r, semaphores.at[k]) for k, (s, r) in enumerate(zip(sources, rooms))]
        puts = [pltpu.make_async_copy(r, t, semaphores.at[count + k]) for k, (r, t) in enumerate(zip(rooms, targets))]
        for take in takes:
            take.start()
        bias_out[...] = bias[:HEADS, :buckets]
        first = (lax.axis_index("batch") * lax.axis_size("head") + lax.axis_index("head")) * share
        turned = pltpu.roll(gains[...], gains.shape[1] - first, 1)
        for k, out in enumerate(gain_outs):
            out[...] = jnp.reshape(turned[k : k + 1, :share], (share,))
        for take, put in zip(takes, puts):
            take.wait()
            put.start()
        for put in puts:
            put.wait()

    def fixed(shape):
        return pl.BlockSpec(shape, lambda: (0,) * len(shape))

    small = [jax.ShapeDtypeStruct((HEADS, buckets), F32)] + [jax.ShapeDtypeStruct((share,), F32)] * 3
    bias, *rest = pl.pallas_call(
        kernel,
        in_specs=[fixed(results["gains"].shape), fixed(results["bias"].shape)] + [anywhere] * count,
        out_specs=[fixed(a.shape) for a in small] + [anywhere] * count,
        out_shape=small + list(outs.values()),
        scratch_shapes=[pltpu.VMEM(a.shape, a.dtype) for a in plain.values()] + [pltpu.SemaphoreType.DMA((2 * count,))],
    )(results["gains"], results["bias"], *plain.values())
    return dict(zip(plain, rest[3:]), bias=bias, gain_0=rest[0], gain_1=rest[1], gain_2=rest[2])


def norm(hidden, gain):
    scale = lax.rsqrt(jnp.mean(hidden * hidden, axis=-1, keepdims=True) + NORM_EPS)
    return (hidden * scale * gain).astype(BF16)


def norm_back(hidden, gain, grad):
    scale = lax.rsqrt(jnp.mean(hidden * hidden, axis=-1, keepdims=True) + NORM_EPS)
    weighted = grad * gain
    inner = jnp.mean(weighted * hidden, axis=-1, keepdims=True)
    return weighted * scale - hidden * (scale * scale * scale * inner), jnp.sum(grad * hidden * scale, axis=0)


def over_tokens(left, right):
    return lax.dot_general(left, right, (((0,), (0,)), ((), ())), preferred_element_type=F32)


def by_transpose(left, right):
    return lax.dot_general(left, right, (((1,), (1,)), ((), ())), preferred_element_type=F32)


def gelu_parts(value):
    inner = np.float32(np.sqrt(2.0 / np.pi)) * (value + 0.044715 * (value * value * value))
    bend = jnp.tanh(inner)
    slope = np.float32(np.sqrt(2.0 / np.pi)) * (1.0 + 3.0 * 0.044715 * (value * value))
    gelu = 0.5 * value * (1.0 + bend)
    return gelu, 0.5 * (1.0 + bend) + 0.5 * value * (1.0 - bend * bend) * slope


def on_device(
    tokens, memory, cotangent, target_segments, memory_segments, self_gain, self_query, self_key,
    self_value, self_out, position_bias, cross_gain, cross_query, cross_key, cross_value, cross_out,
    ff_gain, ff_gate, ff_up, ff_down,
):
    heads_axis, batch_axis = lax.axis_size("head"), lax.axis_size("batch")
    core = lax.axis_index("head") & 1
    rows, part, model = tokens.shape
    assert part * 2 == BLOCK and rows == 2 and heads_axis == 4
    assert position_bias.shape[1] == HEADS and self_query.shape[1] == GROUP
    one_hot = jnp.asarray(bucket_one_hot(position_bias.shape[0]))

    fwd = forward_call(
        dict(
            tokens=tokens, memory=memory, cotangent=cotangent, segs=target_segments, memsegs=memory_segments, hot=one_hot,
            self_gain=self_gain, cross_gain=cross_gain, table=position_bias.T,
            self_query=self_query.T, self_key=self_key.T, self_value=self_value.T, self_out=self_out,
            cross_query=cross_query.T, cross_key=cross_key.T, cross_value=cross_value.T, cross_out=cross_out,
        )
    )
    second_sum, cot = fwd.second, fwd.cot
    normed_three = norm(second_sum, ff_gain)
    gate_value = dot(normed_three, ff_gate)
    up_value = dot(normed_three, ff_up)
    gelu, slope = gelu_parts(gate_value)
    activation = (gelu * up_value).astype(BF16)
    layer = (second_sum + dot(activation, ff_down)).astype(BF16)

    grad_act = by_transpose(cot, ff_down)
    grad_gate = (grad_act * up_value * slope).astype(BF16)
    grad_up = (grad_act * gelu).astype(BF16)
    grad_three = by_transpose(grad_gate, ff_gate) + by_transpose(grad_up, ff_up)
    back, ff_gain_grad = norm_back(second_sum, ff_gain, grad_three)
    grad_second = cot.astype(F32) + back

    def halves(left, right, pieces):
        lanes = left.shape[1] // (2 * pieces)
        chunks = batch_axis // 2, 2, 2, right.shape[1] // (2 * batch_axis), lanes
        found = []
        for piece in range(pieces):
            found.append([
                over_tokens(
                    right, lax.dynamic_slice_in_dim(left, (which * pieces + piece) * lanes, lanes, 1)
                ).astype(BF16).reshape(chunks)
                for which in (1 - core, core)
            ])
        return found

    (gate,) = halves(normed_three, grad_gate, 1)
    (up,) = halves(normed_three, grad_up, 1)
    down_a, down_b = halves(activation, cot, 2)
    done = backward_call(
        batch_axis,
        dict(
            segs=target_segments, memsegs=memory_segments, hot=one_hot, self_gain=self_gain, cross_gain=cross_gain,
            ff_gain_grad=ff_gain_grad,
            kv_two=fwd.kv_two, q_two=fwd.q_two, lse_two=fwd.lse_two, wt_two=fwd.wt_two,
            qkv_one=fwd.qkv_one, lse_one=fwd.lse_one, wt_one=fwd.wt_one, table=fwd.table,
            loaded=dict(
                after=grad_second, wo_two=cross_out, ctx_two=fwd.ctx_two, n_two=fwd.n_two, mem=fwd.mem,
                first=fwd.first, wo_one=self_out, ctx_one=fwd.ctx_one, n_one=fwd.n_one, tok=fwd.tok,
            ),
            sends=dict(gate=gate[0], up=up[0], down_a=down_a[0], down_b=down_b[0]),
            keeps=dict(gate=gate[1], up=up[1], down_a=down_a[1], down_b=down_b[1]),
            layer=layer.reshape(2, part, model),
        ),
    )
    done = Named(finish_call(vars(done), heads_axis * batch_axis, position_bias.shape[0]))
    return (
        done.layer, done.tokens, done.memory, done.gain_0, done.wq_one, done.wk_one, done.wv_one, done.out_one.T,
        done.bias.T, done.gain_1, done.wq_two, done.wk_two, done.wv_two, done.out_two.T, done.gain_2,
        done.gate.T, done.up.T, done.down.T,
    )


def solution(mesh):
    tokens = P("batch", "head", None)
    rows = P("batch", None)
    columns = P(None, "head")
    split = P("batch", "head")
    every = P(None, ("batch", "head"))
    gain = P(("batch", "head"))
    return jax.shard_map(
        on_device,
        mesh=mesh,
        in_specs=(
            tokens, tokens, tokens, rows, rows, P(), columns, columns, columns, P(), columns, P(),
            columns, columns, columns, P(), P(), P(), P(), P(),
        ),
        out_specs=(
            tokens, tokens, tokens, gain, split, split, split, every, columns, gain,
            split, split, split, every, gain, every, every, every,
        ),
        check_vma=False,
    )
```

```python
import jax
import jax.numpy as jnp
import numpy as np
from jax import lax
from jax.experimental import pallas as pl
from jax.experimental.pallas import tpu as pltpu
from jax.sharding import PartitionSpec as P

NORM_EPS = 1e-06
MASKED = -1e30
BLOCK = 512
TILE = 128
HALF = 256
SIZE = 64
HEADS = 3
GROUP = HEADS * SIZE
F32 = jnp.float32
BF16 = jnp.bfloat16
MESH = pl.DeviceIdType.MESH


def bucket_edges():
    distance = np.arange(1.0, 8192.0)
    far_bucket = 16.0 + np.floor(np.log(np.maximum(distance, 16.0) / 16.0) / np.log(8.0) * 16.0)
    bucket_value = np.where(distance < 16, distance, np.minimum(far_bucket, 31.0))
    return [int(distance[np.argmax(bucket_value >= bucket_level)]) for bucket_level in range(1, 32)]


def bucket_one_hot(buckets):
    ids = np.zeros(2 * TILE, np.int32)
    for edge in bucket_edges():
        ids += np.arange(2 * TILE) >= edge
    assert bucket_edges()[-1] <= TILE + 1
    assert buckets <= TILE and ids[-1] == buckets - 1
    return (np.arange(TILE)[:, None] == ids[None, :]).astype(np.float32)


def dot(left, right):
    return lax.dot_general(left, right, (((1,), (0,)), ((), ())), preferred_element_type=F32)


KEY_AT = ((0, 0), (0, 1), (2, 0))
VALUE_AT = ((1, 0), (1, 1), (2, 1))
QUERY_START = 2 * GROUP


def rows_of(at):
    tile, place = at
    return slice(tile * 128 + place * SIZE, tile * 128 + (place + 1) * SIZE)


def lanes_of(at):
    return slice(at[0] * 128, (at[0] + 1) * 128)


def spread(head_rows, place):
    blank = jnp.zeros_like(head_rows)
    return jnp.concatenate((head_rows, blank) if place == 0 else (blank, head_rows), axis=0)


def bias_tiles(table, index, one_hot):
    by_distance = jnp.dot(
        table, one_hot, precision=lax.Precision.HIGHEST, preferred_element_type=F32
    )[index : index + 1]
    wide = jnp.broadcast_to(by_distance, (TILE, 2 * TILE))
    turned = pltpu.roll(wide, 0, 1, stride=1, stride_axis=0)
    key = lax.broadcasted_iota(jnp.int32, (TILE, TILE), 0)
    query = lax.broadcasted_iota(jnp.int32, (TILE, TILE), 1)
    near = jnp.where(key <= query, turned[:, :TILE], MASKED)
    return near, turned[:, TILE:], by_distance[0, 2 * TILE - 1]


def self_tile(scores, key_tile, query_tile, tiles, seg_ref, base):
    near, next_one, far = tiles
    if key_tile == query_tile:
        return scores + near
    same = seg_ref[base + key_tile] == seg_ref[base + query_tile]
    shift = jnp.where(same, 0.0, MASKED)
    if key_tile == query_tile - 1:
        return scores + next_one + shift
    return scores + (far + shift)


def self_forward(kv, q, table, one_hot, seg_ref, out, lse, tick):
    key_values = jnp.transpose(kv[...])
    for index in range(HEADS):
        rows = slice(index * SIZE, (index + 1) * SIZE)
        keys = key_values[:, lanes_of(KEY_AT[index])]
        query = spread(q[rows, :], KEY_AT[index][1])
        tiles = bias_tiles(table, index, one_hot)
        for half in range(2):
            end = (half + 1) * HALF
            scores = dot(keys[:end], query[:, half * HALF : (half + 1) * HALF])
            columns, totals = [], []
            for part in range(2):
                query_tile = 2 * half + part
                parts = [
                    self_tile(
                        scores[kt * TILE : (kt + 1) * TILE, part * TILE : (part + 1) * TILE],
                        kt, query_tile, tiles, seg_ref, 0,
                    )
                    for kt in range(query_tile + 1)
                ]
                top = jnp.max(parts[0], axis=0, keepdims=True)
                for piece in parts[1:]:
                    top = jnp.maximum(top, jnp.max(piece, axis=0, keepdims=True))
                probs = [jnp.exp(piece - top) for piece in parts]
                total = jnp.sum(probs[0], axis=0, keepdims=True)
                for piece in probs[1:]:
                    total = total + jnp.sum(piece, axis=0, keepdims=True)
                probs = [piece.astype(BF16) for piece in probs]
                if part == 0:
                    probs.append(jnp.zeros((TILE, TILE), BF16))
                columns.append(jnp.concatenate(probs, axis=0))
                totals.append(total)
                lse[index : index + 1, query_tile * TILE : (query_tile + 1) * TILE] = top + jnp.log(total)
            weights = jnp.concatenate(columns, axis=1)
            context = dot(kv[rows_of(VALUE_AT[index]), :end], weights)
            context = context / jnp.concatenate(totals, axis=1)
            out[rows, half * HALF : (half + 1) * HALF] = context.astype(BF16)
        tick(index)


def key_mask(seg_ref, memseg, mask_ref):
    rows = jnp.transpose(jnp.broadcast_to(memseg.astype(F32), (TILE, BLOCK)))
    for tile in range(BLOCK // TILE):
        wanted = seg_ref[tile].astype(F32)
        shift = jnp.where(rows == wanted, 0.0, MASKED)
        mask_ref[:, tile * TILE : (tile + 1) * TILE] = shift.astype(mask_ref.dtype)


def cross_forward(kv, q, mask, out, lse, tick):
    key_values = jnp.transpose(kv[...])
    for index in range(HEADS):
        rows = slice(index * SIZE, (index + 1) * SIZE)
        keys = key_values[:, lanes_of(KEY_AT[index])]
        query = spread(q[rows, :], KEY_AT[index][1])
        for half in range(2):
            lanes = slice(half * HALF, (half + 1) * HALF)
            scores = dot(keys, query[:, lanes]) + mask[:, lanes]
            top = jnp.max(scores, axis=0, keepdims=True)
            probs = jnp.exp(scores - top)
            total = jnp.sum(probs, axis=0, keepdims=True)
            context = dot(kv[rows_of(VALUE_AT[index]), :], probs.astype(BF16)) / total
            out[rows, lanes] = context.astype(BF16)
            lse[index : index + 1, lanes] = top + jnp.log(total)
        tick(index)


def grow(old, new):
    if old is None:
        return new
    shared = old.shape[0]
    if shared == new.shape[0]:
        return old + new
    return jnp.concatenate((old + new[:shared], new[shared:]), axis=0)


def only_lanes(wide, at):
    pair = wide[:, lanes_of(at)]
    lane = lax.broadcasted_iota(jnp.int32, pair.shape, 1)
    keep = lane < SIZE if at[1] == 0 else lane >= SIZE
    return jnp.where(keep, pair, jnp.zeros_like(pair))


def moved(wide, index, place):
    if index < 2:
        assert place == index
        return only_lanes(wide, (0, index))
    part = wide[:, 128:192]
    blank = jnp.zeros_like(part)
    return jnp.concatenate((part, blank) if place == 0 else (blank, part), axis=1)


def attention_back(read, tile_of, skip, note, dq_ref, sums_ref, tick):
    key_values = jnp.transpose(read.kv())
    query_tok = jnp.transpose(read.q(slice(0, GROUP)))
    grad_tok = jnp.transpose(read.do(slice(0, GROUP)))
    sums = [None, None, None]
    for index in range(HEADS):
        rows = slice(index * SIZE, (index + 1) * SIZE)
        k_at, v_at = KEY_AT[index], VALUE_AT[index]
        key_pair, value_pair = key_values[:, lanes_of(k_at)], key_values[:, lanes_of(v_at)]
        query_pair = moved(query_tok, index, k_at[1])
        grad_pair = moved(grad_tok, index, v_at[1])
        query_rows = spread(read.q(rows), k_at[1])
        grad_rows = spread(read.do(rows), v_at[1])
        inner = jnp.sum(read.do(rows).astype(F32) * read.o(rows).astype(F32), axis=0, keepdims=True)
        key_sum = value_sum = None
        for half in range(2):
            end = (half + 1) * HALF if skip else BLOCK
            lanes = slice(half * HALF, (half + 1) * HALF)
            scores = dot(key_pair[:end], query_rows[:, lanes])
            grad_probs = dot(value_pair[:end], grad_rows[:, lanes])
            prob_columns, grad_columns = [], []
            for part in range(2):
                query_tile = 2 * half + part
                cut = slice(query_tile * TILE, (query_tile + 1) * TILE)
                here = slice(part * TILE, (part + 1) * TILE)
                total = read.lse(index, cut)
                probs, grads = [], []
                for kt in range(query_tile + 1 if skip else BLOCK // TILE):
                    there = slice(kt * TILE, (kt + 1) * TILE)
                    prob = jnp.exp(tile_of(scores[there, here], index, kt, query_tile) - total)
                    ds = prob * (grad_probs[there, here] - inner[:, cut])
                    note(index, kt, query_tile, ds)
                    probs.append(prob.astype(BF16))
                    grads.append(ds.astype(BF16))
                if skip and part == 0:
                    probs.append(jnp.zeros((TILE, TILE), BF16))
                    grads.append(jnp.zeros((TILE, TILE), BF16))
                prob_columns.append(jnp.concatenate(probs, axis=0))
                grad_columns.append(jnp.concatenate(grads, axis=0))
            probs = jnp.concatenate(prob_columns, axis=1)
            grads = jnp.concatenate(grad_columns, axis=1)
            value_sum = grow(value_sum, dot(probs, grad_pair[lanes]))
            key_sum = grow(key_sum, dot(grads, query_pair[lanes]))
            dq_ref[rows, lanes] = dot(read.k(index, end), grads).astype(BF16)
        for at, total in ((k_at, key_sum), (v_at, value_sum)):
            sums[at[0]] = total if sums[at[0]] is None else sums[at[0]] + total
        tick(index)
    for tile in range(3):
        sums_ref[:, tile * 128 : (tile + 1) * 128] = sums[tile].astype(BF16)
    sums_ref[:, QUERY_START : QUERY_START + GROUP] = jnp.transpose(dq_ref[...])


def row_of(ref):
    return jnp.reshape(ref[...], (1, ref.shape[0]))


class Tiles:
    def __init__(self, place, ref):
        self.place, self.ref = place, ref

    def __getitem__(self, tile):
        return self.ref[self.place.core, self.place.y * BLOCK + tile * TILE]


def key_segments(place, ref):
    lanes = pl.ds(pl.multiple_of(place.y * BLOCK, BLOCK), BLOCK)
    return jnp.where(place.core == 0, ref[0:1, lanes], ref[1:2, lanes])


class Read:
    def __init__(self, kv, k, q, do, o, lse):
        self.kv, self.k, self.q, self.do, self.o, self.lse = kv, k, q, do, o, lse


class Named:
    def __init__(self, tree):
        for key, value in tree.items():
            setattr(self, key, Named(value) if isinstance(value, dict) else value)


class Copies:
    def __init__(self, send, recv):
        self.send, self.recv, self.count, self.sent = send, recv, 0, []

    def new(self, source, target, device):
        at = self.count
        self.count += 1
        return Copy(self, at, source, target, device)


class Copy:
    def __init__(self, owner, at, source, target, device):
        self.owner, self.at, self.source, self.target, self.device = owner, at, source, target, device

    def make(self):
        return pltpu.make_async_remote_copy(
            src_ref=self.source(), dst_ref=self.target(), send_sem=self.owner.send.at[self.at],
            recv_sem=self.owner.recv.at[self.at], device_id=self.device, device_id_type=MESH,
        )

    def start(self):
        self.make().start()

    def got(self):
        self.make().wait_recv()

    def sent(self):
        self.make().wait_send()

    def done(self):
        self.make().wait()


class Place:
    def __init__(self, depth):
        b, h = lax.axis_index("batch"), lax.axis_index("head")
        self.depth = depth
        self.core, self.y, self.x, self.z = h % 2, h // 2, b % 2, b // 2
        self.to_core = (b, h + 1 - 2 * self.core)
        self.to_y = (b, h + 2 - 4 * self.y)
        self.to_x = (b + 1 - 2 * self.x, h)
        self.to_z = [(lax.rem(self.z + k, depth) * 2 + self.x, h) for k in range(1, depth)]

    def group(self, slot):
        low, high = slot % 2, slot // 2
        return (self.core + low - 2 * self.core * low) + 2 * (self.y + high - 2 * self.y * high)

    def everyone(self):
        return [self.to_core, self.to_y, self.to_x] + self.to_z


Z, X, Y = range(3)


class Sum:
    def __init__(self, place, copies, total, got, order):
        self.place, self.total, self.got, self.order = place, total, got, order
        self.dims = len(total.shape) - 2
        self.stages = []
        for at, axis in enumerate(order):
            room = got[at]
            if axis == Z:
                stage = [
                    copies.new(self.source(at, k), (lambda room, k: lambda: room.at[k - 1])(room, k), place.to_z[k - 1])
                    for k in range(1, place.depth)
                ]
            else:
                device = place.to_x if axis == X else place.to_y
                stage = [copies.new(self.source(at, 1), (lambda room: lambda: room)(room), device)]
            self.stages.append(stage)

    @staticmethod
    def rooms(depth, dims, order, rows, lanes):
        sizes = {Z: depth, X: 2, Y: 2}
        free = list(range(dims))
        shapes = []
        for axis in order:
            free.remove(axis)
            lead = (depth - 1,) if axis == Z else ()
            shapes.append(lead + tuple(sizes[d] for d in free) + (rows, lanes))
        return shapes

    def mine(self, axis):
        return (self.place.z, self.place.x, self.place.y)[axis]

    def source(self, at, k):
        def view():
            index = [slice(None)] * self.dims
            for axis in self.order[:at]:
                index[axis] = self.mine(axis)
            axis = self.order[at]
            index[axis] = lax.rem(self.place.z + k, self.place.depth) if axis == Z else 1 - self.mine(axis)
            return self.total.at[tuple(index)]

        return view

    def start(self, at):
        for copy in self.stages[at]:
            copy.start()

    def value(self, at, free):
        axis = self.order[at]
        later = sorted(self.order[at + 1 :])
        index = [None] * self.dims
        for done in self.order[: at + 1]:
            index[done] = self.mine(done)
        for d, i in zip(later, free):
            index[d] = i
        got = [self.got[at].at[k] for k in range(self.place.depth - 1)] if axis == Z else [self.got[at]]
        return tuple(index), [g[tuple(free)] if free else g[...] for g in got]

    def add(self, at):
        for copy in self.stages[at]:
            copy.got()
        later = sorted(self.order[at + 1 :])

        def one(free):
            index, got = self.value(at, free)
            if len(got) == 1:
                self.total[index] = self.total[index] + got[0]
            else:
                total = self.total[index].astype(F32)
                for g in got:
                    total = total + g.astype(F32)
                self.total[index] = total.astype(BF16)

        def over(dims, free):
            if not dims:
                one(free)
            elif dims[0] == Z:

                @pl.loop(0, self.place.depth)
                def _(z):
                    over(dims[1:], free + [z])

            else:
                for i in range(2):
                    over(dims[1:], free + [i])

        over(later, [])
        self.start(at + 1)

    def finish(self):
        at = len(self.order) - 1
        for copy in self.stages[at]:
            copy.got()
        index, got = self.value(at, [])
        total = self.total[index].astype(F32)
        for g in got:
            total = total + g.astype(F32)
        return total

    def sent(self):
        for stage in self.stages:
            for copy in stage:
                copy.sent()


def add_loop(depth, target, other, inner):
    @pl.loop(0, depth)
    def _(z):
        for index in np.ndindex(*inner):
            target[(z, *index)] = target[(z, *index)] + other[(z, *index)]


class Shared:
    def __init__(self, place, copies, room, order, send, pair):
        self.place, self.room, self.from_pair = place, room, pair
        self.sum = Sum(place, copies, room.total, room.got, order)
        self.pair = copies.new(lambda: send, lambda: pair, place.to_core)
        self.swap = copies.new(lambda: room.last.at[1 - place.core], lambda: room.other, place.to_core)

    def enter(self, keep=None):
        self.pair.got()
        if keep is not None:
            keep.wait()
        add_loop(self.place.depth, self.room.total, self.from_pair, (2, 2))
        self.sum.start(0)

    def last(self):
        total = self.sum.finish()
        rows = total.shape[0] // 2
        self.room.last[0] = total[:rows]
        self.room.last[1] = total[rows:]
        self.swap.start()

    def store(self, out, offset, half):
        self.swap.got()
        lanes = self.room.other.shape[1]
        mine, other = self.room.last[self.place.core], self.room.other[...]
        for which in range(2):
            at = slice(which * half + offset, which * half + offset + lanes)
            out[:, at] = jnp.where(self.place.core == which, mine, other)

    def sent(self):
        self.swap.sent()
        self.sum.sent()


class Slots:
    def __init__(self, place, copies, room, sends, y_first, order):
        self.place, self.room, self.y_first = place, room, y_first
        self.pair = [copies.new((lambda j: lambda: sends.at[j])(j), (lambda j: lambda: room.pair.at[j])(j), place.to_core) for j in range(2)]
        self.own = Sum(place, copies, room.total.at[0], room.got, order)
        if y_first:
            self.across = copies.new(lambda: room.total.at[1], lambda: room.across, place.to_y)
        else:
            self.far = Sum(place, copies, room.total.at[1], room.far, order)
            self.across = copies.new(lambda: room.chunk, lambda: room.across, place.to_y)

    def enter(self, j):
        self.pair[j].got()
        add_loop(self.place.depth, self.room.total.at[j], self.room.pair.at[j], (2,))
        if j == 1:
            if self.y_first:
                self.across.start()
            else:
                self.far.start(0)
        elif not self.y_first:
            self.own.start(0)

    def take(self):
        self.across.got()
        add_loop(self.place.depth, self.room.total.at[0], self.room.across, (2,))
        self.own.start(0)

    def give(self):
        self.room.chunk[...] = self.far.finish().astype(BF16)
        self.across.start()

    def finish(self):
        total = self.own.finish()
        if not self.y_first:
            self.across.got()
            total = total + self.room.across[...].astype(F32)
        return total

    def sent(self):
        self.own.sent()
        self.across.sent()
        if not self.y_first:
            self.far.sent()


SHARED_ORDER = dict(
    gate=(Z, X, Y), up=(Y, X, Z), down_a=(X, Y, Z), down_b=(X, Y, Z), out_two=(X, Y, Z), out_one=(X, Y, Z)
)
SLOT_ORDER = dict(kv_two=(True, (X, Z)), q_two=(False, (X, Z)), kv_one=(True, (X, Z)), q_one=(True, (X, Z)))
KV = slice(0, 2 * GROUP)
QS = slice(2 * GROUP, 3 * GROUP)


def put_heads(ref, kv):
    key_out, value_out = ref
    key_out[:, :128] = kv[:, :128]
    key_out[:, 128:] = kv[:, 256:320]
    value_out[:, :128] = kv[:, 128:256]
    value_out[:, 128:] = kv[:, 320:384]


def backward_kernel(depth, ins, outs, r):
    place = Place(depth)
    step = pl.program_id(0)
    core = place.core
    copies = Copies(r.send, r.recv)
    segs = Tiles(place, ins.segs)

    shared = Named({
        name: Shared(
            place, copies, getattr(r, name), order, getattr(ins.sends, name, r.out_send), getattr(r.pairs, name, r.out_pair)
        )
        for name, order in SHARED_ORDER.items()
    })
    slots = Named({
        name: Slots(place, copies, getattr(r, name), r.kv_send if order_at < 1 else r.q_send, y_first, order)
        for name, (y_first, order), order_at in (
            (n, o, int(getattr(r, n).total.shape[-1] == GROUP)) for n, o in SLOT_ORDER.items()
        )
    })
    layer_swap = copies.new(lambda: r.block.at[1 - core], lambda: outs.layer.at[core], place.to_core)
    memory_swap = copies.new(lambda: r.block.at[1 - core], lambda: outs.memory.at[core], place.to_core)
    tokens_swap = copies.new(lambda: r.block.at[1 - core], lambda: outs.tokens.at[core], place.to_core)
    gain_copies = [
        copies.new(lambda: r.gains, (lambda k: lambda: r.gains_got.at[k])(k), d)
        for k, d in enumerate([place.to_core, place.to_y, place.to_x] + place.to_z)
    ]
    bias_copies = [
        copies.new((lambda s: lambda: r.bias.at[s])(s), (lambda k: lambda: r.bias_got.at[k])(k), d)
        for k, (s, d) in enumerate(
            zip([1, 3, 2, 0] + [0] * (depth - 1), [place.to_core, place.to_core, place.to_y, place.to_x] + place.to_z)
        )
    ]
    assert copies.count == r.send.shape[0], copies.count

    loads = []

    def load(source, target):
        loads.append(pltpu.make_async_copy(source, target, r.load.at[len(loads)]))
        return loads[-1]

    i = ins.loaded
    after, wo_two, ctx_two = load(i.after, r.after), load(i.wo_two, r.wo), load(i.ctx_two, r.ctx)
    n_two, mem, first, tok = load(i.n_two, r.n), load(i.mem, r.mem), load(i.first, r.hidden), load(i.tok, r.hidden)
    wo_one, ctx_one, n_one = load(i.wo_one, r.wo), load(i.ctx_one, r.ctx), load(i.n_one, r.n)
    keeps = Named({
        name: load(getattr(ins.keeps, name), getattr(r, name).total) for name in SHARED_ORDER if hasattr(ins.keeps, name)
    })
    layer_in = load(ins.layer, r.block)
    layer_put = load(r.block.at[core], outs.layer.at[core])
    memory_put = load(r.block.at[core], outs.memory.at[core])
    tokens_put = load(r.block.at[core], outs.tokens.at[core])

    def out_products(unit, context, branch):
        lanes = context.shape[0] // 2
        for which, target in ((1 - core, r.out_send), (core, unit.room.total)):
            side = jnp.transpose(context[pl.ds(pl.multiple_of(which * lanes, 16), lanes), :])
            per = branch.shape[0] // 2
            for part in range(2):
                product = dot(branch[part * per : (part + 1) * per, :], side).astype(BF16)
                rows = target.shape[3]
                for piece in range(per // rows):
                    at = part * (per // rows) + piece
                    target[at // 4, (at // 2) % 2, at % 2] = product[piece * rows : (piece + 1) * rows]
            if which is not core:
                unit.pair.start()

    def weight_products(target, left, lanes):
        rows = target.shape[2]
        per = left.shape[0] // 2
        for part in range(2):
            product = dot(left[part * per : (part + 1) * per, :], r.dqkv[:, lanes]).astype(BF16)
            for piece in range(per // rows):
                at = part * (per // rows) + piece
                target[at // 2, at % 2] = product[piece * rows : (piece + 1) * rows]

    def add_rows(target, lanes, weights, fresh):
        for part in range(2):
            rows = slice(part * HALF, (part + 1) * HALF)
            product = dot(r.dqkv[rows, lanes], weights)

            @pl.when(fresh)
            def _():
                target[rows, :] = product

            @pl.when(jnp.logical_not(fresh))
            def _():
                target[rows, :] = target[rows, :] + product

    def norm_back(hidden, gain, incoming, onto, gain_row, branch):
        total = jnp.zeros((1, hidden.shape[1]), F32)
        for part in range(4):
            rows = slice(part * TILE, (part + 1) * TILE)
            h = hidden[rows, :].astype(F32)
            e = incoming[rows, :]
            scale = lax.rsqrt(jnp.mean(h * h, axis=-1, keepdims=True) + NORM_EPS)
            weighted = e * row_of(gain)
            inner = jnp.mean(weighted * h, axis=-1, keepdims=True)
            result = onto[rows, :] + weighted * scale - h * (scale * scale * scale * inner)
            total = total + jnp.sum(e * h * scale, axis=0, keepdims=True)
            if branch is None:
                r.block[part // 2, (part % 2) * TILE : (part % 2 + 1) * TILE, :] = result.astype(BF16)
            else:
                onto[rows, :] = result
                branch[:, rows] = jnp.transpose(result.astype(BF16))
        r.gains[gain_row : gain_row + 1, :] = total

    plan = {}

    def at(point, *tasks):
        plan.setdefault(point, []).extend(tasks)

    sh, sl = shared, slots
    at((0, 0), lambda: sh.up.enter(keeps.up), sh.out_two.enter)
    at((0, 1), lambda: sh.down_a.enter(keeps.down_a))
    at((0, 2), lambda: sh.down_b.enter(keeps.down_b))
    at((0, 3), sl.kv_two.pair[1].start, sl.q_two.pair[1].start)
    at((1, 0), lambda: sh.out_two.sum.add(0))
    at((1, 3), lambda: sl.kv_two.enter(1), lambda: sl.q_two.enter(1))
    at((2, 3), sl.kv_two.pair[0].start, sl.q_two.pair[0].start)
    at((3, 0), lambda: sh.up.sum.add(0), lambda: sh.down_a.sum.add(0))
    at((3, 3), lambda: sl.kv_two.enter(0), lambda: sl.q_two.enter(0))
    at((4, 0), lambda: sh.down_b.sum.add(0), sh.out_one.enter, lambda: sl.q_two.far.add(0))
    at((4, 2), sl.kv_two.take)
    at((4, 3), sl.kv_one.pair[1].start, sl.q_one.pair[1].start, lambda: sh.gate.sum.add(0), lambda: sl.q_two.own.add(0))
    at((5, 0), lambda: sh.out_two.sum.add(1))
    at((5, 2), lambda: sh.down_a.sum.add(1))
    at((5, 3), lambda: sl.kv_one.enter(1), lambda: sl.q_one.enter(1), sl.q_two.give)
    at((6, 0), lambda: sh.up.sum.add(1), lambda: sh.down_b.sum.add(1))
    at((6, 2), lambda: sh.out_one.sum.add(0))
    at((6, 3), sl.kv_one.pair[0].start, sl.q_one.pair[0].start)
    at((7, 2), lambda: sl.kv_two.own.add(0))

    def tick(steps, index):
        for k in steps:
            if (k, index) in plan:

                def run(tasks=plan[k, index]):
                    for task in tasks:
                        task()

                pl.when(step == k)(run)

    @pl.when(step == 0)
    def _():
        barrier = pltpu.get_barrier_semaphore()
        for device in place.everyone():
            pl.semaphore_signal(barrier, inc=1, device_id=device, device_id_type=MESH)
        for copy in (after, wo_two, ctx_two, layer_in):
            copy.start()
        pl.semaphore_wait(barrier, len(place.everyone()))
        for name in SHARED_ORDER:
            if hasattr(keeps, name):
                getattr(shared, name).pair.start()
                getattr(keeps, name).start()
        for copy in (n_two, mem, first):
            copy.start()
        after.wait()
        for part in range(4):
            rows = slice(part * TILE, (part + 1) * TILE)
            r.branch[:, rows] = jnp.transpose(r.after[rows, :].astype(BF16))
        key_mask(segs, key_segments(place, ins.memsegs), r.mask)
        wo_two.wait()
        ctx_two.wait()
        layer_in.wait()
        layer_swap.start()
        layer_put.start()
        sh.gate.enter(keeps.gate)
        out_products(sh.out_two, r.ctx, r.branch)
        n_two.wait()
        mem.wait()
        r.gains[...] = jnp.zeros_like(r.gains)
        r.gains[2:3, :] = row_of(ins.ff_gain_grad)

    slot = 3 - step % 4
    odd = slot % 2 == 1
    rows_at = pl.ds(pl.multiple_of(place.group(slot) * GROUP, 16), GROUP)

    def slot_products(kv, q, kv_left, q_left):
        @pl.when(odd)
        def _():
            weight_products(r.kv_send.at[slot // 2], kv_left, KV)
            weight_products(r.q_send.at[slot // 2], q_left, QS)

        @pl.when(jnp.logical_not(odd))
        def _():
            weight_products(kv.room.total.at[slot // 2], kv_left, KV)
            weight_products(q.room.total.at[slot // 2], q_left, QS)

    @pl.when(step < 4)
    def _():
        r.do[...] = dot(r.wo[rows_at, :], r.branch[...]).astype(BF16)
        kv, q, lse = ins.kv_two, ins.q_two, ins.lse_two
        context = r.ctx.at[rows_at, :]
        read = Read(
            lambda: kv[0], lambda h, end: kv[0, rows_of(KEY_AT[h]), :end], lambda rows: q[0, rows, :],
            lambda rows: r.do[rows, :], lambda rows: context[rows, :], lambda h, cut: lse[0, h : h + 1, cut],
        )

        def tile_of(scores, index, kt, qt):
            return scores + r.mask[kt * TILE : (kt + 1) * TILE, qt * TILE : (qt + 1) * TILE].astype(F32)

        attention_back(read, tile_of, False, lambda *a: None, r.dq, r.dqkv, lambda h: tick(range(4), h))
        slot_products(sl.kv_two, sl.q_two, r.mem, r.n)
        tick(range(4), 3)
        add_rows(r.acc_b, KV, ins.wt_two[0, KV, :], step == 0)
        add_rows(r.acc_a, QS, ins.wt_two[0, QS, :], step == 0)

    @pl.when(step == 3)
    def _():
        for copy in (wo_one, ctx_one, n_one):
            copy.start()
        first.wait()
        layer_swap.sent()
        layer_put.wait()
        norm_back(r.hidden, ins.cross_gain, r.acc_a, r.after, 1, r.branch)
        tok.start()
        for part in range(4):
            rows = slice(part * TILE, (part + 1) * TILE)
            r.block[part // 2, (part % 2) * TILE : (part % 2 + 1) * TILE, :] = r.acc_b[rows, :].astype(BF16)
        memory_swap.start()
        memory_put.start()
        for copy in (wo_one, ctx_one, n_one):
            copy.wait()
        sh.out_two.pair.sent()
        out_products(sh.out_one, r.ctx, r.branch)

    @pl.when(step >= 4)
    def _():
        r.do[...] = dot(r.wo[rows_at, :], r.branch[...]).astype(BF16)
        qkv, lse = ins.qkv_one, ins.lse_one
        context = r.ctx.at[rows_at, :]
        read = Read(
            lambda: qkv[0, KV, :], lambda h, end: qkv[0, rows_of(KEY_AT[h]), :end],
            lambda rows: qkv[0, QUERY_START + rows.start : QUERY_START + rows.stop, :],
            lambda rows: r.do[rows, :], lambda rows: context[rows, :], lambda h, cut: lse[0, h : h + 1, cut],
        )
        table, one_hot = ins.table[0], ins.hot[...]
        tiles = [bias_tiles(table, index, one_hot) for index in range(HEADS)]
        kept = {}

        def note(index, kt, qt, ds):
            key = (index, min(qt - kt, 2))
            kept[key] = kept[key] + ds if key in kept else ds

        attention_back(
            read, lambda scores, index, kt, qt: self_tile(scores, kt, qt, tiles[index], segs, 0), True, note,
            r.dq, r.dqkv, lambda h: tick(range(4, 8), h),
        )
        key = lax.broadcasted_iota(jnp.int32, (TILE, TILE), 0)
        query = lax.broadcasted_iota(jnp.int32, (TILE, TILE), 1)
        flip = (key + query == TILE - 1).astype(F32)
        row = lax.broadcasted_iota(jnp.int32, (8, 2 * TILE), 0)
        lane = lax.broadcasted_iota(jnp.int32, (8, 2 * TILE), 1)
        by_distance = jnp.zeros((8, 2 * TILE), F32)
        for index in range(HEADS):
            both = jnp.concatenate((kept[index, 0], kept[index, 1]), axis=1)
            both = jnp.dot(flip, both, precision=lax.Precision.HIGHEST, preferred_element_type=F32)
            turned = jnp.sum(pltpu.roll(both, TILE + 1, 1, stride=1, stride_axis=0), axis=0, keepdims=True)
            far_total = jnp.sum(jnp.sum(kept[index, 2], axis=0, keepdims=True), axis=1, keepdims=True)
            turned = turned + jnp.where(lane[:1] == 2 * TILE - 1, far_total, 0.0)
            by_distance = by_distance + jnp.where(row == index, turned, 0.0)
        r.bias[slot] = lax.dot_general(
            by_distance, one_hot, (((1,), (1,)), ((), ())), precision=lax.Precision.HIGHEST, preferred_element_type=F32
        )
        for k, j in ((4, 1), (6, 0)):

            @pl.when(step == k)
            def _(j=j):
                sl.kv_two.pair[j].sent()
                sl.q_two.pair[j].sent()

        slot_products(sl.kv_one, sl.q_one, r.n, r.n)
        tick(range(4, 8), 3)
        add_rows(r.acc_a, slice(0, 3 * GROUP), ins.wt_one[0], step == 4)

    @pl.when(step == 7)
    def _():
        sl.kv_one.enter(0)
        sl.q_one.enter(0)
        gains, bias = r.gains, r.bias
        memory_swap.sent()
        memory_put.wait()
        tok.wait()
        norm_back(r.hidden, ins.self_gain, r.acc_a, r.after, 0, None)
        tokens_swap.start()
        tokens_put.start()
        gain_copies[0].start()
        bias_copies[0].start()
        bias_copies[1].start()
        sl.kv_one.take()
        sh.gate.sum.add(1)
        sh.up.last()
        sh.down_a.last()
        gain_copies[0].done()
        gains[...] = gains[...] + r.gains_got[0]
        bias_copies[0].done()
        bias_copies[1].done()
        bias[0] = bias[0] + r.bias_got[0]
        bias[2] = bias[2] + r.bias_got[1]
        gain_copies[1].start()
        bias_copies[2].start()
        sh.down_b.last()
        sl.q_one.take()
        sl.kv_one.own.add(0)
        gain_copies[1].done()
        gains[...] = gains[...] + r.gains_got[1]
        bias_copies[2].done()
        bias[0] = bias[0] + r.bias_got[2]
        gain_copies[2].start()
        bias_copies[3].start()
        sh.out_one.sum.add(1)
        sl.q_one.own.add(0)
        sh.gate.last()
        sh.out_two.last()
        gain_copies[2].done()
        gains[...] = gains[...] + r.gains_got[2]
        bias_copies[3].done()
        bias[0] = bias[0] + r.bias_got[3]
        for k in range(depth - 1):
            gain_copies[3 + k].start()
            bias_copies[4 + k].start()
        outs.wq_two[...] = sl.q_two.finish()
        put_heads((outs.wk_two, outs.wv_two), sl.kv_two.finish())
        put_heads((outs.wk_one, outs.wv_one), sl.kv_one.finish())
        gain_total, bias_total = gains[...], bias[0]
        for k in range(depth - 1):
            gain_copies[3 + k].done()
            bias_copies[4 + k].done()
            gain_total = gain_total + r.gains_got[3 + k]
            bias_total = bias_total + r.bias_got[4 + k]
        outs.gains[...] = gain_total
        outs.bias[...] = bias_total
        sh.up.store(outs.up, 0, outs.up.shape[1] // 2)
        sh.down_a.store(outs.down, 0, outs.down.shape[1] // 2)
        sh.down_b.store(outs.down, outs.down.shape[1] // 4, outs.down.shape[1] // 2)
        sh.gate.store(outs.gate, 0, outs.gate.shape[1] // 2)
        sh.out_two.store(outs.out_two, 0, outs.out_two.shape[1] // 2)
        sh.out_one.last()
        outs.wq_one[...] = sl.q_one.finish()
        sh.out_one.store(outs.out_one, 0, outs.out_one.shape[1] // 2)
        for name in SHARED_ORDER:
            unit = getattr(shared, name)
            unit.sent()
            if unit is not sh.out_two:
                unit.pair.sent()
        for name in SLOT_ORDER:
            getattr(slots, name).sent()
        for j in range(2):
            sl.kv_one.pair[j].sent()
            sl.q_one.pair[j].sent()
        layer_swap.got()
        memory_swap.got()
        tokens_swap.done()
        tokens_put.wait()


def backward_call(batch_size, operands):
    depth = batch_size // 2
    tok = operands["loaded"]["tok"]
    model = tok.shape[1]
    share = model // batch_size
    anywhere = pl.BlockSpec(memory_space=pl.ANY)

    def fixed(shape):
        return pl.BlockSpec(shape, lambda t: (0,) * len(shape))

    def early(array):
        return pl.BlockSpec((1,) + array.shape[1:], lambda t: (3 - t + (t // 4) * (t - 3), 0, 0))

    def late(array):
        return pl.BlockSpec((1,) + array.shape[1:], lambda t: (3 - (t // 4) * (t - 4), 0, 0))

    kinds = dict(
        segs=lambda a: pl.BlockSpec(memory_space=pltpu.SMEM), kv_two=early, q_two=early, lse_two=early, wt_two=early,
        qkv_one=late, lse_one=late, wt_one=late, table=late, loaded=lambda a: anywhere, sends=lambda a: anywhere,
        keeps=lambda a: anywhere, layer=lambda a: anywhere,
    )
    in_specs = {
        name: jax.tree.map(kinds.get(name, lambda a: fixed(a.shape)), value) for name, value in operands.items()
    }
    keeps = operands["keeps"]
    shapes = {name: keeps[name].shape[3:] for name in keeps}
    shapes.update(out_two=(model // (4 * depth), model // 2), out_one=(model // (4 * depth), model // 2))
    block = jax.ShapeDtypeStruct((2, HALF, model), BF16)

    def wide(rows, columns):
        return jax.ShapeDtypeStruct((rows, columns), F32)

    head = wide(share, GROUP)
    outs = dict(
        layer=block, memory=block, tokens=block,
        gate=wide(shapes["gate"][0] // 2, 2 * shapes["gate"][1]), up=wide(shapes["up"][0] // 2, 2 * shapes["up"][1]),
        down=wide(shapes["down_a"][0] // 2, 4 * shapes["down_a"][1]),
        out_two=wide(shapes["out_two"][0] // 2, model), out_one=wide(shapes["out_one"][0] // 2, model),
        wq_two=head, wk_two=head, wv_two=head, wq_one=head, wk_one=head, wv_one=head,
        gains=wide(8, model), bias=wide(8, TILE),
    )
    out_specs = {name: anywhere if s is block else fixed(s.shape) for name, s in outs.items()}

    def room(*shape, kind=BF16):
        return pltpu.VMEM(shape, kind)

    scratch = {}
    for name, order in SHARED_ORDER.items():
        rows, lanes = shapes[name]
        scratch[name] = dict(
            total=room(depth, 2, 2, rows, lanes),
            got=[room(*s) for s in Sum.rooms(depth, 3, order, rows, lanes)],
            last=room(2, rows // 2, lanes, kind=F32), other=room(rows // 2, lanes, kind=F32),
        )
    for name, (y_first, order) in SLOT_ORDER.items():
        lanes = 2 * GROUP if name.startswith("kv") else GROUP
        got = [room(*s) for s in Sum.rooms(depth, 2, order, share, lanes)]
        both = room(2, depth, 2, share, lanes)
        scratch[name] = dict(total=both, pair=both, got=got)
        if y_first:
            scratch[name].update(across=room(depth, 2, share, lanes))
        else:
            scratch[name].update(across=room(share, lanes), chunk=room(share, lanes), far=list(got))
    scratch.update(
        pairs={name: room(depth, 2, 2, *shapes[name]) for name in keeps},
        out_send=room(depth, 2, 2, *shapes["out_one"]), out_pair=room(depth, 2, 2, *shapes["out_one"]), kv_send=room(2, depth, 2, share, 2 * GROUP),
        q_send=room(2, depth, 2, share, GROUP), block=room(2, HALF, model), branch=room(model, BLOCK),
        acc_a=room(BLOCK, model, kind=F32), acc_b=room(BLOCK, model, kind=F32), dqkv=room(BLOCK, 3 * GROUP),
        dq=room(GROUP, BLOCK), do=room(GROUP, BLOCK), mask=room(BLOCK, BLOCK), gains=room(8, model, kind=F32),
        gains_got=room(depth + 2, 8, model, kind=F32), bias=room(4, 8, TILE, kind=F32),
        bias_got=room(depth + 3, 8, TILE, kind=F32),
        after=room(BLOCK, model, kind=F32), hidden=room(BLOCK, model, kind=F32),
        wo=room(model, model), ctx=room(model, BLOCK), n=room(model, BLOCK), mem=room(model, BLOCK),
    )
    z = depth - 1
    copies = sum(2 + 2 + z for _ in SHARED_ORDER) + 3 + (3 + z) + (4 + z)
    copies += sum(2 + (1 + z) + 1 + (0 if y_first else 1 + z) for y_first, _ in SLOT_ORDER.values())
    scratch.update(send=pltpu.SemaphoreType.DMA((copies,)), recv=pltpu.SemaphoreType.DMA((copies,)))
    scratch.update(load=pltpu.SemaphoreType.DMA((18,)))

    arrays, in_tree = jax.tree.flatten(operands)
    out_shapes, out_tree = jax.tree.flatten(outs)
    rooms, room_tree = jax.tree.flatten(scratch)

    def kernel(*refs):
        a, b = len(arrays), len(arrays) + len(out_shapes)
        backward_kernel(
            depth, Named(jax.tree.unflatten(in_tree, refs[:a])), Named(jax.tree.unflatten(out_tree, refs[a:b])),
            Named(jax.tree.unflatten(room_tree, refs[b:])),
        )

    results = pl.pallas_call(
        kernel,
        grid=(8,),
        in_specs=jax.tree.leaves(in_specs),
        out_specs=jax.tree.leaves(out_specs),
        out_shape=out_shapes,
        scratch_shapes=rooms,
        compiler_params=pltpu.CompilerParams(
            collective_id=0, has_side_effects=True, vmem_limit_bytes=66_000_000, dimension_semantics=("arbitrary",)
        ),
        cost_estimate=pl.CostEstimate(flops=20_000_000_000, bytes_accessed=40_000_000, transcendentals=6_000_000),
    )(*arrays)
    return Named(jax.tree.unflatten(out_tree, results))


PIECES = 3


class Gather:
    def __init__(self, place, copies, slots):
        self.slots = slots
        half = slots.shape[1] // 2
        size = half // PIECES
        self.core = copies.new(lambda: slots.at[0], lambda: slots.at[1], place.to_core)

        def rows(side, j):
            return pl.ds(pl.multiple_of(side * half + j * size, 32), size)

        def make(source, target, side, device):
            return [
                copies.new(
                    (lambda j: lambda: slots.at[source, rows(side, j)])(j),
                    (lambda j: lambda: slots.at[target, rows(side, j)])(j), device,
                )
                for j in range(PIECES)
            ]

        self.over_y = make(0, 2, place.x, place.to_y)
        self.over_x = make(2, 2, place.x, place.to_x)
        self.near = make(2, 3, place.x, place.to_core)
        self.far = make(2, 3, 1 - place.x, place.to_core)

    def start(self):
        for copy in self.over_y:
            copy.start()
        self.core.start()

    def pass_y(self, j):
        self.over_y[j].got()
        self.over_x[j].start()
        self.near[j].start()

    def pass_x(self, j):
        self.over_x[j].got()
        self.far[j].start()

    def ready(self):
        for copy in self.near + self.far:
            copy.got()

    def sent(self):
        for copy in [self.core] + self.over_y + self.over_x + self.near + self.far:
            copy.sent()


def forward_kernel(ins, outs, r):
    place = Place(1)
    step = pl.program_id(0)
    core = place.core
    copies = Copies(r.send, r.recv)
    segs = Tiles(place, ins.segs)
    gather_one = Gather(place, copies, r.wt_one)
    gather_two = Gather(place, copies, r.wt_two)
    tables = [
        copies.new((lambda a: lambda: r.table.at[a])(a), (lambda b: lambda: r.table.at[b])(b), d)
        for a, b, d in ((0, 1, place.to_core), (0, 2, place.to_y), (2, 3, place.to_core))
    ]
    swaps = {}
    tok_swap = copies.new(lambda: ins.tokens.at[1 - core], lambda: r.tok_in.at[core], place.to_core)
    mem_swap = copies.new(lambda: ins.memory.at[1 - core], lambda: r.mem_in.at[core], place.to_core)
    cot_swap = copies.new(lambda: ins.cotangent.at[1 - core], lambda: r.cot_in.at[core], place.to_core)
    assert copies.count == r.send.shape[0], copies.count
    count = [0]

    def load(source, target):
        count[0] += 1
        return pltpu.make_async_copy(source, target, r.load.at[count[0] - 1])

    tok_own = load(ins.tokens.at[core], r.tok_in.at[core])
    mem_own = load(ins.memory.at[core], r.mem_in.at[core])
    cot_own = load(ins.cotangent.at[core], r.cot_in.at[core])

    def load_group(key, value, query, slots):
        return [
            load(source.at[pl.ds(at, size)], slots.at[0, pl.ds(to, size)])
            for source, at, to, size in (
                (key, 0, 0, 128), (value, 0, 128, 128), (key, 128, 256, 64), (value, 128, 320, 64), (query, 0, 384, GROUP)
            )
        ]

    raw_one = load_group(ins.self_key, ins.self_value, ins.self_query, r.wt_one)
    raw_two = load_group(ins.cross_key, ins.cross_value, ins.cross_query, r.wt_two)
    out_one, out_two = load(ins.self_out, r.wo_one), load(ins.cross_out, r.wo_two)
    puts = Named({name: load(getattr(r, name), getattr(outs, name)) for name in vars(outs)})


    def normed(hidden, gain, target):
        for part in range(4):
            rows = slice(part * TILE, (part + 1) * TILE)
            h = hidden[rows, :]
            scale = lax.rsqrt(jnp.mean(h * h, axis=-1, keepdims=True) + NORM_EPS)
            target[:, rows] = jnp.transpose((h * scale * row_of(gain)).astype(BF16))

    def project_out(context, weights, base, target):
        for part in range(2):
            rows = slice(part * HALF, (part + 1) * HALF)
            target[rows, :] = base[rows, :] + dot(jnp.transpose(context[:, rows]), weights[...])

    def cross_keys(slot):
        r.kv_two[slot] = dot(r.wt_two[slot, KV, :], r.mem[...]).astype(BF16)

    plan = {}

    def at(point, *tasks):
        plan.setdefault(point, []).extend(tasks)

    one, two = gather_one, gather_two
    at((0, 0), lambda: one.pass_y(1))
    at((0, 2), lambda: one.pass_y(2))
    at((1, 0), lambda: one.pass_x(0))
    at((1, 1), tables[1].got, tables[2].start)
    at((1, 2), lambda: one.pass_x(1))
    at((2, 0), lambda: two.pass_y(1))
    at((2, 2), lambda: two.pass_x(0))
    at((3, 0), lambda: two.pass_y(2))
    at((3, 2), lambda: two.pass_x(1))
    at((4, 1), lambda: two.pass_x(2))

    def tick(steps, index):
        for k in steps:
            if (k, index) in plan:

                def run(tasks=plan[k, index]):
                    for task in tasks:
                        task()

                pl.when(step == k)(run)

    @pl.when(step == 0)
    def _():
        barrier = pltpu.get_barrier_semaphore()
        for device in (place.to_core, place.to_y, place.to_x):
            pl.semaphore_signal(barrier, inc=1, device_id=device, device_id_type=MESH)
        for copy in raw_one + [tok_own] + raw_two + [mem_own, out_one, out_two, cot_own]:
            copy.start()
        r.table[0] = jnp.zeros_like(r.table[0])
        r.table[0, :HEADS, : ins.table.shape[1]] = ins.table[...]
        for copy in raw_one:
            copy.wait()
        pl.semaphore_wait(barrier, 3)
        tok_swap.start()
        tables[0].start()
        tables[1].start()
        gather_one.start()
        mem_swap.start()
        cot_swap.start()
        tok_own.wait()
        tok_swap.got()
        for half in range(2):
            r.tok[half * HALF : (half + 1) * HALF, :] = r.tok_in[half].astype(F32)
        puts.tok.start()
        one.pass_y(0)
        normed(r.tok, ins.self_gain, r.n_one)
        puts.n_one.start()
        for copy in raw_two:
            copy.wait()
        gather_two.start()

    @pl.when(step == 1)
    def _():
        gather_one.core.got()
        tables[0].got()

    @pl.when(step == 2)
    def _():
        mem_own.wait()
        mem_swap.got()
        for half in range(2):
            r.mem[:, half * HALF : (half + 1) * HALF] = jnp.transpose(r.mem_in[half])
        puts.mem.start()
        cot_own.wait()
        cot_swap.got()
        for half in range(2):
            r.cot[half * HALF : (half + 1) * HALF, :] = r.cot_in[half]
        puts.cot.start()
        gather_two.core.got()
        cross_keys(0)
        cross_keys(1)
        two.pass_y(0)
        one.pass_x(2)
        one.ready()
        puts.wt_one.start()
        tables[2].got()
        puts.table.start()

    slot = step % 4
    rows_at = pl.ds(pl.multiple_of(place.group(slot) * GROUP, 16), GROUP)

    @pl.when(step < 4)
    def _():
        r.qkv_one[slot] = dot(r.wt_one[slot], r.n_one[...]).astype(BF16)
        self_forward(
            r.qkv_one.at[slot, KV], r.qkv_one.at[slot, QS], r.table[slot], ins.hot[...], segs,
            r.ctx_one.at[rows_at], r.lse_one.at[slot], lambda h: tick(range(4), h),
        )

    @pl.when(step == 4)
    def _():
        puts.qkv_one.start()
        puts.ctx_one.start()
        puts.lse_one.start()
        out_one.wait()
        project_out(r.ctx_one, r.wo_one, r.tok, r.first)
        puts.first.start()
        normed(r.first, ins.cross_gain, r.n_two)
        puts.n_two.start()
        key_mask(segs, key_segments(place, ins.memsegs), r.mask)

    @pl.when(step == 6)
    def _():
        two.ready()
        puts.wt_two.start()

    @pl.when(step >= 4)
    def _():
        @pl.when(step >= 6)
        def _():
            cross_keys(slot)

        r.q_two[slot] = dot(r.wt_two[slot, QS, :], r.n_two[...]).astype(BF16)
        cross_forward(
            r.kv_two.at[slot], r.q_two.at[slot], r.mask, r.ctx_two.at[rows_at], r.lse_two.at[slot],
            lambda h: tick(range(4, 8), h),
        )

    @pl.when(step == 7)
    def _():
        out_two.wait()
        project_out(r.ctx_two, r.wo_two, r.first, r.second)
        for put in (puts.second, puts.ctx_two, puts.q_two, puts.kv_two, puts.lse_two):
            put.start()
        gather_one.sent()
        gather_two.sent()
        for copy in tables + [tok_swap, mem_swap, cot_swap]:
            copy.sent()
        for name in vars(outs):
            getattr(puts, name).wait()


def forward_call(operands):
    tokens = operands["tokens"]
    model = tokens.shape[2]
    anywhere = pl.BlockSpec(memory_space=pl.ANY)

    def fixed(array):
        return pl.BlockSpec(array.shape, lambda t: (0,) * array.ndim)

    small = dict(self_gain=fixed, cross_gain=fixed, table=fixed, hot=fixed, memsegs=fixed)
    small.update(segs=lambda a: pl.BlockSpec(memory_space=pltpu.SMEM))
    in_specs = {name: small.get(name, lambda a: anywhere)(a) for name, a in operands.items()}

    def room(*shape, kind=BF16):
        return pltpu.VMEM(shape, kind)

    kept = dict(
        tok=room(BLOCK, model, kind=F32), mem=room(model, BLOCK), cot=room(BLOCK, model), n_one=room(model, BLOCK),
        n_two=room(model, BLOCK), qkv_one=room(4, 3 * GROUP, BLOCK), kv_two=room(4, 2 * GROUP, BLOCK),
        q_two=room(4, GROUP, BLOCK), ctx_one=room(model, BLOCK), ctx_two=room(model, BLOCK),
        lse_one=room(4, 8, BLOCK, kind=F32), lse_two=room(4, 8, BLOCK, kind=F32),
        first=room(BLOCK, model, kind=F32), second=room(BLOCK, model, kind=F32),
        wt_one=room(4, 3 * GROUP, model), wt_two=room(4, 3 * GROUP, model), table=room(4, 8, TILE, kind=F32),
    )
    block = tokens.shape[1:]
    copies = 2 * (1 + 4 * PIECES) + 3 + 3
    scratch = dict(
        kept, tok_in=room(2, *block), mem_in=room(2, *block), cot_in=room(2, *block),
        wo_one=room(model, model), wo_two=room(model, model), mask=room(BLOCK, BLOCK, kind=F32),
        send=pltpu.SemaphoreType.DMA((copies,)), recv=pltpu.SemaphoreType.DMA((copies,)),
        load=pltpu.SemaphoreType.DMA((15 + len(kept),)),
    )
    outs = {name: jax.ShapeDtypeStruct(m.shape, m.dtype) for name, m in kept.items()}
    arrays, in_tree = jax.tree.flatten(operands)
    out_shapes, out_tree = jax.tree.flatten(outs)
    rooms, room_tree = jax.tree.flatten(scratch)

    def kernel(*refs):
        a, b = len(arrays), len(arrays) + len(out_shapes)
        forward_kernel(
            Named(jax.tree.unflatten(in_tree, refs[:a])), Named(jax.tree.unflatten(out_tree, refs[a:b])),
            Named(jax.tree.unflatten(room_tree, refs[b:])),
        )

    results = pl.pallas_call(
        kernel,
        grid=(8,),
        in_specs=jax.tree.leaves(in_specs),
        out_specs=[anywhere] * len(out_shapes),
        out_shape=out_shapes,
        scratch_shapes=rooms,
        compiler_params=pltpu.CompilerParams(
            collective_id=1, has_side_effects=True, vmem_limit_bytes=60_000_000, dimension_semantics=("arbitrary",)
        ),
        cost_estimate=pl.CostEstimate(flops=10_000_000_000, bytes_accessed=40_000_000, transcendentals=6_000_000),
    )(*arrays)
    return Named(jax.tree.unflatten(out_tree, results))


def finish_call(results, devices, buckets):
    plain = {name: a for name, a in results.items() if name not in ("gains", "bias")}
    share = results["gains"].shape[1] // devices
    outs = {name: jax.ShapeDtypeStruct(a.shape, a.dtype) for name, a in plain.items()}
    anywhere = pl.BlockSpec(memory_space=pl.ANY)
    count = len(plain)

    def kernel(gains, bias, *refs):
        sources, (bias_out, *gain_outs), targets = refs[:count], refs[count : count + 4], refs[count + 4 : 2 * count + 4]
        rooms, semaphores = refs[2 * count + 4 : 3 * count + 4], refs[3 * count + 4]
        takes = [pltpu.make_async_copy(s, r, semaphores.at[k]) for k, (s, r) in enumerate(zip(sources, rooms))]
        puts = [pltpu.make_async_copy(r, t, semaphores.at[count + k]) for k, (r, t) in enumerate(zip(rooms, targets))]
        for take in takes:
            take.start()
        bias_out[...] = bias[:HEADS, :buckets]
        first = (lax.axis_index("batch") * lax.axis_size("head") + lax.axis_index("head")) * share
        turned = pltpu.roll(gains[...], gains.shape[1] - first, 1)
        for k, out in enumerate(gain_outs):
            out[...] = jnp.reshape(turned[k : k + 1, :share], (share,))
        for take, put in zip(takes, puts):
            take.wait()
            put.start()
        for put in puts:
            put.wait()

    def fixed(shape):
        return pl.BlockSpec(shape, lambda: (0,) * len(shape))

    small = [jax.ShapeDtypeStruct((HEADS, buckets), F32)] + [jax.ShapeDtypeStruct((share,), F32)] * 3
    bias, *rest = pl.pallas_call(
        kernel,
        in_specs=[fixed(results["gains"].shape), fixed(results["bias"].shape)] + [anywhere] * count,
        out_specs=[fixed(a.shape) for a in small] + [anywhere] * count,
        out_shape=small + list(outs.values()),
        scratch_shapes=[pltpu.VMEM(a.shape, a.dtype) for a in plain.values()] + [pltpu.SemaphoreType.DMA((2 * count,))],
    )(results["gains"], results["bias"], *plain.values())
    return dict(zip(plain, rest[3:]), bias=bias, gain_0=rest[0], gain_1=rest[1], gain_2=rest[2])


FF_STEPS = 4


def ff_tile(t):
    core = lax.axis_index("head") % 2
    half = t // 2
    other = 1 - core
    return 2 * (half + other - 2 * half * other) + t % 2


def over_rows(left, right):
    return lax.dot_general(left, right, (((1,), (1,)), ((), ())), preferred_element_type=F32)


def ff_kernel(ins, outs, r):
    step = pl.program_id(0)
    core = lax.axis_index("head") % 2
    model = ins.second.shape[1]
    root = np.float32(np.sqrt(2.0 / np.pi))

    @pl.when(step == 0)
    def _():
        for part in range(4):
            rows = slice(part * TILE, (part + 1) * TILE)
            h = ins.second[rows, :]
            scale = lax.rsqrt(jnp.mean(h * h, axis=-1, keepdims=True) + NORM_EPS)
            r.normed[rows, :] = (h * scale * row_of(ins.gain)).astype(BF16)
            r.cot[:, rows] = jnp.transpose(ins.cot[rows, :])
            r.layer[rows, :] = h
            r.back[rows, :] = jnp.zeros_like(h)

    for part in range(4):
        rows = slice(part * TILE, (part + 1) * TILE)
        normed = r.normed[rows, :]
        gate, up = dot(normed, ins.gate[...]), dot(normed, ins.up[...])
        grad = over_rows(ins.cot[rows, :], ins.down[...])
        square = gate * gate
        half = 0.5 + 0.5 * jnp.tanh(gate * (root + (root * 0.044715) * square))
        gelu = gate * half
        slope = half + gelu * (2.0 - 2.0 * half) * (root + (3.0 * 0.044715 * root) * square)
        activation = (gelu * up).astype(BF16)
        grad_gate = (grad * up * slope).astype(BF16)
        grad_up = (grad * gelu).astype(BF16)
        r.act[rows, :] = activation
        r.grad_gate[:, rows] = jnp.transpose(grad_gate)
        r.grad_up[:, rows] = jnp.transpose(grad_up)
        r.layer[rows, :] = r.layer[rows, :] + dot(activation, ins.down[...])
        r.back[rows, :] = r.back[rows, :] + over_rows(grad_gate, ins.gate[...]) + over_rows(grad_up, ins.up[...])

    lanes = model // 2

    def spread_out(target, product, first):
        rows = target.shape[3]
        for piece in range(product.shape[0] // rows):
            at = first + piece
            target[at // 4, (at // 2) % 2, at % 2] = product[piece * rows : (piece + 1) * rows]

    for which, name in ((1 - core, 0), (core, 1)):
        right = r.normed[:, pl.ds(pl.multiple_of(which * lanes, 128), lanes)]
        for grads, target in ((r.grad_gate, outs.gate[name]), (r.grad_up, outs.up[name])):
            spread_out(target, dot(grads[...], right).astype(BF16), 0)
    for t, target in enumerate((outs.down_a[0], outs.down_b[0], outs.down_a[1], outs.down_b[1])):

        @pl.when(step == t)
        def _(target=target):
            per = model // 2
            for part in range(2):
                product = dot(r.cot[part * per : (part + 1) * per, :], r.act[...]).astype(BF16)
                spread_out(target, product, part * (per // target.shape[3]))

    @pl.when(step == FF_STEPS - 1)
    def _():
        total = jnp.zeros((1, model), F32)
        for part in range(4):
            rows = slice(part * TILE, (part + 1) * TILE)
            h, e = ins.second[rows, :], r.back[rows, :]
            scale = lax.rsqrt(jnp.mean(h * h, axis=-1, keepdims=True) + NORM_EPS)
            weighted = e * row_of(ins.gain)
            inner = jnp.mean(weighted * h, axis=-1, keepdims=True)
            outs.after[rows, :] = ins.cot[rows, :].astype(F32) + weighted * scale - h * (scale * scale * scale * inner)
            total = total + jnp.sum(e * h * scale, axis=0, keepdims=True)
            outs.layer[part // 2, (part % 2) * TILE : (part % 2 + 1) * TILE, :] = r.layer[rows, :].astype(BF16)
        outs.gain_grad[...] = jnp.reshape(total, (model,))


def ff_call(depth, operands):
    model, columns = operands["gate"].shape
    tile = columns // FF_STEPS

    def fixed(shape):
        return pl.BlockSpec(shape, lambda t: (0,) * len(shape))

    in_specs = {name: fixed(a.shape) for name, a in operands.items()}
    in_specs.update(
        gate=pl.BlockSpec((model, tile), lambda t: (0, ff_tile(t))),
        up=pl.BlockSpec((model, tile), lambda t: (0, ff_tile(t))),
        down=pl.BlockSpec((tile, model), lambda t: (ff_tile(t), 0)),
    )
    wide = jax.ShapeDtypeStruct((depth, 2, 2, columns // (4 * depth), model // 2), BF16)
    deep = jax.ShapeDtypeStruct((depth, 2, 2, model // (4 * depth), tile), BF16)
    by_tile = pl.BlockSpec((depth // FF_STEPS,) + wide.shape[1:], lambda t: (ff_tile(t), 0, 0, 0, 0))
    outs = dict(
        layer=jax.ShapeDtypeStruct((2, HALF, model), BF16), after=jax.ShapeDtypeStruct((BLOCK, model), F32),
        gain_grad=jax.ShapeDtypeStruct((model,), F32), gate=[wide, wide], up=[wide, wide],
        down_a=[deep, deep], down_b=[deep, deep],
    )
    out_specs = jax.tree.map(lambda a: by_tile if a is wide else fixed(a.shape), outs)
    scratch = dict(
        normed=pltpu.VMEM((BLOCK, model), BF16), cot=pltpu.VMEM((model, BLOCK), BF16),
        layer=pltpu.VMEM((BLOCK, model), F32), back=pltpu.VMEM((BLOCK, model), F32),
        act=pltpu.VMEM((BLOCK, tile), BF16), grad_gate=pltpu.VMEM((tile, BLOCK), BF16),
        grad_up=pltpu.VMEM((tile, BLOCK), BF16),
    )
    arrays, in_tree = jax.tree.flatten(operands)
    out_shapes, out_tree = jax.tree.flatten(outs)
    rooms, room_tree = jax.tree.flatten(scratch)

    def kernel(*refs):
        a, b = len(arrays), len(arrays) + len(out_shapes)
        ff_kernel(
            Named(jax.tree.unflatten(in_tree, refs[:a])), Named(jax.tree.unflatten(out_tree, refs[a:b])),
            Named(jax.tree.unflatten(room_tree, refs[b:])),
        )

    results = pl.pallas_call(
        kernel,
        grid=(FF_STEPS,),
        in_specs=jax.tree.leaves(in_specs),
        out_specs=jax.tree.leaves(out_specs),
        out_shape=out_shapes,
        scratch_shapes=rooms,
        compiler_params=pltpu.CompilerParams(vmem_limit_bytes=60_000_000, dimension_semantics=("arbitrary",)),
        cost_estimate=pl.CostEstimate(flops=14_500_000_000, bytes_accessed=24_000_000, transcendentals=1_000_000),
    )(*arrays)
    return Named(jax.tree.unflatten(out_tree, results))


def on_device(
    tokens, memory, cotangent, target_segments, memory_segments, self_gain, self_query, self_key,
    self_value, self_out, position_bias, cross_gain, cross_query, cross_key, cross_value, cross_out,
    ff_gain, ff_gate, ff_up, ff_down,
):
    heads_axis, batch_axis = lax.axis_size("head"), lax.axis_size("batch")
    rows, part, model = tokens.shape
    assert part * 2 == BLOCK and rows == 2 and heads_axis == 4
    assert position_bias.shape[1] == HEADS and self_query.shape[1] == GROUP
    one_hot = jnp.asarray(bucket_one_hot(position_bias.shape[0]))

    fwd = forward_call(
        dict(
            tokens=tokens, memory=memory, cotangent=cotangent, segs=target_segments, memsegs=memory_segments, hot=one_hot,
            self_gain=self_gain, cross_gain=cross_gain, table=position_bias.T,
            self_query=self_query.T, self_key=self_key.T, self_value=self_value.T, self_out=self_out,
            cross_query=cross_query.T, cross_key=cross_key.T, cross_value=cross_value.T, cross_out=cross_out,
        )
    )
    ff = ff_call(
        batch_axis // 2,
        dict(second=fwd.second, cot=fwd.cot, gain=ff_gain, gate=ff_gate, up=ff_up, down=ff_down),
    )
    done = backward_call(
        batch_axis,
        dict(
            segs=target_segments, memsegs=memory_segments, hot=one_hot, self_gain=self_gain, cross_gain=cross_gain,
            ff_gain_grad=ff.gain_grad,
            kv_two=fwd.kv_two, q_two=fwd.q_two, lse_two=fwd.lse_two, wt_two=fwd.wt_two,
            qkv_one=fwd.qkv_one, lse_one=fwd.lse_one, wt_one=fwd.wt_one, table=fwd.table,
            loaded=dict(
                after=ff.after, wo_two=cross_out, ctx_two=fwd.ctx_two, n_two=fwd.n_two, mem=fwd.mem,
                first=fwd.first, wo_one=self_out, ctx_one=fwd.ctx_one, n_one=fwd.n_one, tok=fwd.tok,
            ),
            sends=dict(gate=ff.gate[0], up=ff.up[0], down_a=ff.down_a[0], down_b=ff.down_b[0]),
            keeps=dict(gate=ff.gate[1], up=ff.up[1], down_a=ff.down_a[1], down_b=ff.down_b[1]),
            layer=ff.layer,
        ),
    )
    done = Named(finish_call(vars(done), heads_axis * batch_axis, position_bias.shape[0]))
    return (
        done.layer, done.tokens, done.memory, done.gain_0, done.wq_one, done.wk_one, done.wv_one, done.out_one.T,
        done.bias.T, done.gain_1, done.wq_two, done.wk_two, done.wv_two, done.out_two.T, done.gain_2,
        done.gate.T, done.up.T, done.down.T,
    )


def solution(mesh):
    tokens = P("batch", "head", None)
    rows = P("batch", None)
    columns = P(None, "head")
    split = P("batch", "head")
    every = P(None, ("batch", "head"))
    gain = P(("batch", "head"))
    return jax.shard_map(
        on_device,
        mesh=mesh,
        in_specs=(
            tokens, tokens, tokens, rows, rows, P(), columns, columns, columns, P(), columns, P(),
            columns, columns, columns, P(), P(), P(), P(), P(),
        ),
        out_specs=(
            tokens, tokens, tokens, gain, split, split, split, every, columns, gain,
            split, split, split, every, gain, every, every, every,
        ),
        check_vma=False,
    )
```

```python
import jax
import jax.numpy as jnp
import numpy as np
from jax import lax
from jax.experimental import pallas as pl
from jax.experimental.pallas import tpu as pltpu
from jax.sharding import PartitionSpec as P

NORM_EPS = 1e-06
MASKED = -1e30
BLOCK = 512
TILE = 128
HALF = 256
SIZE = 64
HEADS = 3
GROUP = HEADS * SIZE
F32 = jnp.float32
BF16 = jnp.bfloat16
MESH = pl.DeviceIdType.MESH


def bucket_edges():
    distance = np.arange(1.0, 8192.0)
    far_bucket = 16.0 + np.floor(np.log(np.maximum(distance, 16.0) / 16.0) / np.log(8.0) * 16.0)
    bucket_value = np.where(distance < 16, distance, np.minimum(far_bucket, 31.0))
    return [int(distance[np.argmax(bucket_value >= bucket_level)]) for bucket_level in range(1, 32)]


def bucket_one_hot(buckets):
    ids = np.zeros(2 * TILE, np.int32)
    for edge in bucket_edges():
        ids += np.arange(2 * TILE) >= edge
    assert bucket_edges()[-1] <= TILE + 1
    assert buckets <= TILE and ids[-1] == buckets - 1
    return (np.arange(TILE)[:, None] == ids[None, :]).astype(np.float32)


def dot(left, right):
    return lax.dot_general(left, right, (((1,), (0,)), ((), ())), preferred_element_type=F32)


KEY_AT = ((0, 0), (0, 1), (2, 0))
VALUE_AT = ((1, 0), (1, 1), (2, 1))
QUERY_START = 2 * GROUP


def rows_of(at):
    tile, place = at
    return slice(tile * 128 + place * SIZE, tile * 128 + (place + 1) * SIZE)


def lanes_of(at):
    return slice(at[0] * 128, (at[0] + 1) * 128)


def spread(head_rows, place):
    blank = jnp.zeros_like(head_rows)
    return jnp.concatenate((head_rows, blank) if place == 0 else (blank, head_rows), axis=0)


def bias_tiles(table, index, one_hot):
    by_distance = jnp.dot(
        table, one_hot, precision=lax.Precision.HIGHEST, preferred_element_type=F32
    )[index : index + 1]
    wide = jnp.broadcast_to(by_distance, (TILE, 2 * TILE))
    turned = pltpu.roll(wide, 0, 1, stride=1, stride_axis=0)
    key = lax.broadcasted_iota(jnp.int32, (TILE, TILE), 0)
    query = lax.broadcasted_iota(jnp.int32, (TILE, TILE), 1)
    near = jnp.where(key <= query, turned[:, :TILE], MASKED)
    return near, turned[:, TILE:], by_distance[0, 2 * TILE - 1]


def self_tile(scores, key_tile, query_tile, tiles, seg_ref, base):
    near, next_one, far = tiles
    if key_tile == query_tile:
        return scores + near
    same = seg_ref[base + key_tile] == seg_ref[base + query_tile]
    shift = jnp.where(same, 0.0, MASKED)
    if key_tile == query_tile - 1:
        return scores + next_one + shift
    return scores + (far + shift)


def self_forward(kv, q, table, one_hot, seg_ref, out, lse, tick):
    key_values = jnp.transpose(kv[...])
    for index in range(HEADS):
        rows = slice(index * SIZE, (index + 1) * SIZE)
        keys = key_values[:, lanes_of(KEY_AT[index])]
        query = spread(q[rows, :], KEY_AT[index][1])
        tiles = bias_tiles(table, index, one_hot)
        for half in range(2):
            end = (half + 1) * HALF
            scores = dot(keys[:end], query[:, half * HALF : (half + 1) * HALF])
            columns, totals = [], []
            for part in range(2):
                query_tile = 2 * half + part
                parts = [
                    self_tile(
                        scores[kt * TILE : (kt + 1) * TILE, part * TILE : (part + 1) * TILE],
                        kt, query_tile, tiles, seg_ref, 0,
                    )
                    for kt in range(query_tile + 1)
                ]
                top = jnp.max(parts[0], axis=0, keepdims=True)
                for piece in parts[1:]:
                    top = jnp.maximum(top, jnp.max(piece, axis=0, keepdims=True))
                probs = [jnp.exp(piece - top) for piece in parts]
                total = jnp.sum(probs[0], axis=0, keepdims=True)
                for piece in probs[1:]:
                    total = total + jnp.sum(piece, axis=0, keepdims=True)
                probs = [piece.astype(BF16) for piece in probs]
                if part == 0:
                    probs.append(jnp.zeros((TILE, TILE), BF16))
                columns.append(jnp.concatenate(probs, axis=0))
                totals.append(total)
                lse[index : index + 1, query_tile * TILE : (query_tile + 1) * TILE] = top + jnp.log(total)
            weights = jnp.concatenate(columns, axis=1)
            context = dot(kv[rows_of(VALUE_AT[index]), :end], weights)
            context = context / jnp.concatenate(totals, axis=1)
            out[rows, half * HALF : (half + 1) * HALF] = context.astype(BF16)
        tick(index)


def key_mask(seg_ref, memseg, mask_ref):
    rows = jnp.transpose(jnp.broadcast_to(memseg.astype(F32), (TILE, BLOCK)))
    for tile in range(BLOCK // TILE):
        wanted = seg_ref[tile].astype(F32)
        shift = jnp.where(rows == wanted, 0.0, MASKED)
        mask_ref[:, tile * TILE : (tile + 1) * TILE] = shift.astype(mask_ref.dtype)


def cross_forward(kv, q, mask, out, lse, tick):
    key_values = jnp.transpose(kv[...])
    for index in range(HEADS):
        rows = slice(index * SIZE, (index + 1) * SIZE)
        keys = key_values[:, lanes_of(KEY_AT[index])]
        query = spread(q[rows, :], KEY_AT[index][1])
        for half in range(2):
            lanes = slice(half * HALF, (half + 1) * HALF)
            scores = dot(keys, query[:, lanes]) + mask[:, lanes]
            top = jnp.max(scores, axis=0, keepdims=True)
            probs = jnp.exp(scores - top)
            total = jnp.sum(probs, axis=0, keepdims=True)
            context = dot(kv[rows_of(VALUE_AT[index]), :], probs.astype(BF16)) / total
            out[rows, lanes] = context.astype(BF16)
            lse[index : index + 1, lanes] = top + jnp.log(total)
        tick(index)


def grow(old, new):
    if old is None:
        return new
    shared = old.shape[0]
    if shared == new.shape[0]:
        return old + new
    return jnp.concatenate((old + new[:shared], new[shared:]), axis=0)


def only_lanes(wide, at):
    pair = wide[:, lanes_of(at)]
    lane = lax.broadcasted_iota(jnp.int32, pair.shape, 1)
    keep = lane < SIZE if at[1] == 0 else lane >= SIZE
    return jnp.where(keep, pair, jnp.zeros_like(pair))


def moved(wide, index, place):
    if index < 2:
        assert place == index
        return only_lanes(wide, (0, index))
    part = wide[:, 128:192]
    blank = jnp.zeros_like(part)
    return jnp.concatenate((part, blank) if place == 0 else (blank, part), axis=1)


def attention_back(read, tile_of, skip, note, dq_ref, sums_ref, tick):
    key_values = jnp.transpose(read.kv())
    query_tok = jnp.transpose(read.q(slice(0, GROUP)))
    grad_tok = jnp.transpose(read.do(slice(0, GROUP)))
    sums = [None, None, None]
    for index in range(HEADS):
        rows = slice(index * SIZE, (index + 1) * SIZE)
        k_at, v_at = KEY_AT[index], VALUE_AT[index]
        key_pair, value_pair = key_values[:, lanes_of(k_at)], key_values[:, lanes_of(v_at)]
        query_pair = moved(query_tok, index, k_at[1])
        grad_pair = moved(grad_tok, index, v_at[1])
        query_rows = spread(read.q(rows), k_at[1])
        grad_rows = spread(read.do(rows), v_at[1])
        inner = jnp.sum(read.do(rows).astype(F32) * read.o(rows).astype(F32), axis=0, keepdims=True)
        key_sum = value_sum = None
        for half in range(2):
            end = (half + 1) * HALF if skip else BLOCK
            lanes = slice(half * HALF, (half + 1) * HALF)
            scores = dot(key_pair[:end], query_rows[:, lanes])
            grad_probs = dot(value_pair[:end], grad_rows[:, lanes])
            prob_columns, grad_columns = [], []
            for part in range(2):
                query_tile = 2 * half + part
                cut = slice(query_tile * TILE, (query_tile + 1) * TILE)
                here = slice(part * TILE, (part + 1) * TILE)
                total = read.lse(index, cut)
                probs, grads = [], []
                for kt in range(query_tile + 1 if skip else BLOCK // TILE):
                    there = slice(kt * TILE, (kt + 1) * TILE)
                    prob = jnp.exp(tile_of(scores[there, here], index, kt, query_tile) - total)
                    ds = prob * (grad_probs[there, here] - inner[:, cut])
                    note(index, kt, query_tile, ds)
                    probs.append(prob.astype(BF16))
                    grads.append(ds.astype(BF16))
                if skip and part == 0:
                    probs.append(jnp.zeros((TILE, TILE), BF16))
                    grads.append(jnp.zeros((TILE, TILE), BF16))
                prob_columns.append(jnp.concatenate(probs, axis=0))
                grad_columns.append(jnp.concatenate(grads, axis=0))
            probs = jnp.concatenate(prob_columns, axis=1)
            grads = jnp.concatenate(grad_columns, axis=1)
            value_sum = grow(value_sum, dot(probs, grad_pair[lanes]))
            key_sum = grow(key_sum, dot(grads, query_pair[lanes]))
            dq_ref[rows, lanes] = dot(read.k(index, end), grads).astype(BF16)
        for at, total in ((k_at, key_sum), (v_at, value_sum)):
            sums[at[0]] = total if sums[at[0]] is None else sums[at[0]] + total
        tick(index)
    for tile in range(3):
        sums_ref[:, tile * 128 : (tile + 1) * 128] = sums[tile].astype(BF16)
    sums_ref[:, QUERY_START : QUERY_START + GROUP] = jnp.transpose(dq_ref[...])


def row_of(ref):
    return jnp.reshape(ref[...], (1, ref.shape[0]))


class Tiles:
    def __init__(self, place, ref):
        self.place, self.ref = place, ref

    def __getitem__(self, tile):
        return self.ref[self.place.core, self.place.y * BLOCK + tile * TILE]


def key_segments(place, ref):
    lanes = pl.ds(pl.multiple_of(place.y * BLOCK, BLOCK), BLOCK)
    return jnp.where(place.core == 0, ref[0:1, lanes], ref[1:2, lanes])


class Read:
    def __init__(self, kv, k, q, do, o, lse):
        self.kv, self.k, self.q, self.do, self.o, self.lse = kv, k, q, do, o, lse


class Named:
    def __init__(self, tree):
        for key, value in tree.items():
            setattr(self, key, Named(value) if isinstance(value, dict) else value)


class Copies:
    def __init__(self, send, recv):
        self.send, self.recv, self.count, self.sent = send, recv, 0, []

    def new(self, source, target, device):
        at = self.count
        self.count += 1
        return Copy(self, at, source, target, device)


class Copy:
    def __init__(self, owner, at, source, target, device):
        self.owner, self.at, self.source, self.target, self.device = owner, at, source, target, device

    def make(self):
        return pltpu.make_async_remote_copy(
            src_ref=self.source(), dst_ref=self.target(), send_sem=self.owner.send.at[self.at],
            recv_sem=self.owner.recv.at[self.at], device_id=self.device, device_id_type=MESH,
        )

    def start(self):
        self.make().start()

    def got(self):
        self.make().wait_recv()

    def sent(self):
        self.make().wait_send()

    def done(self):
        self.make().wait()


class Place:
    def __init__(self, depth):
        b, h = lax.axis_index("batch"), lax.axis_index("head")
        self.depth = depth
        self.core, self.y, self.x, self.z = h % 2, h // 2, b % 2, b // 2
        self.to_core = (b, h + 1 - 2 * self.core)
        self.to_y = (b, h + 2 - 4 * self.y)
        self.to_x = (b + 1 - 2 * self.x, h)
        self.to_z = [(lax.rem(self.z + k, depth) * 2 + self.x, h) for k in range(1, depth)]
        self.z0, self.zh, self.far = self.z % 2, self.z // 2, depth // 2
        self.to_z0 = ((self.z + 1 - 2 * self.z0) * 2 + self.x, h)
        self.to_zh = [((lax.rem(self.zh + k, self.far) * 2 + self.z0) * 2 + self.x, h) for k in range(1, self.far)]

    def group(self, slot):
        low, high = slot % 2, slot // 2
        return (self.core + low - 2 * self.core * low) + 2 * (self.y + high - 2 * self.y * high)

    def everyone(self):
        return [self.to_core, self.to_y, self.to_x] + self.to_z


ZH, Z0, X, Y = range(4)


class Sum:
    def __init__(self, place, copies, total, got, order):
        self.place, self.total, self.got, self.order = place, total, got, order
        self.dims = len(total.shape) - 2
        self.stages = []
        for at, axis in enumerate(order):
            room = got[at]
            if axis == ZH:
                stage = [
                    copies.new(self.source(at, k), (lambda room, k: lambda: room.at[k - 1])(room, k), place.to_zh[k - 1])
                    for k in range(1, place.far)
                ]
            else:
                device = (None, place.to_z0, place.to_x, place.to_y)[axis]
                stage = [copies.new(self.source(at, 1), (lambda room: lambda: room)(room), device)]
            self.stages.append(stage)

    @staticmethod
    def rooms(far, dims, order, rows, lanes):
        sizes = (far, 2, 2, 2)
        free = list(range(dims))
        shapes = []
        for axis in order:
            free.remove(axis)
            lead = (far - 1,) if axis == ZH else ()
            shapes.append(lead + tuple(sizes[d] for d in free) + (rows, lanes))
        return shapes

    @staticmethod
    def count(far, order):
        return sum(far - 1 if axis == ZH else 1 for axis in order)

    def mine(self, axis):
        return (self.place.zh, self.place.z0, self.place.x, self.place.y)[axis]

    def source(self, at, k):
        def view():
            index = [slice(None)] * self.dims
            for axis in self.order[:at]:
                index[axis] = self.mine(axis)
            axis = self.order[at]
            index[axis] = lax.rem(self.place.zh + k, self.place.far) if axis == ZH else 1 - self.mine(axis)
            return self.total.at[tuple(index)]

        return view

    def start(self, at):
        for copy in self.stages[at]:
            copy.start()

    def value(self, at, free):
        axis = self.order[at]
        later = sorted(self.order[at + 1 :])
        index = [None] * self.dims
        for done in self.order[: at + 1]:
            index[done] = self.mine(done)
        for d, i in zip(later, free):
            index[d] = i
        got = [self.got[at].at[k] for k in range(self.place.far - 1)] if axis == ZH else [self.got[at]]
        return tuple(index), [g[tuple(free)] if free else g[...] for g in got]

    def add(self, at):
        for copy in self.stages[at]:
            copy.got()
        later = sorted(self.order[at + 1 :])

        def one(free):
            index, got = self.value(at, free)
            if len(got) == 1:
                self.total[index] = self.total[index] + got[0]
            else:
                total = self.total[index].astype(F32)
                for g in got:
                    total = total + g.astype(F32)
                self.total[index] = total.astype(BF16)

        def over(dims, free):
            if not dims:
                one(free)
            elif dims[0] == ZH:

                @pl.loop(0, self.place.far)
                def _(z):
                    over(dims[1:], free + [z])

            else:
                for i in range(2):
                    over(dims[1:], free + [i])

        over(later, [])
        self.start(at + 1)

    def finish(self):
        at = len(self.order) - 1
        for copy in self.stages[at]:
            copy.got()
        index, got = self.value(at, [])
        total = self.total[index].astype(F32)
        for g in got:
            total = total + g.astype(F32)
        return total

    def sent(self):
        for stage in self.stages:
            for copy in stage:
                copy.sent()


def add_loop(target, other):
    inner = target.shape[1:-2]

    @pl.loop(0, target.shape[0])
    def _(z):
        for index in np.ndindex(*inner):
            target[(z, *index)] = target[(z, *index)] + other[(z, *index)]


class Shared:
    def __init__(self, place, copies, room, order, send, pair):
        self.place, self.room, self.from_pair = place, room, pair
        self.sum = Sum(place, copies, room.total, room.got, order)
        self.pair = copies.new(lambda: send, lambda: pair, place.to_core)
        self.swap = copies.new(lambda: room.last.at[1 - place.core], lambda: room.other, place.to_core)

    def enter(self, keep=None):
        self.pair.got()
        if keep is not None:
            keep.wait()
        add_loop(self.room.total, self.from_pair)
        self.sum.start(0)

    def last(self):
        total = self.sum.finish()
        rows = total.shape[0] // 2
        self.room.last[0] = total[:rows]
        self.room.last[1] = total[rows:]
        self.swap.start()

    def store(self, out, offset, half):
        self.swap.got()
        lanes = self.room.other.shape[1]
        mine, other = self.room.last[self.place.core], self.room.other[...]
        for which in range(2):
            at = slice(which * half + offset, which * half + offset + lanes)
            out[:, at] = jnp.where(self.place.core == which, mine, other)

    def sent(self):
        self.swap.sent()
        self.sum.sent()


class Slots:
    def __init__(self, place, copies, room, sends, y_first, order):
        self.place, self.room, self.y_first = place, room, y_first
        self.pair = [copies.new((lambda j: lambda: sends.at[j])(j), (lambda j: lambda: room.pair.at[j])(j), place.to_core) for j in range(2)]
        self.own = Sum(place, copies, room.total.at[0], room.got, order)
        if y_first:
            self.across = copies.new(lambda: room.total.at[1], lambda: room.across, place.to_y)
        else:
            self.far = Sum(place, copies, room.total.at[1], room.far, order)
            self.across = copies.new(lambda: room.chunk, lambda: room.across, place.to_y)

    def enter(self, j):
        self.pair[j].got()
        add_loop(self.room.total.at[j], self.room.pair.at[j])
        if j == 1:
            if self.y_first:
                self.across.start()
            else:
                self.far.start(0)
        elif not self.y_first:
            self.own.start(0)

    def take(self):
        self.across.got()
        add_loop(self.room.total.at[0], self.room.across)
        self.own.start(0)

    def give(self):
        self.room.chunk[...] = self.far.finish().astype(BF16)
        self.across.start()

    def finish(self):
        total = self.own.finish()
        if not self.y_first:
            self.across.got()
            total = total + self.room.across[...].astype(F32)
        return total

    def sent(self):
        self.own.sent()
        self.across.sent()
        if not self.y_first:
            self.far.sent()


SHARED_ORDER = dict(
    gate=(Y, X, Z0, ZH), up=(Z0, Y, X, ZH), down_a=(X, Z0, Y, ZH), down_b=(Y, X, Z0, ZH),
    out_two=(Z0, X, Y, ZH), out_one=(Y, Z0, X, ZH),
)
SLOT_ORDER = dict(
    kv_two=(False, (X, Z0, ZH)), q_two=(True, (X, Z0, ZH)), kv_one=(False, (X, Z0, ZH)), q_one=(True, (X, Z0, ZH))
)
KV = slice(0, 2 * GROUP)
QS = slice(2 * GROUP, 3 * GROUP)


def packed(share):
    return share % 32 == 0


def query_shape(share):
    return (share + share // 2, 128) if packed(share) else (share, GROUP)


def put_query(ref, total):
    share = ref.shape[0]
    if not packed(share):
        ref[...] = total
        return
    ref[:, :128] = total[:share]
    ref[: share // 2, 128:] = total[share:, :64]
    ref[share // 2 :, 128:] = total[share:, 64:]


def put_heads(ref, kv):
    key_out, value_out = ref
    key_out[:, :128] = kv[:, :128]
    key_out[:, 128:] = kv[:, 256:320]
    value_out[:, :128] = kv[:, 128:256]
    value_out[:, 128:] = kv[:, 320:384]


def backward_kernel(depth, ins, outs, r):
    place = Place(depth)
    step = pl.program_id(0)
    core = place.core
    copies = Copies(r.send, r.recv)
    segs = Tiles(place, ins.segs)

    shared = Named({
        name: Shared(
            place, copies, getattr(r, name), order, getattr(ins.sends, name, r.out_send), getattr(r.pairs, name, r.out_pair)
        )
        for name, order in SHARED_ORDER.items()
    })
    slots = Named({
        name: Slots(place, copies, getattr(r, name), r.kv_send if name.startswith("kv") else r.q_send, *way)
        for name, way in SLOT_ORDER.items()
    })
    layer_swap = copies.new(lambda: r.block.at[1 - core], lambda: outs.layer.at[core], place.to_core)
    memory_swap = copies.new(lambda: r.block.at[1 - core], lambda: outs.memory.at[core], place.to_core)
    tokens_swap = copies.new(lambda: r.block.at[1 - core], lambda: outs.tokens.at[core], place.to_core)
    gain_copies = [
        copies.new(lambda: r.gains, (lambda k: lambda: r.gains_got.at[k])(k), d)
        for k, d in enumerate([place.to_core, place.to_y, place.to_x] + place.to_z)
    ]
    bias_copies = [
        copies.new((lambda s: lambda: r.bias.at[s])(s), (lambda k: lambda: r.bias_got.at[k])(k), d)
        for k, (s, d) in enumerate(
            zip([1, 3, 2, 0] + [0] * (depth - 1), [place.to_core, place.to_core, place.to_y, place.to_x] + place.to_z)
        )
    ]
    assert copies.count == r.send.shape[0], copies.count

    loads = []

    def load(source, target):
        loads.append(pltpu.make_async_copy(source, target, r.load.at[len(loads)]))
        return loads[-1]

    i = ins.loaded
    after, wo_two, ctx_two = load(i.after, r.after), load(i.wo_two, r.wo), load(i.ctx_two, r.ctx)
    n_two, mem, first, tok = load(i.n_two, r.n), load(i.mem, r.mem), load(i.first, r.hidden), load(i.tok, r.hidden)
    wo_one, ctx_one, n_one = load(i.wo_one, r.wo), load(i.ctx_one, r.ctx), load(i.n_one, r.n)
    keeps = Named({
        name: load(getattr(ins.keeps, name), getattr(r, name).total) for name in SHARED_ORDER if hasattr(ins.keeps, name)
    })
    layer_in = load(ins.layer, r.block)
    layer_put = load(r.block.at[core], outs.layer.at[core])
    memory_put = load(r.block.at[core], outs.memory.at[core])
    tokens_put = load(r.block.at[core], outs.tokens.at[core])

    def out_products(unit, context, branch):
        lanes = context.shape[0] // 2
        for which, target in ((1 - core, r.out_send), (core, unit.room.total)):
            side = jnp.transpose(context[pl.ds(pl.multiple_of(which * lanes, 16), lanes), :])
            per = branch.shape[0] // 2
            for part in range(2):
                product = dot(branch[part * per : (part + 1) * per, :], side).astype(BF16)
                rows = target.shape[4]
                for piece in range(per // rows):
                    at = part * (per // rows) + piece
                    to = (at // 8, (at // 4) % 2, (at // 2) % 2, at % 2)
                    target[to] = product[piece * rows : (piece + 1) * rows]
            if which is not core:
                unit.pair.start()

    def weight_products(target, left, lanes):
        rows = left.shape[0] // (2 * depth)
        per = left.shape[0] // 2
        for part in range(2):
            product = dot(left[part * per : (part + 1) * per, :], r.dqkv[:, lanes]).astype(BF16)
            for piece in range(per // rows):
                at = part * (per // rows) + piece
                to = (at // 4, (at // 2) % 2, at % 2)
                share = product[piece * rows : (piece + 1) * rows]
                if target.shape[-1] == share.shape[1]:
                    target[to] = share
                else:
                    target[(*to, slice(0, rows))] = share[:, :128]
                    rest = share[:, 128:]
                    target[(*to, slice(rows, rows + rows // 2))] = jnp.concatenate((rest[: rows // 2], rest[rows // 2 :]), axis=1)

    def add_rows(target, lanes, weights, fresh):
        for part in range(2):
            rows = slice(part * HALF, (part + 1) * HALF)
            product = dot(r.dqkv[rows, lanes], weights)

            @pl.when(fresh)
            def _():
                target[rows, :] = product

            @pl.when(jnp.logical_not(fresh))
            def _():
                target[rows, :] = target[rows, :] + product

    def norm_back(hidden, gain, incoming, onto, gain_row, branch):
        total = jnp.zeros((1, hidden.shape[1]), F32)
        for part in range(4):
            rows = slice(part * TILE, (part + 1) * TILE)
            h = hidden[rows, :].astype(F32)
            e = incoming[rows, :]
            scale = lax.rsqrt(jnp.mean(h * h, axis=-1, keepdims=True) + NORM_EPS)
            weighted = e * row_of(gain)
            inner = jnp.mean(weighted * h, axis=-1, keepdims=True)
            result = onto[rows, :] + weighted * scale - h * (scale * scale * scale * inner)
            total = total + jnp.sum(e * h * scale, axis=0, keepdims=True)
            if branch is None:
                r.block[part // 2, (part % 2) * TILE : (part % 2 + 1) * TILE, :] = result.astype(BF16)
            else:
                onto[rows, :] = result
                branch[:, rows] = jnp.transpose(result.astype(BF16))
        r.gains[gain_row : gain_row + 1, :] = total

    plan = {}

    def at(point, *tasks):
        plan.setdefault(point, []).extend(tasks)

    sh, sl = shared, slots
    at((0, 0), sh.out_two.enter, lambda: sh.up.enter(keeps.up))
    at((0, 1), lambda: sh.down_a.enter(keeps.down_a))
    at((0, 2), lambda: sh.down_b.enter(keeps.down_b))
    at((0, 3), sl.kv_two.pair[1].start, sl.q_two.pair[1].start)
    at((1, 1), lambda: sh.out_two.sum.add(0))
    at((1, 3), lambda: sl.kv_two.enter(1), lambda: sl.q_two.enter(1))
    at((2, 0), lambda: sh.down_a.sum.add(0))
    at((2, 2), lambda: sh.out_two.sum.add(1))
    at((2, 3), sl.kv_two.pair[0].start, sl.q_two.pair[0].start, lambda: sh.gate.sum.add(0))
    at((3, 2), lambda: sl.kv_two.far.add(0))
    at((3, 3), lambda: sl.kv_two.enter(0), lambda: sl.q_two.enter(0))
    at((3, 4), lambda: sh.up.sum.add(0), lambda: sh.down_b.sum.add(0))
    at((4, 0), lambda: sh.down_a.sum.add(1), sh.out_one.enter, lambda: sh.gate.sum.add(1))
    at((4, 1), sl.q_two.take)
    at((4, 2), lambda: sl.kv_two.far.add(1), lambda: sh.out_two.sum.add(2))
    at((4, 3), sl.kv_one.pair[1].start, sl.q_one.pair[1].start)
    at((5, 0), lambda: sl.kv_two.own.add(0))
    at((5, 1), lambda: sh.gate.sum.add(2))
    at((5, 2), sl.kv_two.give)
    at((5, 3), lambda: sl.kv_one.enter(1), lambda: sl.q_one.enter(1))
    at((6, 0), lambda: sh.up.sum.add(1), lambda: sh.down_b.sum.add(1))
    at((6, 1), lambda: sl.kv_two.own.add(1), lambda: sl.q_two.own.add(0))
    at((6, 3), sl.kv_one.pair[0].start, sl.q_one.pair[0].start)
    at((7, 0), lambda: sh.out_one.sum.add(0), lambda: sh.down_b.sum.add(2))
    at((7, 1), lambda: sh.down_a.sum.add(2), lambda: sl.kv_one.far.add(0))
    at((7, 2), lambda: sl.q_two.own.add(1))

    def tick(steps, index):
        for k in steps:
            if (k, index) in plan:

                def run(tasks=plan[k, index]):
                    for task in tasks:
                        task()

                pl.when(step == k)(run)

    @pl.when(step == 0)
    def _():
        barrier = pltpu.get_barrier_semaphore()
        for device in place.everyone():
            pl.semaphore_signal(barrier, inc=1, device_id=device, device_id_type=MESH)
        for copy in (after, wo_two, ctx_two, layer_in):
            copy.start()
        pl.semaphore_wait(barrier, len(place.everyone()))
        for name in SHARED_ORDER:
            if hasattr(keeps, name):
                getattr(shared, name).pair.start()
                getattr(keeps, name).start()
        for copy in (n_two, mem, first):
            copy.start()
        after.wait()
        for part in range(4):
            rows = slice(part * TILE, (part + 1) * TILE)
            r.branch[:, rows] = jnp.transpose(r.after[rows, :].astype(BF16))
        key_mask(segs, key_segments(place, ins.memsegs), r.mask)
        wo_two.wait()
        ctx_two.wait()
        layer_in.wait()
        layer_swap.start()
        layer_put.start()
        sh.gate.enter(keeps.gate)
        out_products(sh.out_two, r.ctx, r.branch)
        n_two.wait()
        mem.wait()
        r.gains[...] = jnp.zeros_like(r.gains)
        r.gains[2:3, :] = row_of(ins.ff_gain_grad)

    slot = 3 - step % 4
    odd = slot % 2 == 1
    rows_at = pl.ds(pl.multiple_of(place.group(slot) * GROUP, 16), GROUP)

    def slot_products(kv, q, kv_left, q_left):
        @pl.when(odd)
        def _():
            weight_products(r.kv_send.at[slot // 2], kv_left, KV)
            weight_products(r.q_send.at[slot // 2], q_left, QS)

        @pl.when(jnp.logical_not(odd))
        def _():
            weight_products(kv.room.total.at[slot // 2], kv_left, KV)
            weight_products(q.room.total.at[slot // 2], q_left, QS)

    @pl.when(step < 4)
    def _():
        r.do[...] = dot(r.wo[rows_at, :], r.branch[...]).astype(BF16)
        kv, q, lse = ins.kv_two, ins.q_two, ins.lse_two
        context = r.ctx.at[rows_at, :]
        read = Read(
            lambda: kv[0], lambda h, end: kv[0, rows_of(KEY_AT[h]), :end], lambda rows: q[0, rows, :],
            lambda rows: r.do[rows, :], lambda rows: context[rows, :], lambda h, cut: lse[0, h : h + 1, cut],
        )

        def tile_of(scores, index, kt, qt):
            return scores + r.mask[kt * TILE : (kt + 1) * TILE, qt * TILE : (qt + 1) * TILE].astype(F32)

        attention_back(read, tile_of, False, lambda *a: None, r.dq, r.dqkv, lambda h: tick(range(4), h))
        slot_products(sl.kv_two, sl.q_two, r.mem, r.n)
        tick(range(4), 3)
        add_rows(r.acc_b, KV, ins.wt_two[0, KV, :], step == 0)
        add_rows(r.acc_a, QS, ins.wt_two[0, QS, :], step == 0)

    @pl.when(step == 3)
    def _():
        for copy in (wo_one, ctx_one, n_one):
            copy.start()
        first.wait()
        layer_swap.sent()
        layer_put.wait()
        norm_back(r.hidden, ins.cross_gain, r.acc_a, r.after, 1, r.branch)
        tok.start()
        for part in range(4):
            rows = slice(part * TILE, (part + 1) * TILE)
            r.block[part // 2, (part % 2) * TILE : (part % 2 + 1) * TILE, :] = r.acc_b[rows, :].astype(BF16)
        memory_swap.start()
        memory_put.start()
        for copy in (wo_one, ctx_one, n_one):
            copy.wait()
        sh.out_two.pair.sent()
        out_products(sh.out_one, r.ctx, r.branch)
        for task in plan[3, 4]:
            task()

    @pl.when(step >= 4)
    def _():
        r.do[...] = dot(r.wo[rows_at, :], r.branch[...]).astype(BF16)
        qkv, lse = ins.qkv_one, ins.lse_one
        context = r.ctx.at[rows_at, :]
        read = Read(
            lambda: qkv[0, KV, :], lambda h, end: qkv[0, rows_of(KEY_AT[h]), :end],
            lambda rows: qkv[0, QUERY_START + rows.start : QUERY_START + rows.stop, :],
            lambda rows: r.do[rows, :], lambda rows: context[rows, :], lambda h, cut: lse[0, h : h + 1, cut],
        )
        table, one_hot = ins.table[0], ins.hot[...]
        tiles = [bias_tiles(table, index, one_hot) for index in range(HEADS)]
        kept = {}

        def note(index, kt, qt, ds):
            key = (index, min(qt - kt, 2))
            kept[key] = kept[key] + ds if key in kept else ds

        attention_back(
            read, lambda scores, index, kt, qt: self_tile(scores, kt, qt, tiles[index], segs, 0), True, note,
            r.dq, r.dqkv, lambda h: tick(range(4, 8), h),
        )
        key = lax.broadcasted_iota(jnp.int32, (TILE, TILE), 0)
        query = lax.broadcasted_iota(jnp.int32, (TILE, TILE), 1)
        flip = (key + query == TILE - 1).astype(F32)
        row = lax.broadcasted_iota(jnp.int32, (8, 2 * TILE), 0)
        lane = lax.broadcasted_iota(jnp.int32, (8, 2 * TILE), 1)
        by_distance = jnp.zeros((8, 2 * TILE), F32)
        for index in range(HEADS):
            both = jnp.concatenate((kept[index, 0], kept[index, 1]), axis=1)
            both = jnp.dot(flip, both, precision=lax.Precision.HIGHEST, preferred_element_type=F32)
            turned = jnp.sum(pltpu.roll(both, TILE + 1, 1, stride=1, stride_axis=0), axis=0, keepdims=True)
            far_total = jnp.sum(jnp.sum(kept[index, 2], axis=0, keepdims=True), axis=1, keepdims=True)
            turned = turned + jnp.where(lane[:1] == 2 * TILE - 1, far_total, 0.0)
            by_distance = by_distance + jnp.where(row == index, turned, 0.0)
        r.bias[slot] = lax.dot_general(
            by_distance, one_hot, (((1,), (1,)), ((), ())), precision=lax.Precision.HIGHEST, preferred_element_type=F32
        )
        for k, j in ((4, 1), (6, 0)):

            @pl.when(step == k)
            def _(j=j):
                sl.kv_two.pair[j].sent()
                sl.q_two.pair[j].sent()

        slot_products(sl.kv_one, sl.q_one, r.n, r.n)
        tick(range(4, 8), 3)
        add_rows(r.acc_a, slice(0, 3 * GROUP), ins.wt_one[0], step == 4)

    @pl.when(step == 7)
    def _():
        sl.kv_one.enter(0)
        sl.q_one.enter(0)
        gains, bias = r.gains, r.bias
        memory_swap.sent()
        memory_put.wait()
        tok.wait()
        norm_back(r.hidden, ins.self_gain, r.acc_a, r.after, 0, None)
        tokens_swap.start()
        tokens_put.start()
        gain_copies[0].start()
        bias_copies[0].start()
        bias_copies[1].start()
        sh.out_one.sum.add(1)
        sh.up.sum.add(2)
        gain_copies[0].done()
        gains[...] = gains[...] + r.gains_got[0]
        bias_copies[0].done()
        bias_copies[1].done()
        bias[0] = bias[0] + r.bias_got[0]
        bias[2] = bias[2] + r.bias_got[1]
        gain_copies[1].start()
        bias_copies[2].start()
        sl.q_one.take()
        sl.kv_one.far.add(1)
        sl.kv_one.own.add(0)
        sh.gate.last()
        sh.out_two.last()
        sh.down_b.last()
        sh.out_one.sum.add(2)
        gain_copies[1].done()
        gains[...] = gains[...] + r.gains_got[1]
        bias_copies[2].done()
        bias[0] = bias[0] + r.bias_got[2]
        gain_copies[2].start()
        bias_copies[3].start()
        sl.q_one.own.add(0)
        sl.kv_one.give()
        sl.kv_one.own.add(1)
        sh.down_a.last()
        gain_copies[2].done()
        gains[...] = gains[...] + r.gains_got[2]
        bias_copies[3].done()
        bias[0] = bias[0] + r.bias_got[3]
        for k in range(depth - 1):
            gain_copies[3 + k].start()
            bias_copies[4 + k].start()
        sl.q_one.own.add(1)
        put_heads((outs.wk_two, outs.wv_two), sl.kv_two.finish())
        put_query(outs.wq_two, sl.q_two.finish())
        sh.up.last()
        sh.out_one.last()
        put_heads((outs.wk_one, outs.wv_one), sl.kv_one.finish())
        gain_total, bias_total = gains[...], bias[0]
        for k in range(depth - 1):
            gain_copies[3 + k].done()
            bias_copies[4 + k].done()
            gain_total = gain_total + r.gains_got[3 + k]
            bias_total = bias_total + r.bias_got[4 + k]
        outs.gains[...] = gain_total
        outs.bias[...] = bias_total
        sh.up.store(outs.up, 0, outs.up.shape[1] // 2)
        sh.down_a.store(outs.down, 0, outs.down.shape[1] // 2)
        sh.down_b.store(outs.down, outs.down.shape[1] // 4, outs.down.shape[1] // 2)
        sh.gate.store(outs.gate, 0, outs.gate.shape[1] // 2)
        sh.out_two.store(outs.out_two, 0, outs.out_two.shape[1] // 2)
        put_query(outs.wq_one, sl.q_one.finish())
        sh.out_one.store(outs.out_one, 0, outs.out_one.shape[1] // 2)
        for name in SHARED_ORDER:
            unit = getattr(shared, name)
            unit.sent()
            if unit is not sh.out_two:
                unit.pair.sent()
        for name in SLOT_ORDER:
            getattr(slots, name).sent()
        for j in range(2):
            sl.kv_one.pair[j].sent()
            sl.q_one.pair[j].sent()
        layer_swap.got()
        memory_swap.got()
        tokens_swap.done()
        tokens_put.wait()


def backward_call(batch_size, operands):
    depth = batch_size // 2
    tok = operands["loaded"]["tok"]
    model = tok.shape[1]
    share = model // batch_size
    anywhere = pl.BlockSpec(memory_space=pl.ANY)

    def fixed(shape):
        return pl.BlockSpec(shape, lambda t: (0,) * len(shape))

    def early(array):
        return pl.BlockSpec((1,) + array.shape[1:], lambda t: (3 - t + (t // 4) * (t - 3), 0, 0))

    def late(array):
        return pl.BlockSpec((1,) + array.shape[1:], lambda t: (3 - (t // 4) * (t - 4), 0, 0))

    kinds = dict(
        segs=lambda a: pl.BlockSpec(memory_space=pltpu.SMEM), kv_two=early, q_two=early, lse_two=early, wt_two=early,
        qkv_one=late, lse_one=late, wt_one=late, table=late, loaded=lambda a: anywhere, sends=lambda a: anywhere,
        keeps=lambda a: anywhere, layer=lambda a: anywhere,
    )
    in_specs = {
        name: jax.tree.map(kinds.get(name, lambda a: fixed(a.shape)), value) for name, value in operands.items()
    }
    keeps = operands["keeps"]
    shapes = {name: keeps[name].shape[4:] for name in keeps}
    shapes.update(out_two=(model // (4 * depth), model // 2), out_one=(model // (4 * depth), model // 2))
    block = jax.ShapeDtypeStruct((2, HALF, model), BF16)

    def wide(rows, columns):
        return jax.ShapeDtypeStruct((rows, columns), F32)

    head = wide(share, GROUP)
    outs = dict(
        layer=block, memory=block, tokens=block,
        gate=wide(shapes["gate"][0] // 2, 2 * shapes["gate"][1]), up=wide(shapes["up"][0] // 2, 2 * shapes["up"][1]),
        down=wide(shapes["down_a"][0] // 2, 4 * shapes["down_a"][1]),
        out_two=wide(shapes["out_two"][0] // 2, model), out_one=wide(shapes["out_one"][0] // 2, model),
        wq_two=head, wk_two=head, wv_two=head, wq_one=head, wk_one=head, wv_one=head,
        gains=wide(8, model), bias=wide(8, TILE),
    )
    out_specs = {name: anywhere if s is block else fixed(s.shape) for name, s in outs.items()}

    def room(*shape, kind=BF16):
        return pltpu.VMEM(shape, kind)

    scratch = {}
    for name, order in SHARED_ORDER.items():
        rows, lanes = shapes[name]
        scratch[name] = dict(
            total=room(depth // 2, 2, 2, 2, rows, lanes),
            got=[room(*s) for s in Sum.rooms(depth // 2, 4, order, rows, lanes)],
            last=room(2, rows // 2, lanes, kind=F32), other=room(rows // 2, lanes, kind=F32),
        )
    for name, (y_first, order) in SLOT_ORDER.items():
        piece = (share, 2 * GROUP) if name.startswith("kv") else query_shape(share)
        got = [room(*s) for s in Sum.rooms(depth // 2, 3, order, *piece)]
        both = room(2, depth // 2, 2, 2, *piece)
        scratch[name] = dict(total=both, pair=both, got=got)
        if y_first:
            scratch[name].update(across=room(depth // 2, 2, 2, *piece))
        else:
            scratch[name].update(across=room(*piece), chunk=room(*piece), far=list(got))
    scratch.update(
        pairs={name: room(depth // 2, 2, 2, 2, *shapes[name]) for name in keeps},
        out_send=room(depth // 2, 2, 2, 2, *shapes["out_one"]), out_pair=room(depth // 2, 2, 2, 2, *shapes["out_one"]), kv_send=room(2, depth // 2, 2, 2, share, 2 * GROUP),
        q_send=room(2, depth // 2, 2, 2, *query_shape(share)), block=room(2, HALF, model), branch=room(model, BLOCK),
        acc_a=room(BLOCK, model, kind=F32), acc_b=room(BLOCK, model, kind=F32), dqkv=room(BLOCK, 3 * GROUP),
        dq=room(GROUP, BLOCK), do=room(GROUP, BLOCK), mask=room(BLOCK, BLOCK), gains=room(8, model, kind=F32),
        gains_got=room(depth + 2, 8, model, kind=F32), bias=room(4, 8, TILE, kind=F32),
        bias_got=room(depth + 3, 8, TILE, kind=F32),
        after=room(BLOCK, model, kind=F32), hidden=room(BLOCK, model, kind=F32),
        wo=room(model, model), ctx=room(model, BLOCK), n=room(model, BLOCK), mem=room(model, BLOCK),
    )
    z = depth - 1
    copies = 3 + (3 + z) + (4 + z)
    copies += sum(2 + Sum.count(depth // 2, order) for order in SHARED_ORDER.values())
    copies += sum(3 + (1 if y_first else 2) * Sum.count(depth // 2, order) for y_first, order in SLOT_ORDER.values())
    scratch.update(send=pltpu.SemaphoreType.DMA((copies,)), recv=pltpu.SemaphoreType.DMA((copies,)))
    scratch.update(load=pltpu.SemaphoreType.DMA((18,)))

    arrays, in_tree = jax.tree.flatten(operands)
    out_shapes, out_tree = jax.tree.flatten(outs)
    rooms, room_tree = jax.tree.flatten(scratch)

    def kernel(*refs):
        a, b = len(arrays), len(arrays) + len(out_shapes)
        backward_kernel(
            depth, Named(jax.tree.unflatten(in_tree, refs[:a])), Named(jax.tree.unflatten(out_tree, refs[a:b])),
            Named(jax.tree.unflatten(room_tree, refs[b:])),
        )

    results = pl.pallas_call(
        kernel,
        grid=(8,),
        in_specs=jax.tree.leaves(in_specs),
        out_specs=jax.tree.leaves(out_specs),
        out_shape=out_shapes,
        scratch_shapes=rooms,
        compiler_params=pltpu.CompilerParams(
            collective_id=0, has_side_effects=True, vmem_limit_bytes=66_000_000, dimension_semantics=("arbitrary",)
        ),
        cost_estimate=pl.CostEstimate(flops=20_000_000_000, bytes_accessed=40_000_000, transcendentals=6_000_000),
    )(*arrays)
    return Named(jax.tree.unflatten(out_tree, results))


PIECES = 3


class Gather:
    def __init__(self, place, copies, slots):
        self.slots = slots
        half = slots.shape[1] // 2
        size = half // PIECES
        self.core = copies.new(lambda: slots.at[0], lambda: slots.at[1], place.to_core)

        def rows(side, j):
            return pl.ds(pl.multiple_of(side * half + j * size, 32), size)

        def make(source, target, side, device):
            return [
                copies.new(
                    (lambda j: lambda: slots.at[source, rows(side, j)])(j),
                    (lambda j: lambda: slots.at[target, rows(side, j)])(j), device,
                )
                for j in range(PIECES)
            ]

        self.over_y = make(0, 2, place.x, place.to_y)
        self.over_x = make(2, 2, place.x, place.to_x)
        self.near = make(2, 3, place.x, place.to_core)
        self.far = make(2, 3, 1 - place.x, place.to_core)

    def start(self):
        for copy in self.over_y:
            copy.start()
        self.core.start()

    def pass_y(self, j):
        self.over_y[j].got()
        self.over_x[j].start()
        self.near[j].start()

    def pass_x(self, j):
        self.over_x[j].got()
        self.far[j].start()

    def ready(self):
        for copy in self.near + self.far:
            copy.got()

    def sent(self):
        for copy in [self.core] + self.over_y + self.over_x + self.near + self.far:
            copy.sent()


def forward_kernel(ins, outs, r):
    place = Place(2)
    step = pl.program_id(0)
    core = place.core
    copies = Copies(r.send, r.recv)
    segs = Tiles(place, ins.segs)
    gather_one = Gather(place, copies, r.wt_one)
    gather_two = Gather(place, copies, r.wt_two)
    tables = [
        copies.new((lambda a: lambda: r.table.at[a])(a), (lambda b: lambda: r.table.at[b])(b), d)
        for a, b, d in ((0, 1, place.to_core), (0, 2, place.to_y), (2, 3, place.to_core))
    ]
    swaps = {}
    tok_swap = copies.new(lambda: ins.tokens.at[1 - core], lambda: r.tok_in.at[core], place.to_core)
    mem_swap = copies.new(lambda: ins.memory.at[1 - core], lambda: r.mem_in.at[core], place.to_core)
    cot_swap = copies.new(lambda: ins.cotangent.at[1 - core], lambda: r.cot_in.at[core], place.to_core)
    assert copies.count == r.send.shape[0], copies.count
    count = [0]

    def load(source, target):
        count[0] += 1
        return pltpu.make_async_copy(source, target, r.load.at[count[0] - 1])

    tok_own = load(ins.tokens.at[core], r.tok_in.at[core])
    mem_own = load(ins.memory.at[core], r.mem_in.at[core])
    cot_own = load(ins.cotangent.at[core], r.cot_in.at[core])

    def load_group(key, value, query, slots):
        return [
            load(source.at[pl.ds(at, size)], slots.at[0, pl.ds(to, size)])
            for source, at, to, size in (
                (key, 0, 0, 128), (value, 0, 128, 128), (key, 128, 256, 64), (value, 128, 320, 64), (query, 0, 384, GROUP)
            )
        ]

    raw_one = load_group(ins.self_key, ins.self_value, ins.self_query, r.wt_one)
    raw_two = load_group(ins.cross_key, ins.cross_value, ins.cross_query, r.wt_two)
    out_one, out_two = load(ins.self_out, r.wo_one), load(ins.cross_out, r.wo_two)
    puts = Named({name: load(getattr(r, name), getattr(outs, name)) for name in vars(outs)})


    def normed(hidden, gain, target):
        for part in range(4):
            rows = slice(part * TILE, (part + 1) * TILE)
            h = hidden[rows, :]
            scale = lax.rsqrt(jnp.mean(h * h, axis=-1, keepdims=True) + NORM_EPS)
            target[:, rows] = jnp.transpose((h * scale * row_of(gain)).astype(BF16))

    def project_out(context, weights, base, target):
        for part in range(2):
            rows = slice(part * HALF, (part + 1) * HALF)
            target[rows, :] = base[rows, :] + dot(jnp.transpose(context[:, rows]), weights[...])

    def cross_keys(slot):
        r.kv_two[slot] = dot(r.wt_two[slot, KV, :], r.mem[...]).astype(BF16)

    plan = {}

    def at(point, *tasks):
        plan.setdefault(point, []).extend(tasks)

    one, two = gather_one, gather_two
    at((0, 0), lambda: one.pass_y(1))
    at((0, 2), lambda: one.pass_y(2))
    at((1, 0), lambda: one.pass_x(0))
    at((1, 1), tables[1].got, tables[2].start)
    at((1, 2), lambda: one.pass_x(1))
    at((2, 0), lambda: two.pass_y(1))
    at((2, 2), lambda: two.pass_x(0))
    at((3, 0), lambda: two.pass_y(2))
    at((3, 2), lambda: two.pass_x(1))
    at((4, 1), lambda: two.pass_x(2))

    def tick(steps, index):
        for k in steps:
            if (k, index) in plan:

                def run(tasks=plan[k, index]):
                    for task in tasks:
                        task()

                pl.when(step == k)(run)

    @pl.when(step == 0)
    def _():
        barrier = pltpu.get_barrier_semaphore()
        for device in (place.to_core, place.to_y, place.to_x):
            pl.semaphore_signal(barrier, inc=1, device_id=device, device_id_type=MESH)
        for copy in raw_one + [tok_own] + raw_two + [mem_own, out_one, out_two, cot_own]:
            copy.start()
        r.table[0] = jnp.zeros_like(r.table[0])
        r.table[0, :HEADS, : ins.table.shape[1]] = ins.table[...]
        for copy in raw_one:
            copy.wait()
        pl.semaphore_wait(barrier, 3)
        tok_swap.start()
        tables[0].start()
        tables[1].start()
        gather_one.start()
        mem_swap.start()
        cot_swap.start()
        tok_own.wait()
        tok_swap.got()
        for half in range(2):
            r.tok[half * HALF : (half + 1) * HALF, :] = r.tok_in[half].astype(F32)
        puts.tok.start()
        one.pass_y(0)
        normed(r.tok, ins.self_gain, r.n_one)
        puts.n_one.start()
        for copy in raw_two:
            copy.wait()
        gather_two.start()

    @pl.when(step == 1)
    def _():
        gather_one.core.got()
        tables[0].got()

    @pl.when(step == 2)
    def _():
        mem_own.wait()
        mem_swap.got()
        for half in range(2):
            r.mem[:, half * HALF : (half + 1) * HALF] = jnp.transpose(r.mem_in[half])
        puts.mem.start()
        cot_own.wait()
        cot_swap.got()
        for half in range(2):
            r.cot[half * HALF : (half + 1) * HALF, :] = r.cot_in[half]
        puts.cot.start()
        gather_two.core.got()
        cross_keys(0)
        cross_keys(1)
        two.pass_y(0)
        one.pass_x(2)
        one.ready()
        puts.wt_one.start()
        tables[2].got()
        puts.table.start()

    slot = step % 4
    rows_at = pl.ds(pl.multiple_of(place.group(slot) * GROUP, 16), GROUP)

    @pl.when(step < 4)
    def _():
        r.qkv_one[slot] = dot(r.wt_one[slot], r.n_one[...]).astype(BF16)
        self_forward(
            r.qkv_one.at[slot, KV], r.qkv_one.at[slot, QS], r.table[slot], ins.hot[...], segs,
            r.ctx_one.at[rows_at], r.lse_one.at[slot], lambda h: tick(range(4), h),
        )

    @pl.when(step == 4)
    def _():
        puts.qkv_one.start()
        puts.ctx_one.start()
        puts.lse_one.start()
        out_one.wait()
        project_out(r.ctx_one, r.wo_one, r.tok, r.first)
        puts.first.start()
        normed(r.first, ins.cross_gain, r.n_two)
        puts.n_two.start()
        key_mask(segs, key_segments(place, ins.memsegs), r.mask)

    @pl.when(step == 6)
    def _():
        two.ready()
        puts.wt_two.start()

    @pl.when(step >= 4)
    def _():
        @pl.when(step >= 6)
        def _():
            cross_keys(slot)

        r.q_two[slot] = dot(r.wt_two[slot, QS, :], r.n_two[...]).astype(BF16)
        cross_forward(
            r.kv_two.at[slot], r.q_two.at[slot], r.mask, r.ctx_two.at[rows_at], r.lse_two.at[slot],
            lambda h: tick(range(4, 8), h),
        )

    @pl.when(step == 7)
    def _():
        out_two.wait()
        project_out(r.ctx_two, r.wo_two, r.first, r.second)
        for put in (puts.second, puts.ctx_two, puts.q_two, puts.kv_two, puts.lse_two):
            put.start()
        gather_one.sent()
        gather_two.sent()
        for copy in tables + [tok_swap, mem_swap, cot_swap]:
            copy.sent()
        for name in vars(outs):
            getattr(puts, name).wait()


def forward_call(operands):
    tokens = operands["tokens"]
    model = tokens.shape[2]
    anywhere = pl.BlockSpec(memory_space=pl.ANY)

    def fixed(array):
        return pl.BlockSpec(array.shape, lambda t: (0,) * array.ndim)

    small = dict(self_gain=fixed, cross_gain=fixed, table=fixed, hot=fixed, memsegs=fixed)
    small.update(segs=lambda a: pl.BlockSpec(memory_space=pltpu.SMEM))
    in_specs = {name: small.get(name, lambda a: anywhere)(a) for name, a in operands.items()}

    def room(*shape, kind=BF16):
        return pltpu.VMEM(shape, kind)

    kept = dict(
        tok=room(BLOCK, model, kind=F32), mem=room(model, BLOCK), cot=room(BLOCK, model), n_one=room(model, BLOCK),
        n_two=room(model, BLOCK), qkv_one=room(4, 3 * GROUP, BLOCK), kv_two=room(4, 2 * GROUP, BLOCK),
        q_two=room(4, GROUP, BLOCK), ctx_one=room(model, BLOCK), ctx_two=room(model, BLOCK),
        lse_one=room(4, 8, BLOCK, kind=F32), lse_two=room(4, 8, BLOCK, kind=F32),
        first=room(BLOCK, model, kind=F32), second=room(BLOCK, model, kind=F32),
        wt_one=room(4, 3 * GROUP, model), wt_two=room(4, 3 * GROUP, model), table=room(4, 8, TILE, kind=F32),
    )
    block = tokens.shape[1:]
    copies = 2 * (1 + 4 * PIECES) + 3 + 3
    scratch = dict(
        kept, tok_in=room(2, *block), mem_in=room(2, *block), cot_in=room(2, *block),
        wo_one=room(model, model), wo_two=room(model, model), mask=room(BLOCK, BLOCK, kind=F32),
        send=pltpu.SemaphoreType.DMA((copies,)), recv=pltpu.SemaphoreType.DMA((copies,)),
        load=pltpu.SemaphoreType.DMA((15 + len(kept),)),
    )
    outs = {name: jax.ShapeDtypeStruct(m.shape, m.dtype) for name, m in kept.items()}
    arrays, in_tree = jax.tree.flatten(operands)
    out_shapes, out_tree = jax.tree.flatten(outs)
    rooms, room_tree = jax.tree.flatten(scratch)

    def kernel(*refs):
        a, b = len(arrays), len(arrays) + len(out_shapes)
        forward_kernel(
            Named(jax.tree.unflatten(in_tree, refs[:a])), Named(jax.tree.unflatten(out_tree, refs[a:b])),
            Named(jax.tree.unflatten(room_tree, refs[b:])),
        )

    results = pl.pallas_call(
        kernel,
        grid=(8,),
        in_specs=jax.tree.leaves(in_specs),
        out_specs=[anywhere] * len(out_shapes),
        out_shape=out_shapes,
        scratch_shapes=rooms,
        compiler_params=pltpu.CompilerParams(
            collective_id=1, has_side_effects=True, vmem_limit_bytes=60_000_000, dimension_semantics=("arbitrary",)
        ),
        cost_estimate=pl.CostEstimate(flops=10_000_000_000, bytes_accessed=40_000_000, transcendentals=6_000_000),
    )(*arrays)
    return Named(jax.tree.unflatten(out_tree, results))


def finish_call(results, devices, buckets):
    plain = {name: a for name, a in results.items() if name not in ("gains", "bias")}
    share = results["gains"].shape[1] // devices
    outs = {name: jax.ShapeDtypeStruct(a.shape, a.dtype) for name, a in plain.items()}
    anywhere = pl.BlockSpec(memory_space=pl.ANY)
    count = len(plain)

    def kernel(gains, bias, *refs):
        sources, (bias_out, *gain_outs), targets = refs[:count], refs[count : count + 4], refs[count + 4 : 2 * count + 4]
        rooms, semaphores = refs[2 * count + 4 : 3 * count + 4], refs[3 * count + 4]
        takes = [pltpu.make_async_copy(s, r, semaphores.at[k]) for k, (s, r) in enumerate(zip(sources, rooms))]
        puts = [pltpu.make_async_copy(r, t, semaphores.at[count + k]) for k, (r, t) in enumerate(zip(rooms, targets))]
        for take in takes:
            take.start()
        bias_out[...] = bias[:HEADS, :buckets]
        first = (lax.axis_index("batch") * lax.axis_size("head") + lax.axis_index("head")) * share
        turned = pltpu.roll(gains[...], gains.shape[1] - first, 1)
        for k, out in enumerate(gain_outs):
            out[...] = jnp.reshape(turned[k : k + 1, :share], (share,))
        for take, put in zip(takes, puts):
            take.wait()
            put.start()
        for put in puts:
            put.wait()

    def fixed(shape):
        return pl.BlockSpec(shape, lambda: (0,) * len(shape))

    small = [jax.ShapeDtypeStruct((HEADS, buckets), F32)] + [jax.ShapeDtypeStruct((share,), F32)] * 3
    bias, *rest = pl.pallas_call(
        kernel,
        in_specs=[fixed(results["gains"].shape), fixed(results["bias"].shape)] + [anywhere] * count,
        out_specs=[fixed(a.shape) for a in small] + [anywhere] * count,
        out_shape=small + list(outs.values()),
        scratch_shapes=[pltpu.VMEM(a.shape, a.dtype) for a in plain.values()] + [pltpu.SemaphoreType.DMA((2 * count,))],
    )(results["gains"], results["bias"], *plain.values())
    return dict(zip(plain, rest[3:]), bias=bias, gain_0=rest[0], gain_1=rest[1], gain_2=rest[2])


FF_STEPS = 4


def ff_tile(t):
    core = lax.axis_index("head") % 2
    half = t // 2
    other = 1 - core
    return 2 * (half + other - 2 * half * other) + t % 2


def over_rows(left, right):
    return lax.dot_general(left, right, (((1,), (1,)), ((), ())), preferred_element_type=F32)


def ff_kernel(ins, outs, r):
    step = pl.program_id(0)
    core = lax.axis_index("head") % 2
    model = ins.second.shape[1]
    root = np.float32(np.sqrt(2.0 / np.pi))

    @pl.when(step == 0)
    def _():
        for part in range(4):
            rows = slice(part * TILE, (part + 1) * TILE)
            h = ins.second[rows, :]
            scale = lax.rsqrt(jnp.mean(h * h, axis=-1, keepdims=True) + NORM_EPS)
            r.normed[rows, :] = (h * scale * row_of(ins.gain)).astype(BF16)
            r.cot[:, rows] = jnp.transpose(ins.cot[rows, :])
            r.layer[rows, :] = h
            r.back[rows, :] = jnp.zeros_like(h)

    for part in range(4):
        rows = slice(part * TILE, (part + 1) * TILE)
        normed = r.normed[rows, :]
        gate, up = dot(normed, ins.gate[...]), dot(normed, ins.up[...])
        grad = over_rows(ins.cot[rows, :], ins.down[...])
        square = gate * gate
        half = 0.5 + 0.5 * jnp.tanh(gate * (root + (root * 0.044715) * square))
        gelu = gate * half
        slope = half + gelu * (2.0 - 2.0 * half) * (root + (3.0 * 0.044715 * root) * square)
        activation = (gelu * up).astype(BF16)
        grad_gate = (grad * up * slope).astype(BF16)
        grad_up = (grad * gelu).astype(BF16)
        r.act[rows, :] = activation
        r.grad_gate[:, rows] = jnp.transpose(grad_gate)
        r.grad_up[:, rows] = jnp.transpose(grad_up)
        r.layer[rows, :] = r.layer[rows, :] + dot(activation, ins.down[...])
        r.back[rows, :] = r.back[rows, :] + over_rows(grad_gate, ins.gate[...]) + over_rows(grad_up, ins.up[...])

    lanes = model // 2

    def spread_out(target, product, first):
        rows = target.shape[3]
        for piece in range(product.shape[0] // rows):
            at = first + piece
            target[at // 4, (at // 2) % 2, at % 2] = product[piece * rows : (piece + 1) * rows]

    for which, name in ((1 - core, 0), (core, 1)):
        right = r.normed[:, pl.ds(pl.multiple_of(which * lanes, 128), lanes)]
        for grads, target in ((r.grad_gate, outs.gate[name]), (r.grad_up, outs.up[name])):
            spread_out(target, dot(grads[...], right).astype(BF16), 0)
    for t, target in enumerate((outs.down_a[0], outs.down_b[0], outs.down_a[1], outs.down_b[1])):

        @pl.when(step == t)
        def _(target=target):
            per = model // 2
            for part in range(2):
                product = dot(r.cot[part * per : (part + 1) * per, :], r.act[...]).astype(BF16)
                spread_out(target, product, part * (per // target.shape[3]))

    @pl.when(step == FF_STEPS - 1)
    def _():
        total = jnp.zeros((1, model), F32)
        for part in range(4):
            rows = slice(part * TILE, (part + 1) * TILE)
            h, e = ins.second[rows, :], r.back[rows, :]
            scale = lax.rsqrt(jnp.mean(h * h, axis=-1, keepdims=True) + NORM_EPS)
            weighted = e * row_of(ins.gain)
            inner = jnp.mean(weighted * h, axis=-1, keepdims=True)
            outs.after[rows, :] = ins.cot[rows, :].astype(F32) + weighted * scale - h * (scale * scale * scale * inner)
            total = total + jnp.sum(e * h * scale, axis=0, keepdims=True)
            outs.layer[part // 2, (part % 2) * TILE : (part % 2 + 1) * TILE, :] = r.layer[rows, :].astype(BF16)
        outs.gain_grad[...] = jnp.reshape(total, (model,))


def ff_call(depth, operands):
    model, columns = operands["gate"].shape
    tile = columns // FF_STEPS

    def fixed(shape):
        return pl.BlockSpec(shape, lambda t: (0,) * len(shape))

    in_specs = {name: fixed(a.shape) for name, a in operands.items()}
    in_specs.update(
        gate=pl.BlockSpec((model, tile), lambda t: (0, ff_tile(t))),
        up=pl.BlockSpec((model, tile), lambda t: (0, ff_tile(t))),
        down=pl.BlockSpec((tile, model), lambda t: (ff_tile(t), 0)),
    )
    wide = jax.ShapeDtypeStruct((depth, 2, 2, columns // (4 * depth), model // 2), BF16)
    deep = jax.ShapeDtypeStruct((depth, 2, 2, model // (4 * depth), tile), BF16)
    by_tile = pl.BlockSpec((depth // FF_STEPS,) + wide.shape[1:], lambda t: (ff_tile(t), 0, 0, 0, 0))
    outs = dict(
        layer=jax.ShapeDtypeStruct((2, HALF, model), BF16), after=jax.ShapeDtypeStruct((BLOCK, model), F32),
        gain_grad=jax.ShapeDtypeStruct((model,), F32), gate=[wide, wide], up=[wide, wide],
        down_a=[deep, deep], down_b=[deep, deep],
    )
    out_specs = jax.tree.map(lambda a: by_tile if a is wide else fixed(a.shape), outs)
    scratch = dict(
        normed=pltpu.VMEM((BLOCK, model), BF16), cot=pltpu.VMEM((model, BLOCK), BF16),
        layer=pltpu.VMEM((BLOCK, model), F32), back=pltpu.VMEM((BLOCK, model), F32),
        act=pltpu.VMEM((BLOCK, tile), BF16), grad_gate=pltpu.VMEM((tile, BLOCK), BF16),
        grad_up=pltpu.VMEM((tile, BLOCK), BF16),
    )
    arrays, in_tree = jax.tree.flatten(operands)
    out_shapes, out_tree = jax.tree.flatten(outs)
    rooms, room_tree = jax.tree.flatten(scratch)

    def kernel(*refs):
        a, b = len(arrays), len(arrays) + len(out_shapes)
        ff_kernel(
            Named(jax.tree.unflatten(in_tree, refs[:a])), Named(jax.tree.unflatten(out_tree, refs[a:b])),
            Named(jax.tree.unflatten(room_tree, refs[b:])),
        )

    results = pl.pallas_call(
        kernel,
        grid=(FF_STEPS,),
        in_specs=jax.tree.leaves(in_specs),
        out_specs=jax.tree.leaves(out_specs),
        out_shape=out_shapes,
        scratch_shapes=rooms,
        compiler_params=pltpu.CompilerParams(vmem_limit_bytes=60_000_000, dimension_semantics=("arbitrary",)),
        cost_estimate=pl.CostEstimate(flops=14_500_000_000, bytes_accessed=24_000_000, transcendentals=1_000_000),
    )(*arrays)
    return Named(jax.tree.unflatten(out_tree, results))


def on_device(
    tokens, memory, cotangent, target_segments, memory_segments, self_gain, self_query, self_key,
    self_value, self_out, position_bias, cross_gain, cross_query, cross_key, cross_value, cross_out,
    ff_gain, ff_gate, ff_up, ff_down,
):
    heads_axis, batch_axis = lax.axis_size("head"), lax.axis_size("batch")
    rows, part, model = tokens.shape
    assert part * 2 == BLOCK and rows == 2 and heads_axis == 4
    assert position_bias.shape[1] == HEADS and self_query.shape[1] == GROUP
    one_hot = jnp.asarray(bucket_one_hot(position_bias.shape[0]))

    fwd = forward_call(
        dict(
            tokens=tokens, memory=memory, cotangent=cotangent, segs=target_segments, memsegs=memory_segments, hot=one_hot,
            self_gain=self_gain, cross_gain=cross_gain, table=position_bias.T,
            self_query=self_query.T, self_key=self_key.T, self_value=self_value.T, self_out=self_out,
            cross_query=cross_query.T, cross_key=cross_key.T, cross_value=cross_value.T, cross_out=cross_out,
        )
    )
    ff = ff_call(
        batch_axis // 2,
        dict(second=fwd.second, cot=fwd.cot, gain=ff_gain, gate=ff_gate, up=ff_up, down=ff_down),
    )

    def split(array):
        return array.reshape(batch_axis // 4, 2, *array.shape[1:])

    done = backward_call(
        batch_axis,
        dict(
            segs=target_segments, memsegs=memory_segments, hot=one_hot, self_gain=self_gain, cross_gain=cross_gain,
            ff_gain_grad=ff.gain_grad,
            kv_two=fwd.kv_two, q_two=fwd.q_two, lse_two=fwd.lse_two, wt_two=fwd.wt_two,
            qkv_one=fwd.qkv_one, lse_one=fwd.lse_one, wt_one=fwd.wt_one, table=fwd.table,
            loaded=dict(
                after=ff.after, wo_two=cross_out, ctx_two=fwd.ctx_two, n_two=fwd.n_two, mem=fwd.mem,
                first=fwd.first, wo_one=self_out, ctx_one=fwd.ctx_one, n_one=fwd.n_one, tok=fwd.tok,
            ),
            sends=dict(gate=split(ff.gate[0]), up=split(ff.up[0]), down_a=split(ff.down_a[0]), down_b=split(ff.down_b[0])),
            keeps=dict(gate=split(ff.gate[1]), up=split(ff.up[1]), down_a=split(ff.down_a[1]), down_b=split(ff.down_b[1])),
            layer=ff.layer,
        ),
    )
    done = Named(finish_call(vars(done), heads_axis * batch_axis, position_bias.shape[0]))
    return (
        done.layer, done.tokens, done.memory, done.gain_0, done.wq_one, done.wk_one, done.wv_one, done.out_one.T,
        done.bias.T, done.gain_1, done.wq_two, done.wk_two, done.wv_two, done.out_two.T, done.gain_2,
        done.gate.T, done.up.T, done.down.T,
    )


def solution(mesh):
    tokens = P("batch", "head", None)
    rows = P("batch", None)
    columns = P(None, "head")
    split = P("batch", "head")
    every = P(None, ("batch", "head"))
    gain = P(("batch", "head"))
    return jax.shard_map(
        on_device,
        mesh=mesh,
        in_specs=(
            tokens, tokens, tokens, rows, rows, P(), columns, columns, columns, P(), columns, P(),
            columns, columns, columns, P(), P(), P(), P(), P(),
        ),
        out_specs=(
            tokens, tokens, tokens, gain, split, split, split, every, columns, gain,
            split, split, split, every, gain, every, every, every,
        ),
        check_vma=False,
    )
```

```python
import jax
import jax.numpy as jnp
import numpy as np
from jax import lax
from jax.experimental import pallas as pl
from jax.experimental.pallas import tpu as pltpu
from jax.sharding import PartitionSpec as P

NORM_EPS = 1e-06
MASKED = -1e30
BLOCK = 512
TILE = 128
HALF = 256
SIZE = 64
HEADS = 3
GROUP = HEADS * SIZE
F32 = jnp.float32
BF16 = jnp.bfloat16
MESH = pl.DeviceIdType.MESH


def bucket_edges():
    distance = np.arange(1.0, 8192.0)
    far_bucket = 16.0 + np.floor(np.log(np.maximum(distance, 16.0) / 16.0) / np.log(8.0) * 16.0)
    bucket_value = np.where(distance < 16, distance, np.minimum(far_bucket, 31.0))
    return [int(distance[np.argmax(bucket_value >= bucket_level)]) for bucket_level in range(1, 32)]


def bucket_one_hot(buckets):
    ids = np.zeros(2 * TILE, np.int32)
    for edge in bucket_edges():
        ids += np.arange(2 * TILE) >= edge
    assert bucket_edges()[-1] <= TILE + 1
    assert buckets <= TILE and ids[-1] == buckets - 1
    return (np.arange(TILE)[:, None] == ids[None, :]).astype(np.float32)


def dot(left, right):
    return lax.dot_general(left, right, (((1,), (0,)), ((), ())), preferred_element_type=F32)


KEY_AT = ((0, 0), (0, 1), (2, 0))
VALUE_AT = ((1, 0), (1, 1), (2, 1))
QUERY_START = 2 * GROUP


def rows_of(at):
    tile, place = at
    return slice(tile * 128 + place * SIZE, tile * 128 + (place + 1) * SIZE)


def lanes_of(at):
    return slice(at[0] * 128, (at[0] + 1) * 128)


def spread(head_rows, place):
    blank = jnp.zeros_like(head_rows)
    return jnp.concatenate((head_rows, blank) if place == 0 else (blank, head_rows), axis=0)


def bias_tiles(table, index, one_hot):
    by_distance = jnp.dot(
        table, one_hot, precision=lax.Precision.HIGHEST, preferred_element_type=F32
    )[index : index + 1]
    wide = jnp.broadcast_to(by_distance, (TILE, 2 * TILE))
    turned = pltpu.roll(wide, 0, 1, stride=1, stride_axis=0)
    key = lax.broadcasted_iota(jnp.int32, (TILE, TILE), 0)
    query = lax.broadcasted_iota(jnp.int32, (TILE, TILE), 1)
    near = jnp.where(key <= query, turned[:, :TILE], MASKED)
    return near, turned[:, TILE:], by_distance[0, 2 * TILE - 1]


def self_tile(scores, key_tile, query_tile, tiles, seg_ref, base):
    near, next_one, far = tiles
    if key_tile == query_tile:
        return scores + near
    same = seg_ref[base + key_tile] == seg_ref[base + query_tile]
    shift = jnp.where(same, 0.0, MASKED)
    if key_tile == query_tile - 1:
        return scores + next_one + shift
    return scores + (far + shift)


def self_forward(kv, q, table, one_hot, seg_ref, out, lse, tick):
    key_values = jnp.transpose(kv[...])
    for index in range(HEADS):
        rows = slice(index * SIZE, (index + 1) * SIZE)
        keys = key_values[:, lanes_of(KEY_AT[index])]
        query = spread(q[rows, :], KEY_AT[index][1])
        tiles = bias_tiles(table, index, one_hot)
        for half in range(2):
            end = (half + 1) * HALF
            scores = dot(keys[:end], query[:, half * HALF : (half + 1) * HALF])
            columns, totals = [], []
            for part in range(2):
                query_tile = 2 * half + part
                parts = [
                    self_tile(
                        scores[kt * TILE : (kt + 1) * TILE, part * TILE : (part + 1) * TILE],
                        kt, query_tile, tiles, seg_ref, 0,
                    )
                    for kt in range(query_tile + 1)
                ]
                top = jnp.max(parts[0], axis=0, keepdims=True)
                for piece in parts[1:]:
                    top = jnp.maximum(top, jnp.max(piece, axis=0, keepdims=True))
                probs = [jnp.exp(piece - top) for piece in parts]
                total = jnp.sum(probs[0], axis=0, keepdims=True)
                for piece in probs[1:]:
                    total = total + jnp.sum(piece, axis=0, keepdims=True)
                probs = [piece.astype(BF16) for piece in probs]
                if part == 0:
                    probs.append(jnp.zeros((TILE, TILE), BF16))
                columns.append(jnp.concatenate(probs, axis=0))
                totals.append(total)
                lse[index : index + 1, query_tile * TILE : (query_tile + 1) * TILE] = top + jnp.log(total)
            weights = jnp.concatenate(columns, axis=1)
            context = dot(kv[rows_of(VALUE_AT[index]), :end], weights)
            context = context / jnp.concatenate(totals, axis=1)
            out[rows, half * HALF : (half + 1) * HALF] = context.astype(BF16)
        tick(index)


def key_mask(seg_ref, memseg, mask_ref):
    rows = jnp.transpose(jnp.broadcast_to(memseg.astype(F32), (TILE, BLOCK)))
    for tile in range(BLOCK // TILE):
        wanted = seg_ref[tile].astype(F32)
        shift = jnp.where(rows == wanted, 0.0, MASKED)
        mask_ref[:, tile * TILE : (tile + 1) * TILE] = shift.astype(mask_ref.dtype)


def cross_forward(kv, q, mask, out, lse, tick):
    key_values = jnp.transpose(kv[...])
    for index in range(HEADS):
        rows = slice(index * SIZE, (index + 1) * SIZE)
        keys = key_values[:, lanes_of(KEY_AT[index])]
        query = spread(q[rows, :], KEY_AT[index][1])
        for half in range(2):
            lanes = slice(half * HALF, (half + 1) * HALF)
            scores = dot(keys, query[:, lanes]) + mask[:, lanes]
            top = jnp.max(scores, axis=0, keepdims=True)
            probs = jnp.exp(scores - top)
            total = jnp.sum(probs, axis=0, keepdims=True)
            context = dot(kv[rows_of(VALUE_AT[index]), :], probs.astype(BF16)) / total
            out[rows, lanes] = context.astype(BF16)
            lse[index : index + 1, lanes] = top + jnp.log(total)
        tick(index)


def grow(old, new):
    if old is None:
        return new
    shared = old.shape[0]
    if shared == new.shape[0]:
        return old + new
    return jnp.concatenate((old + new[:shared], new[shared:]), axis=0)


def only_lanes(wide, at):
    pair = wide[:, lanes_of(at)]
    lane = lax.broadcasted_iota(jnp.int32, pair.shape, 1)
    keep = lane < SIZE if at[1] == 0 else lane >= SIZE
    return jnp.where(keep, pair, jnp.zeros_like(pair))


def moved(wide, index, place):
    if index < 2:
        assert place == index
        return only_lanes(wide, (0, index))
    part = wide[:, 128:192]
    blank = jnp.zeros_like(part)
    return jnp.concatenate((part, blank) if place == 0 else (blank, part), axis=1)


def attention_back(read, tile_of, skip, note, dq_ref, sums_ref, tick):
    key_values = jnp.transpose(read.kv())
    query_tok = jnp.transpose(read.q(slice(0, GROUP)))
    grad_tok = jnp.transpose(read.do(slice(0, GROUP)))
    sums = [None, None, None]
    for index in range(HEADS):
        rows = slice(index * SIZE, (index + 1) * SIZE)
        k_at, v_at = KEY_AT[index], VALUE_AT[index]
        key_pair, value_pair = key_values[:, lanes_of(k_at)], key_values[:, lanes_of(v_at)]
        query_pair = moved(query_tok, index, k_at[1])
        grad_pair = moved(grad_tok, index, v_at[1])
        query_rows = spread(read.q(rows), k_at[1])
        grad_rows = spread(read.do(rows), v_at[1])
        inner = jnp.sum(read.do(rows).astype(F32) * read.o(rows).astype(F32), axis=0, keepdims=True)
        key_sum = value_sum = None
        for half in range(2):
            end = (half + 1) * HALF if skip else BLOCK
            lanes = slice(half * HALF, (half + 1) * HALF)
            scores = dot(key_pair[:end], query_rows[:, lanes])
            grad_probs = dot(value_pair[:end], grad_rows[:, lanes])
            prob_columns, grad_columns = [], []
            for part in range(2):
                query_tile = 2 * half + part
                cut = slice(query_tile * TILE, (query_tile + 1) * TILE)
                here = slice(part * TILE, (part + 1) * TILE)
                total = read.lse(index, cut)
                probs, grads = [], []
                for kt in range(query_tile + 1 if skip else BLOCK // TILE):
                    there = slice(kt * TILE, (kt + 1) * TILE)
                    prob = jnp.exp(tile_of(scores[there, here], index, kt, query_tile) - total)
                    ds = prob * (grad_probs[there, here] - inner[:, cut])
                    note(index, kt, query_tile, ds)
                    probs.append(prob.astype(BF16))
                    grads.append(ds.astype(BF16))
                if skip and part == 0:
                    probs.append(jnp.zeros((TILE, TILE), BF16))
                    grads.append(jnp.zeros((TILE, TILE), BF16))
                prob_columns.append(jnp.concatenate(probs, axis=0))
                grad_columns.append(jnp.concatenate(grads, axis=0))
            probs = jnp.concatenate(prob_columns, axis=1)
            grads = jnp.concatenate(grad_columns, axis=1)
            value_sum = grow(value_sum, dot(probs, grad_pair[lanes]))
            key_sum = grow(key_sum, dot(grads, query_pair[lanes]))
            dq_ref[rows, lanes] = dot(read.k(index, end), grads).astype(BF16)
        for at, total in ((k_at, key_sum), (v_at, value_sum)):
            sums[at[0]] = total if sums[at[0]] is None else sums[at[0]] + total
        tick(index)
    for tile in range(3):
        sums_ref[:, tile * 128 : (tile + 1) * 128] = sums[tile].astype(BF16)
    sums_ref[:, QUERY_START : QUERY_START + GROUP] = jnp.transpose(dq_ref[...])


def row_of(ref):
    return jnp.reshape(ref[...], (1, ref.shape[0]))


class Tiles:
    def __init__(self, place, ref):
        self.place, self.ref = place, ref

    def __getitem__(self, tile):
        return self.ref[self.place.core, self.place.y * BLOCK + tile * TILE]


def key_segments(place, ref):
    lanes = pl.ds(pl.multiple_of(place.y * BLOCK, BLOCK), BLOCK)
    return jnp.where(place.core == 0, ref[0:1, lanes], ref[1:2, lanes])


class Read:
    def __init__(self, kv, k, q, do, o, lse):
        self.kv, self.k, self.q, self.do, self.o, self.lse = kv, k, q, do, o, lse


class Named:
    def __init__(self, tree):
        for key, value in tree.items():
            setattr(self, key, Named(value) if isinstance(value, dict) else value)


class Copies:
    def __init__(self, send, recv):
        self.send, self.recv, self.count, self.sent = send, recv, 0, []

    def new(self, source, target, device):
        at = self.count
        self.count += 1
        return Copy(self, at, source, target, device)


class Copy:
    def __init__(self, owner, at, source, target, device):
        self.owner, self.at, self.source, self.target, self.device = owner, at, source, target, device

    def make(self):
        return pltpu.make_async_remote_copy(
            src_ref=self.source(), dst_ref=self.target(), send_sem=self.owner.send.at[self.at],
            recv_sem=self.owner.recv.at[self.at], device_id=self.device, device_id_type=MESH,
        )

    def start(self):
        self.make().start()

    def got(self):
        self.make().wait_recv()

    def sent(self):
        self.make().wait_send()

    def done(self):
        self.make().wait()


class Place:
    def __init__(self, depth):
        b, h = lax.axis_index("batch"), lax.axis_index("head")
        self.depth = depth
        self.core, self.y, self.x, self.z = h % 2, h // 2, b % 2, b // 2
        self.to_core = (b, h + 1 - 2 * self.core)
        self.to_y = (b, h + 2 - 4 * self.y)
        self.to_x = (b + 1 - 2 * self.x, h)
        self.to_z = [(lax.rem(self.z + k, depth) * 2 + self.x, h) for k in range(1, depth)]
        self.z0, self.zh, self.far = self.z % 2, self.z // 2, depth // 2
        self.to_z0 = ((self.z + 1 - 2 * self.z0) * 2 + self.x, h)
        self.to_zh = [((lax.rem(self.zh + k, self.far) * 2 + self.z0) * 2 + self.x, h) for k in range(1, self.far)]

    def group(self, slot):
        low, high = slot % 2, slot // 2
        return (self.core + low - 2 * self.core * low) + 2 * (self.y + high - 2 * self.y * high)

    def everyone(self):
        return [self.to_core, self.to_y, self.to_x] + self.to_z


ZH, Z0, X, Y = range(4)


class Sum:
    def __init__(self, place, copies, total, got, order, tiles=()):
        self.place, self.total, self.got, self.order = place, total, got, order
        self.dims = len(total.shape) - 2
        self.stages = []
        for at, axis in enumerate(order):
            room = got[at]
            if at == 0 and tiles:
                assert axis in (X, Y)
                self.stages.append([
                    copies.new(
                        self.source(0, 1, tile), (lambda room, tile: lambda: room.at[tile])(room, tile),
                        place.to_x if axis == X else place.to_y,
                    )
                    for tile in tiles
                ])
                continue
            if axis == ZH:
                stage = [
                    copies.new(self.source(at, k), (lambda room, k: lambda: room.at[k - 1])(room, k), place.to_zh[k - 1])
                    for k in range(1, place.far)
                ]
            else:
                device = (None, place.to_z0, place.to_x, place.to_y)[axis]
                stage = [copies.new(self.source(at, 1), (lambda room: lambda: room)(room), device)]
            self.stages.append(stage)

    @staticmethod
    def rooms(far, dims, order, rows, lanes):
        sizes = (far, 2, 2, 2)
        free = list(range(dims))
        shapes = []
        for axis in order:
            free.remove(axis)
            lead = (far - 1,) if axis == ZH else ()
            shapes.append(lead + tuple(sizes[d] for d in free) + (rows, lanes))
        return shapes

    @staticmethod
    def count(far, order):
        return sum(far - 1 if axis == ZH else 1 for axis in order)

    def mine(self, axis):
        return (self.place.zh, self.place.z0, self.place.x, self.place.y)[axis]

    def source(self, at, k, tile=()):
        def view():
            index = list(tile) + [slice(None)] * (self.dims - len(tile))
            for axis in self.order[:at]:
                index[axis] = self.mine(axis)
            axis = self.order[at]
            index[axis] = lax.rem(self.place.zh + k, self.place.far) if axis == ZH else 1 - self.mine(axis)
            return self.total.at[tuple(index)]

        return view

    def start(self, at):
        for copy in self.stages[at]:
            copy.start()

    def value(self, at, free):
        axis = self.order[at]
        later = sorted(self.order[at + 1 :])
        index = [None] * self.dims
        for done in self.order[: at + 1]:
            index[done] = self.mine(done)
        for d, i in zip(later, free):
            index[d] = i
        got = [self.got[at].at[k] for k in range(self.place.far - 1)] if axis == ZH else [self.got[at]]
        return tuple(index), [g[tuple(free)] if free else g[...] for g in got]

    def add(self, at):
        for copy in self.stages[at]:
            copy.got()
        later = sorted(self.order[at + 1 :])

        def one(free):
            index, got = self.value(at, free)
            if len(got) == 1:
                self.total[index] = self.total[index] + got[0]
            else:
                total = self.total[index].astype(F32)
                for g in got:
                    total = total + g.astype(F32)
                self.total[index] = total.astype(BF16)

        def over(dims, free):
            if not dims:
                one(free)
            elif dims[0] == ZH:

                @pl.loop(0, self.place.far)
                def _(z):
                    over(dims[1:], free + [z])

            else:
                for i in range(2):
                    over(dims[1:], free + [i])

        over(later, [])
        self.start(at + 1)

    def finish(self):
        at = len(self.order) - 1
        for copy in self.stages[at]:
            copy.got()
        index, got = self.value(at, [])
        total = self.total[index].astype(F32)
        for g in got:
            total = total + g.astype(F32)
        return total

    def sent(self):
        for stage in self.stages:
            for copy in stage:
                copy.sent()


def add_loop(target, other):
    inner = target.shape[1:-2]

    @pl.loop(0, target.shape[0])
    def _(z):
        for index in np.ndindex(*inner):
            target[(z, *index)] = target[(z, *index)] + other[(z, *index)]


class Shared:
    def __init__(self, place, copies, room, order, send, pair):
        self.place, self.room, self.from_pair = place, room, pair
        self.sum = Sum(place, copies, room.total, room.got, order)
        self.pair = copies.new(lambda: send, lambda: pair, place.to_core)
        self.swap = copies.new(lambda: room.last.at[1 - place.core], lambda: room.other, place.to_core)

    def enter(self):
        self.pair.got()
        add_loop(self.room.total, self.from_pair)
        self.sum.start(0)

    def last(self):
        total = self.sum.finish()
        rows = total.shape[0] // 2
        self.room.last[0] = total[:rows]
        self.room.last[1] = total[rows:]
        self.swap.start()

    def store(self, out, offset, half):
        self.swap.got()
        lanes = self.room.other.shape[1]
        mine, other = self.room.last[self.place.core], self.room.other[...]
        for which in range(2):
            at = slice(which * half + offset, which * half + offset + lanes)
            out[:, at] = jnp.where(self.place.core == which, mine, other)

    def sent(self):
        self.swap.sent()
        self.sum.sent()


class Tiled(Shared):
    def __init__(self, place, copies, room, order, stage, pair):
        self.place, self.room, self.from_pair = place, room, pair
        self.tiles = [tile_of_steps(place.far, t) for t in range(FF_STEPS)]
        self.sum = Sum(place, copies, room.total, room.got, order, self.tiles)
        self.pairs = [
            copies.new(
                (lambda t: lambda: stage.at[t % stage.shape[0]])(t), (lambda tile: lambda: pair.at[tile])(tile), place.to_core
            )
            for t, tile in enumerate(self.tiles)
        ]
        self.swap = copies.new(lambda: room.last.at[1 - place.core], lambda: room.other, place.to_core)

    def enter_tile(self, t):
        self.pairs[t].got()
        add_loop(self.room.total.at[self.tiles[t]], self.from_pair.at[self.tiles[t]])
        self.sum.stages[0][t].start()


FF_STEPS = 4


def tile_of_steps(far, t):
    return (t // 2, t % 2) if far == 2 else (slice(t * far // FF_STEPS, (t + 1) * far // FF_STEPS),)


def over_rows(left, right):
    return lax.dot_general(left, right, (((1,), (1,)), ((), ())), preferred_element_type=F32)


class Slots:
    def __init__(self, place, copies, room, sends, y_first, order):
        self.place, self.room, self.y_first = place, room, y_first
        self.pair = [copies.new((lambda j: lambda: sends.at[j])(j), (lambda j: lambda: room.pair.at[j])(j), place.to_core) for j in range(2)]
        self.own = Sum(place, copies, room.total.at[0], room.got, order)
        if y_first:
            self.across = copies.new(lambda: room.total.at[1], lambda: room.across, place.to_y)
        else:
            self.far = Sum(place, copies, room.total.at[1], room.far, order)
            self.across = copies.new(lambda: room.chunk, lambda: room.across, place.to_y)

    def enter(self, j):
        self.pair[j].got()
        add_loop(self.room.total.at[j], self.room.pair.at[j])
        if j == 1:
            if self.y_first:
                self.across.start()
            else:
                self.far.start(0)
        elif not self.y_first:
            self.own.start(0)

    def take(self):
        self.across.got()
        add_loop(self.room.total.at[0], self.room.across)
        self.own.start(0)

    def give(self):
        self.room.chunk[...] = self.far.finish().astype(BF16)
        self.across.start()

    def finish(self):
        total = self.own.finish()
        if not self.y_first:
            self.across.got()
            total = total + self.room.across[...].astype(F32)
        return total

    def sent(self):
        self.own.sent()
        self.across.sent()
        if not self.y_first:
            self.far.sent()


SHARED_ORDER = dict(
    gate=(Y, X, Z0, ZH), up=(X, Z0, Y, ZH), down_a=(Y, X, Z0, ZH), down_b=(Z0, X, Y, ZH),
    out_two=(X, Z0, ZH, Y), out_one=(Y, X, Z0, ZH),
)
SLOT_ORDER = dict(
    kv_two=(True, (X, Z0, ZH)), q_two=(True, (X, Z0, ZH)), kv_one=(False, (X, Z0, ZH)), q_one=(True, (Z0, X, ZH))
)
KV = slice(0, 2 * GROUP)
QS = slice(2 * GROUP, 3 * GROUP)


def packed(share):
    return share % 32 == 0


def query_shape(share):
    return (share + share // 2, 128) if packed(share) else (share, GROUP)


def put_query(ref, total):
    share = ref.shape[0]
    if not packed(share):
        ref[...] = total
        return
    ref[:, :128] = total[:share]
    ref[: share // 2, 128:] = total[share:, :64]
    ref[share // 2 :, 128:] = total[share:, 64:]


def put_heads(ref, kv):
    key_out, value_out = ref
    key_out[:, :128] = kv[:, :128]
    key_out[:, 128:] = kv[:, 256:320]
    value_out[:, :128] = kv[:, 128:256]
    value_out[:, 128:] = kv[:, 320:384]


def backward_kernel(depth, ins, outs, r):
    place = Place(depth)
    step = pl.program_id(0)
    core = place.core
    copies = Copies(r.send, r.recv)
    segs = Tiles(place, ins.segs)

    parities, downs = r.gate_stage.shape[0], r.down_stage.shape[0]
    down_stages = [r.down_stage.at[t % downs] for t in range(2)]
    stages = dict(gate=r.gate_stage, up=r.up_stage, down_a=down_stages[0], down_b=down_stages[1])
    shared = Named({
        name: (Tiled if name in ("gate", "up") else Shared)(
            place, copies, getattr(r, name), order, stages.get(name, r.out_send), getattr(r.pairs, name, r.out_pair)
        )
        for name, order in SHARED_ORDER.items()
    })
    slots = Named({
        name: Slots(place, copies, getattr(r, name), r.kv_send if name.startswith("kv") else r.q_send, *way)
        for name, way in SLOT_ORDER.items()
    })
    layer_swap = copies.new(lambda: r.block.at[1 - core], lambda: outs.layer.at[core], place.to_core)
    memory_swap = copies.new(lambda: r.block.at[1 - core], lambda: outs.memory.at[core], place.to_core)
    tokens_swap = copies.new(lambda: r.block.at[1 - core], lambda: outs.tokens.at[core], place.to_core)
    gain_copies = [
        copies.new(lambda: r.gains, (lambda k: lambda: r.gains_got.at[k])(k), d)
        for k, d in enumerate([place.to_core, place.to_y, place.to_x] + place.to_z)
    ]
    bias_copies = [
        copies.new((lambda s: lambda: r.bias.at[s])(s), (lambda k: lambda: r.bias_got.at[k])(k), d)
        for k, (s, d) in enumerate(
            zip([1, 3, 2, 0] + [0] * (depth - 1), [place.to_core, place.to_core, place.to_y, place.to_x] + place.to_z)
        )
    ]
    assert copies.count == r.send.shape[0], copies.count

    loads = []

    def load(source, target):
        loads.append(pltpu.make_async_copy(source, target, r.load.at[len(loads)]))
        return loads[-1]

    i = ins.loaded
    second, wo_two, ctx_two = load(i.second, r.hidden), load(i.wo_two, r.wo), load(i.ctx_two, r.ctx)
    cots = [load(i.cot.at[pl.ds(half * HALF, HALF)], r.block.at[half]) for half in range(2)]
    n_two, mem, first, tok = load(i.n_two, r.n), load(i.mem, r.mem), load(i.first, r.hidden), load(i.tok, r.hidden)
    wo_one, ctx_one, n_one = load(i.wo_one, r.wo), load(i.ctx_one, r.ctx), load(i.n_one, r.n)
    layer_put = load(r.block.at[core], outs.layer.at[core])
    memory_put = load(r.block.at[core], outs.memory.at[core])
    tokens_put = load(r.block.at[core], outs.tokens.at[core])

    def out_products(unit, context, branch):
        lanes = context.shape[0] // 2
        for which, target in ((1 - core, r.out_send), (core, unit.room.total)):
            side = jnp.transpose(context[pl.ds(pl.multiple_of(which * lanes, 16), lanes), :])
            per = branch.shape[0] // 2
            for part in range(2):
                product = dot(branch[part * per : (part + 1) * per, :], side).astype(BF16)
                rows = target.shape[4]
                for piece in range(per // rows):
                    at = part * (per // rows) + piece
                    to = (at // 8, (at // 4) % 2, (at // 2) % 2, at % 2)
                    target[to] = product[piece * rows : (piece + 1) * rows]
            if which is not core:
                unit.pair.start()

    def weight_products(target, left, lanes):
        rows = left.shape[0] // (2 * depth)
        per = left.shape[0] // 2
        for part in range(2):
            product = dot(left[part * per : (part + 1) * per, :], r.dqkv[:, lanes]).astype(BF16)
            for piece in range(per // rows):
                at = part * (per // rows) + piece
                to = (at // 4, (at // 2) % 2, at % 2)
                share = product[piece * rows : (piece + 1) * rows]
                if target.shape[-1] == share.shape[1]:
                    target[to] = share
                else:
                    target[(*to, slice(0, rows))] = share[:, :128]
                    rest = share[:, 128:]
                    target[(*to, slice(rows, rows + rows // 2))] = jnp.concatenate((rest[: rows // 2], rest[rows // 2 :]), axis=1)

    def add_rows(target, lanes, weights, fresh):
        for part in range(2):
            rows = slice(part * HALF, (part + 1) * HALF)
            product = dot(r.dqkv[rows, lanes], weights)

            @pl.when(fresh)
            def _():
                target[rows, :] = product

            @pl.when(jnp.logical_not(fresh))
            def _():
                target[rows, :] = target[rows, :] + product

    def norm_back(hidden, gain, incoming, onto, gain_row, branch):
        total = jnp.zeros((1, hidden.shape[1]), F32)
        for part in range(4):
            rows = slice(part * TILE, (part + 1) * TILE)
            h = hidden[rows, :].astype(F32)
            e = incoming[rows, :]
            scale = lax.rsqrt(jnp.mean(h * h, axis=-1, keepdims=True) + NORM_EPS)
            weighted = e * row_of(gain)
            inner = jnp.mean(weighted * h, axis=-1, keepdims=True)
            result = onto[rows, :] + weighted * scale - h * (scale * scale * scale * inner)
            total = total + jnp.sum(e * h * scale, axis=0, keepdims=True)
            if branch is None:
                r.block[part // 2, (part % 2) * TILE : (part % 2 + 1) * TILE, :] = result.astype(BF16)
            else:
                onto[rows, :] = result
                branch[:, rows] = jnp.transpose(result.astype(BF16))
        r.gains[gain_row : gain_row + 1, :] = total

    plan = {}

    def at(point, *tasks):
        plan.setdefault(point, []).extend(tasks)

    sh, sl = shared, slots
    def when_core(which, *tasks):
        def run():
            for task in tasks:
                task()

        return lambda: pl.when(core == which)(run)

    for t in range(FF_STEPS):
        at((t, 4), sh.gate.pairs[t].start, sh.up.pairs[t].start)
        if t < FF_STEPS - 1:
            at((t + 1, 1), lambda t=t: sh.gate.enter_tile(t), lambda t=t: sh.up.enter_tile(t))
        at((t, 5), when_core(1 - t // 2, (sh.down_a, sh.down_b)[t % 2].pair.start))
    at((2, 2), when_core(0, sh.down_a.enter))
    at((2, 3), when_core(0, sh.down_b.enter))
    at((4, 0), when_core(1, sh.down_a.enter, sh.down_b.enter))
    at((4, 1), sh.out_two.enter)
    at((4, 3), sl.kv_two.pair[1].start, sl.q_two.pair[1].start)
    at((5, 0), lambda: sh.gate.sum.add(0), lambda: sh.up.sum.add(0))
    at((5, 3), lambda: sl.kv_two.enter(1), lambda: sl.q_two.enter(1))
    at((6, 0), lambda: sh.out_two.sum.add(0), lambda: sh.down_b.sum.add(0))
    at((6, 1), lambda: sh.down_a.sum.add(0))
    at((6, 3), sl.kv_two.pair[0].start, sl.q_two.pair[0].start)
    at((7, 0), lambda: sh.up.sum.add(1), lambda: sh.gate.sum.add(1))
    at((7, 2), lambda: sh.out_two.sum.add(1))
    at((7, 3), lambda: sl.kv_two.enter(0), lambda: sl.q_two.enter(0), lambda: sh.down_b.sum.add(1))
    at((7, 4), sl.kv_two.take, lambda: sh.gate.sum.add(2), lambda: sh.down_a.sum.add(1))
    at((8, 0), lambda: sh.out_two.sum.add(2), sh.out_one.enter)
    at((8, 2), sl.q_two.take, lambda: sh.down_a.sum.add(2))
    at((8, 3), sl.kv_one.pair[1].start, sl.q_one.pair[1].start)
    at((9, 0), lambda: sl.kv_two.own.add(0), sh.gate.last)
    at((9, 1), lambda: sh.up.sum.add(2))
    at((9, 2), lambda: sl.q_two.own.add(0))
    at((9, 3), lambda: sl.kv_one.enter(1), lambda: sl.q_one.enter(1), lambda: sh.down_b.sum.add(2), sh.down_a.last)
    at((10, 0), lambda: sl.kv_two.own.add(1), sh.out_two.last)
    at((10, 1), lambda: sh.out_one.sum.add(0), lambda: sl.q_two.own.add(1))
    at((10, 2), sh.up.last, sh.down_b.last)
    at((10, 3), sl.kv_one.pair[0].start, sl.q_one.pair[0].start)
    at((11, 1), lambda: sl.kv_one.far.add(0))
    at((11, 3), lambda: sl.kv_one.enter(0), lambda: sl.q_one.enter(0), lambda: sh.out_one.sum.add(1))

    def tick(steps, index):
        for k in steps:
            if (k, index) in plan:

                def run(tasks=plan[k, index]):
                    for task in tasks:
                        task()

                pl.when(step == k)(run)

    @pl.when(step == 0)
    def _():
        barrier = pltpu.get_barrier_semaphore()
        for device in place.everyone():
            pl.semaphore_signal(barrier, inc=1, device_id=device, device_id_type=MESH)
        for copy in [second] + cots + [wo_two, ctx_two, n_two, mem]:
            copy.start()
        r.gains[...] = jnp.zeros_like(r.gains)
        second.wait()
        for part in range(4):
            rows = slice(part * TILE, (part + 1) * TILE)
            h = r.hidden[rows, :]
            scale = lax.rsqrt(jnp.mean(h * h, axis=-1, keepdims=True) + NORM_EPS)
            r.normed[rows, :] = (h * scale * row_of(ins.ff_gain)).astype(BF16)
            r.acc_a[rows, :] = h
            r.acc_b[rows, :] = jnp.zeros_like(h)
        for part in range(4):
            if part % 2 == 0:
                cots[part // 2].wait()
            rows = slice(part * TILE, (part + 1) * TILE)
            r.branch[:, rows] = jnp.transpose(r.block[part // 2, (part % 2) * TILE : (part % 2 + 1) * TILE, :])
        pl.semaphore_wait(barrier, len(place.everyone()))

    for t in range(parities, FF_STEPS):

        @pl.when(step == t)
        def _(t=t):
            sh.gate.pairs[t - parities].sent()
            sh.up.pairs[t - parities].sent()

    @pl.when(step < FF_STEPS)
    def _():
        root = np.float32(np.sqrt(2.0 / np.pi))
        model = r.normed.shape[1]
        for part in range(4):
            rows = slice(part * TILE, (part + 1) * TILE)
            normed = r.normed[rows, :]
            gate, up = dot(normed, ins.ff_gate[...]), dot(normed, ins.ff_up[...])
            grad = over_rows(r.block[part // 2, (part % 2) * TILE : (part % 2 + 1) * TILE, :], ins.ff_down[...])
            square = gate * gate
            half = 0.5 + 0.5 * jnp.tanh(gate * (root + (root * 0.044715) * square))
            gelu = gate * half
            slope = half + gelu * (2.0 - 2.0 * half) * (root + (3.0 * 0.044715 * root) * square)
            activation = (gelu * up).astype(BF16)
            grad_gate = (grad * up * slope).astype(BF16)
            grad_up = (grad * gelu).astype(BF16)
            r.mask[rows, :] = activation
            r.grad_gate[:, rows] = jnp.transpose(grad_gate)
            r.grad_up[:, rows] = jnp.transpose(grad_up)
            r.acc_a[rows, :] = r.acc_a[rows, :] + dot(activation, ins.ff_down[...])
            r.acc_b[rows, :] = r.acc_b[rows, :] + over_rows(grad_gate, ins.ff_gate[...]) + over_rows(grad_up, ins.ff_up[...])
            tick(range(FF_STEPS), part)
        lanes = model // 2
        for which, keep in ((1 - core, False), (core, True)):
            right = r.normed[:, pl.ds(pl.multiple_of(which * lanes, 128), lanes)]
            for grads, total, stage in ((r.grad_gate, r.gate.total, r.gate_stage), (r.grad_up, r.up.total, r.up_stage)):
                product = dot(grads[...], right).astype(BF16)
                rows = total.shape[4]
                for piece in range(product.shape[0] // rows):
                    inner = ((piece // 4) % 2, (piece // 2) % 2, piece % 2)
                    share = product[piece * rows : (piece + 1) * rows]
                    if place.far == 2:
                        head = (step // 2, step % 2) if keep else (step % parities,)
                        inner = inner[1:]
                    else:
                        head = (step * (place.far // FF_STEPS) + piece // 8,) if keep else (step % parities, piece // 8)
                    (total if keep else stage)[(*head, *inner)] = share
            if not keep:
                tick(range(FF_STEPS), 4)
        per = model // 2
        for part in range(2):
            product = dot(r.branch[part * per : (part + 1) * per, :], r.mask[...]).astype(BF16)
            for t in range(FF_STEPS):
                total = (r.down_a, r.down_b)[t % 2].total
                for target, mine in ((total, t // 2), (down_stages[t % 2], 1 - t // 2)):

                    @pl.when(jnp.logical_and(step == t, core == mine))
                    def _(target=target, product=product, part=part, t=t, mine=mine):
                        if downs == 1 and t % 2 == 1 and part == 0 and mine != t // 2:
                            sh.down_a.pair.sent()
                        rows = target.shape[4]
                        for piece in range(per // rows):
                            to = part * (per // rows) + piece
                            to = (to // 8, (to // 4) % 2, (to // 2) % 2, to % 2)
                            target[to] = product[piece * rows : (piece + 1) * rows]

        tick(range(FF_STEPS), 5)

    @pl.when(step == FF_STEPS - 1)
    def _():
        total = jnp.zeros((1, r.hidden.shape[1]), F32)
        for part in range(4):
            rows = slice(part * TILE, (part + 1) * TILE)
            block_rows = (part // 2, slice((part % 2) * TILE, (part % 2 + 1) * TILE))
            h, e = r.hidden[rows, :], r.acc_b[rows, :]
            scale = lax.rsqrt(jnp.mean(h * h, axis=-1, keepdims=True) + NORM_EPS)
            weighted = e * row_of(ins.ff_gain)
            inner = jnp.mean(weighted * h, axis=-1, keepdims=True)
            result = r.block[block_rows].astype(F32) + weighted * scale - h * (scale * scale * scale * inner)
            total = total + jnp.sum(e * h * scale, axis=0, keepdims=True)
            r.after[rows, :] = result
            r.branch[:, rows] = jnp.transpose(result.astype(BF16))
            r.block[block_rows] = r.acc_a[rows, :].astype(BF16)
        r.gains[2:3, :] = total
        layer_swap.start()
        layer_put.start()
        sh.gate.enter_tile(FF_STEPS - 1)
        sh.up.enter_tile(FF_STEPS - 1)
        key_mask(segs, key_segments(place, ins.memsegs), r.mask)
        first.start()
        for copy in (wo_two, ctx_two, n_two, mem):
            copy.wait()
        out_products(sh.out_two, r.ctx, r.branch)

    slot = 3 - step % 4
    odd = slot % 2 == 1
    rows_at = pl.ds(pl.multiple_of(place.group(slot) * GROUP, 16), GROUP)

    def slot_products(kv, q, kv_left, q_left):
        @pl.when(odd)
        def _():
            weight_products(r.kv_send.at[slot // 2], kv_left, KV)
            weight_products(r.q_send.at[slot // 2], q_left, QS)

        @pl.when(jnp.logical_not(odd))
        def _():
            weight_products(kv.room.total.at[slot // 2], kv_left, KV)
            weight_products(q.room.total.at[slot // 2], q_left, QS)

    @pl.when(step // 4 == 1)
    def _():
        r.do[...] = dot(r.wo[rows_at, :], r.branch[...]).astype(BF16)
        kv, q, lse = ins.kv_two, ins.q_two, ins.lse_two
        context = r.ctx.at[rows_at, :]
        read = Read(
            lambda: kv[0], lambda h, end: kv[0, rows_of(KEY_AT[h]), :end], lambda rows: q[0, rows, :],
            lambda rows: r.do[rows, :], lambda rows: context[rows, :], lambda h, cut: lse[0, h : h + 1, cut],
        )

        def tile_of(scores, index, kt, qt):
            return scores + r.mask[kt * TILE : (kt + 1) * TILE, qt * TILE : (qt + 1) * TILE].astype(F32)

        attention_back(read, tile_of, False, lambda *a: None, r.dq, r.dqkv, lambda h: tick(range(4, 8), h))
        slot_products(sl.kv_two, sl.q_two, r.mem, r.n)
        tick(range(4, 8), 3)
        add_rows(r.acc_b, KV, ins.wt_two[0, KV, :], step == 4)
        add_rows(r.acc_a, QS, ins.wt_two[0, QS, :], step == 4)

    @pl.when(step == 7)
    def _():
        for copy in (wo_one, ctx_one, n_one):
            copy.start()
        first.wait()
        layer_swap.sent()
        layer_put.wait()
        norm_back(r.hidden, ins.cross_gain, r.acc_a, r.after, 1, r.branch)
        tok.start()
        for part in range(4):
            rows = slice(part * TILE, (part + 1) * TILE)
            r.block[part // 2, (part % 2) * TILE : (part % 2 + 1) * TILE, :] = r.acc_b[rows, :].astype(BF16)
        memory_swap.start()
        memory_put.start()
        for copy in (wo_one, ctx_one, n_one):
            copy.wait()
        sh.out_two.pair.sent()
        out_products(sh.out_one, r.ctx, r.branch)
        for task in plan[7, 4]:
            task()

    @pl.when(step >= 8)
    def _():
        r.do[...] = dot(r.wo[rows_at, :], r.branch[...]).astype(BF16)
        qkv, lse = ins.qkv_one, ins.lse_one
        context = r.ctx.at[rows_at, :]
        read = Read(
            lambda: qkv[0, KV, :], lambda h, end: qkv[0, rows_of(KEY_AT[h]), :end],
            lambda rows: qkv[0, QUERY_START + rows.start : QUERY_START + rows.stop, :],
            lambda rows: r.do[rows, :], lambda rows: context[rows, :], lambda h, cut: lse[0, h : h + 1, cut],
        )
        table, one_hot = ins.table[0], ins.hot[...]
        tiles = [bias_tiles(table, index, one_hot) for index in range(HEADS)]
        kept = {}

        def note(index, kt, qt, ds):
            key = (index, min(qt - kt, 2))
            kept[key] = kept[key] + ds if key in kept else ds

        attention_back(
            read, lambda scores, index, kt, qt: self_tile(scores, kt, qt, tiles[index], segs, 0), True, note,
            r.dq, r.dqkv, lambda h: tick(range(8, 12), h),
        )
        key = lax.broadcasted_iota(jnp.int32, (TILE, TILE), 0)
        query = lax.broadcasted_iota(jnp.int32, (TILE, TILE), 1)
        flip = (key + query == TILE - 1).astype(F32)
        row = lax.broadcasted_iota(jnp.int32, (8, 2 * TILE), 0)
        lane = lax.broadcasted_iota(jnp.int32, (8, 2 * TILE), 1)
        by_distance = jnp.zeros((8, 2 * TILE), F32)
        for index in range(HEADS):
            both = jnp.concatenate((kept[index, 0], kept[index, 1]), axis=1)
            both = jnp.dot(flip, both, precision=lax.Precision.HIGHEST, preferred_element_type=F32)
            turned = jnp.sum(pltpu.roll(both, TILE + 1, 1, stride=1, stride_axis=0), axis=0, keepdims=True)
            far_total = jnp.sum(jnp.sum(kept[index, 2], axis=0, keepdims=True), axis=1, keepdims=True)
            turned = turned + jnp.where(lane[:1] == 2 * TILE - 1, far_total, 0.0)
            by_distance = by_distance + jnp.where(row == index, turned, 0.0)
        r.bias[slot] = lax.dot_general(
            by_distance, one_hot, (((1,), (1,)), ((), ())), precision=lax.Precision.HIGHEST, preferred_element_type=F32
        )
        for k, j in ((8, 1), (10, 0)):

            @pl.when(step == k)
            def _(j=j):
                sl.kv_two.pair[j].sent()
                sl.q_two.pair[j].sent()

        slot_products(sl.kv_one, sl.q_one, r.n, r.n)
        tick(range(8, 12), 3)
        add_rows(r.acc_a, slice(0, 3 * GROUP), ins.wt_one[0], step == 8)

    @pl.when(step == 11)
    def _():
        gains, bias = r.gains, r.bias
        memory_swap.sent()
        memory_put.wait()
        tok.wait()
        norm_back(r.hidden, ins.self_gain, r.acc_a, r.after, 0, None)
        tokens_swap.start()
        tokens_put.start()
        gain_copies[0].start()
        bias_copies[0].start()
        bias_copies[1].start()
        sl.q_one.take()
        sl.kv_one.far.add(1)
        gain_copies[0].done()
        gains[...] = gains[...] + r.gains_got[0]
        bias_copies[0].done()
        bias_copies[1].done()
        bias[0] = bias[0] + r.bias_got[0]
        bias[2] = bias[2] + r.bias_got[1]
        gain_copies[1].start()
        bias_copies[2].start()
        sl.q_one.own.add(0)
        sh.out_one.sum.add(2)
        sl.kv_one.own.add(0)
        put_heads((outs.wk_two, outs.wv_two), sl.kv_two.finish())
        put_query(outs.wq_two, sl.q_two.finish())
        gain_copies[1].done()
        gains[...] = gains[...] + r.gains_got[1]
        bias_copies[2].done()
        bias[0] = bias[0] + r.bias_got[2]
        gain_copies[2].start()
        bias_copies[3].start()
        sl.kv_one.give()
        sl.q_one.own.add(1)
        sh.out_one.last()
        gain_copies[2].done()
        gains[...] = gains[...] + r.gains_got[2]
        bias_copies[3].done()
        bias[0] = bias[0] + r.bias_got[3]
        for k in range(depth - 1):
            gain_copies[3 + k].start()
            bias_copies[4 + k].start()
        sl.kv_one.own.add(1)
        sh.up.store(outs.up, 0, outs.up.shape[1] // 2)
        sh.down_a.store(outs.down, 0, outs.down.shape[1] // 2)
        sh.down_b.store(outs.down, outs.down.shape[1] // 4, outs.down.shape[1] // 2)
        sh.gate.store(outs.gate, 0, outs.gate.shape[1] // 2)
        sh.out_two.store(outs.out_two, 0, outs.out_two.shape[1] // 2)
        sh.out_one.store(outs.out_one, 0, outs.out_one.shape[1] // 2)
        gain_total, bias_total = gains[...], bias[0]
        for k in range(depth - 1):
            gain_copies[3 + k].done()
            bias_copies[4 + k].done()
            gain_total = gain_total + r.gains_got[3 + k]
            bias_total = bias_total + r.bias_got[4 + k]
        outs.gains[...] = gain_total
        outs.bias[...] = bias_total
        put_query(outs.wq_one, sl.q_one.finish())
        put_heads((outs.wk_one, outs.wv_one), sl.kv_one.finish())
        for name in SHARED_ORDER:
            unit = getattr(shared, name)
            unit.sent()
            if name in ("gate", "up"):
                for copy in unit.pairs[-parities:]:
                    copy.sent()
            elif unit is not sh.out_two and (unit is not sh.down_a or downs == 2):
                unit.pair.sent()
        for name in SLOT_ORDER:
            getattr(slots, name).sent()
        for j in range(2):
            sl.kv_one.pair[j].sent()
            sl.q_one.pair[j].sent()
        layer_swap.got()
        memory_swap.got()
        tokens_swap.done()
        tokens_put.wait()


def backward_call(batch_size, operands):
    depth = batch_size // 2
    tight = depth > 4
    once = dict(pipeline_mode=pl.Buffered(1)) if tight else {}
    tok = operands["loaded"]["tok"]
    model = tok.shape[1]
    share = model // batch_size
    anywhere = pl.BlockSpec(memory_space=pl.ANY)

    def fixed(shape):
        return pl.BlockSpec(shape, lambda t: (0,) * len(shape))

    def phase(t):
        c = t // 4
        return (1 - c) * (2 - c) // 2, c * (2 - c), c * (c - 1) // 2

    def early(array):
        def at(t):
            _, cross, own = phase(t)
            return (3 - cross * (t % 4) - 3 * own, 0, 0)

        return pl.BlockSpec((1,) + array.shape[1:], at, **once)

    def late(array):
        return pl.BlockSpec((1,) + array.shape[1:], lambda t: (3 - phase(t)[2] * (t % 4), 0, 0))

    def tile(t):
        return 3 - phase(t)[0] * (3 - t % 4)

    def wide_tile(array):
        return pl.BlockSpec((array.shape[0], array.shape[1] // FF_STEPS), lambda t: (0, tile(t)), **once)

    def deep_tile(array):
        return pl.BlockSpec((array.shape[0] // FF_STEPS, array.shape[1]), lambda t: (tile(t), 0), **once)

    kinds = dict(
        segs=lambda a: pl.BlockSpec(memory_space=pltpu.SMEM), kv_two=early, q_two=early, lse_two=early, wt_two=early,
        qkv_one=late, lse_one=late, wt_one=late, table=late, loaded=lambda a: anywhere,
        ff_gate=wide_tile, ff_up=wide_tile, ff_down=deep_tile,
    )
    in_specs = {
        name: jax.tree.map(kinds.get(name, lambda a: fixed(a.shape)), value) for name, value in operands.items()
    }
    columns = operands["ff_gate"].shape[1]
    made = ("gate", "up", "down_a", "down_b")
    shapes = dict(gate=(columns // (4 * depth), model // 2), down_a=(model // (4 * depth), columns // 4))
    shapes.update(up=shapes["gate"], down_b=shapes["down_a"])
    shapes.update(out_two=(model // (4 * depth), model // 2), out_one=(model // (4 * depth), model // 2))
    tile_room = (2, 2, 2) if depth == 4 else (1, depth // 8, 2, 2, 2)
    block = jax.ShapeDtypeStruct((2, HALF, model), BF16)

    def wide(rows, columns):
        return jax.ShapeDtypeStruct((rows, columns), F32)

    head = wide(share, GROUP)
    outs = dict(
        layer=block, memory=block, tokens=block,
        gate=wide(shapes["gate"][0] // 2, 2 * shapes["gate"][1]), up=wide(shapes["up"][0] // 2, 2 * shapes["up"][1]),
        down=wide(shapes["down_a"][0] // 2, 4 * shapes["down_a"][1]),
        out_two=wide(shapes["out_two"][0] // 2, model), out_one=wide(shapes["out_one"][0] // 2, model),
        wq_two=head, wk_two=head, wv_two=head, wq_one=head, wk_one=head, wv_one=head,
        gains=wide(8, model), bias=wide(8, TILE),
    )
    out_specs = {name: anywhere if s is block else fixed(s.shape) for name, s in outs.items()}

    def room(*shape, kind=BF16):
        return pltpu.VMEM(shape, kind)

    scratch = {}
    for name, order in SHARED_ORDER.items():
        rows, lanes = shapes[name]
        scratch[name] = dict(
            total=room(depth // 2, 2, 2, 2, rows, lanes),
            got=[room(*s) for s in Sum.rooms(depth // 2, 4, order, rows, lanes)],
            last=room(2, rows // 2, lanes, kind=F32), other=room(rows // 2, lanes, kind=F32),
        )
    for name, (y_first, order) in SLOT_ORDER.items():
        piece = (share, 2 * GROUP) if name.startswith("kv") else query_shape(share)
        got = [room(*s) for s in Sum.rooms(depth // 2, 3, order, *piece)]
        both = room(2, depth // 2, 2, 2, *piece)
        scratch[name] = dict(total=both, pair=both, got=got)
        if y_first:
            scratch[name].update(across=room(depth // 2, 2, 2, *piece))
        else:
            scratch[name].update(across=room(*piece), chunk=room(*piece), far=list(got))
    scratch.update(
        pairs={name: room(depth // 2, 2, 2, 2, *shapes[name]) for name in made},
        gate_stage=room(*tile_room, *shapes["gate"]), up_stage=room(*tile_room, *shapes["up"]),
        down_stage=room(1 if tight else 2, depth // 2, 2, 2, 2, *shapes["down_a"]), normed=room(BLOCK, model),
        grad_gate=room(columns // FF_STEPS, BLOCK),
        grad_up=room(columns // FF_STEPS, BLOCK),
        out_send=room(depth // 2, 2, 2, 2, *shapes["out_one"]), out_pair=room(depth // 2, 2, 2, 2, *shapes["out_one"]), kv_send=room(2, depth // 2, 2, 2, share, 2 * GROUP),
        q_send=room(2, depth // 2, 2, 2, *query_shape(share)), block=room(2, HALF, model), branch=room(model, BLOCK),
        acc_a=room(BLOCK, model, kind=F32), acc_b=room(BLOCK, model, kind=F32), dqkv=room(BLOCK, 3 * GROUP),
        dq=room(GROUP, BLOCK), do=room(GROUP, BLOCK), mask=room(BLOCK, columns // FF_STEPS), gains=room(8, model, kind=F32),
        gains_got=room(depth + 2, 8, model, kind=F32), bias=room(4, 8, TILE, kind=F32),
        bias_got=room(depth + 3, 8, TILE, kind=F32),
        after=room(BLOCK, model, kind=F32), hidden=room(BLOCK, model, kind=F32),
        wo=room(model, model), ctx=room(model, BLOCK), n=room(model, BLOCK), mem=room(model, BLOCK),
    )
    z = depth - 1
    copies = 3 + (3 + z) + (4 + z)
    copies += sum(2 + Sum.count(depth // 2, order) for order in SHARED_ORDER.values()) + 2 * 2 * (FF_STEPS - 1)
    copies += sum(3 + (1 if y_first else 2) * Sum.count(depth // 2, order) for y_first, order in SLOT_ORDER.values())
    scratch.update(send=pltpu.SemaphoreType.DMA((copies,)), recv=pltpu.SemaphoreType.DMA((copies,)))
    scratch.update(load=pltpu.SemaphoreType.DMA((18,)))

    arrays, in_tree = jax.tree.flatten(operands)
    out_shapes, out_tree = jax.tree.flatten(outs)
    rooms, room_tree = jax.tree.flatten(scratch)

    def kernel(*refs):
        a, b = len(arrays), len(arrays) + len(out_shapes)
        backward_kernel(
            depth, Named(jax.tree.unflatten(in_tree, refs[:a])), Named(jax.tree.unflatten(out_tree, refs[a:b])),
            Named(jax.tree.unflatten(room_tree, refs[b:])),
        )

    results = pl.pallas_call(
        kernel,
        grid=(12,),
        in_specs=jax.tree.leaves(in_specs),
        out_specs=jax.tree.leaves(out_specs),
        out_shape=out_shapes,
        scratch_shapes=rooms,
        compiler_params=pltpu.CompilerParams(
            collective_id=0, has_side_effects=True, vmem_limit_bytes=67_000_000, dimension_semantics=("arbitrary",)
        ),
        cost_estimate=pl.CostEstimate(flops=20_000_000_000, bytes_accessed=40_000_000, transcendentals=6_000_000),
    )(*arrays)
    return Named(jax.tree.unflatten(out_tree, results))


PIECES = 3


class Gather:
    def __init__(self, place, copies, slots):
        self.slots = slots
        half = slots.shape[1] // 2
        size = half // PIECES
        self.core = copies.new(lambda: slots.at[0], lambda: slots.at[1], place.to_core)

        def rows(side, j):
            return pl.ds(pl.multiple_of(side * half + j * size, 32), size)

        def make(source, target, side, device):
            return [
                copies.new(
                    (lambda j: lambda: slots.at[source, rows(side, j)])(j),
                    (lambda j: lambda: slots.at[target, rows(side, j)])(j), device,
                )
                for j in range(PIECES)
            ]

        self.over_y = make(0, 2, place.x, place.to_y)
        self.over_x = make(2, 2, place.x, place.to_x)
        self.near = make(2, 3, place.x, place.to_core)
        self.far = make(2, 3, 1 - place.x, place.to_core)

    def start(self):
        for copy in self.over_y:
            copy.start()
        self.core.start()

    def pass_y(self, j):
        self.over_y[j].got()
        self.over_x[j].start()
        self.near[j].start()

    def pass_x(self, j):
        self.over_x[j].got()
        self.far[j].start()

    def ready(self):
        for copy in self.near + self.far:
            copy.got()

    def sent(self):
        for copy in [self.core] + self.over_y + self.over_x + self.near + self.far:
            copy.sent()


def forward_kernel(ins, outs, r):
    place = Place(2)
    step = pl.program_id(0)
    core = place.core
    copies = Copies(r.send, r.recv)
    segs = Tiles(place, ins.segs)
    gather_one = Gather(place, copies, r.wt_one)
    gather_two = Gather(place, copies, r.wt_two)
    tables = [
        copies.new((lambda a: lambda: r.table.at[a])(a), (lambda b: lambda: r.table.at[b])(b), d)
        for a, b, d in ((0, 1, place.to_core), (0, 2, place.to_y), (2, 3, place.to_core))
    ]
    swaps = {}
    tok_swap = copies.new(lambda: ins.tokens.at[1 - core], lambda: r.tok_in.at[core], place.to_core)
    mem_swap = copies.new(lambda: ins.memory.at[1 - core], lambda: r.mem_in.at[core], place.to_core)
    cot_swap = copies.new(lambda: ins.cotangent.at[1 - core], lambda: r.cot_in.at[core], place.to_core)
    assert copies.count == r.send.shape[0], copies.count
    count = [0]

    def load(source, target):
        count[0] += 1
        return pltpu.make_async_copy(source, target, r.load.at[count[0] - 1])

    tok_own = load(ins.tokens.at[core], r.tok_in.at[core])
    mem_own = load(ins.memory.at[core], r.mem_in.at[core])
    cot_own = load(ins.cotangent.at[core], r.cot_in.at[core])

    def load_group(key, value, query, slots):
        return [
            load(source.at[pl.ds(at, size)], slots.at[0, pl.ds(to, size)])
            for source, at, to, size in (
                (key, 0, 0, 128), (value, 0, 128, 128), (key, 128, 256, 64), (value, 128, 320, 64), (query, 0, 384, GROUP)
            )
        ]

    raw_one = load_group(ins.self_key, ins.self_value, ins.self_query, r.wt_one)
    raw_two = load_group(ins.cross_key, ins.cross_value, ins.cross_query, r.wt_two)
    out_one, out_two = load(ins.self_out, r.wo_one), load(ins.cross_out, r.wo_two)
    puts = Named({name: load(getattr(r, name), getattr(outs, name)) for name in vars(outs)})


    def normed(hidden, gain, target):
        for part in range(4):
            rows = slice(part * TILE, (part + 1) * TILE)
            h = hidden[rows, :]
            scale = lax.rsqrt(jnp.mean(h * h, axis=-1, keepdims=True) + NORM_EPS)
            target[:, rows] = jnp.transpose((h * scale * row_of(gain)).astype(BF16))

    def project_out(context, weights, base, target):
        for part in range(2):
            rows = slice(part * HALF, (part + 1) * HALF)
            target[rows, :] = base[rows, :] + dot(jnp.transpose(context[:, rows]), weights[...])

    def cross_keys(slot):
        r.kv_two[slot] = dot(r.wt_two[slot, KV, :], r.mem[...]).astype(BF16)

    plan = {}

    def at(point, *tasks):
        plan.setdefault(point, []).extend(tasks)

    one, two = gather_one, gather_two
    at((0, 0), lambda: one.pass_y(1))
    at((0, 2), lambda: one.pass_y(2))
    at((1, 0), lambda: one.pass_x(0))
    at((1, 1), tables[1].got, tables[2].start)
    at((1, 2), lambda: one.pass_x(1))
    at((2, 0), lambda: two.pass_y(1))
    at((2, 2), lambda: two.pass_x(0))
    at((3, 0), lambda: two.pass_y(2))
    at((3, 2), lambda: two.pass_x(1))
    at((4, 1), lambda: two.pass_x(2))

    def tick(steps, index):
        for k in steps:
            if (k, index) in plan:

                def run(tasks=plan[k, index]):
                    for task in tasks:
                        task()

                pl.when(step == k)(run)

    @pl.when(step == 0)
    def _():
        barrier = pltpu.get_barrier_semaphore()
        for device in (place.to_core, place.to_y, place.to_x):
            pl.semaphore_signal(barrier, inc=1, device_id=device, device_id_type=MESH)
        for copy in raw_one + [tok_own] + raw_two + [mem_own, out_one, out_two, cot_own]:
            copy.start()
        r.table[0] = jnp.zeros_like(r.table[0])
        r.table[0, :HEADS, : ins.table.shape[1]] = ins.table[...]
        for copy in raw_one:
            copy.wait()
        pl.semaphore_wait(barrier, 3)
        tok_swap.start()
        tables[0].start()
        tables[1].start()
        gather_one.start()
        mem_swap.start()
        cot_swap.start()
        tok_own.wait()
        tok_swap.got()
        for half in range(2):
            r.tok[half * HALF : (half + 1) * HALF, :] = r.tok_in[half].astype(F32)
        puts.tok.start()
        one.pass_y(0)
        normed(r.tok, ins.self_gain, r.n_one)
        puts.n_one.start()
        for copy in raw_two:
            copy.wait()
        gather_two.start()

    @pl.when(step == 1)
    def _():
        gather_one.core.got()
        tables[0].got()

    @pl.when(step == 2)
    def _():
        mem_own.wait()
        mem_swap.got()
        for half in range(2):
            r.mem[:, half * HALF : (half + 1) * HALF] = jnp.transpose(r.mem_in[half])
        puts.mem.start()
        cot_own.wait()
        cot_swap.got()
        for half in range(2):
            r.cot[half * HALF : (half + 1) * HALF, :] = r.cot_in[half]
        puts.cot.start()
        gather_two.core.got()
        cross_keys(0)
        cross_keys(1)
        two.pass_y(0)
        one.pass_x(2)
        one.ready()
        puts.wt_one.start()
        tables[2].got()
        puts.table.start()

    slot = step % 4
    rows_at = pl.ds(pl.multiple_of(place.group(slot) * GROUP, 16), GROUP)

    @pl.when(step < 4)
    def _():
        r.qkv_one[slot] = dot(r.wt_one[slot], r.n_one[...]).astype(BF16)
        self_forward(
            r.qkv_one.at[slot, KV], r.qkv_one.at[slot, QS], r.table[slot], ins.hot[...], segs,
            r.ctx_one.at[rows_at], r.lse_one.at[slot], lambda h: tick(range(4), h),
        )

    @pl.when(step == 4)
    def _():
        puts.qkv_one.start()
        puts.ctx_one.start()
        puts.lse_one.start()
        out_one.wait()
        project_out(r.ctx_one, r.wo_one, r.tok, r.first)
        puts.first.start()
        normed(r.first, ins.cross_gain, r.n_two)
        puts.n_two.start()
        key_mask(segs, key_segments(place, ins.memsegs), r.mask)

    @pl.when(step == 6)
    def _():
        two.ready()
        puts.wt_two.start()

    @pl.when(step >= 4)
    def _():
        @pl.when(step >= 6)
        def _():
            cross_keys(slot)

        r.q_two[slot] = dot(r.wt_two[slot, QS, :], r.n_two[...]).astype(BF16)
        cross_forward(
            r.kv_two.at[slot], r.q_two.at[slot], r.mask, r.ctx_two.at[rows_at], r.lse_two.at[slot],
            lambda h: tick(range(4, 8), h),
        )

    @pl.when(step == 7)
    def _():
        out_two.wait()
        project_out(r.ctx_two, r.wo_two, r.first, r.second)
        for put in (puts.second, puts.ctx_two, puts.q_two, puts.kv_two, puts.lse_two):
            put.start()
        gather_one.sent()
        gather_two.sent()
        for copy in tables + [tok_swap, mem_swap, cot_swap]:
            copy.sent()
        for name in vars(outs):
            getattr(puts, name).wait()


def forward_call(operands):
    tokens = operands["tokens"]
    model = tokens.shape[2]
    anywhere = pl.BlockSpec(memory_space=pl.ANY)

    def fixed(array):
        return pl.BlockSpec(array.shape, lambda t: (0,) * array.ndim)

    small = dict(self_gain=fixed, cross_gain=fixed, table=fixed, hot=fixed, memsegs=fixed)
    small.update(segs=lambda a: pl.BlockSpec(memory_space=pltpu.SMEM))
    in_specs = {name: small.get(name, lambda a: anywhere)(a) for name, a in operands.items()}

    def room(*shape, kind=BF16):
        return pltpu.VMEM(shape, kind)

    kept = dict(
        tok=room(BLOCK, model, kind=F32), mem=room(model, BLOCK), cot=room(BLOCK, model), n_one=room(model, BLOCK),
        n_two=room(model, BLOCK), qkv_one=room(4, 3 * GROUP, BLOCK), kv_two=room(4, 2 * GROUP, BLOCK),
        q_two=room(4, GROUP, BLOCK), ctx_one=room(model, BLOCK), ctx_two=room(model, BLOCK),
        lse_one=room(4, 8, BLOCK, kind=F32), lse_two=room(4, 8, BLOCK, kind=F32),
        first=room(BLOCK, model, kind=F32), second=room(BLOCK, model, kind=F32),
        wt_one=room(4, 3 * GROUP, model), wt_two=room(4, 3 * GROUP, model), table=room(4, 8, TILE, kind=F32),
    )
    block = tokens.shape[1:]
    copies = 2 * (1 + 4 * PIECES) + 3 + 3
    scratch = dict(
        kept, tok_in=room(2, *block), mem_in=room(2, *block), cot_in=room(2, *block),
        wo_one=room(model, model), wo_two=room(model, model), mask=room(BLOCK, BLOCK, kind=F32),
        send=pltpu.SemaphoreType.DMA((copies,)), recv=pltpu.SemaphoreType.DMA((copies,)),
        load=pltpu.SemaphoreType.DMA((15 + len(kept),)),
    )
    outs = {name: jax.ShapeDtypeStruct(m.shape, m.dtype) for name, m in kept.items()}
    arrays, in_tree = jax.tree.flatten(operands)
    out_shapes, out_tree = jax.tree.flatten(outs)
    rooms, room_tree = jax.tree.flatten(scratch)

    def kernel(*refs):
        a, b = len(arrays), len(arrays) + len(out_shapes)
        forward_kernel(
            Named(jax.tree.unflatten(in_tree, refs[:a])), Named(jax.tree.unflatten(out_tree, refs[a:b])),
            Named(jax.tree.unflatten(room_tree, refs[b:])),
        )

    results = pl.pallas_call(
        kernel,
        grid=(8,),
        in_specs=jax.tree.leaves(in_specs),
        out_specs=[anywhere] * len(out_shapes),
        out_shape=out_shapes,
        scratch_shapes=rooms,
        compiler_params=pltpu.CompilerParams(
            collective_id=1, has_side_effects=True, vmem_limit_bytes=60_000_000, dimension_semantics=("arbitrary",)
        ),
        cost_estimate=pl.CostEstimate(flops=10_000_000_000, bytes_accessed=40_000_000, transcendentals=6_000_000),
    )(*arrays)
    return Named(jax.tree.unflatten(out_tree, results))


def finish_call(results, devices, buckets):
    plain = {name: a for name, a in results.items() if name not in ("gains", "bias")}
    share = results["gains"].shape[1] // devices
    outs = {name: jax.ShapeDtypeStruct(a.shape, a.dtype) for name, a in plain.items()}
    anywhere = pl.BlockSpec(memory_space=pl.ANY)
    count = len(plain)

    def kernel(gains, bias, *refs):
        sources, (bias_out, *gain_outs), targets = refs[:count], refs[count : count + 4], refs[count + 4 : 2 * count + 4]
        rooms, semaphores = refs[2 * count + 4 : 3 * count + 4], refs[3 * count + 4]
        takes = [pltpu.make_async_copy(s, r, semaphores.at[k]) for k, (s, r) in enumerate(zip(sources, rooms))]
        puts = [pltpu.make_async_copy(r, t, semaphores.at[count + k]) for k, (r, t) in enumerate(zip(rooms, targets))]
        for take in takes:
            take.start()
        bias_out[...] = bias[:HEADS, :buckets]
        first = (lax.axis_index("batch") * lax.axis_size("head") + lax.axis_index("head")) * share
        turned = pltpu.roll(gains[...], gains.shape[1] - first, 1)
        for k, out in enumerate(gain_outs):
            out[...] = jnp.reshape(turned[k : k + 1, :share], (share,))
        for take, put in zip(takes, puts):
            take.wait()
            put.start()
        for put in puts:
            put.wait()

    def fixed(shape):
        return pl.BlockSpec(shape, lambda: (0,) * len(shape))

    small = [jax.ShapeDtypeStruct((HEADS, buckets), F32)] + [jax.ShapeDtypeStruct((share,), F32)] * 3
    bias, *rest = pl.pallas_call(
        kernel,
        in_specs=[fixed(results["gains"].shape), fixed(results["bias"].shape)] + [anywhere] * count,
        out_specs=[fixed(a.shape) for a in small] + [anywhere] * count,
        out_shape=small + list(outs.values()),
        scratch_shapes=[pltpu.VMEM(a.shape, a.dtype) for a in plain.values()] + [pltpu.SemaphoreType.DMA((2 * count,))],
    )(results["gains"], results["bias"], *plain.values())
    return dict(zip(plain, rest[3:]), bias=bias, gain_0=rest[0], gain_1=rest[1], gain_2=rest[2])


def on_device(
    tokens, memory, cotangent, target_segments, memory_segments, self_gain, self_query, self_key,
    self_value, self_out, position_bias, cross_gain, cross_query, cross_key, cross_value, cross_out,
    ff_gain, ff_gate, ff_up, ff_down,
):
    heads_axis, batch_axis = lax.axis_size("head"), lax.axis_size("batch")
    rows, part, model = tokens.shape
    assert part * 2 == BLOCK and rows == 2 and heads_axis == 4
    assert position_bias.shape[1] == HEADS and self_query.shape[1] == GROUP
    one_hot = jnp.asarray(bucket_one_hot(position_bias.shape[0]))

    fwd = forward_call(
        dict(
            tokens=tokens, memory=memory, cotangent=cotangent, segs=target_segments, memsegs=memory_segments, hot=one_hot,
            self_gain=self_gain, cross_gain=cross_gain, table=position_bias.T,
            self_query=self_query.T, self_key=self_key.T, self_value=self_value.T, self_out=self_out,
            cross_query=cross_query.T, cross_key=cross_key.T, cross_value=cross_value.T, cross_out=cross_out,
        )
    )
    done = backward_call(
        batch_axis,
        dict(
            segs=target_segments, memsegs=memory_segments, hot=one_hot, self_gain=self_gain, cross_gain=cross_gain,
            ff_gain=ff_gain, ff_gate=ff_gate, ff_up=ff_up, ff_down=ff_down,
            kv_two=fwd.kv_two, q_two=fwd.q_two, lse_two=fwd.lse_two, wt_two=fwd.wt_two,
            qkv_one=fwd.qkv_one, lse_one=fwd.lse_one, wt_one=fwd.wt_one, table=fwd.table,
            loaded=dict(
                second=fwd.second, cot=fwd.cot, wo_two=cross_out, ctx_two=fwd.ctx_two, n_two=fwd.n_two, mem=fwd.mem,
                first=fwd.first, wo_one=self_out, ctx_one=fwd.ctx_one, n_one=fwd.n_one, tok=fwd.tok,
            ),
        ),
    )
    done = Named(finish_call(vars(done), heads_axis * batch_axis, position_bias.shape[0]))
    return (
        done.layer, done.tokens, done.memory, done.gain_0, done.wq_one, done.wk_one, done.wv_one, done.out_one.T,
        done.bias.T, done.gain_1, done.wq_two, done.wk_two, done.wv_two, done.out_two.T, done.gain_2,
        done.gate.T, done.up.T, done.down.T,
    )


def solution(mesh):
    tokens = P("batch", "head", None)
    rows = P("batch", None)
    columns = P(None, "head")
    split = P("batch", "head")
    every = P(None, ("batch", "head"))
    gain = P(("batch", "head"))
    return jax.shard_map(
        on_device,
        mesh=mesh,
        in_specs=(
            tokens, tokens, tokens, rows, rows, P(), columns, columns, columns, P(), columns, P(),
            columns, columns, columns, P(), P(), P(), P(), P(),
        ),
        out_specs=(
            tokens, tokens, tokens, gain, split, split, split, every, columns, gain,
            split, split, split, every, gain, every, every, every,
        ),
        check_vma=False,
    )
```

```python
import jax
import jax.numpy as jnp
import numpy as np
from jax import lax
from jax.experimental import pallas as pl
from jax.experimental.pallas import tpu as pltpu
from jax.sharding import PartitionSpec as P

NORM_EPS = 1e-06
MASKED = -1e30
BLOCK = 512
TILE = 128
HALF = 256
SIZE = 64
HEADS = 3
GROUP = HEADS * SIZE
F32 = jnp.float32
BF16 = jnp.bfloat16
MESH = pl.DeviceIdType.MESH


def bucket_edges():
    distance = np.arange(1.0, 8192.0)
    far_bucket = 16.0 + np.floor(np.log(np.maximum(distance, 16.0) / 16.0) / np.log(8.0) * 16.0)
    bucket_value = np.where(distance < 16, distance, np.minimum(far_bucket, 31.0))
    return [int(distance[np.argmax(bucket_value >= bucket_level)]) for bucket_level in range(1, 32)]


def bucket_one_hot(buckets):
    ids = np.zeros(2 * TILE, np.int32)
    for edge in bucket_edges():
        ids += np.arange(2 * TILE) >= edge
    assert bucket_edges()[-1] <= TILE + 1
    assert buckets <= TILE and ids[-1] == buckets - 1
    return (np.arange(TILE)[:, None] == ids[None, :]).astype(np.float32)


def dot(left, right):
    return lax.dot_general(left, right, (((1,), (0,)), ((), ())), preferred_element_type=F32)


KEY_AT = ((0, 0), (0, 1), (2, 0))
VALUE_AT = ((1, 0), (1, 1), (2, 1))
QUERY_START = 2 * GROUP


def rows_of(at):
    tile, place = at
    return slice(tile * 128 + place * SIZE, tile * 128 + (place + 1) * SIZE)


def lanes_of(at):
    return slice(at[0] * 128, (at[0] + 1) * 128)


def spread(head_rows, place):
    blank = jnp.zeros_like(head_rows)
    return jnp.concatenate((head_rows, blank) if place == 0 else (blank, head_rows), axis=0)


def bias_tiles(table, index, one_hot):
    by_distance = jnp.dot(
        table, one_hot, precision=lax.Precision.HIGHEST, preferred_element_type=F32
    )[index : index + 1]
    wide = jnp.broadcast_to(by_distance, (TILE, 2 * TILE))
    turned = pltpu.roll(wide, 0, 1, stride=1, stride_axis=0)
    key = lax.broadcasted_iota(jnp.int32, (TILE, TILE), 0)
    query = lax.broadcasted_iota(jnp.int32, (TILE, TILE), 1)
    near = jnp.where(key <= query, turned[:, :TILE], MASKED)
    return near, turned[:, TILE:], by_distance[0, 2 * TILE - 1]


def self_tile(scores, key_tile, query_tile, tiles, seg_ref, base):
    near, next_one, far = tiles
    if key_tile == query_tile:
        return scores + near
    same = seg_ref[base + key_tile] == seg_ref[base + query_tile]
    shift = jnp.where(same, 0.0, MASKED)
    if key_tile == query_tile - 1:
        return scores + next_one + shift
    return scores + (far + shift)


def self_forward(kv, q, table, one_hot, seg_ref, out, lse, tick):
    key_values = jnp.transpose(kv[...])
    for index in range(HEADS):
        rows = slice(index * SIZE, (index + 1) * SIZE)
        keys = key_values[:, lanes_of(KEY_AT[index])]
        query = spread(q[rows, :], KEY_AT[index][1])
        tiles = bias_tiles(table, index, one_hot)
        for half in range(2):
            end = (half + 1) * HALF
            scores = dot(keys[:end], query[:, half * HALF : (half + 1) * HALF])
            columns, totals = [], []
            for part in range(2):
                query_tile = 2 * half + part
                parts = [
                    self_tile(
                        scores[kt * TILE : (kt + 1) * TILE, part * TILE : (part + 1) * TILE],
                        kt, query_tile, tiles, seg_ref, 0,
                    )
                    for kt in range(query_tile + 1)
                ]
                top = jnp.max(parts[0], axis=0, keepdims=True)
                for piece in parts[1:]:
                    top = jnp.maximum(top, jnp.max(piece, axis=0, keepdims=True))
                probs = [jnp.exp(piece - top) for piece in parts]
                total = jnp.sum(probs[0], axis=0, keepdims=True)
                for piece in probs[1:]:
                    total = total + jnp.sum(piece, axis=0, keepdims=True)
                probs = [piece.astype(BF16) for piece in probs]
                if part == 0:
                    probs.append(jnp.zeros((TILE, TILE), BF16))
                columns.append(jnp.concatenate(probs, axis=0))
                totals.append(total)
                lse[index : index + 1, query_tile * TILE : (query_tile + 1) * TILE] = top + jnp.log(total)
            weights = jnp.concatenate(columns, axis=1)
            context = dot(kv[rows_of(VALUE_AT[index]), :end], weights)
            context = context / jnp.concatenate(totals, axis=1)
            out[rows, half * HALF : (half + 1) * HALF] = context.astype(BF16)
        tick(index)


def key_mask(seg_ref, memseg, mask_ref):
    rows = jnp.transpose(jnp.broadcast_to(memseg.astype(F32), (TILE, BLOCK)))
    for tile in range(BLOCK // TILE):
        wanted = seg_ref[tile].astype(F32)
        shift = jnp.where(rows == wanted, 0.0, MASKED)
        mask_ref[:, tile * TILE : (tile + 1) * TILE] = shift.astype(mask_ref.dtype)


def cross_forward(kv, q, mask, out, lse, tick):
    key_values = jnp.transpose(kv[...])
    for index in range(HEADS):
        rows = slice(index * SIZE, (index + 1) * SIZE)
        keys = key_values[:, lanes_of(KEY_AT[index])]
        query = spread(q[rows, :], KEY_AT[index][1])
        for half in range(2):
            lanes = slice(half * HALF, (half + 1) * HALF)
            scores = dot(keys, query[:, lanes]) + mask[:, lanes]
            top = jnp.max(scores, axis=0, keepdims=True)
            probs = jnp.exp(scores - top)
            total = jnp.sum(probs, axis=0, keepdims=True)
            context = dot(kv[rows_of(VALUE_AT[index]), :], probs.astype(BF16)) / total
            out[rows, lanes] = context.astype(BF16)
            lse[index : index + 1, lanes] = top + jnp.log(total)
        tick(index)


def grow(old, new):
    if old is None:
        return new
    shared = old.shape[0]
    if shared == new.shape[0]:
        return old + new
    return jnp.concatenate((old + new[:shared], new[shared:]), axis=0)


def only_lanes(wide, at):
    pair = wide[:, lanes_of(at)]
    lane = lax.broadcasted_iota(jnp.int32, pair.shape, 1)
    keep = lane < SIZE if at[1] == 0 else lane >= SIZE
    return jnp.where(keep, pair, jnp.zeros_like(pair))


def moved(wide, index, place):
    if index < 2:
        assert place == index
        return only_lanes(wide, (0, index))
    part = wide[:, 128:192]
    blank = jnp.zeros_like(part)
    return jnp.concatenate((part, blank) if place == 0 else (blank, part), axis=1)


def attention_back(read, tile_of, skip, note, dq_ref, sums_ref, tick):
    key_values = jnp.transpose(read.kv())
    query_tok = jnp.transpose(read.q(slice(0, GROUP)))
    grad_tok = jnp.transpose(read.do(slice(0, GROUP)))
    sums = [None, None, None]
    for index in range(HEADS):
        rows = slice(index * SIZE, (index + 1) * SIZE)
        k_at, v_at = KEY_AT[index], VALUE_AT[index]
        key_pair, value_pair = key_values[:, lanes_of(k_at)], key_values[:, lanes_of(v_at)]
        query_pair = moved(query_tok, index, k_at[1])
        grad_pair = moved(grad_tok, index, v_at[1])
        query_rows = spread(read.q(rows), k_at[1])
        grad_rows = spread(read.do(rows), v_at[1])
        inner = jnp.sum(read.do(rows).astype(F32) * read.o(rows).astype(F32), axis=0, keepdims=True)
        key_sum = value_sum = None
        for half in range(2):
            end = (half + 1) * HALF if skip else BLOCK
            lanes = slice(half * HALF, (half + 1) * HALF)
            scores = dot(key_pair[:end], query_rows[:, lanes])
            grad_probs = dot(value_pair[:end], grad_rows[:, lanes])
            prob_columns, grad_columns = [], []
            for part in range(2):
                query_tile = 2 * half + part
                cut = slice(query_tile * TILE, (query_tile + 1) * TILE)
                here = slice(part * TILE, (part + 1) * TILE)
                total = read.lse(index, cut)
                probs, grads = [], []
                for kt in range(query_tile + 1 if skip else BLOCK // TILE):
                    there = slice(kt * TILE, (kt + 1) * TILE)
                    prob = jnp.exp(tile_of(scores[there, here], index, kt, query_tile) - total)
                    ds = prob * (grad_probs[there, here] - inner[:, cut])
                    note(index, kt, query_tile, ds)
                    probs.append(prob.astype(BF16))
                    grads.append(ds.astype(BF16))
                if skip and part == 0:
                    probs.append(jnp.zeros((TILE, TILE), BF16))
                    grads.append(jnp.zeros((TILE, TILE), BF16))
                prob_columns.append(jnp.concatenate(probs, axis=0))
                grad_columns.append(jnp.concatenate(grads, axis=0))
            probs = jnp.concatenate(prob_columns, axis=1)
            grads = jnp.concatenate(grad_columns, axis=1)
            value_sum = grow(value_sum, dot(probs, grad_pair[lanes]))
            key_sum = grow(key_sum, dot(grads, query_pair[lanes]))
            dq_ref[rows, lanes] = dot(read.k(index, end), grads).astype(BF16)
        for at, total in ((k_at, key_sum), (v_at, value_sum)):
            sums[at[0]] = total if sums[at[0]] is None else sums[at[0]] + total
        tick(index)
    for tile in range(3):
        sums_ref[:, tile * 128 : (tile + 1) * 128] = sums[tile].astype(BF16)
    sums_ref[:, QUERY_START : QUERY_START + GROUP] = jnp.transpose(dq_ref[...])


def row_of(ref):
    return jnp.reshape(ref[...], (1, ref.shape[0]))


class Tiles:
    def __init__(self, place, ref):
        self.place, self.ref = place, ref

    def __getitem__(self, tile):
        return self.ref[self.place.core, self.place.y * BLOCK + tile * TILE]


def key_segments(place, ref):
    lanes = pl.ds(pl.multiple_of(place.y * BLOCK, BLOCK), BLOCK)
    return jnp.where(place.core == 0, ref[0:1, lanes], ref[1:2, lanes])


class Read:
    def __init__(self, kv, k, q, do, o, lse):
        self.kv, self.k, self.q, self.do, self.o, self.lse = kv, k, q, do, o, lse


class Named:
    def __init__(self, tree):
        for key, value in tree.items():
            setattr(self, key, Named(value) if isinstance(value, dict) else value)


class Copies:
    def __init__(self, send, recv):
        self.send, self.recv, self.count, self.sent = send, recv, 0, []

    def new(self, source, target, device):
        at = self.count
        self.count += 1
        return Copy(self, at, source, target, device)


class Copy:
    def __init__(self, owner, at, source, target, device):
        self.owner, self.at, self.source, self.target, self.device = owner, at, source, target, device

    def make(self):
        return pltpu.make_async_remote_copy(
            src_ref=self.source(), dst_ref=self.target(), send_sem=self.owner.send.at[self.at],
            recv_sem=self.owner.recv.at[self.at], device_id=self.device, device_id_type=MESH,
        )

    def start(self):
        self.make().start()

    def got(self):
        self.make().wait_recv()

    def sent(self):
        self.make().wait_send()

    def done(self):
        self.make().wait()


class Place:
    def __init__(self, depth):
        b, h = lax.axis_index("batch"), lax.axis_index("head")
        self.depth = depth
        self.core, self.y, self.x, self.z = h % 2, h // 2, b % 2, b // 2
        self.to_core = (b, h + 1 - 2 * self.core)
        self.to_y = (b, h + 2 - 4 * self.y)
        self.to_x = (b + 1 - 2 * self.x, h)
        self.to_z = [(lax.rem(self.z + k, depth) * 2 + self.x, h) for k in range(1, depth)]
        self.z0, self.zh, self.far = self.z % 2, self.z // 2, depth // 2
        self.to_z0 = ((self.z + 1 - 2 * self.z0) * 2 + self.x, h)
        self.to_zh = [((lax.rem(self.zh + k, self.far) * 2 + self.z0) * 2 + self.x, h) for k in range(1, self.far)]

    def group(self, slot):
        low, high = slot % 2, slot // 2
        return (self.core + low - 2 * self.core * low) + 2 * (self.y + high - 2 * self.y * high)

    def everyone(self):
        return [self.to_core, self.to_y, self.to_x] + self.to_z


ZH, Z0, X, Y = range(4)


class Sum:
    def __init__(self, place, copies, total, got, order, tiles=()):
        self.place, self.total, self.got, self.order = place, total, got, order
        self.dims = len(total.shape) - 2
        self.stages = []
        for at, axis in enumerate(order):
            room = got[at]
            if at == 0 and tiles:
                assert axis in (X, Y)
                self.stages.append([
                    copies.new(
                        self.source(0, 1, tile), (lambda room, tile: lambda: room.at[tile])(room, tile),
                        place.to_x if axis == X else place.to_y,
                    )
                    for tile in tiles
                ])
                continue
            if axis == ZH:
                stage = [
                    copies.new(self.source(at, k), (lambda room, k: lambda: room.at[k - 1])(room, k), place.to_zh[k - 1])
                    for k in range(1, place.far)
                ]
            else:
                device = (None, place.to_z0, place.to_x, place.to_y)[axis]
                stage = [copies.new(self.source(at, 1), (lambda room: lambda: room)(room), device)]
            self.stages.append(stage)

    @staticmethod
    def rooms(far, dims, order, rows, lanes):
        sizes = (far, 2, 2, 2)
        free = list(range(dims))
        shapes = []
        for axis in order:
            free.remove(axis)
            lead = (far - 1,) if axis == ZH else ()
            shapes.append(lead + tuple(sizes[d] for d in free) + (rows, lanes))
        return shapes

    @staticmethod
    def count(far, order):
        return sum(far - 1 if axis == ZH else 1 for axis in order)

    def mine(self, axis):
        return (self.place.zh, self.place.z0, self.place.x, self.place.y)[axis]

    def source(self, at, k, tile=()):
        def view():
            index = list(tile) + [slice(None)] * (self.dims - len(tile))
            for axis in self.order[:at]:
                index[axis] = self.mine(axis)
            axis = self.order[at]
            index[axis] = lax.rem(self.place.zh + k, self.place.far) if axis == ZH else 1 - self.mine(axis)
            return self.total.at[tuple(index)]

        return view

    def start(self, at):
        for copy in self.stages[at]:
            copy.start()

    def value(self, at, free):
        axis = self.order[at]
        later = sorted(self.order[at + 1 :])
        index = [None] * self.dims
        for done in self.order[: at + 1]:
            index[done] = self.mine(done)
        for d, i in zip(later, free):
            index[d] = i
        got = [self.got[at].at[k] for k in range(self.place.far - 1)] if axis == ZH else [self.got[at]]
        return tuple(index), [g[tuple(free)] if free else g[...] for g in got]

    def add(self, at):
        for copy in self.stages[at]:
            copy.got()
        later = sorted(self.order[at + 1 :])

        def one(free):
            index, got = self.value(at, free)
            if len(got) == 1:
                self.total[index] = self.total[index] + got[0]
            else:
                total = self.total[index].astype(F32)
                for g in got:
                    total = total + g.astype(F32)
                self.total[index] = total.astype(BF16)

        def over(dims, free):
            if not dims:
                one(free)
            elif dims[0] == ZH:

                @pl.loop(0, self.place.far)
                def _(z):
                    over(dims[1:], free + [z])

            else:
                for i in range(2):
                    over(dims[1:], free + [i])

        over(later, [])
        self.start(at + 1)

    def finish(self):
        at = len(self.order) - 1
        for copy in self.stages[at]:
            copy.got()
        index, got = self.value(at, [])
        total = self.total[index].astype(F32)
        for g in got:
            total = total + g.astype(F32)
        return total

    def sent(self):
        for stage in self.stages:
            for copy in stage:
                copy.sent()


def add_loop(target, other):
    inner = target.shape[1:-2]

    @pl.loop(0, target.shape[0])
    def _(z):
        for index in np.ndindex(*inner):
            target[(z, *index)] = target[(z, *index)] + other[(z, *index)]


class Shared:
    def __init__(self, place, copies, room, order, send, pair):
        self.place, self.room, self.from_pair = place, room, pair
        self.sum = Sum(place, copies, room.total, room.got, order)
        self.pair = copies.new(lambda: send, lambda: pair, place.to_core)
        self.swap = copies.new(lambda: room.last.at[1 - place.core], lambda: room.other, place.to_core)

    def enter(self):
        self.pair.got()
        add_loop(self.room.total, self.from_pair)
        self.sum.start(0)

    def last(self):
        total = self.sum.finish()
        rows = total.shape[0] // 2
        self.room.last[0] = total[:rows]
        self.room.last[1] = total[rows:]
        self.swap.start()

    def store(self, out, offset, half):
        self.swap.got()
        lanes = self.room.other.shape[1]
        mine, other = self.room.last[self.place.core], self.room.other[...]
        for which in range(2):
            at = slice(which * half + offset, which * half + offset + lanes)
            out[:, at] = jnp.where(self.place.core == which, mine, other)

    def sent(self):
        self.swap.sent()
        self.sum.sent()


class Tiled(Shared):
    def __init__(self, place, copies, room, order, stage, pair):
        self.place, self.room, self.from_pair = place, room, pair
        self.tiles = [tile_of_steps(place.far, t) for t in range(FF_STEPS)]
        self.sum = Sum(place, copies, room.total, room.got, order, self.tiles)
        self.pairs = [
            copies.new(
                (lambda t: lambda: stage.at[t % stage.shape[0]])(t), (lambda tile: lambda: pair.at[tile])(tile), place.to_core
            )
            for t, tile in enumerate(self.tiles)
        ]
        self.swap = copies.new(lambda: room.last.at[1 - place.core], lambda: room.other, place.to_core)

    def enter_tile(self, t):
        self.pairs[t].got()
        add_loop(self.room.total.at[self.tiles[t]], self.from_pair.at[self.tiles[t]])
        self.sum.stages[0][t].start()


FF_STEPS = 4


def tile_of_steps(far, t):
    return (t // 2, t % 2) if far == 2 else (slice(t * far // FF_STEPS, (t + 1) * far // FF_STEPS),)


def over_rows(left, right):
    return lax.dot_general(left, right, (((1,), (1,)), ((), ())), preferred_element_type=F32)


class Slots:
    def __init__(self, place, copies, room, sends, y_first, order):
        self.place, self.room, self.y_first = place, room, y_first
        self.pair = [copies.new((lambda j: lambda: sends.at[j])(j), (lambda j: lambda: room.pair.at[j])(j), place.to_core) for j in range(2)]
        self.own = Sum(place, copies, room.total.at[0], room.got, order)
        if y_first:
            self.across = copies.new(lambda: room.total.at[1], lambda: room.across, place.to_y)
        else:
            self.far = Sum(place, copies, room.total.at[1], room.far, order)
            self.across = copies.new(lambda: room.chunk, lambda: room.across, place.to_y)

    def enter(self, j):
        self.pair[j].got()
        add_loop(self.room.total.at[j], self.room.pair.at[j])
        if j == 1:
            if self.y_first:
                self.across.start()
            else:
                self.far.start(0)
        elif not self.y_first:
            self.own.start(0)

    def take(self):
        self.across.got()
        add_loop(self.room.total.at[0], self.room.across)
        self.own.start(0)

    def give(self):
        self.room.chunk[...] = self.far.finish().astype(BF16)
        self.across.start()

    def finish(self):
        total = self.own.finish()
        if not self.y_first:
            self.across.got()
            total = total + self.room.across[...].astype(F32)
        return total

    def sent(self):
        self.own.sent()
        self.across.sent()
        if not self.y_first:
            self.far.sent()


SHARED_ORDER = dict(
    gate=(Y, X, Z0, ZH), up=(X, Z0, Y, ZH), down_a=(Y, X, Z0, ZH), down_b=(Z0, X, Y, ZH),
    out_two=(X, Z0, ZH, Y), out_one=(Y, X, Z0, ZH),
)
SLOT_ORDER = dict(
    kv_two=(True, (X, Z0, ZH)), q_two=(True, (X, Z0, ZH)), kv_one=(False, (X, Z0, ZH)), q_one=(True, (Z0, X, ZH))
)
KV = slice(0, 2 * GROUP)
QS = slice(2 * GROUP, 3 * GROUP)


def packed(share):
    return share % 32 == 0


def query_shape(share):
    return (share + share // 2, 128) if packed(share) else (share, GROUP)


def put_query(ref, total):
    share = ref.shape[0]
    if not packed(share):
        ref[...] = total
        return
    ref[:, :128] = total[:share]
    ref[: share // 2, 128:] = total[share:, :64]
    ref[share // 2 :, 128:] = total[share:, 64:]


def put_heads(ref, kv):
    key_out, value_out = ref
    key_out[:, :128] = kv[:, :128]
    key_out[:, 128:] = kv[:, 256:320]
    value_out[:, :128] = kv[:, 128:256]
    value_out[:, 128:] = kv[:, 320:384]


def backward_kernel(depth, ins, outs, r):
    place = Place(depth)
    step = pl.program_id(0)
    core = place.core
    copies = Copies(r.send, r.recv)
    segs = Tiles(place, ins.segs)

    parities, downs = r.gate_stage.shape[0], r.down_stage.shape[0]
    down_stages = [r.down_stage.at[t % downs] for t in range(2)]
    stages = dict(gate=r.gate_stage, up=r.up_stage, down_a=down_stages[0], down_b=down_stages[1])
    shared = Named({
        name: (Tiled if name in ("gate", "up") else Shared)(
            place, copies, getattr(r, name), order, stages.get(name, r.out_send), getattr(r.pairs, name, r.out_pair)
        )
        for name, order in SHARED_ORDER.items()
    })
    slots = Named({
        name: Slots(place, copies, getattr(r, name), r.kv_send if name.startswith("kv") else r.q_send, *way)
        for name, way in SLOT_ORDER.items()
    })
    layer_swap = copies.new(lambda: r.block.at[1 - core], lambda: outs.layer.at[core], place.to_core)
    memory_swap = copies.new(lambda: r.block.at[1 - core], lambda: outs.memory.at[core], place.to_core)
    tokens_swap = copies.new(lambda: r.block.at[1 - core], lambda: outs.tokens.at[core], place.to_core)
    gain_copies = [
        copies.new(lambda: r.gains, (lambda k: lambda: r.gains_got.at[k])(k), d)
        for k, d in enumerate([place.to_core, place.to_y, place.to_x] + place.to_z)
    ]
    bias_copies = [
        copies.new((lambda s: lambda: r.bias.at[s])(s), (lambda k: lambda: r.bias_got.at[k])(k), d)
        for k, (s, d) in enumerate(
            zip([1, 3, 2, 0] + [0] * (depth - 1), [place.to_core, place.to_core, place.to_y, place.to_x] + place.to_z)
        )
    ]
    assert copies.count == r.send.shape[0], copies.count

    loads = []

    def load(source, target):
        loads.append(pltpu.make_async_copy(source, target, r.load.at[len(loads)]))
        return loads[-1]

    i = ins.loaded
    second, wo_two, ctx_two = load(i.second, r.hidden), load(i.wo_two, r.wo), load(i.ctx_two, r.ctx)
    cots = [load(i.cot.at[pl.ds(half * HALF, HALF)], r.block.at[half]) for half in range(2)]
    n_two, mem, first, tok = load(i.n_two, r.n), load(i.mem, r.mem), load(i.first, r.hidden), load(i.tok, r.hidden)
    wo_one, ctx_one, n_one = load(i.wo_one, r.wo), load(i.ctx_one, r.ctx), load(i.n_one, r.n)
    layer_put = load(r.block.at[core], outs.layer.at[core])
    memory_put = load(r.block.at[core], outs.memory.at[core])
    tokens_put = load(r.block.at[core], outs.tokens.at[core])

    def out_products(unit, context, branch):
        lanes = context.shape[0] // 2
        for which, target in ((1 - core, r.out_send), (core, unit.room.total)):
            side = jnp.transpose(context[pl.ds(pl.multiple_of(which * lanes, 16), lanes), :])
            per = branch.shape[0] // 2
            for part in range(2):
                product = dot(branch[part * per : (part + 1) * per, :], side).astype(BF16)
                rows = target.shape[4]
                for piece in range(per // rows):
                    at = part * (per // rows) + piece
                    to = (at // 8, (at // 4) % 2, (at // 2) % 2, at % 2)
                    target[to] = product[piece * rows : (piece + 1) * rows]
            if which is not core:
                unit.pair.start()

    def weight_products(target, left, lanes):
        rows = left.shape[0] // (2 * depth)
        per = left.shape[0]
        for part in range(1):
            product = dot(left[part * per : (part + 1) * per, :], r.dqkv[:, lanes]).astype(BF16)
            for piece in range(per // rows):
                at = part * (per // rows) + piece
                to = (at // 4, (at // 2) % 2, at % 2)
                share = product[piece * rows : (piece + 1) * rows]
                if target.shape[-1] == share.shape[1]:
                    target[to] = share
                else:
                    target[(*to, slice(0, rows))] = share[:, :128]
                    rest = share[:, 128:]
                    target[(*to, slice(rows, rows + rows // 2))] = jnp.concatenate((rest[: rows // 2], rest[rows // 2 :]), axis=1)

    def add_rows(target, lanes, weights, fresh):
        for part in range(1):
            rows = slice(0, BLOCK)
            product = dot(r.dqkv[rows, lanes], weights)

            @pl.when(fresh)
            def _():
                target[rows, :] = product

            @pl.when(jnp.logical_not(fresh))
            def _():
                target[rows, :] = target[rows, :] + product

    def norm_back(hidden, gain, incoming, onto, gain_row, branch):
        total = jnp.zeros((1, hidden.shape[1]), F32)
        for part in range(4):
            rows = slice(part * TILE, (part + 1) * TILE)
            h = hidden[rows, :].astype(F32)
            e = incoming[rows, :]
            scale = lax.rsqrt(jnp.mean(h * h, axis=-1, keepdims=True) + NORM_EPS)
            weighted = e * row_of(gain)
            inner = jnp.mean(weighted * h, axis=-1, keepdims=True)
            result = onto[rows, :] + weighted * scale - h * (scale * scale * scale * inner)
            total = total + jnp.sum(e * h * scale, axis=0, keepdims=True)
            if branch is None:
                r.block[part // 2, (part % 2) * TILE : (part % 2 + 1) * TILE, :] = result.astype(BF16)
            else:
                onto[rows, :] = result
                branch[:, rows] = jnp.transpose(result.astype(BF16))
        r.gains[gain_row : gain_row + 1, :] = total

    plan = {}

    def at(point, *tasks):
        plan.setdefault(point, []).extend(tasks)

    sh, sl = shared, slots
    def when_core(which, *tasks):
        def run():
            for task in tasks:
                task()

        return lambda: pl.when(core == which)(run)

    for t in range(FF_STEPS):
        at((t, 4), sh.gate.pairs[t].start, sh.up.pairs[t].start)
        if t < FF_STEPS - 1:
            at((t + 1, 1), lambda t=t: sh.gate.enter_tile(t), lambda t=t: sh.up.enter_tile(t))
        at((t, 5), when_core(1 - t // 2, (sh.down_a, sh.down_b)[t % 2].pair.start))
    at((2, 2), when_core(0, sh.down_a.enter))
    at((2, 3), when_core(0, sh.down_b.enter))
    at((4, 0), when_core(1, sh.down_a.enter, sh.down_b.enter))
    at((4, 1), sh.out_two.enter)
    at((4, 3), sl.kv_two.pair[1].start, sl.q_two.pair[1].start)
    at((5, 0), lambda: sh.gate.sum.add(0), lambda: sh.up.sum.add(0))
    at((5, 3), lambda: sl.kv_two.enter(1), lambda: sl.q_two.enter(1))
    at((6, 0), lambda: sh.out_two.sum.add(0), lambda: sh.down_b.sum.add(0))
    at((6, 1), lambda: sh.down_a.sum.add(0))
    at((6, 3), sl.kv_two.pair[0].start, sl.q_two.pair[0].start)
    at((7, 0), lambda: sh.up.sum.add(1), lambda: sh.gate.sum.add(1))
    at((7, 2), lambda: sh.out_two.sum.add(1))
    at((7, 3), lambda: sl.kv_two.enter(0), lambda: sl.q_two.enter(0), lambda: sh.down_b.sum.add(1))
    at((7, 4), sl.kv_two.take, lambda: sh.gate.sum.add(2), lambda: sh.down_a.sum.add(1))
    at((8, 0), lambda: sh.out_two.sum.add(2), sh.out_one.enter)
    at((8, 2), sl.q_two.take, lambda: sh.down_a.sum.add(2))
    at((8, 3), sl.kv_one.pair[1].start, sl.q_one.pair[1].start)
    at((9, 0), lambda: sl.kv_two.own.add(0), sh.gate.last)
    at((9, 1), lambda: sh.up.sum.add(2))
    at((9, 2), lambda: sl.q_two.own.add(0))
    at((9, 3), lambda: sl.kv_one.enter(1), lambda: sl.q_one.enter(1), lambda: sh.down_b.sum.add(2), sh.down_a.last)
    at((10, 0), lambda: sl.kv_two.own.add(1), sh.out_two.last)
    at((10, 1), lambda: sh.out_one.sum.add(0), lambda: sl.q_two.own.add(1))
    at((10, 2), sh.up.last, sh.down_b.last)
    at((10, 3), sl.kv_one.pair[0].start, sl.q_one.pair[0].start)
    at((11, 1), lambda: sl.kv_one.far.add(0))
    at((11, 3), lambda: sl.kv_one.enter(0), lambda: sl.q_one.enter(0), lambda: sh.out_one.sum.add(1))

    def tick(steps, index):
        for k in steps:
            if (k, index) in plan:

                def run(tasks=plan[k, index]):
                    for task in tasks:
                        task()

                pl.when(step == k)(run)

    @pl.when(step == 0)
    def _():
        barrier = pltpu.get_barrier_semaphore()
        for device in place.everyone():
            pl.semaphore_signal(barrier, inc=1, device_id=device, device_id_type=MESH)
        for copy in [second] + cots + [wo_two, ctx_two, n_two, mem]:
            copy.start()
        r.gains[...] = jnp.zeros_like(r.gains)
        second.wait()
        for part in range(4):
            rows = slice(part * TILE, (part + 1) * TILE)
            h = r.hidden[rows, :]
            scale = lax.rsqrt(jnp.mean(h * h, axis=-1, keepdims=True) + NORM_EPS)
            r.normed[rows, :] = (h * scale * row_of(ins.ff_gain)).astype(BF16)
            r.acc_a[rows, :] = h
            r.acc_b[rows, :] = jnp.zeros_like(h)
        for part in range(4):
            if part % 2 == 0:
                cots[part // 2].wait()
            rows = slice(part * TILE, (part + 1) * TILE)
            r.branch[:, rows] = jnp.transpose(r.block[part // 2, (part % 2) * TILE : (part % 2 + 1) * TILE, :])
        pl.semaphore_wait(barrier, len(place.everyone()))

    for t in range(parities, FF_STEPS):

        @pl.when(step == t)
        def _(t=t):
            sh.gate.pairs[t - parities].sent()
            sh.up.pairs[t - parities].sent()

    @pl.when(step < FF_STEPS)
    def _():
        root = np.float32(np.sqrt(2.0 / np.pi))
        model = r.normed.shape[1]
        for part in range(2):
            rows = slice(part * HALF, (part + 1) * HALF)
            normed = r.normed[rows, :]
            gate, up = dot(normed, ins.ff_gate[...]), dot(normed, ins.ff_up[...])
            grad = over_rows(r.block[part], ins.ff_down[...])
            square = gate * gate
            half = 0.5 + 0.5 * jnp.tanh(gate * (root + (root * 0.044715) * square))
            gelu = gate * half
            slope = half + gelu * (2.0 - 2.0 * half) * (root + (3.0 * 0.044715 * root) * square)
            activation = (gelu * up).astype(BF16)
            grad_gate = (grad * up * slope).astype(BF16)
            grad_up = (grad * gelu).astype(BF16)
            r.mask[rows, :] = activation
            r.grad_gate[:, rows] = jnp.transpose(grad_gate)
            r.grad_up[:, rows] = jnp.transpose(grad_up)
            r.acc_a[rows, :] = r.acc_a[rows, :] + dot(activation, ins.ff_down[...])
            r.acc_b[rows, :] = r.acc_b[rows, :] + over_rows(grad_gate, ins.ff_gate[...]) + over_rows(grad_up, ins.ff_up[...])
            for point in (2 * part, 2 * part + 1):
                tick(range(FF_STEPS), point)
        lanes = model // 2
        for which, keep in ((1 - core, False), (core, True)):
            right = r.normed[:, pl.ds(pl.multiple_of(which * lanes, 128), lanes)]
            for grads, total, stage in ((r.grad_gate, r.gate.total, r.gate_stage), (r.grad_up, r.up.total, r.up_stage)):
                product = dot(grads[...], right).astype(BF16)
                rows = total.shape[4]
                for piece in range(product.shape[0] // rows):
                    inner = ((piece // 4) % 2, (piece // 2) % 2, piece % 2)
                    share = product[piece * rows : (piece + 1) * rows]
                    if place.far == 2:
                        head = (step // 2, step % 2) if keep else (step % parities,)
                        inner = inner[1:]
                    else:
                        head = (step * (place.far // FF_STEPS) + piece // 8,) if keep else (step % parities, piece // 8)
                    (total if keep else stage)[(*head, *inner)] = share
            if not keep:
                tick(range(FF_STEPS), 4)
        per = model // 2
        for part in range(2):
            product = dot(r.branch[part * per : (part + 1) * per, :], r.mask[...]).astype(BF16)
            for t in range(FF_STEPS):
                total = (r.down_a, r.down_b)[t % 2].total
                for target, mine in ((total, t // 2), (down_stages[t % 2], 1 - t // 2)):

                    @pl.when(jnp.logical_and(step == t, core == mine))
                    def _(target=target, product=product, part=part, t=t, mine=mine):
                        if downs == 1 and t % 2 == 1 and part == 0 and mine != t // 2:
                            sh.down_a.pair.sent()
                        rows = target.shape[4]
                        for piece in range(per // rows):
                            to = part * (per // rows) + piece
                            to = (to // 8, (to // 4) % 2, (to // 2) % 2, to % 2)
                            target[to] = product[piece * rows : (piece + 1) * rows]

        tick(range(FF_STEPS), 5)

    @pl.when(step == FF_STEPS - 1)
    def _():
        total = jnp.zeros((1, r.hidden.shape[1]), F32)
        for part in range(4):
            rows = slice(part * TILE, (part + 1) * TILE)
            block_rows = (part // 2, slice((part % 2) * TILE, (part % 2 + 1) * TILE))
            h, e = r.hidden[rows, :], r.acc_b[rows, :]
            scale = lax.rsqrt(jnp.mean(h * h, axis=-1, keepdims=True) + NORM_EPS)
            weighted = e * row_of(ins.ff_gain)
            inner = jnp.mean(weighted * h, axis=-1, keepdims=True)
            result = r.block[block_rows].astype(F32) + weighted * scale - h * (scale * scale * scale * inner)
            total = total + jnp.sum(e * h * scale, axis=0, keepdims=True)
            r.after[rows, :] = result
            r.branch[:, rows] = jnp.transpose(result.astype(BF16))
            r.block[block_rows] = r.acc_a[rows, :].astype(BF16)
        r.gains[2:3, :] = total
        layer_swap.start()
        layer_put.start()
        sh.gate.enter_tile(FF_STEPS - 1)
        sh.up.enter_tile(FF_STEPS - 1)
        key_mask(segs, key_segments(place, ins.memsegs), r.mask)
        first.start()
        for copy in (wo_two, ctx_two, n_two, mem):
            copy.wait()
        out_products(sh.out_two, r.ctx, r.branch)

    slot = 3 - step % 4
    odd = slot % 2 == 1
    rows_at = pl.ds(pl.multiple_of(place.group(slot) * GROUP, 16), GROUP)

    def slot_products(kv, q, kv_left, q_left):
        @pl.when(odd)
        def _():
            weight_products(r.kv_send.at[slot // 2], kv_left, KV)
            weight_products(r.q_send.at[slot // 2], q_left, QS)

        @pl.when(jnp.logical_not(odd))
        def _():
            weight_products(kv.room.total.at[slot // 2], kv_left, KV)
            weight_products(q.room.total.at[slot // 2], q_left, QS)

    @pl.when(step // 4 == 1)
    def _():
        r.do[...] = dot(r.wo[rows_at, :], r.branch[...]).astype(BF16)
        kv, q, lse = ins.kv_two, ins.q_two, ins.lse_two
        context = r.ctx.at[rows_at, :]
        read = Read(
            lambda: kv[0], lambda h, end: kv[0, rows_of(KEY_AT[h]), :end], lambda rows: q[0, rows, :],
            lambda rows: r.do[rows, :], lambda rows: context[rows, :], lambda h, cut: lse[0, h : h + 1, cut],
        )

        def tile_of(scores, index, kt, qt):
            return scores + r.mask[kt * TILE : (kt + 1) * TILE, qt * TILE : (qt + 1) * TILE].astype(F32)

        attention_back(read, tile_of, False, lambda *a: None, r.dq, r.dqkv, lambda h: tick(range(4, 8), h))
        slot_products(sl.kv_two, sl.q_two, r.mem, r.n)
        tick(range(4, 8), 3)
        add_rows(r.acc_b, KV, ins.wt_two[0, KV, :], step == 4)
        add_rows(r.acc_a, QS, ins.wt_two[0, QS, :], step == 4)

    @pl.when(step == 7)
    def _():
        for copy in (wo_one, ctx_one, n_one):
            copy.start()
        first.wait()
        layer_swap.sent()
        layer_put.wait()
        norm_back(r.hidden, ins.cross_gain, r.acc_a, r.after, 1, r.branch)
        tok.start()
        for part in range(4):
            rows = slice(part * TILE, (part + 1) * TILE)
            r.block[part // 2, (part % 2) * TILE : (part % 2 + 1) * TILE, :] = r.acc_b[rows, :].astype(BF16)
        memory_swap.start()
        memory_put.start()
        for copy in (wo_one, ctx_one, n_one):
            copy.wait()
        sh.out_two.pair.sent()
        out_products(sh.out_one, r.ctx, r.branch)
        for task in plan[7, 4]:
            task()

    @pl.when(step >= 8)
    def _():
        r.do[...] = dot(r.wo[rows_at, :], r.branch[...]).astype(BF16)
        qkv, lse = ins.qkv_one, ins.lse_one
        context = r.ctx.at[rows_at, :]
        read = Read(
            lambda: qkv[0, KV, :], lambda h, end: qkv[0, rows_of(KEY_AT[h]), :end],
            lambda rows: qkv[0, QUERY_START + rows.start : QUERY_START + rows.stop, :],
            lambda rows: r.do[rows, :], lambda rows: context[rows, :], lambda h, cut: lse[0, h : h + 1, cut],
        )
        table, one_hot = ins.table[0], ins.hot[...]
        tiles = [bias_tiles(table, index, one_hot) for index in range(HEADS)]
        kept = {}

        def note(index, kt, qt, ds):
            key = (index, min(qt - kt, 2))
            kept[key] = kept[key] + ds if key in kept else ds

        attention_back(
            read, lambda scores, index, kt, qt: self_tile(scores, kt, qt, tiles[index], segs, 0), True, note,
            r.dq, r.dqkv, lambda h: tick(range(8, 12), h),
        )
        key = lax.broadcasted_iota(jnp.int32, (TILE, TILE), 0)
        query = lax.broadcasted_iota(jnp.int32, (TILE, TILE), 1)
        flip = (key + query == TILE - 1).astype(F32)
        row = lax.broadcasted_iota(jnp.int32, (8, 2 * TILE), 0)
        lane = lax.broadcasted_iota(jnp.int32, (8, 2 * TILE), 1)
        by_distance = jnp.zeros((8, 2 * TILE), F32)
        for index in range(HEADS):
            both = jnp.concatenate((kept[index, 0], kept[index, 1]), axis=1)
            both = jnp.dot(flip, both, precision=lax.Precision.HIGHEST, preferred_element_type=F32)
            turned = jnp.sum(pltpu.roll(both, TILE + 1, 1, stride=1, stride_axis=0), axis=0, keepdims=True)
            far_total = jnp.sum(jnp.sum(kept[index, 2], axis=0, keepdims=True), axis=1, keepdims=True)
            turned = turned + jnp.where(lane[:1] == 2 * TILE - 1, far_total, 0.0)
            by_distance = by_distance + jnp.where(row == index, turned, 0.0)
        r.bias[slot] = lax.dot_general(
            by_distance, one_hot, (((1,), (1,)), ((), ())), precision=lax.Precision.HIGHEST, preferred_element_type=F32
        )
        for k, j in ((8, 1), (10, 0)):

            @pl.when(step == k)
            def _(j=j):
                sl.kv_two.pair[j].sent()
                sl.q_two.pair[j].sent()

        slot_products(sl.kv_one, sl.q_one, r.n, r.n)
        tick(range(8, 12), 3)
        add_rows(r.acc_a, slice(0, 3 * GROUP), ins.wt_one[0], step == 8)

    @pl.when(step == 11)
    def _():
        gains, bias = r.gains, r.bias
        memory_swap.sent()
        memory_put.wait()
        tok.wait()
        norm_back(r.hidden, ins.self_gain, r.acc_a, r.after, 0, None)
        tokens_swap.start()
        tokens_put.start()
        gain_copies[0].start()
        bias_copies[0].start()
        bias_copies[1].start()
        sl.q_one.take()
        sl.kv_one.far.add(1)
        gain_copies[0].done()
        gains[...] = gains[...] + r.gains_got[0]
        bias_copies[0].done()
        bias_copies[1].done()
        bias[0] = bias[0] + r.bias_got[0]
        bias[2] = bias[2] + r.bias_got[1]
        gain_copies[1].start()
        bias_copies[2].start()
        sl.q_one.own.add(0)
        sh.out_one.sum.add(2)
        sl.kv_one.own.add(0)
        put_heads((outs.wk_two, outs.wv_two), sl.kv_two.finish())
        put_query(outs.wq_two, sl.q_two.finish())
        gain_copies[1].done()
        gains[...] = gains[...] + r.gains_got[1]
        bias_copies[2].done()
        bias[0] = bias[0] + r.bias_got[2]
        gain_copies[2].start()
        bias_copies[3].start()
        sl.kv_one.give()
        sl.q_one.own.add(1)
        sh.out_one.last()
        gain_copies[2].done()
        gains[...] = gains[...] + r.gains_got[2]
        bias_copies[3].done()
        bias[0] = bias[0] + r.bias_got[3]
        for k in range(depth - 1):
            gain_copies[3 + k].start()
            bias_copies[4 + k].start()
        sl.kv_one.own.add(1)
        sh.up.store(outs.up, 0, outs.up.shape[1] // 2)
        sh.down_a.store(outs.down, 0, outs.down.shape[1] // 2)
        sh.down_b.store(outs.down, outs.down.shape[1] // 4, outs.down.shape[1] // 2)
        sh.gate.store(outs.gate, 0, outs.gate.shape[1] // 2)
        sh.out_two.store(outs.out_two, 0, outs.out_two.shape[1] // 2)
        sh.out_one.store(outs.out_one, 0, outs.out_one.shape[1] // 2)
        gain_total, bias_total = gains[...], bias[0]
        for k in range(depth - 1):
            gain_copies[3 + k].done()
            bias_copies[4 + k].done()
            gain_total = gain_total + r.gains_got[3 + k]
            bias_total = bias_total + r.bias_got[4 + k]
        outs.gains[...] = gain_total
        outs.bias[...] = bias_total
        put_query(outs.wq_one, sl.q_one.finish())
        put_heads((outs.wk_one, outs.wv_one), sl.kv_one.finish())
        for name in SHARED_ORDER:
            unit = getattr(shared, name)
            unit.sent()
            if name in ("gate", "up"):
                for copy in unit.pairs[-parities:]:
                    copy.sent()
            elif unit is not sh.out_two and (unit is not sh.down_a or downs == 2):
                unit.pair.sent()
        for name in SLOT_ORDER:
            getattr(slots, name).sent()
        for j in range(2):
            sl.kv_one.pair[j].sent()
            sl.q_one.pair[j].sent()
        layer_swap.got()
        memory_swap.got()
        tokens_swap.done()
        tokens_put.wait()


def backward_call(batch_size, operands):
    depth = batch_size // 2
    tight = depth > 4
    once = dict(pipeline_mode=pl.Buffered(1)) if tight else {}
    tok = operands["loaded"]["tok"]
    model = tok.shape[1]
    share = model // batch_size
    anywhere = pl.BlockSpec(memory_space=pl.ANY)

    def fixed(shape):
        return pl.BlockSpec(shape, lambda t: (0,) * len(shape))

    def phase(t):
        c = t // 4
        return (1 - c) * (2 - c) // 2, c * (2 - c), c * (c - 1) // 2

    def early(array):
        def at(t):
            _, cross, own = phase(t)
            return (3 - cross * (t % 4) - 3 * own, 0, 0)

        return pl.BlockSpec((1,) + array.shape[1:], at, **once)

    def late(array):
        return pl.BlockSpec((1,) + array.shape[1:], lambda t: (3 - phase(t)[2] * (t % 4), 0, 0))

    def tile(t):
        return 3 - phase(t)[0] * (3 - t % 4)

    def wide_tile(array):
        return pl.BlockSpec((array.shape[0], array.shape[1] // FF_STEPS), lambda t: (0, tile(t)), **once)

    def deep_tile(array):
        return pl.BlockSpec((array.shape[0] // FF_STEPS, array.shape[1]), lambda t: (tile(t), 0), **once)

    kinds = dict(
        segs=lambda a: pl.BlockSpec(memory_space=pltpu.SMEM), kv_two=early, q_two=early, lse_two=early, wt_two=early,
        qkv_one=late, lse_one=late, wt_one=late, table=late, loaded=lambda a: anywhere,
        ff_gate=wide_tile, ff_up=wide_tile, ff_down=deep_tile,
    )
    in_specs = {
        name: jax.tree.map(kinds.get(name, lambda a: fixed(a.shape)), value) for name, value in operands.items()
    }
    columns = operands["ff_gate"].shape[1]
    made = ("gate", "up", "down_a", "down_b")
    shapes = dict(gate=(columns // (4 * depth), model // 2), down_a=(model // (4 * depth), columns // 4))
    shapes.update(up=shapes["gate"], down_b=shapes["down_a"])
    shapes.update(out_two=(model // (4 * depth), model // 2), out_one=(model // (4 * depth), model // 2))
    tile_room = (2, 2, 2) if depth == 4 else (1, depth // 8, 2, 2, 2)
    block = jax.ShapeDtypeStruct((2, HALF, model), BF16)

    def wide(rows, columns):
        return jax.ShapeDtypeStruct((rows, columns), F32)

    head = wide(share, GROUP)
    outs = dict(
        layer=block, memory=block, tokens=block,
        gate=wide(shapes["gate"][0] // 2, 2 * shapes["gate"][1]), up=wide(shapes["up"][0] // 2, 2 * shapes["up"][1]),
        down=wide(shapes["down_a"][0] // 2, 4 * shapes["down_a"][1]),
        out_two=wide(shapes["out_two"][0] // 2, model), out_one=wide(shapes["out_one"][0] // 2, model),
        wq_two=head, wk_two=head, wv_two=head, wq_one=head, wk_one=head, wv_one=head,
        gains=wide(8, model), bias=wide(8, TILE),
    )
    out_specs = {name: anywhere if s is block else fixed(s.shape) for name, s in outs.items()}

    def room(*shape, kind=BF16):
        return pltpu.VMEM(shape, kind)

    scratch = {}
    for name, order in SHARED_ORDER.items():
        rows, lanes = shapes[name]
        scratch[name] = dict(
            total=room(depth // 2, 2, 2, 2, rows, lanes),
            got=[room(*s) for s in Sum.rooms(depth // 2, 4, order, rows, lanes)],
            last=room(2, rows // 2, lanes, kind=F32), other=room(rows // 2, lanes, kind=F32),
        )
    for name, (y_first, order) in SLOT_ORDER.items():
        piece = (share, 2 * GROUP) if name.startswith("kv") else query_shape(share)
        got = [room(*s) for s in Sum.rooms(depth // 2, 3, order, *piece)]
        both = room(2, depth // 2, 2, 2, *piece)
        scratch[name] = dict(total=both, pair=both, got=got)
        if y_first:
            scratch[name].update(across=room(depth // 2, 2, 2, *piece))
        else:
            scratch[name].update(across=room(*piece), chunk=room(*piece), far=list(got))
    scratch.update(
        pairs={name: room(depth // 2, 2, 2, 2, *shapes[name]) for name in made},
        gate_stage=room(*tile_room, *shapes["gate"]), up_stage=room(*tile_room, *shapes["up"]),
        down_stage=room(1 if tight else 2, depth // 2, 2, 2, 2, *shapes["down_a"]), normed=room(BLOCK, model),
        grad_gate=room(columns // FF_STEPS, BLOCK),
        grad_up=room(columns // FF_STEPS, BLOCK),
        out_send=room(depth // 2, 2, 2, 2, *shapes["out_one"]), out_pair=room(depth // 2, 2, 2, 2, *shapes["out_one"]), kv_send=room(2, depth // 2, 2, 2, share, 2 * GROUP),
        q_send=room(2, depth // 2, 2, 2, *query_shape(share)), block=room(2, HALF, model), branch=room(model, BLOCK),
        acc_a=room(BLOCK, model, kind=F32), acc_b=room(BLOCK, model, kind=F32), dqkv=room(BLOCK, 3 * GROUP),
        dq=room(GROUP, BLOCK), do=room(GROUP, BLOCK), mask=room(BLOCK, columns // FF_STEPS), gains=room(8, model, kind=F32),
        gains_got=room(depth + 2, 8, model, kind=F32), bias=room(4, 8, TILE, kind=F32),
        bias_got=room(depth + 3, 8, TILE, kind=F32),
        after=room(BLOCK, model, kind=F32), hidden=room(BLOCK, model, kind=F32),
        wo=room(model, model), ctx=room(model, BLOCK), n=room(model, BLOCK), mem=room(model, BLOCK),
    )
    z = depth - 1
    copies = 3 + (3 + z) + (4 + z)
    copies += sum(2 + Sum.count(depth // 2, order) for order in SHARED_ORDER.values()) + 2 * 2 * (FF_STEPS - 1)
    copies += sum(3 + (1 if y_first else 2) * Sum.count(depth // 2, order) for y_first, order in SLOT_ORDER.values())
    scratch.update(send=pltpu.SemaphoreType.DMA((copies,)), recv=pltpu.SemaphoreType.DMA((copies,)))
    scratch.update(load=pltpu.SemaphoreType.DMA((18,)))

    arrays, in_tree = jax.tree.flatten(operands)
    out_shapes, out_tree = jax.tree.flatten(outs)
    rooms, room_tree = jax.tree.flatten(scratch)

    def kernel(*refs):
        a, b = len(arrays), len(arrays) + len(out_shapes)
        backward_kernel(
            depth, Named(jax.tree.unflatten(in_tree, refs[:a])), Named(jax.tree.unflatten(out_tree, refs[a:b])),
            Named(jax.tree.unflatten(room_tree, refs[b:])),
        )

    results = pl.pallas_call(
        kernel,
        grid=(12,),
        in_specs=jax.tree.leaves(in_specs),
        out_specs=jax.tree.leaves(out_specs),
        out_shape=out_shapes,
        scratch_shapes=rooms,
        compiler_params=pltpu.CompilerParams(
            collective_id=0, has_side_effects=True, vmem_limit_bytes=67_000_000, dimension_semantics=("arbitrary",)
        ),
        cost_estimate=pl.CostEstimate(flops=20_000_000_000, bytes_accessed=40_000_000, transcendentals=6_000_000),
    )(*arrays)
    return Named(jax.tree.unflatten(out_tree, results))


PIECES = 3


class Gather:
    def __init__(self, place, copies, slots):
        self.slots = slots
        half = slots.shape[1] // 2
        size = half // PIECES
        self.core = copies.new(lambda: slots.at[0], lambda: slots.at[1], place.to_core)

        def rows(side, j):
            return pl.ds(pl.multiple_of(side * half + j * size, 32), size)

        def make(source, target, side, device):
            return [
                copies.new(
                    (lambda j: lambda: slots.at[source, rows(side, j)])(j),
                    (lambda j: lambda: slots.at[target, rows(side, j)])(j), device,
                )
                for j in range(PIECES)
            ]

        self.over_y = make(0, 2, place.x, place.to_y)
        self.over_x = make(2, 2, place.x, place.to_x)
        self.near = make(2, 3, place.x, place.to_core)
        self.far = make(2, 3, 1 - place.x, place.to_core)

    def start(self):
        for copy in self.over_y:
            copy.start()
        self.core.start()

    def pass_y(self, j):
        self.over_y[j].got()
        self.over_x[j].start()
        self.near[j].start()

    def pass_x(self, j):
        self.over_x[j].got()
        self.far[j].start()

    def ready(self):
        for copy in self.near + self.far:
            copy.got()

    def sent(self):
        for copy in [self.core] + self.over_y + self.over_x + self.near + self.far:
            copy.sent()


def forward_kernel(ins, outs, r):
    place = Place(2)
    step = pl.program_id(0)
    core = place.core
    copies = Copies(r.send, r.recv)
    segs = Tiles(place, ins.segs)
    gather_one = Gather(place, copies, r.wt_one)
    gather_two = Gather(place, copies, r.wt_two)
    tables = [
        copies.new((lambda a: lambda: r.table.at[a])(a), (lambda b: lambda: r.table.at[b])(b), d)
        for a, b, d in ((0, 1, place.to_core), (0, 2, place.to_y), (2, 3, place.to_core))
    ]
    swaps = {}
    tok_swap = copies.new(lambda: ins.tokens.at[1 - core], lambda: r.tok_in.at[core], place.to_core)
    mem_swap = copies.new(lambda: ins.memory.at[1 - core], lambda: r.mem_in.at[core], place.to_core)
    cot_swap = copies.new(lambda: ins.cotangent.at[1 - core], lambda: r.cot_in.at[core], place.to_core)
    assert copies.count == r.send.shape[0], copies.count
    count = [0]

    def load(source, target):
        count[0] += 1
        return pltpu.make_async_copy(source, target, r.load.at[count[0] - 1])

    tok_own = load(ins.tokens.at[core], r.tok_in.at[core])
    mem_own = load(ins.memory.at[core], r.mem_in.at[core])
    cot_own = load(ins.cotangent.at[core], r.cot_in.at[core])

    def load_group(key, value, query, slots):
        return [
            load(source.at[pl.ds(at, size)], slots.at[0, pl.ds(to, size)])
            for source, at, to, size in (
                (key, 0, 0, 128), (value, 0, 128, 128), (key, 128, 256, 64), (value, 128, 320, 64), (query, 0, 384, GROUP)
            )
        ]

    raw_one = load_group(ins.self_key, ins.self_value, ins.self_query, r.wt_one)
    raw_two = load_group(ins.cross_key, ins.cross_value, ins.cross_query, r.wt_two)
    out_one, out_two = load(ins.self_out, r.wo_one), load(ins.cross_out, r.wo_two)
    puts = Named({name: load(getattr(r, name), getattr(outs, name)) for name in vars(outs)})


    def normed(hidden, gain, target):
        for part in range(4):
            rows = slice(part * TILE, (part + 1) * TILE)
            h = hidden[rows, :]
            scale = lax.rsqrt(jnp.mean(h * h, axis=-1, keepdims=True) + NORM_EPS)
            target[:, rows] = jnp.transpose((h * scale * row_of(gain)).astype(BF16))

    def project_out(context, weights, base, target):
        for part in range(2):
            rows = slice(part * HALF, (part + 1) * HALF)
            target[rows, :] = base[rows, :] + dot(jnp.transpose(context[:, rows]), weights[...])

    def cross_keys(slot):
        r.kv_two[slot] = dot(r.wt_two[slot, KV, :], r.mem[...]).astype(BF16)

    plan = {}

    def at(point, *tasks):
        plan.setdefault(point, []).extend(tasks)

    one, two = gather_one, gather_two
    at((0, 0), lambda: one.pass_y(1))
    at((0, 2), lambda: one.pass_y(2))
    at((1, 0), lambda: one.pass_x(0))
    at((1, 1), tables[1].got, tables[2].start)
    at((1, 2), lambda: one.pass_x(1))
    at((2, 0), lambda: two.pass_y(1))
    at((2, 2), lambda: two.pass_x(0))
    at((3, 0), lambda: two.pass_y(2))
    at((3, 2), lambda: two.pass_x(1))
    at((4, 1), lambda: two.pass_x(2))

    def tick(steps, index):
        for k in steps:
            if (k, index) in plan:

                def run(tasks=plan[k, index]):
                    for task in tasks:
                        task()

                pl.when(step == k)(run)

    @pl.when(step == 0)
    def _():
        barrier = pltpu.get_barrier_semaphore()
        for device in (place.to_core, place.to_y, place.to_x):
            pl.semaphore_signal(barrier, inc=1, device_id=device, device_id_type=MESH)
        for copy in raw_one + [tok_own] + raw_two + [mem_own, out_one, out_two, cot_own]:
            copy.start()
        r.table[0] = jnp.zeros_like(r.table[0])
        r.table[0, :HEADS, : ins.table.shape[1]] = ins.table[...]
        for copy in raw_one:
            copy.wait()
        pl.semaphore_wait(barrier, 3)
        tok_swap.start()
        tables[0].start()
        tables[1].start()
        gather_one.start()
        mem_swap.start()
        cot_swap.start()
        tok_own.wait()
        tok_swap.got()
        for half in range(2):
            r.tok[half * HALF : (half + 1) * HALF, :] = r.tok_in[half].astype(F32)
        puts.tok.start()
        one.pass_y(0)
        normed(r.tok, ins.self_gain, r.n_one)
        puts.n_one.start()
        for copy in raw_two:
            copy.wait()
        gather_two.start()

    @pl.when(step == 1)
    def _():
        gather_one.core.got()
        tables[0].got()

    @pl.when(step == 2)
    def _():
        mem_own.wait()
        mem_swap.got()
        for half in range(2):
            r.mem[:, half * HALF : (half + 1) * HALF] = jnp.transpose(r.mem_in[half])
        puts.mem.start()
        cot_own.wait()
        cot_swap.got()
        for half in range(2):
            r.cot[half * HALF : (half + 1) * HALF, :] = r.cot_in[half]
        puts.cot.start()
        gather_two.core.got()
        cross_keys(0)
        cross_keys(1)
        two.pass_y(0)
        one.pass_x(2)
        one.ready()
        puts.wt_one.start()
        tables[2].got()
        puts.table.start()

    slot = step % 4
    rows_at = pl.ds(pl.multiple_of(place.group(slot) * GROUP, 16), GROUP)

    @pl.when(step < 4)
    def _():
        r.qkv_one[slot] = dot(r.wt_one[slot], r.n_one[...]).astype(BF16)
        self_forward(
            r.qkv_one.at[slot, KV], r.qkv_one.at[slot, QS], r.table[slot], ins.hot[...], segs,
            r.ctx_one.at[rows_at], r.lse_one.at[slot], lambda h: tick(range(4), h),
        )

    @pl.when(step == 4)
    def _():
        puts.qkv_one.start()
        puts.ctx_one.start()
        puts.lse_one.start()
        out_one.wait()
        project_out(r.ctx_one, r.wo_one, r.tok, r.first)
        puts.first.start()
        normed(r.first, ins.cross_gain, r.n_two)
        puts.n_two.start()
        key_mask(segs, key_segments(place, ins.memsegs), r.mask)

    @pl.when(step == 6)
    def _():
        two.ready()
        puts.wt_two.start()

    @pl.when(step >= 4)
    def _():
        @pl.when(step >= 6)
        def _():
            cross_keys(slot)

        r.q_two[slot] = dot(r.wt_two[slot, QS, :], r.n_two[...]).astype(BF16)
        cross_forward(
            r.kv_two.at[slot], r.q_two.at[slot], r.mask, r.ctx_two.at[rows_at], r.lse_two.at[slot],
            lambda h: tick(range(4, 8), h),
        )

    @pl.when(step == 7)
    def _():
        out_two.wait()
        project_out(r.ctx_two, r.wo_two, r.first, r.second)
        for put in (puts.second, puts.ctx_two, puts.q_two, puts.kv_two, puts.lse_two):
            put.start()
        gather_one.sent()
        gather_two.sent()
        for copy in tables + [tok_swap, mem_swap, cot_swap]:
            copy.sent()
        for name in vars(outs):
            getattr(puts, name).wait()


def forward_call(operands):
    tokens = operands["tokens"]
    model = tokens.shape[2]
    anywhere = pl.BlockSpec(memory_space=pl.ANY)

    def fixed(array):
        return pl.BlockSpec(array.shape, lambda t: (0,) * array.ndim)

    small = dict(self_gain=fixed, cross_gain=fixed, table=fixed, hot=fixed, memsegs=fixed)
    small.update(segs=lambda a: pl.BlockSpec(memory_space=pltpu.SMEM))
    in_specs = {name: small.get(name, lambda a: anywhere)(a) for name, a in operands.items()}

    def room(*shape, kind=BF16):
        return pltpu.VMEM(shape, kind)

    kept = dict(
        tok=room(BLOCK, model, kind=F32), mem=room(model, BLOCK), cot=room(BLOCK, model), n_one=room(model, BLOCK),
        n_two=room(model, BLOCK), qkv_one=room(4, 3 * GROUP, BLOCK), kv_two=room(4, 2 * GROUP, BLOCK),
        q_two=room(4, GROUP, BLOCK), ctx_one=room(model, BLOCK), ctx_two=room(model, BLOCK),
        lse_one=room(4, 8, BLOCK, kind=F32), lse_two=room(4, 8, BLOCK, kind=F32),
        first=room(BLOCK, model, kind=F32), second=room(BLOCK, model, kind=F32),
        wt_one=room(4, 3 * GROUP, model), wt_two=room(4, 3 * GROUP, model), table=room(4, 8, TILE, kind=F32),
    )
    block = tokens.shape[1:]
    copies = 2 * (1 + 4 * PIECES) + 3 + 3
    scratch = dict(
        kept, tok_in=room(2, *block), mem_in=room(2, *block), cot_in=room(2, *block),
        wo_one=room(model, model), wo_two=room(model, model), mask=room(BLOCK, BLOCK, kind=F32),
        send=pltpu.SemaphoreType.DMA((copies,)), recv=pltpu.SemaphoreType.DMA((copies,)),
        load=pltpu.SemaphoreType.DMA((15 + len(kept),)),
    )
    outs = {name: jax.ShapeDtypeStruct(m.shape, m.dtype) for name, m in kept.items()}
    arrays, in_tree = jax.tree.flatten(operands)
    out_shapes, out_tree = jax.tree.flatten(outs)
    rooms, room_tree = jax.tree.flatten(scratch)

    def kernel(*refs):
        a, b = len(arrays), len(arrays) + len(out_shapes)
        forward_kernel(
            Named(jax.tree.unflatten(in_tree, refs[:a])), Named(jax.tree.unflatten(out_tree, refs[a:b])),
            Named(jax.tree.unflatten(room_tree, refs[b:])),
        )

    results = pl.pallas_call(
        kernel,
        grid=(8,),
        in_specs=jax.tree.leaves(in_specs),
        out_specs=[anywhere] * len(out_shapes),
        out_shape=out_shapes,
        scratch_shapes=rooms,
        compiler_params=pltpu.CompilerParams(
            collective_id=1, has_side_effects=True, vmem_limit_bytes=60_000_000, dimension_semantics=("arbitrary",)
        ),
        cost_estimate=pl.CostEstimate(flops=10_000_000_000, bytes_accessed=40_000_000, transcendentals=6_000_000),
    )(*arrays)
    return Named(jax.tree.unflatten(out_tree, results))


def finish_call(results, devices, buckets):
    plain = {name: a for name, a in results.items() if name not in ("gains", "bias")}
    share = results["gains"].shape[1] // devices
    outs = {name: jax.ShapeDtypeStruct(a.shape, a.dtype) for name, a in plain.items()}
    anywhere = pl.BlockSpec(memory_space=pl.ANY)
    count = len(plain)

    def kernel(gains, bias, *refs):
        sources, (bias_out, *gain_outs), targets = refs[:count], refs[count : count + 4], refs[count + 4 : 2 * count + 4]
        rooms, semaphores = refs[2 * count + 4 : 3 * count + 4], refs[3 * count + 4]
        takes = [pltpu.make_async_copy(s, r, semaphores.at[k]) for k, (s, r) in enumerate(zip(sources, rooms))]
        puts = [pltpu.make_async_copy(r, t, semaphores.at[count + k]) for k, (r, t) in enumerate(zip(rooms, targets))]
        for take in takes:
            take.start()
        bias_out[...] = bias[:HEADS, :buckets]
        first = (lax.axis_index("batch") * lax.axis_size("head") + lax.axis_index("head")) * share
        turned = pltpu.roll(gains[...], gains.shape[1] - first, 1)
        for k, out in enumerate(gain_outs):
            out[...] = jnp.reshape(turned[k : k + 1, :share], (share,))
        for take, put in zip(takes, puts):
            take.wait()
            put.start()
        for put in puts:
            put.wait()

    def fixed(shape):
        return pl.BlockSpec(shape, lambda: (0,) * len(shape))

    small = [jax.ShapeDtypeStruct((HEADS, buckets), F32)] + [jax.ShapeDtypeStruct((share,), F32)] * 3
    bias, *rest = pl.pallas_call(
        kernel,
        in_specs=[fixed(results["gains"].shape), fixed(results["bias"].shape)] + [anywhere] * count,
        out_specs=[fixed(a.shape) for a in small] + [anywhere] * count,
        out_shape=small + list(outs.values()),
        scratch_shapes=[pltpu.VMEM(a.shape, a.dtype) for a in plain.values()] + [pltpu.SemaphoreType.DMA((2 * count,))],
    )(results["gains"], results["bias"], *plain.values())
    return dict(zip(plain, rest[3:]), bias=bias, gain_0=rest[0], gain_1=rest[1], gain_2=rest[2])


def on_device(
    tokens, memory, cotangent, target_segments, memory_segments, self_gain, self_query, self_key,
    self_value, self_out, position_bias, cross_gain, cross_query, cross_key, cross_value, cross_out,
    ff_gain, ff_gate, ff_up, ff_down,
):
    heads_axis, batch_axis = lax.axis_size("head"), lax.axis_size("batch")
    rows, part, model = tokens.shape
    assert part * 2 == BLOCK and rows == 2 and heads_axis == 4
    assert position_bias.shape[1] == HEADS and self_query.shape[1] == GROUP
    one_hot = jnp.asarray(bucket_one_hot(position_bias.shape[0]))

    fwd = forward_call(
        dict(
            tokens=tokens, memory=memory, cotangent=cotangent, segs=target_segments, memsegs=memory_segments, hot=one_hot,
            self_gain=self_gain, cross_gain=cross_gain, table=position_bias.T,
            self_query=self_query.T, self_key=self_key.T, self_value=self_value.T, self_out=self_out,
            cross_query=cross_query.T, cross_key=cross_key.T, cross_value=cross_value.T, cross_out=cross_out,
        )
    )
    done = backward_call(
        batch_axis,
        dict(
            segs=target_segments, memsegs=memory_segments, hot=one_hot, self_gain=self_gain, cross_gain=cross_gain,
            ff_gain=ff_gain, ff_gate=ff_gate, ff_up=ff_up, ff_down=ff_down,
            kv_two=fwd.kv_two, q_two=fwd.q_two, lse_two=fwd.lse_two, wt_two=fwd.wt_two,
            qkv_one=fwd.qkv_one, lse_one=fwd.lse_one, wt_one=fwd.wt_one, table=fwd.table,
            loaded=dict(
                second=fwd.second, cot=fwd.cot, wo_two=cross_out, ctx_two=fwd.ctx_two, n_two=fwd.n_two, mem=fwd.mem,
                first=fwd.first, wo_one=self_out, ctx_one=fwd.ctx_one, n_one=fwd.n_one, tok=fwd.tok,
            ),
        ),
    )
    done = Named(finish_call(vars(done), heads_axis * batch_axis, position_bias.shape[0]))
    return (
        done.layer, done.tokens, done.memory, done.gain_0, done.wq_one, done.wk_one, done.wv_one, done.out_one.T,
        done.bias.T, done.gain_1, done.wq_two, done.wk_two, done.wv_two, done.out_two.T, done.gain_2,
        done.gate.T, done.up.T, done.down.T,
    )


def solution(mesh):
    tokens = P("batch", "head", None)
    rows = P("batch", None)
    columns = P(None, "head")
    split = P("batch", "head")
    every = P(None, ("batch", "head"))
    gain = P(("batch", "head"))
    return jax.shard_map(
        on_device,
        mesh=mesh,
        in_specs=(
            tokens, tokens, tokens, rows, rows, P(), columns, columns, columns, P(), columns, P(),
            columns, columns, columns, P(), P(), P(), P(), P(),
        ),
        out_specs=(
            tokens, tokens, tokens, gain, split, split, split, every, columns, gain,
            split, split, split, every, gain, every, every, every,
        ),
        check_vma=False,
    )
```

```python
import jax
import jax.numpy as jnp
import numpy as np
from jax import lax
from jax.experimental import pallas as pl
from jax.experimental.pallas import tpu as pltpu
from jax.sharding import PartitionSpec as P

NORM_EPS = 1e-06
MASKED = -1e30
BLOCK = 512
TILE = 128
HALF = 256
SIZE = 64
HEADS = 3
GROUP = HEADS * SIZE
F32 = jnp.float32
BF16 = jnp.bfloat16
MESH = pl.DeviceIdType.MESH


def bucket_edges():
    distance = np.arange(1.0, 8192.0)
    far_bucket = 16.0 + np.floor(np.log(np.maximum(distance, 16.0) / 16.0) / np.log(8.0) * 16.0)
    bucket_value = np.where(distance < 16, distance, np.minimum(far_bucket, 31.0))
    return [int(distance[np.argmax(bucket_value >= bucket_level)]) for bucket_level in range(1, 32)]


def bucket_one_hot(buckets):
    ids = np.zeros(2 * TILE, np.int32)
    for edge in bucket_edges():
        ids += np.arange(2 * TILE) >= edge
    assert bucket_edges()[-1] <= TILE + 1
    assert buckets <= TILE and ids[-1] == buckets - 1
    return (np.arange(TILE)[:, None] == ids[None, :]).astype(np.float32)


def dot(left, right):
    return lax.dot_general(left, right, (((1,), (0,)), ((), ())), preferred_element_type=F32)


KEY_AT = ((0, 0), (0, 1), (2, 0))
VALUE_AT = ((1, 0), (1, 1), (2, 1))
QUERY_START = 2 * GROUP


def rows_of(at):
    tile, place = at
    return slice(tile * 128 + place * SIZE, tile * 128 + (place + 1) * SIZE)


def lanes_of(at):
    return slice(at[0] * 128, (at[0] + 1) * 128)


def spread(head_rows, place):
    blank = jnp.zeros_like(head_rows)
    return jnp.concatenate((head_rows, blank) if place == 0 else (blank, head_rows), axis=0)


def bias_tiles(table, index, one_hot):
    by_distance = jnp.dot(
        table, one_hot, precision=lax.Precision.HIGHEST, preferred_element_type=F32
    )[index : index + 1]
    wide = jnp.broadcast_to(by_distance, (TILE, 2 * TILE))
    turned = pltpu.roll(wide, 0, 1, stride=1, stride_axis=0)
    key = lax.broadcasted_iota(jnp.int32, (TILE, TILE), 0)
    query = lax.broadcasted_iota(jnp.int32, (TILE, TILE), 1)
    near = jnp.where(key <= query, turned[:, :TILE], MASKED)
    return near, turned[:, TILE:], by_distance[0, 2 * TILE - 1]


def self_tile(scores, key_tile, query_tile, tiles, seg_ref, base):
    near, next_one, far = tiles
    if key_tile == query_tile:
        return scores + near
    same = seg_ref[base + key_tile] == seg_ref[base + query_tile]
    shift = jnp.where(same, 0.0, MASKED)
    if key_tile == query_tile - 1:
        return scores + next_one + shift
    return scores + (far + shift)


def self_forward(kv, q, table, one_hot, seg_ref, out, lse, tick):
    key_values = jnp.transpose(kv[...])
    for index in range(HEADS):
        rows = slice(index * SIZE, (index + 1) * SIZE)
        keys = key_values[:, lanes_of(KEY_AT[index])]
        query = spread(q[rows, :], KEY_AT[index][1])
        tiles = bias_tiles(table, index, one_hot)
        for half in range(2):
            end = (half + 1) * HALF
            scores = dot(keys[:end], query[:, half * HALF : (half + 1) * HALF])
            columns, totals = [], []
            for part in range(2):
                query_tile = 2 * half + part
                parts = [
                    self_tile(
                        scores[kt * TILE : (kt + 1) * TILE, part * TILE : (part + 1) * TILE],
                        kt, query_tile, tiles, seg_ref, 0,
                    )
                    for kt in range(query_tile + 1)
                ]
                top = jnp.max(parts[0], axis=0, keepdims=True)
                for piece in parts[1:]:
                    top = jnp.maximum(top, jnp.max(piece, axis=0, keepdims=True))
                probs = [jnp.exp(piece - top) for piece in parts]
                total = jnp.sum(probs[0], axis=0, keepdims=True)
                for piece in probs[1:]:
                    total = total + jnp.sum(piece, axis=0, keepdims=True)
                probs = [piece.astype(BF16) for piece in probs]
                if part == 0:
                    probs.append(jnp.zeros((TILE, TILE), BF16))
                columns.append(jnp.concatenate(probs, axis=0))
                totals.append(total)
                lse[index : index + 1, query_tile * TILE : (query_tile + 1) * TILE] = top + jnp.log(total)
            weights = jnp.concatenate(columns, axis=1)
            context = dot(kv[rows_of(VALUE_AT[index]), :end], weights)
            context = context / jnp.concatenate(totals, axis=1)
            out[rows, half * HALF : (half + 1) * HALF] = context.astype(BF16)
        tick(index)


def key_mask(seg_ref, memseg, mask_ref):
    rows = jnp.transpose(jnp.broadcast_to(memseg.astype(F32), (TILE, BLOCK)))
    for tile in range(BLOCK // TILE):
        wanted = seg_ref[tile].astype(F32)
        shift = jnp.where(rows == wanted, 0.0, MASKED)
        mask_ref[:, tile * TILE : (tile + 1) * TILE] = shift.astype(mask_ref.dtype)


def cross_forward(kv, q, mask, out, lse, tick):
    key_values = jnp.transpose(kv[...])
    for index in range(HEADS):
        rows = slice(index * SIZE, (index + 1) * SIZE)
        keys = key_values[:, lanes_of(KEY_AT[index])]
        query = spread(q[rows, :], KEY_AT[index][1])
        for half in range(2):
            lanes = slice(half * HALF, (half + 1) * HALF)
            scores = dot(keys, query[:, lanes]) + mask[:, lanes]
            top = jnp.max(scores, axis=0, keepdims=True)
            probs = jnp.exp(scores - top)
            total = jnp.sum(probs, axis=0, keepdims=True)
            context = dot(kv[rows_of(VALUE_AT[index]), :], probs.astype(BF16)) / total
            out[rows, lanes] = context.astype(BF16)
            lse[index : index + 1, lanes] = top + jnp.log(total)
        tick(index)


def grow(old, new):
    if old is None:
        return new
    shared = old.shape[0]
    if shared == new.shape[0]:
        return old + new
    return jnp.concatenate((old + new[:shared], new[shared:]), axis=0)


def only_lanes(wide, at):
    pair = wide[:, lanes_of(at)]
    lane = lax.broadcasted_iota(jnp.int32, pair.shape, 1)
    keep = lane < SIZE if at[1] == 0 else lane >= SIZE
    return jnp.where(keep, pair, jnp.zeros_like(pair))


def moved(wide, index, place):
    if index < 2:
        assert place == index
        return only_lanes(wide, (0, index))
    part = wide[:, 128:192]
    blank = jnp.zeros_like(part)
    return jnp.concatenate((part, blank) if place == 0 else (blank, part), axis=1)


def attention_back(read, tile_of, skip, note, dq_ref, sums_ref, tick):
    key_values = jnp.transpose(read.kv())
    query_tok = jnp.transpose(read.q(slice(0, GROUP)))
    grad_tok = jnp.transpose(read.do(slice(0, GROUP)))
    sums = [None, None, None]
    for index in range(HEADS):
        rows = slice(index * SIZE, (index + 1) * SIZE)
        k_at, v_at = KEY_AT[index], VALUE_AT[index]
        key_pair, value_pair = key_values[:, lanes_of(k_at)], key_values[:, lanes_of(v_at)]
        query_pair = moved(query_tok, index, k_at[1])
        grad_pair = moved(grad_tok, index, v_at[1])
        query_rows = spread(read.q(rows), k_at[1])
        grad_rows = spread(read.do(rows), v_at[1])
        inner = jnp.sum(read.do(rows).astype(F32) * read.o(rows).astype(F32), axis=0, keepdims=True)
        key_sum = value_sum = None
        for half in range(2):
            end = (half + 1) * HALF if skip else BLOCK
            lanes = slice(half * HALF, (half + 1) * HALF)
            scores = dot(key_pair[:end], query_rows[:, lanes])
            grad_probs = dot(value_pair[:end], grad_rows[:, lanes])
            prob_columns, grad_columns = [], []
            for part in range(2):
                query_tile = 2 * half + part
                cut = slice(query_tile * TILE, (query_tile + 1) * TILE)
                here = slice(part * TILE, (part + 1) * TILE)
                total = read.lse(index, cut)
                probs, grads = [], []
                for kt in range(query_tile + 1 if skip else BLOCK // TILE):
                    there = slice(kt * TILE, (kt + 1) * TILE)
                    prob = jnp.exp(tile_of(scores[there, here], index, kt, query_tile) - total)
                    ds = prob * (grad_probs[there, here] - inner[:, cut])
                    note(index, kt, query_tile, ds)
                    probs.append(prob.astype(BF16))
                    grads.append(ds.astype(BF16))
                if skip and part == 0:
                    probs.append(jnp.zeros((TILE, TILE), BF16))
                    grads.append(jnp.zeros((TILE, TILE), BF16))
                prob_columns.append(jnp.concatenate(probs, axis=0))
                grad_columns.append(jnp.concatenate(grads, axis=0))
            probs = jnp.concatenate(prob_columns, axis=1)
            grads = jnp.concatenate(grad_columns, axis=1)
            value_sum = grow(value_sum, dot(probs, grad_pair[lanes]))
            key_sum = grow(key_sum, dot(grads, query_pair[lanes]))
            dq_ref[rows, lanes] = dot(read.k(index, end), grads).astype(BF16)
        for at, total in ((k_at, key_sum), (v_at, value_sum)):
            sums[at[0]] = total if sums[at[0]] is None else sums[at[0]] + total
        tick(index)
    for tile in range(3):
        sums_ref[:, tile * 128 : (tile + 1) * 128] = sums[tile].astype(BF16)
    sums_ref[:, QUERY_START : QUERY_START + GROUP] = jnp.transpose(dq_ref[...])


def row_of(ref):
    return jnp.reshape(ref[...], (1, ref.shape[0]))


class Tiles:
    def __init__(self, place, ref):
        self.place, self.ref = place, ref

    def __getitem__(self, tile):
        return self.ref[self.place.core, self.place.y * BLOCK + tile * TILE]


def key_segments(place, ref):
    lanes = pl.ds(pl.multiple_of(place.y * BLOCK, BLOCK), BLOCK)
    return jnp.where(place.core == 0, ref[0:1, lanes], ref[1:2, lanes])


class Read:
    def __init__(self, kv, k, q, do, o, lse):
        self.kv, self.k, self.q, self.do, self.o, self.lse = kv, k, q, do, o, lse


class Named:
    def __init__(self, tree):
        for key, value in tree.items():
            setattr(self, key, Named(value) if isinstance(value, dict) else value)


class Copies:
    def __init__(self, send, recv):
        self.send, self.recv, self.count, self.sent = send, recv, 0, []

    def new(self, source, target, device):
        at = self.count
        self.count += 1
        return Copy(self, at, source, target, device)


class Copy:
    def __init__(self, owner, at, source, target, device):
        self.owner, self.at, self.source, self.target, self.device = owner, at, source, target, device

    def make(self):
        return pltpu.make_async_remote_copy(
            src_ref=self.source(), dst_ref=self.target(), send_sem=self.owner.send.at[self.at],
            recv_sem=self.owner.recv.at[self.at], device_id=self.device, device_id_type=MESH,
        )

    def start(self):
        self.make().start()

    def got(self):
        self.make().wait_recv()

    def sent(self):
        self.make().wait_send()

    def done(self):
        self.make().wait()


class Place:
    def __init__(self, depth):
        b, h = lax.axis_index("batch"), lax.axis_index("head")
        self.depth = depth
        self.core, self.y, self.x, self.z = h % 2, h // 2, b % 2, b // 2
        self.to_core = (b, h + 1 - 2 * self.core)
        self.to_y = (b, h + 2 - 4 * self.y)
        self.to_x = (b + 1 - 2 * self.x, h)
        self.to_z = [(lax.rem(self.z + k, depth) * 2 + self.x, h) for k in range(1, depth)]
        self.z0, self.zh, self.far = self.z % 2, self.z // 2, depth // 2
        self.to_z0 = ((self.z + 1 - 2 * self.z0) * 2 + self.x, h)
        self.to_zh = [((lax.rem(self.zh + k, self.far) * 2 + self.z0) * 2 + self.x, h) for k in range(1, self.far)]

    def group(self, slot):
        low, high = slot % 2, slot // 2
        return (self.core + low - 2 * self.core * low) + 2 * (self.y + high - 2 * self.y * high)

    def everyone(self):
        return [self.to_core, self.to_y, self.to_x] + self.to_z


ZH, Z0, X, Y = range(4)


class Sum:
    def __init__(self, place, copies, total, got, order, tiles=()):
        self.place, self.total, self.got, self.order = place, total, got, order
        self.dims = len(total.shape) - 2
        self.stages = []
        for at, axis in enumerate(order):
            room = got[at]
            if at == 0 and tiles:
                assert axis in (X, Y)
                self.stages.append([
                    copies.new(
                        self.source(0, 1, tile), (lambda room, tile: lambda: room.at[tile])(room, tile),
                        place.to_x if axis == X else place.to_y,
                    )
                    for tile in tiles
                ])
                continue
            if axis == ZH:
                stage = [
                    copies.new(self.source(at, k), (lambda room, k: lambda: room.at[k - 1])(room, k), place.to_zh[k - 1])
                    for k in range(1, place.far)
                ]
            else:
                device = (None, place.to_z0, place.to_x, place.to_y)[axis]
                stage = [copies.new(self.source(at, 1), (lambda room: lambda: room)(room), device)]
            self.stages.append(stage)

    @staticmethod
    def rooms(far, dims, order, rows, lanes):
        sizes = (far, 2, 2, 2)
        free = list(range(dims))
        shapes = []
        for axis in order:
            free.remove(axis)
            lead = (far - 1,) if axis == ZH else ()
            shapes.append(lead + tuple(sizes[d] for d in free) + (rows, lanes))
        return shapes

    @staticmethod
    def count(far, order):
        return sum(far - 1 if axis == ZH else 1 for axis in order)

    def mine(self, axis):
        return (self.place.zh, self.place.z0, self.place.x, self.place.y)[axis]

    def source(self, at, k, tile=()):
        def view():
            index = list(tile) + [slice(None)] * (self.dims - len(tile))
            for axis in self.order[:at]:
                index[axis] = self.mine(axis)
            axis = self.order[at]
            index[axis] = lax.rem(self.place.zh + k, self.place.far) if axis == ZH else 1 - self.mine(axis)
            return self.total.at[tuple(index)]

        return view

    def start(self, at):
        for copy in self.stages[at]:
            copy.start()

    def value(self, at, free):
        axis = self.order[at]
        later = sorted(self.order[at + 1 :])
        index = [None] * self.dims
        for done in self.order[: at + 1]:
            index[done] = self.mine(done)
        for d, i in zip(later, free):
            index[d] = i
        got = [self.got[at].at[k] for k in range(self.place.far - 1)] if axis == ZH else [self.got[at]]
        return tuple(index), [g[tuple(free)] if free else g[...] for g in got]

    def add(self, at):
        for copy in self.stages[at]:
            copy.got()
        later = sorted(self.order[at + 1 :])

        def one(free):
            index, got = self.value(at, free)
            if len(got) == 1:
                self.total[index] = self.total[index] + got[0]
            else:
                total = self.total[index].astype(F32)
                for g in got:
                    total = total + g.astype(F32)
                self.total[index] = total.astype(BF16)

        def over(dims, free):
            if not dims:
                one(free)
            elif dims[0] == ZH:

                @pl.loop(0, self.place.far)
                def _(z):
                    over(dims[1:], free + [z])

            else:
                for i in range(2):
                    over(dims[1:], free + [i])

        over(later, [])
        self.start(at + 1)

    def finish(self):
        at = len(self.order) - 1
        for copy in self.stages[at]:
            copy.got()
        index, got = self.value(at, [])
        total = self.total[index].astype(F32)
        for g in got:
            total = total + g.astype(F32)
        return total

    def sent(self):
        for stage in self.stages:
            for copy in stage:
                copy.sent()


def add_loop(target, other):
    inner = target.shape[1:-2]

    @pl.loop(0, target.shape[0])
    def _(z):
        for index in np.ndindex(*inner):
            target[(z, *index)] = target[(z, *index)] + other[(z, *index)]


class Shared:
    def __init__(self, place, copies, room, order, send, pair):
        self.place, self.room, self.from_pair = place, room, pair
        self.sum = Sum(place, copies, room.total, room.got, order)
        self.pair = copies.new(lambda: send, lambda: pair, place.to_core)
        self.swap = copies.new(lambda: room.last.at[1 - place.core], lambda: room.other, place.to_core)

    def enter(self):
        self.pair.got()
        add_loop(self.room.total, self.from_pair)
        self.sum.start(0)

    def last(self):
        total = self.sum.finish()
        rows = total.shape[0] // 2
        self.room.last[0] = total[:rows]
        self.room.last[1] = total[rows:]
        self.swap.start()

    def store(self, out, offset, half):
        self.swap.got()
        lanes = self.room.other.shape[1]
        mine, other = self.room.last[self.place.core], self.room.other[...]
        for which in range(2):
            at = slice(which * half + offset, which * half + offset + lanes)
            out[:, at] = jnp.where(self.place.core == which, mine, other)

    def sent(self):
        self.swap.sent()
        self.sum.sent()


class Tiled(Shared):
    def __init__(self, place, copies, room, order, stage, pair):
        self.place, self.room, self.from_pair = place, room, pair
        self.tiles = [tile_of_steps(place.far, t) for t in range(FF_STEPS)]
        self.sum = Sum(place, copies, room.total, room.got, order, self.tiles)
        self.pairs = [
            copies.new(
                (lambda t: lambda: stage.at[t % stage.shape[0]])(t), (lambda tile: lambda: pair.at[tile])(tile), place.to_core
            )
            for t, tile in enumerate(self.tiles)
        ]
        self.swap = copies.new(lambda: room.last.at[1 - place.core], lambda: room.other, place.to_core)

    def enter_tile(self, t):
        self.pairs[t].got()
        add_loop(self.room.total.at[self.tiles[t]], self.from_pair.at[self.tiles[t]])
        self.sum.stages[0][t].start()


FF_STEPS = 4


def tile_of_steps(far, t):
    return (t // 2, t % 2) if far == 2 else (slice(t * far // FF_STEPS, (t + 1) * far // FF_STEPS),)


def over_rows(left, right):
    return lax.dot_general(left, right, (((1,), (1,)), ((), ())), preferred_element_type=F32)


class Slots:
    def __init__(self, place, copies, room, sends, y_first, order):
        self.place, self.room, self.y_first = place, room, y_first
        self.pair = [copies.new((lambda j: lambda: sends.at[j])(j), (lambda j: lambda: room.pair.at[j])(j), place.to_core) for j in range(2)]
        self.own = Sum(place, copies, room.total.at[0], room.got, order)
        if y_first:
            self.across = copies.new(lambda: room.total.at[1], lambda: room.across, place.to_y)
        else:
            self.far = Sum(place, copies, room.total.at[1], room.far, order)
            self.across = copies.new(lambda: room.chunk, lambda: room.across, place.to_y)

    def enter(self, j):
        self.pair[j].got()
        add_loop(self.room.total.at[j], self.room.pair.at[j])
        if j == 1:
            if self.y_first:
                self.across.start()
            else:
                self.far.start(0)
        elif not self.y_first:
            self.own.start(0)

    def take(self):
        self.across.got()
        add_loop(self.room.total.at[0], self.room.across)
        self.own.start(0)

    def give(self):
        self.room.chunk[...] = self.far.finish().astype(BF16)
        self.across.start()

    def finish(self):
        total = self.own.finish()
        if not self.y_first:
            self.across.got()
            total = total + self.room.across[...].astype(F32)
        return total

    def sent(self):
        self.own.sent()
        self.across.sent()
        if not self.y_first:
            self.far.sent()


SHARED_ORDER = dict(
    gate=(Y, X, Z0, ZH), up=(X, Z0, Y, ZH), down_a=(Y, X, Z0, ZH), down_b=(Z0, X, Y, ZH),
    out_two=(X, Z0, ZH, Y), out_one=(Y, X, Z0, ZH),
)
SLOT_ORDER = dict(
    kv_two=(True, (X, Z0, ZH)), q_two=(True, (X, Z0, ZH)), kv_one=(False, (X, Z0, ZH)), q_one=(True, (Z0, X, ZH))
)
KV = slice(0, 2 * GROUP)
QS = slice(2 * GROUP, 3 * GROUP)


def packed(share):
    return share % 32 == 0


def query_shape(share):
    return (share + share // 2, 128) if packed(share) else (share, GROUP)


def put_query(ref, total):
    share = ref.shape[0]
    if not packed(share):
        ref[...] = total
        return
    ref[:, :128] = total[:share]
    ref[: share // 2, 128:] = total[share:, :64]
    ref[share // 2 :, 128:] = total[share:, 64:]


def put_heads(ref, kv):
    key_out, value_out = ref
    key_out[:, :128] = kv[:, :128]
    key_out[:, 128:] = kv[:, 256:320]
    value_out[:, :128] = kv[:, 128:256]
    value_out[:, 128:] = kv[:, 320:384]


def backward_kernel(depth, ins, outs, r):
    place = Place(depth)
    step = pl.program_id(0)
    core = place.core
    copies = Copies(r.send, r.recv)
    segs = Tiles(place, ins.segs)

    parities, downs = r.gate_stage.shape[0], r.down_stage.shape[0]
    down_stages = [r.down_stage.at[t % downs] for t in range(2)]
    stages = dict(gate=r.gate_stage, up=r.up_stage, down_a=down_stages[0], down_b=down_stages[1])
    shared = Named({
        name: (Tiled if name in ("gate", "up") else Shared)(
            place, copies, getattr(r, name), order, stages.get(name, r.out_send), getattr(r.pairs, name, r.out_pair)
        )
        for name, order in SHARED_ORDER.items()
    })
    slots = Named({
        name: Slots(place, copies, getattr(r, name), r.kv_send if name.startswith("kv") else r.q_send, *way)
        for name, way in SLOT_ORDER.items()
    })
    layer_swap = copies.new(lambda: r.block.at[1 - core], lambda: outs.layer.at[core], place.to_core)
    memory_swap = copies.new(lambda: r.block.at[1 - core], lambda: outs.memory.at[core], place.to_core)
    tokens_swap = copies.new(lambda: r.block.at[1 - core], lambda: outs.tokens.at[core], place.to_core)
    gain_copies = [
        copies.new(lambda: r.gains, (lambda k: lambda: r.gains_got.at[k])(k), d)
        for k, d in enumerate([place.to_core, place.to_y, place.to_x] + place.to_z)
    ]
    bias_copies = [
        copies.new((lambda s: lambda: r.bias.at[s])(s), (lambda k: lambda: r.bias_got.at[k])(k), d)
        for k, (s, d) in enumerate(
            zip([1, 3, 2, 0] + [0] * (depth - 1), [place.to_core, place.to_core, place.to_y, place.to_x] + place.to_z)
        )
    ]
    assert copies.count == r.send.shape[0], copies.count

    loads = []

    def load(source, target):
        loads.append(pltpu.make_async_copy(source, target, r.load.at[len(loads)]))
        return loads[-1]

    i = ins.loaded
    second, wo_two, ctx_two = load(i.second, r.hidden), load(i.wo_two, r.wo), load(i.ctx_two, r.ctx)
    cots = [load(i.cot.at[pl.ds(half * HALF, HALF)], r.block.at[half]) for half in range(2)]
    n_two, mem, first, tok = load(i.n_two, r.n), load(i.mem, r.mem), load(i.first, r.hidden), load(i.tok, r.hidden)
    wo_one, ctx_one, n_one = load(i.wo_one, r.wo), load(i.ctx_one, r.ctx), load(i.n_one, r.n)
    layer_put = load(r.block.at[core], outs.layer.at[core])
    memory_put = load(r.block.at[core], outs.memory.at[core])
    tokens_put = load(r.block.at[core], outs.tokens.at[core])

    def out_products(unit, context, branch):
        lanes = context.shape[0] // 2
        for which, target in ((1 - core, r.out_send), (core, unit.room.total)):
            side = jnp.transpose(context[pl.ds(pl.multiple_of(which * lanes, 16), lanes), :])
            per = branch.shape[0] // 2
            for part in range(2):
                product = dot(branch[part * per : (part + 1) * per, :], side).astype(BF16)
                rows = target.shape[4]
                for piece in range(per // rows):
                    at = part * (per // rows) + piece
                    to = (at // 8, (at // 4) % 2, (at // 2) % 2, at % 2)
                    target[to] = product[piece * rows : (piece + 1) * rows]
            if which is not core:
                unit.pair.start()

    def weight_products(target, left, lanes):
        rows = left.shape[0] // (2 * depth)
        per = left.shape[0]
        for part in range(1):
            product = dot(left[part * per : (part + 1) * per, :], r.dqkv[:, lanes]).astype(BF16)
            for piece in range(per // rows):
                at = part * (per // rows) + piece
                to = (at // 4, (at // 2) % 2, at % 2)
                share = product[piece * rows : (piece + 1) * rows]
                if target.shape[-1] == share.shape[1]:
                    target[to] = share
                else:
                    target[(*to, slice(0, rows))] = share[:, :128]
                    rest = share[:, 128:]
                    target[(*to, slice(rows, rows + rows // 2))] = jnp.concatenate((rest[: rows // 2], rest[rows // 2 :]), axis=1)

    def add_rows(target, lanes, weights, fresh):
        for part in range(1):
            rows = slice(0, BLOCK)
            product = dot(r.dqkv[rows, lanes], weights)

            @pl.when(fresh)
            def _():
                target[rows, :] = product

            @pl.when(jnp.logical_not(fresh))
            def _():
                target[rows, :] = target[rows, :] + product

    def norm_back(hidden, gain, incoming, onto, gain_row, branch):
        total = jnp.zeros((1, hidden.shape[1]), F32)
        for part in range(4):
            rows = slice(part * TILE, (part + 1) * TILE)
            h = hidden[rows, :].astype(F32)
            e = incoming[rows, :]
            scale = lax.rsqrt(jnp.mean(h * h, axis=-1, keepdims=True) + NORM_EPS)
            weighted = e * row_of(gain)
            inner = jnp.mean(weighted * h, axis=-1, keepdims=True)
            result = onto[rows, :] + weighted * scale - h * (scale * scale * scale * inner)
            total = total + jnp.sum(e * h * scale, axis=0, keepdims=True)
            if branch is None:
                r.block[part // 2, (part % 2) * TILE : (part % 2 + 1) * TILE, :] = result.astype(BF16)
            else:
                onto[rows, :] = result
                branch[:, rows] = jnp.transpose(result.astype(BF16))
        r.gains[gain_row : gain_row + 1, :] = total

    plan = {}

    def at(point, *tasks):
        plan.setdefault(point, []).extend(tasks)

    sh, sl = shared, slots
    def when_core(which, *tasks):
        def run():
            for task in tasks:
                task()

        return lambda: pl.when(core == which)(run)

    for t in range(FF_STEPS):
        at((t, 4), sh.gate.pairs[t].start, sh.up.pairs[t].start)
        if t < FF_STEPS - 1:
            at((t + 1, 1), lambda t=t: sh.gate.enter_tile(t), lambda t=t: sh.up.enter_tile(t))
        at((t, 5), when_core(1 - t // 2, (sh.down_a, sh.down_b)[t % 2].pair.start))
    at((2, 2), when_core(0, sh.down_a.enter))
    at((2, 3), when_core(0, sh.down_b.enter))
    at((4, 0), when_core(1, sh.down_a.enter, sh.down_b.enter))
    at((4, 1), sh.out_two.enter)
    at((4, 3), sl.kv_two.pair[1].start, sl.q_two.pair[1].start)
    at((5, 0), lambda: sh.gate.sum.add(0), lambda: sh.up.sum.add(0))
    at((5, 3), lambda: sl.kv_two.enter(1), lambda: sl.q_two.enter(1))
    at((6, 0), lambda: sh.out_two.sum.add(0), lambda: sh.down_b.sum.add(0))
    at((6, 1), lambda: sh.down_a.sum.add(0))
    at((6, 3), sl.kv_two.pair[0].start, sl.q_two.pair[0].start)
    at((7, 0), lambda: sh.up.sum.add(1), lambda: sh.gate.sum.add(1))
    at((7, 2), lambda: sh.out_two.sum.add(1))
    at((7, 3), lambda: sl.kv_two.enter(0), lambda: sl.q_two.enter(0), lambda: sh.down_b.sum.add(1))
    at((7, 4), sl.kv_two.take, lambda: sh.gate.sum.add(2), lambda: sh.down_a.sum.add(1))
    at((8, 0), lambda: sh.out_two.sum.add(2), sh.out_one.enter)
    at((8, 2), sl.q_two.take, lambda: sh.down_a.sum.add(2))
    at((8, 3), sl.kv_one.pair[1].start, sl.q_one.pair[1].start)
    at((9, 0), lambda: sl.kv_two.own.add(0), sh.gate.last)
    at((9, 1), lambda: sh.up.sum.add(2))
    at((9, 2), lambda: sl.q_two.own.add(0))
    at((9, 3), lambda: sl.kv_one.enter(1), lambda: sl.q_one.enter(1), lambda: sh.down_b.sum.add(2), sh.down_a.last)
    at((10, 0), lambda: sl.kv_two.own.add(1), sh.out_two.last)
    at((10, 1), lambda: sh.out_one.sum.add(0), lambda: sl.q_two.own.add(1))
    at((10, 2), sh.up.last, sh.down_b.last)
    at((10, 3), sl.kv_one.pair[0].start, sl.q_one.pair[0].start)
    at((11, 1), lambda: sl.kv_one.far.add(0))
    at((11, 3), lambda: sl.kv_one.enter(0), lambda: sl.q_one.enter(0), lambda: sh.out_one.sum.add(1))

    def tick(steps, index):
        for k in steps:
            if (k, index) in plan:

                def run(tasks=plan[k, index]):
                    for task in tasks:
                        task()

                pl.when(step == k)(run)

    @pl.when(step == 0)
    def _():
        barrier = pltpu.get_barrier_semaphore()
        for device in place.everyone():
            pl.semaphore_signal(barrier, inc=1, device_id=device, device_id_type=MESH)
        for copy in [second] + cots + [wo_two, ctx_two, n_two, mem]:
            copy.start()
        r.gains[...] = jnp.zeros_like(r.gains)
        second.wait()
        for part in range(4):
            rows = slice(part * TILE, (part + 1) * TILE)
            h = r.hidden[rows, :]
            scale = lax.rsqrt(jnp.mean(h * h, axis=-1, keepdims=True) + NORM_EPS)
            r.normed[rows, :] = (h * scale * row_of(ins.ff_gain)).astype(BF16)
            r.acc_a[rows, :] = h
            r.acc_b[rows, :] = jnp.zeros_like(h)
        for part in range(4):
            if part % 2 == 0:
                cots[part // 2].wait()
            rows = slice(part * TILE, (part + 1) * TILE)
            r.branch[:, rows] = jnp.transpose(r.block[part // 2, (part % 2) * TILE : (part % 2 + 1) * TILE, :])
        pl.semaphore_wait(barrier, len(place.everyone()))

    for t in range(parities, FF_STEPS):

        @pl.when(step == t)
        def _(t=t):
            sh.gate.pairs[t - parities].sent()
            sh.up.pairs[t - parities].sent()

    @pl.when(step < FF_STEPS)
    def _():
        root = np.float32(np.sqrt(2.0 / np.pi))
        model = r.normed.shape[1]
        for part in range(2):
            rows = slice(part * HALF, (part + 1) * HALF)
            normed = r.normed[rows, :]
            gate, up = dot(normed, ins.ff_gate[...]), dot(normed, ins.ff_up[...])
            grad = over_rows(r.block[part], ins.ff_down[...])
            square = gate * gate
            half = 0.5 + 0.5 * jnp.tanh(gate * (root + (root * 0.044715) * square))
            gelu = gate * half
            slope = half + gelu * (2.0 - 2.0 * half) * (root + (3.0 * 0.044715 * root) * square)
            activation = (gelu * up).astype(BF16)
            grad_gate = (grad * up * slope).astype(BF16)
            grad_up = (grad * gelu).astype(BF16)
            r.mask[rows, :] = activation
            r.grad_gate[:, rows] = jnp.transpose(grad_gate)
            r.grad_up[:, rows] = jnp.transpose(grad_up)
            r.acc_a[rows, :] = r.acc_a[rows, :] + dot(activation, ins.ff_down[...])
            r.acc_b[rows, :] = r.acc_b[rows, :] + over_rows(grad_gate, ins.ff_gate[...]) + over_rows(grad_up, ins.ff_up[...])
            for point in (2 * part, 2 * part + 1):
                tick(range(FF_STEPS), point)
        lanes = model // 2
        for which, keep in ((1 - core, False), (core, True)):
            right = r.normed[:, pl.ds(pl.multiple_of(which * lanes, 128), lanes)]
            for grads, total, stage in ((r.grad_gate, r.gate.total, r.gate_stage), (r.grad_up, r.up.total, r.up_stage)):
                product = dot(grads[...], right).astype(BF16)
                rows = total.shape[4]
                for piece in range(product.shape[0] // rows):
                    inner = ((piece // 4) % 2, (piece // 2) % 2, piece % 2)
                    share = product[piece * rows : (piece + 1) * rows]
                    if place.far == 2:
                        head = (step // 2, step % 2) if keep else (step % parities,)
                        inner = inner[1:]
                    else:
                        head = (step * (place.far // FF_STEPS) + piece // 8,) if keep else (step % parities, piece // 8)
                    (total if keep else stage)[(*head, *inner)] = share
            if not keep:
                tick(range(FF_STEPS), 4)
        per = model // 2
        for part in range(2):
            product = dot(r.branch[part * per : (part + 1) * per, :], r.mask[...]).astype(BF16)
            for t in range(FF_STEPS):
                total = (r.down_a, r.down_b)[t % 2].total
                for target, mine in ((total, t // 2), (down_stages[t % 2], 1 - t // 2)):

                    @pl.when(jnp.logical_and(step == t, core == mine))
                    def _(target=target, product=product, part=part, t=t, mine=mine):
                        if downs == 1 and t % 2 == 1 and part == 0 and mine != t // 2:
                            sh.down_a.pair.sent()
                        rows = target.shape[4]
                        for piece in range(per // rows):
                            to = part * (per // rows) + piece
                            to = (to // 8, (to // 4) % 2, (to // 2) % 2, to % 2)
                            target[to] = product[piece * rows : (piece + 1) * rows]

        tick(range(FF_STEPS), 5)

    @pl.when(step == FF_STEPS - 1)
    def _():
        total = jnp.zeros((1, r.hidden.shape[1]), F32)
        for part in range(4):
            rows = slice(part * TILE, (part + 1) * TILE)
            block_rows = (part // 2, slice((part % 2) * TILE, (part % 2 + 1) * TILE))
            h, e = r.hidden[rows, :], r.acc_b[rows, :]
            scale = lax.rsqrt(jnp.mean(h * h, axis=-1, keepdims=True) + NORM_EPS)
            weighted = e * row_of(ins.ff_gain)
            inner = jnp.mean(weighted * h, axis=-1, keepdims=True)
            result = r.block[block_rows].astype(F32) + weighted * scale - h * (scale * scale * scale * inner)
            total = total + jnp.sum(e * h * scale, axis=0, keepdims=True)
            r.after[rows, :] = result
            r.branch[:, rows] = jnp.transpose(result.astype(BF16))
            r.block[block_rows] = r.acc_a[rows, :].astype(BF16)
        r.gains[2:3, :] = total
        layer_swap.start()
        layer_put.start()
        sh.gate.enter_tile(FF_STEPS - 1)
        sh.up.enter_tile(FF_STEPS - 1)
        key_mask(segs, key_segments(place, ins.memsegs), r.mask)
        first.start()
        for copy in (wo_two, ctx_two, n_two, mem):
            copy.wait()
        out_products(sh.out_two, r.ctx, r.branch)

    slot = 3 - step % 4
    odd = slot % 2 == 1
    rows_at = pl.ds(pl.multiple_of(place.group(slot) * GROUP, 16), GROUP)

    def slot_products(kv, q, kv_left, q_left):
        @pl.when(odd)
        def _():
            weight_products(r.kv_send.at[slot // 2], kv_left, KV)
            weight_products(r.q_send.at[slot // 2], q_left, QS)

        @pl.when(jnp.logical_not(odd))
        def _():
            weight_products(kv.room.total.at[slot // 2], kv_left, KV)
            weight_products(q.room.total.at[slot // 2], q_left, QS)

    @pl.when(step // 4 == 1)
    def _():
        r.do[...] = dot(r.wo[rows_at, :], r.branch[...]).astype(BF16)
        kv, q, lse = ins.kv_two, ins.q_two, ins.lse_two
        context = r.ctx.at[rows_at, :]
        read = Read(
            lambda: kv[0], lambda h, end: kv[0, rows_of(KEY_AT[h]), :end], lambda rows: q[0, rows, :],
            lambda rows: r.do[rows, :], lambda rows: context[rows, :], lambda h, cut: lse[0, h : h + 1, cut],
        )

        def tile_of(scores, index, kt, qt):
            return scores + r.mask[kt * TILE : (kt + 1) * TILE, qt * TILE : (qt + 1) * TILE].astype(F32)

        attention_back(read, tile_of, False, lambda *a: None, r.dq, r.dqkv, lambda h: tick(range(4, 8), h))
        slot_products(sl.kv_two, sl.q_two, r.mem, r.n)
        tick(range(4, 8), 3)
        add_rows(r.acc_b, KV, ins.wt_two[0, KV, :], step == 4)
        add_rows(r.acc_a, QS, ins.wt_two[0, QS, :], step == 4)

    @pl.when(step == 7)
    def _():
        for copy in (wo_one, ctx_one, n_one):
            copy.start()
        first.wait()
        layer_swap.sent()
        layer_put.wait()
        norm_back(r.hidden, ins.cross_gain, r.acc_a, r.after, 1, r.branch)
        tok.start()
        for part in range(4):
            rows = slice(part * TILE, (part + 1) * TILE)
            r.block[part // 2, (part % 2) * TILE : (part % 2 + 1) * TILE, :] = r.acc_b[rows, :].astype(BF16)
        memory_swap.start()
        memory_put.start()
        for copy in (wo_one, ctx_one, n_one):
            copy.wait()
        sh.out_two.pair.sent()
        out_products(sh.out_one, r.ctx, r.branch)
        for task in plan[7, 4]:
            task()

    @pl.when(step >= 8)
    def _():
        r.do[...] = dot(r.wo[rows_at, :], r.branch[...]).astype(BF16)
        qkv, lse = ins.qkv_one, ins.lse_one
        context = r.ctx.at[rows_at, :]
        read = Read(
            lambda: qkv[0, KV, :], lambda h, end: qkv[0, rows_of(KEY_AT[h]), :end],
            lambda rows: qkv[0, QUERY_START + rows.start : QUERY_START + rows.stop, :],
            lambda rows: r.do[rows, :], lambda rows: context[rows, :], lambda h, cut: lse[0, h : h + 1, cut],
        )
        table, one_hot = ins.table[0], ins.hot[...]
        tiles = [bias_tiles(table, index, one_hot) for index in range(HEADS)]
        kept = {}

        def note(index, kt, qt, ds):
            key = (index, min(qt - kt, 2))
            kept[key] = kept[key] + ds if key in kept else ds

        attention_back(
            read, lambda scores, index, kt, qt: self_tile(scores, kt, qt, tiles[index], segs, 0), True, note,
            r.dq, r.dqkv, lambda h: tick(range(8, 12), h),
        )
        key = lax.broadcasted_iota(jnp.int32, (TILE, TILE), 0)
        query = lax.broadcasted_iota(jnp.int32, (TILE, TILE), 1)
        flip = (key + query == TILE - 1).astype(F32)
        row = lax.broadcasted_iota(jnp.int32, (8, 2 * TILE), 0)
        lane = lax.broadcasted_iota(jnp.int32, (8, 2 * TILE), 1)
        by_distance = jnp.zeros((8, 2 * TILE), F32)
        for index in range(HEADS):
            both = jnp.concatenate((kept[index, 0], kept[index, 1]), axis=1)
            both = jnp.dot(flip, both, precision=lax.Precision.HIGHEST, preferred_element_type=F32)
            turned = jnp.sum(pltpu.roll(both, TILE + 1, 1, stride=1, stride_axis=0), axis=0, keepdims=True)
            far_total = jnp.sum(jnp.sum(kept[index, 2], axis=0, keepdims=True), axis=1, keepdims=True)
            turned = turned + jnp.where(lane[:1] == 2 * TILE - 1, far_total, 0.0)
            by_distance = by_distance + jnp.where(row == index, turned, 0.0)
        r.bias[slot] = lax.dot_general(
            by_distance, one_hot, (((1,), (1,)), ((), ())), precision=lax.Precision.HIGHEST, preferred_element_type=F32
        )
        for k, j in ((8, 1), (10, 0)):

            @pl.when(step == k)
            def _(j=j):
                sl.kv_two.pair[j].sent()
                sl.q_two.pair[j].sent()

        slot_products(sl.kv_one, sl.q_one, r.n, r.n)
        tick(range(8, 12), 3)
        add_rows(r.acc_a, slice(0, 3 * GROUP), ins.wt_one[0], step == 8)

    @pl.when(step == 11)
    def _():
        gains, bias = r.gains, r.bias
        sl.q_one.take()
        memory_swap.sent()
        memory_put.wait()
        tok.wait()
        norm_back(r.hidden, ins.self_gain, r.acc_a, r.after, 0, None)
        tokens_swap.start()
        tokens_put.start()
        gain_copies[0].start()
        bias_copies[0].start()
        bias_copies[1].start()
        sl.kv_one.far.add(1)
        gain_copies[0].done()
        gains[...] = gains[...] + r.gains_got[0]
        bias_copies[0].done()
        bias_copies[1].done()
        bias[0] = bias[0] + r.bias_got[0]
        bias[2] = bias[2] + r.bias_got[1]
        gain_copies[1].start()
        bias_copies[2].start()
        sl.q_one.own.add(0)
        sh.out_one.sum.add(2)
        sl.kv_one.own.add(0)
        put_heads((outs.wk_two, outs.wv_two), sl.kv_two.finish())
        put_query(outs.wq_two, sl.q_two.finish())
        gain_copies[1].done()
        gains[...] = gains[...] + r.gains_got[1]
        bias_copies[2].done()
        bias[0] = bias[0] + r.bias_got[2]
        gain_copies[2].start()
        bias_copies[3].start()
        sl.kv_one.give()
        sl.q_one.own.add(1)
        sh.out_one.last()
        gain_copies[2].done()
        gains[...] = gains[...] + r.gains_got[2]
        bias_copies[3].done()
        bias[0] = bias[0] + r.bias_got[3]
        for k in range(depth - 1):
            gain_copies[3 + k].start()
            bias_copies[4 + k].start()
        sl.kv_one.own.add(1)
        sh.up.store(outs.up, 0, outs.up.shape[1] // 2)
        sh.down_a.store(outs.down, 0, outs.down.shape[1] // 2)
        sh.down_b.store(outs.down, outs.down.shape[1] // 4, outs.down.shape[1] // 2)
        sh.gate.store(outs.gate, 0, outs.gate.shape[1] // 2)
        sh.out_two.store(outs.out_two, 0, outs.out_two.shape[1] // 2)
        sh.out_one.store(outs.out_one, 0, outs.out_one.shape[1] // 2)
        gain_total, bias_total = gains[...], bias[0]
        for k in range(depth - 1):
            gain_copies[3 + k].done()
            bias_copies[4 + k].done()
            gain_total = gain_total + r.gains_got[3 + k]
            bias_total = bias_total + r.bias_got[4 + k]
        outs.gains[...] = gain_total
        outs.bias[...] = bias_total
        put_query(outs.wq_one, sl.q_one.finish())
        put_heads((outs.wk_one, outs.wv_one), sl.kv_one.finish())
        for name in SHARED_ORDER:
            unit = getattr(shared, name)
            unit.sent()
            if name in ("gate", "up"):
                for copy in unit.pairs[-parities:]:
                    copy.sent()
            elif unit is not sh.out_two and (unit is not sh.down_a or downs == 2):
                unit.pair.sent()
        for name in SLOT_ORDER:
            getattr(slots, name).sent()
        for j in range(2):
            sl.kv_one.pair[j].sent()
            sl.q_one.pair[j].sent()
        layer_swap.got()
        memory_swap.got()
        tokens_swap.done()
        tokens_put.wait()


def backward_call(batch_size, operands):
    depth = batch_size // 2
    tight = depth > 4
    once = dict(pipeline_mode=pl.Buffered(1)) if tight else {}
    tok = operands["loaded"]["tok"]
    model = tok.shape[1]
    share = model // batch_size
    anywhere = pl.BlockSpec(memory_space=pl.ANY)

    def fixed(shape):
        return pl.BlockSpec(shape, lambda t: (0,) * len(shape))

    def phase(t):
        c = t // 4
        return (1 - c) * (2 - c) // 2, c * (2 - c), c * (c - 1) // 2

    def early(array):
        def at(t):
            _, cross, own = phase(t)
            return (3 - cross * (t % 4) - 3 * own, 0, 0)

        return pl.BlockSpec((1,) + array.shape[1:], at, **once)

    def late(array):
        return pl.BlockSpec((1,) + array.shape[1:], lambda t: (3 - phase(t)[2] * (t % 4), 0, 0))

    def tile(t):
        return 3 - phase(t)[0] * (3 - t % 4)

    def wide_tile(array):
        return pl.BlockSpec((array.shape[0], array.shape[1] // FF_STEPS), lambda t: (0, tile(t)), **once)

    def deep_tile(array):
        return pl.BlockSpec((array.shape[0] // FF_STEPS, array.shape[1]), lambda t: (tile(t), 0), **once)

    kinds = dict(
        segs=lambda a: pl.BlockSpec(memory_space=pltpu.SMEM), kv_two=early, q_two=early, lse_two=early, wt_two=early,
        qkv_one=late, lse_one=late, wt_one=late, table=late, loaded=lambda a: anywhere,
        ff_gate=wide_tile, ff_up=wide_tile, ff_down=deep_tile,
    )
    in_specs = {
        name: jax.tree.map(kinds.get(name, lambda a: fixed(a.shape)), value) for name, value in operands.items()
    }
    columns = operands["ff_gate"].shape[1]
    made = ("gate", "up", "down_a", "down_b")
    shapes = dict(gate=(columns // (4 * depth), model // 2), down_a=(model // (4 * depth), columns // 4))
    shapes.update(up=shapes["gate"], down_b=shapes["down_a"])
    shapes.update(out_two=(model // (4 * depth), model // 2), out_one=(model // (4 * depth), model // 2))
    tile_room = (2, 2, 2) if depth == 4 else (1, depth // 8, 2, 2, 2)
    block = jax.ShapeDtypeStruct((2, HALF, model), BF16)

    def wide(rows, columns):
        return jax.ShapeDtypeStruct((rows, columns), F32)

    head = wide(share, GROUP)
    outs = dict(
        layer=block, memory=block, tokens=block,
        gate=wide(shapes["gate"][0] // 2, 2 * shapes["gate"][1]), up=wide(shapes["up"][0] // 2, 2 * shapes["up"][1]),
        down=wide(shapes["down_a"][0] // 2, 4 * shapes["down_a"][1]),
        out_two=wide(shapes["out_two"][0] // 2, model), out_one=wide(shapes["out_one"][0] // 2, model),
        wq_two=head, wk_two=head, wv_two=head, wq_one=head, wk_one=head, wv_one=head,
        gains=wide(8, model), bias=wide(8, TILE),
    )
    out_specs = {name: anywhere if s is block else fixed(s.shape) for name, s in outs.items()}

    def room(*shape, kind=BF16):
        return pltpu.VMEM(shape, kind)

    scratch = {}
    for name, order in SHARED_ORDER.items():
        rows, lanes = shapes[name]
        scratch[name] = dict(
            total=room(depth // 2, 2, 2, 2, rows, lanes),
            got=[room(*s) for s in Sum.rooms(depth // 2, 4, order, rows, lanes)],
            last=room(2, rows // 2, lanes, kind=F32), other=room(rows // 2, lanes, kind=F32),
        )
    for name, (y_first, order) in SLOT_ORDER.items():
        piece = (share, 2 * GROUP) if name.startswith("kv") else query_shape(share)
        got = [room(*s) for s in Sum.rooms(depth // 2, 3, order, *piece)]
        both = room(2, depth // 2, 2, 2, *piece)
        scratch[name] = dict(total=both, pair=both, got=got)
        if y_first:
            scratch[name].update(across=room(depth // 2, 2, 2, *piece))
        else:
            scratch[name].update(across=room(*piece), chunk=room(*piece), far=list(got))
    scratch.update(
        pairs={name: room(depth // 2, 2, 2, 2, *shapes[name]) for name in made},
        gate_stage=room(*tile_room, *shapes["gate"]), up_stage=room(*tile_room, *shapes["up"]),
        down_stage=room(1 if tight else 2, depth // 2, 2, 2, 2, *shapes["down_a"]), normed=room(BLOCK, model),
        grad_gate=room(columns // FF_STEPS, BLOCK),
        grad_up=room(columns // FF_STEPS, BLOCK),
        out_send=room(depth // 2, 2, 2, 2, *shapes["out_one"]), out_pair=room(depth // 2, 2, 2, 2, *shapes["out_one"]), kv_send=room(2, depth // 2, 2, 2, share, 2 * GROUP),
        q_send=room(2, depth // 2, 2, 2, *query_shape(share)), block=room(2, HALF, model), branch=room(model, BLOCK),
        acc_a=room(BLOCK, model, kind=F32), acc_b=room(BLOCK, model, kind=F32), dqkv=room(BLOCK, 3 * GROUP),
        dq=room(GROUP, BLOCK), do=room(GROUP, BLOCK), mask=room(BLOCK, columns // FF_STEPS), gains=room(8, model, kind=F32),
        gains_got=room(depth + 2, 8, model, kind=F32), bias=room(4, 8, TILE, kind=F32),
        bias_got=room(depth + 3, 8, TILE, kind=F32),
        after=room(BLOCK, model, kind=F32), hidden=room(BLOCK, model, kind=F32),
        wo=room(model, model), ctx=room(model, BLOCK), n=room(model, BLOCK), mem=room(model, BLOCK),
    )
    z = depth - 1
    copies = 3 + (3 + z) + (4 + z)
    copies += sum(2 + Sum.count(depth // 2, order) for order in SHARED_ORDER.values()) + 2 * 2 * (FF_STEPS - 1)
    copies += sum(3 + (1 if y_first else 2) * Sum.count(depth // 2, order) for y_first, order in SLOT_ORDER.values())
    scratch.update(send=pltpu.SemaphoreType.DMA((copies,)), recv=pltpu.SemaphoreType.DMA((copies,)))
    scratch.update(load=pltpu.SemaphoreType.DMA((18,)))

    arrays, in_tree = jax.tree.flatten(operands)
    out_shapes, out_tree = jax.tree.flatten(outs)
    rooms, room_tree = jax.tree.flatten(scratch)

    def kernel(*refs):
        a, b = len(arrays), len(arrays) + len(out_shapes)
        backward_kernel(
            depth, Named(jax.tree.unflatten(in_tree, refs[:a])), Named(jax.tree.unflatten(out_tree, refs[a:b])),
            Named(jax.tree.unflatten(room_tree, refs[b:])),
        )

    results = pl.pallas_call(
        kernel,
        grid=(12,),
        in_specs=jax.tree.leaves(in_specs),
        out_specs=jax.tree.leaves(out_specs),
        out_shape=out_shapes,
        scratch_shapes=rooms,
        compiler_params=pltpu.CompilerParams(
            collective_id=0, has_side_effects=True, vmem_limit_bytes=67_000_000, dimension_semantics=("arbitrary",)
        ),
        cost_estimate=pl.CostEstimate(flops=20_000_000_000, bytes_accessed=40_000_000, transcendentals=6_000_000),
    )(*arrays)
    return Named(jax.tree.unflatten(out_tree, results))


PIECES = 3


class Gather:
    def __init__(self, place, copies, slots):
        self.slots = slots
        half = slots.shape[1] // 2
        size = half // PIECES
        self.core = copies.new(lambda: slots.at[0], lambda: slots.at[1], place.to_core)

        def rows(side, j):
            return pl.ds(pl.multiple_of(side * half + j * size, 32), size)

        def make(source, target, side, device):
            return [
                copies.new(
                    (lambda j: lambda: slots.at[source, rows(side, j)])(j),
                    (lambda j: lambda: slots.at[target, rows(side, j)])(j), device,
                )
                for j in range(PIECES)
            ]

        self.over_y = make(0, 2, place.x, place.to_y)
        self.over_x = make(2, 2, place.x, place.to_x)
        self.near = make(2, 3, place.x, place.to_core)
        self.far = make(2, 3, 1 - place.x, place.to_core)

    def start(self):
        for copy in self.over_y:
            copy.start()
        self.core.start()

    def pass_y(self, j):
        self.over_y[j].got()
        self.over_x[j].start()
        self.near[j].start()

    def pass_x(self, j):
        self.over_x[j].got()
        self.far[j].start()

    def ready(self):
        for copy in self.near + self.far:
            copy.got()

    def sent(self):
        for copy in [self.core] + self.over_y + self.over_x + self.near + self.far:
            copy.sent()


def forward_kernel(ins, outs, r):
    place = Place(2)
    step = pl.program_id(0)
    core = place.core
    copies = Copies(r.send, r.recv)
    segs = Tiles(place, ins.segs)
    gather_one = Gather(place, copies, r.wt_one)
    gather_two = Gather(place, copies, r.wt_two)
    tables = [
        copies.new((lambda a: lambda: r.table.at[a])(a), (lambda b: lambda: r.table.at[b])(b), d)
        for a, b, d in ((0, 1, place.to_core), (0, 2, place.to_y), (2, 3, place.to_core))
    ]
    swaps = {}
    tok_swap = copies.new(lambda: ins.tokens.at[1 - core], lambda: r.tok_in.at[core], place.to_core)
    mem_swap = copies.new(lambda: ins.memory.at[1 - core], lambda: r.mem_in.at[core], place.to_core)
    cot_swap = copies.new(lambda: ins.cotangent.at[1 - core], lambda: r.cot_in.at[core], place.to_core)
    assert copies.count == r.send.shape[0], copies.count
    count = [0]

    def load(source, target):
        count[0] += 1
        return pltpu.make_async_copy(source, target, r.load.at[count[0] - 1])

    tok_own = load(ins.tokens.at[core], r.tok_in.at[core])
    mem_own = load(ins.memory.at[core], r.mem_in.at[core])
    cot_own = load(ins.cotangent.at[core], r.cot_in.at[core])

    def load_group(key, value, query, slots):
        return [
            load(source.at[pl.ds(at, size)], slots.at[0, pl.ds(to, size)])
            for source, at, to, size in (
                (key, 0, 0, 128), (value, 0, 128, 128), (key, 128, 256, 64), (value, 128, 320, 64), (query, 0, 384, GROUP)
            )
        ]

    raw_one = load_group(ins.self_key, ins.self_value, ins.self_query, r.wt_one)
    raw_two = load_group(ins.cross_key, ins.cross_value, ins.cross_query, r.wt_two)
    out_one, out_two = load(ins.self_out, r.wo_one), load(ins.cross_out, r.wo_two)
    puts = Named({name: load(getattr(r, name), getattr(outs, name)) for name in vars(outs)})


    def normed(hidden, gain, target):
        for part in range(4):
            rows = slice(part * TILE, (part + 1) * TILE)
            h = hidden[rows, :]
            scale = lax.rsqrt(jnp.mean(h * h, axis=-1, keepdims=True) + NORM_EPS)
            target[:, rows] = jnp.transpose((h * scale * row_of(gain)).astype(BF16))

    def project_out(context, weights, base, target):
        for part in range(2):
            rows = slice(part * HALF, (part + 1) * HALF)
            target[rows, :] = base[rows, :] + dot(jnp.transpose(context[:, rows]), weights[...])

    def cross_keys(slot):
        r.kv_two[slot] = dot(r.wt_two[slot, KV, :], r.mem[...]).astype(BF16)

    plan = {}

    def at(point, *tasks):
        plan.setdefault(point, []).extend(tasks)

    one, two = gather_one, gather_two
    at((0, 0), lambda: one.pass_y(1))
    at((0, 2), lambda: one.pass_y(2))
    at((1, 0), lambda: one.pass_x(0))
    at((1, 1), tables[1].got, tables[2].start)
    at((1, 2), lambda: one.pass_x(1))
    at((2, 0), lambda: two.pass_y(1))
    at((2, 2), lambda: two.pass_x(0))
    at((3, 0), lambda: two.pass_y(2))
    at((3, 2), lambda: two.pass_x(1))
    at((4, 1), lambda: two.pass_x(2))

    def tick(steps, index):
        for k in steps:
            if (k, index) in plan:

                def run(tasks=plan[k, index]):
                    for task in tasks:
                        task()

                pl.when(step == k)(run)

    @pl.when(step == 0)
    def _():
        barrier = pltpu.get_barrier_semaphore()
        for device in (place.to_core, place.to_y, place.to_x):
            pl.semaphore_signal(barrier, inc=1, device_id=device, device_id_type=MESH)
        for copy in raw_one + [tok_own] + raw_two + [mem_own, out_one, out_two, cot_own]:
            copy.start()
        r.table[0] = jnp.zeros_like(r.table[0])
        r.table[0, :HEADS, : ins.table.shape[1]] = ins.table[...]
        for copy in raw_one:
            copy.wait()
        pl.semaphore_wait(barrier, 3)
        tok_swap.start()
        tables[0].start()
        tables[1].start()
        gather_one.start()
        mem_swap.start()
        cot_swap.start()
        tok_own.wait()
        tok_swap.got()
        for half in range(2):
            r.tok[half * HALF : (half + 1) * HALF, :] = r.tok_in[half].astype(F32)
        puts.tok.start()
        one.pass_y(0)
        normed(r.tok, ins.self_gain, r.n_one)
        puts.n_one.start()
        for copy in raw_two:
            copy.wait()
        gather_two.start()

    @pl.when(step == 1)
    def _():
        gather_one.core.got()
        tables[0].got()

    @pl.when(step == 2)
    def _():
        mem_own.wait()
        mem_swap.got()
        for half in range(2):
            r.mem[:, half * HALF : (half + 1) * HALF] = jnp.transpose(r.mem_in[half])
        puts.mem.start()
        cot_own.wait()
        cot_swap.got()
        for half in range(2):
            r.cot[half * HALF : (half + 1) * HALF, :] = r.cot_in[half]
        puts.cot.start()
        gather_two.core.got()
        cross_keys(0)
        cross_keys(1)
        two.pass_y(0)
        one.pass_x(2)
        one.ready()
        puts.wt_one.start()
        tables[2].got()
        puts.table.start()

    slot = step % 4
    rows_at = pl.ds(pl.multiple_of(place.group(slot) * GROUP, 16), GROUP)

    @pl.when(step < 4)
    def _():
        r.qkv_one[slot] = dot(r.wt_one[slot], r.n_one[...]).astype(BF16)
        self_forward(
            r.qkv_one.at[slot, KV], r.qkv_one.at[slot, QS], r.table[slot], ins.hot[...], segs,
            r.ctx_one.at[rows_at], r.lse_one.at[slot], lambda h: tick(range(4), h),
        )

    @pl.when(step == 4)
    def _():
        puts.qkv_one.start()
        puts.ctx_one.start()
        puts.lse_one.start()
        out_one.wait()
        project_out(r.ctx_one, r.wo_one, r.tok, r.first)
        puts.first.start()
        normed(r.first, ins.cross_gain, r.n_two)
        puts.n_two.start()
        key_mask(segs, key_segments(place, ins.memsegs), r.mask)

    @pl.when(step == 6)
    def _():
        two.ready()
        puts.wt_two.start()

    @pl.when(step >= 4)
    def _():
        @pl.when(step >= 6)
        def _():
            cross_keys(slot)

        r.q_two[slot] = dot(r.wt_two[slot, QS, :], r.n_two[...]).astype(BF16)

        @pl.when(step == 7)
        def _():
            puts.q_two.start()
            puts.kv_two.start()

        cross_forward(
            r.kv_two.at[slot], r.q_two.at[slot], r.mask, r.ctx_two.at[rows_at], r.lse_two.at[slot],
            lambda h: tick(range(4, 8), h),
        )

    @pl.when(step == 7)
    def _():
        out_two.wait()
        project_out(r.ctx_two, r.wo_two, r.first, r.second)
        for put in (puts.second, puts.ctx_two, puts.lse_two):
            put.start()
        gather_one.sent()
        gather_two.sent()
        for copy in tables + [tok_swap, mem_swap, cot_swap]:
            copy.sent()
        for name in vars(outs):
            getattr(puts, name).wait()


def forward_call(operands):
    tokens = operands["tokens"]
    model = tokens.shape[2]
    anywhere = pl.BlockSpec(memory_space=pl.ANY)

    def fixed(array):
        return pl.BlockSpec(array.shape, lambda t: (0,) * array.ndim)

    small = dict(self_gain=fixed, cross_gain=fixed, table=fixed, hot=fixed, memsegs=fixed)
    small.update(segs=lambda a: pl.BlockSpec(memory_space=pltpu.SMEM))
    in_specs = {name: small.get(name, lambda a: anywhere)(a) for name, a in operands.items()}

    def room(*shape, kind=BF16):
        return pltpu.VMEM(shape, kind)

    kept = dict(
        tok=room(BLOCK, model, kind=F32), mem=room(model, BLOCK), cot=room(BLOCK, model), n_one=room(model, BLOCK),
        n_two=room(model, BLOCK), qkv_one=room(4, 3 * GROUP, BLOCK), kv_two=room(4, 2 * GROUP, BLOCK),
        q_two=room(4, GROUP, BLOCK), ctx_one=room(model, BLOCK), ctx_two=room(model, BLOCK),
        lse_one=room(4, 8, BLOCK, kind=F32), lse_two=room(4, 8, BLOCK, kind=F32),
        first=room(BLOCK, model, kind=F32), second=room(BLOCK, model, kind=F32),
        wt_one=room(4, 3 * GROUP, model), wt_two=room(4, 3 * GROUP, model), table=room(4, 8, TILE, kind=F32),
    )
    block = tokens.shape[1:]
    copies = 2 * (1 + 4 * PIECES) + 3 + 3
    scratch = dict(
        kept, tok_in=room(2, *block), mem_in=room(2, *block), cot_in=room(2, *block),
        wo_one=room(model, model), wo_two=room(model, model), mask=room(BLOCK, BLOCK, kind=F32),
        send=pltpu.SemaphoreType.DMA((copies,)), recv=pltpu.SemaphoreType.DMA((copies,)),
        load=pltpu.SemaphoreType.DMA((15 + len(kept),)),
    )
    outs = {name: jax.ShapeDtypeStruct(m.shape, m.dtype) for name, m in kept.items()}
    arrays, in_tree = jax.tree.flatten(operands)
    out_shapes, out_tree = jax.tree.flatten(outs)
    rooms, room_tree = jax.tree.flatten(scratch)

    def kernel(*refs):
        a, b = len(arrays), len(arrays) + len(out_shapes)
        forward_kernel(
            Named(jax.tree.unflatten(in_tree, refs[:a])), Named(jax.tree.unflatten(out_tree, refs[a:b])),
            Named(jax.tree.unflatten(room_tree, refs[b:])),
        )

    results = pl.pallas_call(
        kernel,
        grid=(8,),
        in_specs=jax.tree.leaves(in_specs),
        out_specs=[anywhere] * len(out_shapes),
        out_shape=out_shapes,
        scratch_shapes=rooms,
        compiler_params=pltpu.CompilerParams(
            collective_id=1, has_side_effects=True, vmem_limit_bytes=60_000_000, dimension_semantics=("arbitrary",)
        ),
        cost_estimate=pl.CostEstimate(flops=10_000_000_000, bytes_accessed=40_000_000, transcendentals=6_000_000),
    )(*arrays)
    return Named(jax.tree.unflatten(out_tree, results))


def finish_call(results, devices, buckets):
    plain = {name: a for name, a in results.items() if name not in ("gains", "bias")}
    share = results["gains"].shape[1] // devices
    outs = {name: jax.ShapeDtypeStruct(a.shape, a.dtype) for name, a in plain.items()}
    anywhere = pl.BlockSpec(memory_space=pl.ANY)
    count = len(plain)

    def kernel(gains, bias, *refs):
        sources, (bias_out, *gain_outs), targets = refs[:count], refs[count : count + 4], refs[count + 4 : 2 * count + 4]
        rooms, semaphores = refs[2 * count + 4 : 3 * count + 4], refs[3 * count + 4]
        takes = [pltpu.make_async_copy(s, r, semaphores.at[k]) for k, (s, r) in enumerate(zip(sources, rooms))]
        puts = [pltpu.make_async_copy(r, t, semaphores.at[count + k]) for k, (r, t) in enumerate(zip(rooms, targets))]
        for take in takes:
            take.start()
        bias_out[...] = bias[:HEADS, :buckets]
        first = (lax.axis_index("batch") * lax.axis_size("head") + lax.axis_index("head")) * share
        turned = pltpu.roll(gains[...], gains.shape[1] - first, 1)
        for k, out in enumerate(gain_outs):
            out[...] = jnp.reshape(turned[k : k + 1, :share], (share,))
        for take, put in zip(takes, puts):
            take.wait()
            put.start()
        for put in puts:
            put.wait()

    def fixed(shape):
        return pl.BlockSpec(shape, lambda: (0,) * len(shape))

    small = [jax.ShapeDtypeStruct((HEADS, buckets), F32)] + [jax.ShapeDtypeStruct((share,), F32)] * 3
    bias, *rest = pl.pallas_call(
        kernel,
        in_specs=[fixed(results["gains"].shape), fixed(results["bias"].shape)] + [anywhere] * count,
        out_specs=[fixed(a.shape) for a in small] + [anywhere] * count,
        out_shape=small + list(outs.values()),
        scratch_shapes=[pltpu.VMEM(a.shape, a.dtype) for a in plain.values()] + [pltpu.SemaphoreType.DMA((2 * count,))],
    )(results["gains"], results["bias"], *plain.values())
    return dict(zip(plain, rest[3:]), bias=bias, gain_0=rest[0], gain_1=rest[1], gain_2=rest[2])


def on_device(
    tokens, memory, cotangent, target_segments, memory_segments, self_gain, self_query, self_key,
    self_value, self_out, position_bias, cross_gain, cross_query, cross_key, cross_value, cross_out,
    ff_gain, ff_gate, ff_up, ff_down,
):
    heads_axis, batch_axis = lax.axis_size("head"), lax.axis_size("batch")
    rows, part, model = tokens.shape
    assert part * 2 == BLOCK and rows == 2 and heads_axis == 4
    assert position_bias.shape[1] == HEADS and self_query.shape[1] == GROUP
    one_hot = jnp.asarray(bucket_one_hot(position_bias.shape[0]))

    fwd = forward_call(
        dict(
            tokens=tokens, memory=memory, cotangent=cotangent, segs=target_segments, memsegs=memory_segments, hot=one_hot,
            self_gain=self_gain, cross_gain=cross_gain, table=position_bias.T,
            self_query=self_query.T, self_key=self_key.T, self_value=self_value.T, self_out=self_out,
            cross_query=cross_query.T, cross_key=cross_key.T, cross_value=cross_value.T, cross_out=cross_out,
        )
    )
    done = backward_call(
        batch_axis,
        dict(
            segs=target_segments, memsegs=memory_segments, hot=one_hot, self_gain=self_gain, cross_gain=cross_gain,
            ff_gain=ff_gain, ff_gate=ff_gate, ff_up=ff_up, ff_down=ff_down,
            kv_two=fwd.kv_two, q_two=fwd.q_two, lse_two=fwd.lse_two, wt_two=fwd.wt_two,
            qkv_one=fwd.qkv_one, lse_one=fwd.lse_one, wt_one=fwd.wt_one, table=fwd.table,
            loaded=dict(
                second=fwd.second, cot=fwd.cot, wo_two=cross_out, ctx_two=fwd.ctx_two, n_two=fwd.n_two, mem=fwd.mem,
                first=fwd.first, wo_one=self_out, ctx_one=fwd.ctx_one, n_one=fwd.n_one, tok=fwd.tok,
            ),
        ),
    )
    done = Named(finish_call(vars(done), heads_axis * batch_axis, position_bias.shape[0]))
    return (
        done.layer, done.tokens, done.memory, done.gain_0, done.wq_one, done.wk_one, done.wv_one, done.out_one.T,
        done.bias.T, done.gain_1, done.wq_two, done.wk_two, done.wv_two, done.out_two.T, done.gain_2,
        done.gate.T, done.up.T, done.down.T,
    )


def solution(mesh):
    tokens = P("batch", "head", None)
    rows = P("batch", None)
    columns = P(None, "head")
    split = P("batch", "head")
    every = P(None, ("batch", "head"))
    gain = P(("batch", "head"))
    return jax.shard_map(
        on_device,
        mesh=mesh,
        in_specs=(
            tokens, tokens, tokens, rows, rows, P(), columns, columns, columns, P(), columns, P(),
            columns, columns, columns, P(), P(), P(), P(), P(),
        ),
        out_specs=(
            tokens, tokens, tokens, gain, split, split, split, every, columns, gain,
            split, split, split, every, gain, every, every, every,
        ),
        check_vma=False,
    )
```
